32 devices in a mesh: dp: 8 (over y, x, core), mp: 4 (over z).
Axes of the slice: x: 2, y: 2, z: 4, core: 2. Of those that a mesh axis runs over, the one named last changes fastest.
Arguments:
- tokens_in: bfloat16 [8192, 2048], P('dp'), may hold values from -6 to 6
- cotangent: bfloat16 [8192, 2048], P('dp'), may hold values from -6 to 6
- seq_lengths: int32 [8, 4], P('dp'), may hold values from 0 to 512, as said below
- qkv_weight: bfloat16 [2, 2048, 6144], P(None, 'dp', 'mp'), may hold values from -0.125 to 0.125
- dense_weight: bfloat16 [2, 2048, 2048], P(None, 'mp', 'dp'), may hold values from -0.5 to 0.5
- up_weight: bfloat16 [2, 2048, 8192], P(None, 'dp', 'mp'), may hold values from -0.125 to 0.125
- down_weight: bfloat16 [2, 8192, 2048], P(None, 'mp', 'dp'), may hold values from -0.0625 to 0.0625
- qkv_bias: bfloat16 [2, 48, 128], P(None, 'mp', 'dp'), may hold values from -3 to 3
- up_bias: bfloat16 [2, 64, 128], P(None, 'mp', 'dp'), may hold values from -3 to 3
- vectors: bfloat16 [2, 6, 2048], P(None, None, 'dp')
- qkv_weight_first: float32 [2, 2048, 6144], P(None, 'dp', 'mp'), may hold values from -96 to 96
- dense_weight_first: float32 [2, 2048, 2048], P(None, 'mp', 'dp'), may hold values from -48 to 48
- up_weight_first: float32 [2, 2048, 8192], P(None, 'dp', 'mp'), may hold values from -16 to 16
- down_weight_first: float32 [2, 8192, 2048], P(None, 'mp', 'dp'), may hold values from -40 to 40
- qkv_bias_first: float32 [2, 48, 128], P(None, 'mp', 'dp'), may hold values from -128 to 128
- up_bias_first: float32 [2, 64, 128], P(None, 'mp', 'dp'), may hold values from -16 to 16
- vectors_first: float32 [2, 6, 2048], P(None, None, 'dp'), may hold values from -128 to 128
- qkv_weight_second: float32 [2, 2048, 6144], P(None, 'dp', 'mp'), may hold values from 1720.32 to 6799.36
- dense_weight_second: float32 [2, 2048, 2048], P(None, 'mp', 'dp'), may hold values from 450.56 to 1802.24
- up_weight_second: float32 [2, 2048, 8192], P(None, 'dp', 'mp'), may hold values from 61.44 to 245.76
- down_weight_second: float32 [2, 8192, 2048], P(None, 'mp', 'dp'), may hold values from 327.68 to 1310.72
- qkv_bias_second: float32 [2, 48, 128], P(None, 'mp', 'dp'), may hold values from 4096 to 16384
- up_bias_second: float32 [2, 64, 128], P(None, 'mp', 'dp'), may hold values from 39.3216 to 155.648
- vectors_second: float32 [2, 6, 2048], P(None, None, 'dp'), may hold values from 2293.76 to 9256.96
Outputs:
- block_output: bfloat16 [8192, 2048], P('dp')
- input_grad: float32 [8192, 2048], P('dp')
- qkv_weight_grad: float32 [2, 2048, 6144], P(None, 'dp', 'mp')
- qkv_weight_first_new: float32 [2, 2048, 6144], P(None, 'dp', 'mp')
- qkv_weight_second_new: float32 [2, 2048, 6144], P(None, 'dp', 'mp')
- qkv_weight_step: float32 [2, 2048, 6144], P(None, 'dp', 'mp')
- dense_weight_grad: float32 [2, 2048, 2048], P(None, 'mp', 'dp')
- dense_weight_first_new: float32 [2, 2048, 2048], P(None, 'mp', 'dp')
- dense_weight_second_new: float32 [2, 2048, 2048], P(None, 'mp', 'dp')
- dense_weight_step: float32 [2, 2048, 2048], P(None, 'mp', 'dp')
- up_weight_grad: float32 [2, 2048, 8192], P(None, 'dp', 'mp')
- up_weight_first_new: float32 [2, 2048, 8192], P(None, 'dp', 'mp')
- up_weight_second_new: float32 [2, 2048, 8192], P(None, 'dp', 'mp')
- up_weight_step: float32 [2, 2048, 8192], P(None, 'dp', 'mp')
- down_weight_grad: float32 [2, 8192, 2048], P(None, 'mp', 'dp')
- down_weight_first_new: float32 [2, 8192, 2048], P(None, 'mp', 'dp')
- down_weight_second_new: float32 [2, 8192, 2048], P(None, 'mp', 'dp')
- down_weight_step: float32 [2, 8192, 2048], P(None, 'mp', 'dp')
- qkv_bias_grad: float32 [2, 48, 128], P(None, 'mp', 'dp')
- qkv_bias_first_new: float32 [2, 48, 128], P(None, 'mp', 'dp')
- qkv_bias_second_new: float32 [2, 48, 128], P(None, 'mp', 'dp')
- qkv_bias_step: float32 [2, 48, 128], P(None, 'mp', 'dp')
- up_bias_grad: float32 [2, 64, 128], P(None, 'mp', 'dp')
- up_bias_first_new: float32 [2, 64, 128], P(None, 'mp', 'dp')
- up_bias_second_new: float32 [2, 64, 128], P(None, 'mp', 'dp')
- up_bias_step: float32 [2, 64, 128], P(None, 'mp', 'dp')
- vectors_grad: float32 [2, 6, 2048], P(None, None, 'dp')
- updated_vector_first_moment: float32 [2, 6, 2048], P(None, None, 'dp')
- vectors_second_new: float32 [2, 6, 2048], P(None, None, 'dp')
- vectors_step: float32 [2, 6, 2048], P(None, None, 'dp')
The draws below stay inside these ranges and needn't reach their ends.
Inputs may be any that keep to these rules, and one draw needn't show every extreme that they name: `seq_lengths`: A zero marks an empty slot; the lengths of one index of dp sum to at most 1024, and in every draw some index of dp sums to exactly 1024 with sequences of 512; any other length lies between 64 and 512.
All inputs are finite; a program needn't handle non-finite values.
Results may differ from the reference program's by a relative error of at most 0.012.
Values may be sent and summed in bfloat16 or wider, within the bound.
A program may use at most 384 MiB of HBM per device.

```python
import math
import jax
import jax.numpy as jnp
from jax import lax

D = 2048
HEADS = 8
HD = 256
ROT = 64
FF = 8192
LAYERS = 2
CAP = 1024
MAXLEN = 512
SLOTS = 4
BROW = 128
ADAM_STEP = 10
TOKENS = 8192
N_DP = 8


def draw_seq_lengths(key, part):
    key_count = jax.random.fold_in(key, 11)
    key_length = jax.random.fold_in(key, 12)
    key_full = jax.random.fold_in(key, 13)
    least = CAP // MAXLEN
    counts = jax.random.randint(key_count, (N_DP, 1), least, SLOTS + 1).astype(jnp.int32)
    full = jax.random.randint(key_full, (), 0, N_DP).astype(jnp.int32)
    device_row = jnp.arange(N_DP, dtype=jnp.int32)[:, None]
    counts = jnp.where(device_row == full, least, counts).astype(jnp.int32)
    limit = jnp.minimum(MAXLEN, CAP // counts).astype(jnp.int32)
    shortest = MAXLEN // 8
    raw = jax.random.randint(key_length, (N_DP, SLOTS), 0, 1 << 20).astype(jnp.int32)
    sequence_length_list = shortest + raw % (limit - shortest + 1)
    sequence_length_list = jnp.where(device_row == full, MAXLEN, sequence_length_list)
    slot = jnp.arange(SLOTS, dtype=jnp.int32)[None, :]
    return jnp.where(slot < counts, sequence_length_list, 0).astype(jnp.int32)


def draw_vectors(key, part):
    noise = jnp.clip(jax.random.normal(key, (LAYERS, 6, D), jnp.float32), -2.5, 2.5)
    kind = jnp.arange(6, dtype=jnp.int32)[None, :, None]
    is_gain = (kind == 0) | (kind == 2)
    return jnp.where(is_gain, 1.0 + 0.3 * noise, 0.3 * noise).astype(jnp.bfloat16)


def block_scale(own_key, extent, shards, smallest, largest):
    def one(axis_at, blocks):
        draws = jax.random.uniform(jax.random.fold_in(jax.random.fold_in(own_key, 6), axis_at), (blocks,), jnp.float32, smallest / len(shards), largest / len(shards))
        return jnp.repeat(jnp.exp(draws), extent[axis_at] // blocks).reshape((-1,) + (1,) * (len(extent) - axis_at - 1))

    loudness = one(*shards[0])
    for cut in shards[1:]:
        loudness = loudness * one(*cut)
    return loudness


def scatter_about(key, extent, scale, reach, split=(), kind=jnp.bfloat16):
    gain = block_scale(key, extent, split, -0.22, 0.18) if split else 1.0
    entries = jax.random.normal(key, extent, jnp.float32) * scale * gain
    return jnp.minimum(jnp.maximum(entries, -reach), reach).astype(kind)


def setup_inputs(seed: int = 0) -> dict:
    arg_keys = jax.random.split(jax.random.key(seed), 25)
    tokens_in = scatter_about(arg_keys[0], (TOKENS, D), 1.0, 6.0, ((0, 8),))
    cotangent = scatter_about(arg_keys[1], (TOKENS, D), 1.0, 6.0, ((0, 8),))
    seq_lengths = draw_seq_lengths(jax.random.fold_in(arg_keys[24], 71), 0)
    qkv_weight = scatter_about(arg_keys[3], (LAYERS, D, 3 * D), D ** -0.5, 0.125, ((1, 8), (2, 4)))
    dense_weight = scatter_about(arg_keys[4], (LAYERS, D, D), (D // 16) ** -0.5, 0.5, ((1, 4), (2, 8)))
    up_weight = scatter_about(arg_keys[5], (LAYERS, D, FF), D ** -0.5, 0.125, ((1, 8), (2, 4)))
    down_weight = scatter_about(arg_keys[6], (LAYERS, FF, D), FF ** -0.5, 0.0625, ((1, 4), (2, 8)))
    qkv_bias = scatter_about(arg_keys[7], (LAYERS, 3 * D // BROW, BROW), 0.5, 3.0, ((1, 4), (2, 8)))
    up_bias = scatter_about(arg_keys[8], (LAYERS, FF // BROW, BROW), 0.5, 3.0, ((1, 4), (2, 8)))
    vectors = draw_vectors(jax.random.fold_in(arg_keys[24], 71), 0)
    qkv_weight_first = scatter_about(arg_keys[10], (LAYERS, D, 3 * D), (0.17 * TOKENS ** 0.5), 96.0, ((1, 8), (2, 4)), jnp.float32)
    dense_weight_first = scatter_about(arg_keys[11], (LAYERS, D, D), (0.09 * TOKENS ** 0.5), 48.0, ((1, 4), (2, 8)), jnp.float32)
    up_weight_first = scatter_about(arg_keys[12], (LAYERS, D, FF), (0.031 * TOKENS ** 0.5), 16.0, ((1, 8), (2, 4)), jnp.float32)
    down_weight_first = scatter_about(arg_keys[13], (LAYERS, FF, D), (0.078 * TOKENS ** 0.5), 40.0, ((1, 4), (2, 8)), jnp.float32)
    qkv_bias_first = scatter_about(arg_keys[14], (LAYERS, 3 * D // BROW, BROW), (0.27 * TOKENS ** 0.5), 128.0, ((1, 4), (2, 8)), jnp.float32)
    up_bias_first = scatter_about(arg_keys[15], (LAYERS, FF // BROW, BROW), (0.033 * TOKENS ** 0.5), 16.0, ((1, 4), (2, 8)), jnp.float32)
    vectors_first = scatter_about(arg_keys[16], (LAYERS, 6, D), (0.27 * TOKENS ** 0.5), 128.0, ((2, 8),), jnp.float32)
    qkv_weight_second = jnp.clip(jnp.exp(math.log(6799.36) - 1.37431818 * jax.random.uniform(arg_keys[17], (LAYERS, D, 3 * D), jnp.float32) ** block_scale(arg_keys[17], (LAYERS, D, 3 * D), ((1, 8), (2, 4)), -0.2, 0.2)), 1720.32, 6799.36)
    dense_weight_second = jnp.clip(jnp.exp(math.log(1802.24) - 1.3862944 * jax.random.uniform(arg_keys[18], (LAYERS, D, D), jnp.float32) ** block_scale(arg_keys[18], (LAYERS, D, D), ((1, 4), (2, 8)), -0.2, 0.2)), 450.56, 1802.24)
    up_weight_second = jnp.clip(jnp.exp(math.log(245.76) - 1.3862944 * jax.random.uniform(arg_keys[19], (LAYERS, D, FF), jnp.float32) ** block_scale(arg_keys[19], (LAYERS, D, FF), ((1, 8), (2, 4)), -0.2, 0.2)), 61.44, 245.76)
    down_weight_second = jnp.clip(jnp.exp(math.log(1310.72) - 1.3862944 * jax.random.uniform(arg_keys[20], (LAYERS, FF, D), jnp.float32) ** block_scale(arg_keys[20], (LAYERS, FF, D), ((1, 4), (2, 8)), -0.2, 0.2)), 327.68, 1310.72)
    qkv_bias_second = jnp.clip(jnp.exp(math.log(16384.0) - 1.3862944 * jax.random.uniform(arg_keys[21], (LAYERS, 3 * D // BROW, BROW), jnp.float32) ** block_scale(arg_keys[21], (LAYERS, 3 * D // BROW, BROW), ((1, 4), (2, 8)), -0.2, 0.2)), 4096.0, 16384.0)
    up_bias_second = jnp.clip(jnp.exp(math.log(155.648) - 1.375823 * jax.random.uniform(arg_keys[22], (LAYERS, FF // BROW, BROW), jnp.float32) ** block_scale(arg_keys[22], (LAYERS, FF // BROW, BROW), ((1, 4), (2, 8)), -0.2, 0.2)), 39.3216, 155.648)
    vectors_second = jnp.clip(jnp.exp(math.log(9256.96) - 1.3951833 * jax.random.uniform(arg_keys[23], (LAYERS, 6, D), jnp.float32) ** block_scale(arg_keys[23], (LAYERS, 6, D), ((2, 8),), -0.2, 0.2)), 2293.76, 9256.96)
    return {"tokens_in": tokens_in, "cotangent": cotangent, "seq_lengths": seq_lengths, "qkv_weight": qkv_weight, "dense_weight": dense_weight, "up_weight": up_weight, "down_weight": down_weight, "qkv_bias": qkv_bias, "up_bias": up_bias, "vectors": vectors, "qkv_weight_first": qkv_weight_first, "dense_weight_first": dense_weight_first, "up_weight_first": up_weight_first, "down_weight_first": down_weight_first, "qkv_bias_first": qkv_bias_first, "up_bias_first": up_bias_first, "vectors_first": vectors_first, "qkv_weight_second": qkv_weight_second, "dense_weight_second": dense_weight_second, "up_weight_second": up_weight_second, "down_weight_second": down_weight_second, "qkv_bias_second": qkv_bias_second, "up_bias_second": up_bias_second, "vectors_second": vectors_second}


norm_eps = 1e-05
beta_one = 0.9
beta_two = 0.95
adam_eps = 1e-08
rate = 0.02
decay = 0.01
masked_score = -1e+30
highest = lax.Precision.HIGHEST

@jax.custom_vjp
def low(v):
    return lax.optimization_barrier(v.astype(jnp.bfloat16)).astype(jnp.float32)

@jax.custom_vjp
def low_back(v):
    return v

def low_keep(v):
    return (low(v), None)

def low_pass(kept, grad):
    return (grad,)

def back_keep(v):
    return (v, None)

def back_low(kept, grad):
    return (low(grad),)
low.defvjp(low_keep, low_pass)
low_back.defvjp(back_keep, back_low)

def layout(lengths_row, rows):
    slots = lengths_row.shape[0]
    ends = jnp.cumsum(lengths_row).astype(jnp.int32)
    starts = (ends - lengths_row).astype(jnp.int32)
    index = jnp.arange(rows, dtype=jnp.int32)
    inside = (index[:, None] >= starts[None, :]) & (index[:, None] < ends[None, :])
    valid = jnp.any(inside, axis=1)
    number = jnp.arange(slots, dtype=jnp.int32)
    slot = lax.optimization_barrier(jnp.sum(jnp.where(inside, number[None, :], 0), axis=1)).astype(jnp.int32)
    first = lax.optimization_barrier(jnp.sum(jnp.where(inside, starts[None, :], 0), axis=1)).astype(jnp.int32)
    segment = jnp.where(valid, slot, slots + index).astype(jnp.int32)
    position = (index - first).astype(jnp.int32)
    return (segment, position, valid)

def rotary_tables(position):
    half = ROT // 2
    freq = 10000.0 ** (-(jnp.arange(half, dtype=jnp.float32) * 2.0) / ROT)
    angle = position.astype(jnp.float32)[:, None] * freq[None, :]
    return (jnp.cos(angle), jnp.sin(angle))

def rotate(values, cosine, sine):
    half = cosine.shape[1]
    first = values[..., :half]
    second = values[..., half:2 * half]
    rest = values[..., 2 * half:]
    cfac = cosine[:, None, :]
    sfac = sine[:, None, :]
    return jnp.concatenate([first * cfac - second * sfac, second * cfac + first * sfac, rest], axis=-1)

def apply_layer_norm(residual_stream):
    centre = lax.optimization_barrier(jnp.mean(residual_stream, axis=1, keepdims=True))
    centred = residual_stream - centre
    spread = lax.optimization_barrier(jnp.mean(centred * centred, axis=1, keepdims=True))
    return centred * lax.rsqrt(spread + norm_eps)

def norm_pair(residual_stream, model_parameters):
    normalized_input_rows = apply_layer_norm(residual_stream)
    return (normalized_input_rows * model_parameters[0] + model_parameters[1], normalized_input_rows * model_parameters[2] + model_parameters[3])

def gelu_exact(values):
    return jax.nn.gelu(values, approximate=False)

def attend(parts):
    query, keys, values, segment = parts
    index = jnp.arange(query.shape[0], dtype=jnp.int32)
    scores = jnp.einsum('qhd,khd->hqk', query, keys, precision=highest) * HD ** (-0.5)
    scores = low_back(scores)
    allowed = (segment[:, None] == segment[None, :]) & (index[None, :] <= index[:, None])
    scores = jnp.where(allowed[None], scores, masked_score)
    top = lax.optimization_barrier(jnp.max(scores, axis=2, keepdims=True))
    expo = jnp.exp(scores - top)
    prob = expo / lax.optimization_barrier(jnp.sum(expo, axis=2, keepdims=True))
    return jnp.einsum('hqk,khd->qhd', low(prob), values, precision=highest)

def matmul(left, right):
    return jnp.dot(left, right, precision=highest, preferred_element_type=jnp.float32)

def block(residual_stream, weights, segment, cosine, sine):
    qkv_w, dense_w, up_w, down_w, qkv_b, up_b, vec = weights
    rows = residual_stream.shape[0]
    first_branch_input, second_in = norm_pair(residual_stream, vec[:4])
    first_branch_input = low(first_branch_input)
    second_in = low(second_in)
    mixed = low_back(matmul(first_branch_input, qkv_w) + qkv_b.reshape(-1))
    mixed = mixed.reshape(rows, HEADS, 3, HD)
    query = low(rotate(mixed[:, :, 0], cosine, sine))
    keys = low(rotate(mixed[:, :, 1], cosine, sine))
    values = low(mixed[:, :, 2])
    context = lax.map(jax.checkpoint(attend), (query.reshape(N_DP, CAP, HEADS, HD), keys.reshape(N_DP, CAP, HEADS, HD), values.reshape(N_DP, CAP, HEADS, HD), segment.reshape(N_DP, CAP)))
    context = low(low_back(context.reshape(rows, D)))
    hidden = low_back(matmul(second_in, up_w) + up_b.reshape(-1))
    active = low(gelu_exact(hidden))
    branch = low_back(matmul(context, dense_w) + matmul(active, down_w))
    return residual_stream + branch + vec[4] + vec[5]

def adam(weight, grad, first, second):
    first_new = beta_one * first + (1.0 - beta_one) * grad
    second_new = beta_two * second + (1.0 - beta_two) * grad * grad
    mean_hat = first_new / (1.0 - beta_one ** ADAM_STEP)
    square_hat = second_new / (1.0 - beta_two ** ADAM_STEP)
    old = weight.astype(jnp.float32)
    new_weight = old - rate * (mean_hat / (jnp.sqrt(square_hat) + adam_eps) + decay * old)
    return (grad, first_new, second_new, new_weight - old)

def reference(tokens_in, cotangent, seq_lengths, qkv_weight, dense_weight, up_weight, down_weight, qkv_bias, up_bias, vectors, qkv_weight_first, dense_weight_first, up_weight_first, down_weight_first, qkv_bias_first, up_bias_first, vectors_first, qkv_weight_second, dense_weight_second, up_weight_second, down_weight_second, qkv_bias_second, up_bias_second, vectors_second):
    segment, position, valid = jax.vmap(lambda row: layout(row, CAP))(seq_lengths)
    segment = segment.reshape(-1)
    position = position.reshape(-1)
    valid = valid.reshape(-1)
    cosine, sine = rotary_tables(position)
    weights = (qkv_weight, dense_weight, up_weight, down_weight, qkv_bias, up_bias, vectors)
    firsts = (qkv_weight_first, dense_weight_first, up_weight_first, down_weight_first, qkv_bias_first, up_bias_first, vectors_first)
    seconds = (qkv_weight_second, dense_weight_second, up_weight_second, down_weight_second, qkv_bias_second, up_bias_second, vectors_second)
    model_parameters = tuple((w.astype(jnp.float32) for w in weights))

    def forward(model_parameters, residual_stream):
        for layer in range(LAYERS):
            residual_stream = block(residual_stream, tuple((p[layer] for p in model_parameters)), segment, cosine, sine)
        return residual_stream
    result, pullback = jax.vjp(forward, model_parameters, tokens_in.astype(jnp.float32))
    live = valid.astype(jnp.float32)[:, None]
    grads, input_grad = pullback(cotangent.astype(jnp.float32) * live)
    outs = [(result * live).astype(jnp.bfloat16), input_grad]
    for weight, grad, first, second in zip(weights, grads, firsts, seconds):
        outs.extend(adam(weight, grad, first, second))
    return (outs[0], outs[1], outs[2], outs[3], outs[4], outs[5], outs[6], outs[7], outs[8], outs[9], outs[10], outs[11], outs[12], outs[13], outs[14], outs[15], outs[16], outs[17], outs[18], outs[19], outs[20], outs[21], outs[22], outs[23], outs[24], outs[25], outs[26], outs[27], outs[28], outs[29])
```

```python
import functools
import jax
import jax.numpy as jnp
from jax import lax
from jax.experimental import pallas as pl
from jax.experimental.pallas import tpu as pltpu
from jax.sharding import PartitionSpec as P

HD = 256
ROT = 64
MAXLEN = 512
norm_eps = 1e-05
masked_score = -1e30
LAYERS = 2
ADAM_STEP = 10
beta_one = 0.9
beta_two = 0.95
adam_eps = 1e-08
rate = 0.02
decay = 0.01
VM = 60 * 1024 * 1024
BF = jnp.bfloat16
F32 = jnp.float32


def call(kernel, grid, in_specs, out_specs, out_shape, scratch=(), flops=0, nbytes=0, name=None):
    return pl.pallas_call(
        kernel,
        grid_spec=pltpu.PrefetchScalarGridSpec(num_scalar_prefetch=0, grid=grid, in_specs=in_specs, out_specs=out_specs, scratch_shapes=list(scratch)),
        out_shape=out_shape,
        compiler_params=pltpu.CompilerParams(vmem_limit_bytes=VM),
        cost_estimate=pl.CostEstimate(flops=flops, bytes_accessed=nbytes, transcendentals=0),
        name=name,
    )


def spec(shape, index, single=False):
    if single:
        return pl.BlockSpec(shape, index, pipeline_mode=pl.Buffered(1))
    return pl.BlockSpec(shape, index)


def rope_tables(position):
    half = ROT // 2
    freq = 10000.0 ** (-(jnp.arange(half, dtype=F32) * 2.0) / ROT)
    angle = position.astype(F32)[:, None] * freq[None, :]
    c, s = jnp.cos(angle), jnp.sin(angle)
    rows = position.shape[0]
    one = jnp.ones((rows, 128 - ROT), F32)
    zero = jnp.zeros((rows, 128 - ROT), F32)
    return jnp.concatenate([c, c, one], axis=1), jnp.concatenate([-s, s, zero], axis=1)


def turn(u, c, s):
    lane = lax.broadcasted_iota(jnp.int32, u.shape, 1)
    other = jnp.where(lane < ROT // 2, pltpu.roll(u, 128 - ROT // 2, 1), pltpu.roll(u, ROT // 2, 1))
    return u * c + other * s


def normed(x):
    mean = jnp.mean(x, axis=1, keepdims=True)
    centred = x - mean
    var = jnp.mean(centred * centred, axis=1, keepdims=True)
    rstd = lax.rsqrt(var + norm_eps)
    return centred * rstd, mean, rstd


def project(base, extra, vec, wq, bq, cos, sin, wu, bu):
    n, D = base.shape
    C, U = wq.shape[1], wu.shape[1]
    NB = 256
    nq, nu = C // NB, U // NB
    RB = min(n, 128)

    def kernel(*refs):
        if extra is None:
            base_r, vec_r, wq_r, bq_r, cos_r, sin_r, wu_r, bu_r, h1_r, h2_r, mix_r, a_r, gp_r, st_r = refs
        else:
            base_r, extra_r, vec_r, wq_r, bq_r, cos_r, sin_r, wu_r, bu_r, h1_r, h2_r, mix_r, a_r, gp_r, st_r = refs
        j = pl.program_id(0)

        @pl.when(j == 0)
        def _():
            @pl.loop(0, n // RB)
            def _(i):
                rows = pl.ds(pl.multiple_of(i * RB, RB), RB)
                x = base_r[rows, :].astype(F32)
                if extra is not None:
                    x = x + extra_r[rows, :].astype(F32) + vec_r[4:5, :] + vec_r[5:6, :]
                xhat, mean, rstd = normed(x)
                st_r[rows, 0:1] = mean
                st_r[rows, 1:2] = rstd
                h1_r[rows, :] = (xhat * vec_r[0:1, :] + vec_r[1:2, :]).astype(BF)
                h2_r[rows, :] = (xhat * vec_r[2:3, :] + vec_r[3:4, :]).astype(BF)

        @pl.when(j < nq)
        def _():
            m = jnp.dot(h1_r[...], wq_r[...], preferred_element_type=F32) + bq_r[...]
            kind = lax.rem(j, 3)

            @pl.when(kind == 2)
            def _():
                mix_r[...] = m.astype(BF)

            @pl.when(kind != 2)
            def _():
                mix_r[:, :128] = turn(m[:, :128], cos_r[...], sin_r[...]).astype(BF)
                mix_r[:, 128:] = m[:, 128:].astype(BF)

        @pl.when(j >= nq)
        def _():
            f = jnp.dot(h2_r[...], wu_r[...], preferred_element_type=F32) + bu_r[...]
            phi = 0.5 * (1.0 + lax.erf(f * 0.7071067811865476))
            a_r[...] = (f * phi).astype(BF)
            gp_r[...] = (phi + f * (jnp.exp(-0.5 * f * f) * 0.3989422804014327)).astype(BF)

    whole = lambda j: (0, 0)
    qcol = lambda j: (0, jnp.minimum(j, nq - 1))
    ucol = lambda j: (0, jnp.maximum(j - nq, 0))
    ins = [spec((n, D), whole, True)] + ([] if extra is None else [spec((n, D), whole, True)]) + [
        spec((6, D), whole), spec((D, NB), qcol), spec((1, NB), qcol), spec((n, 128), whole, True), spec((n, 128), whole, True),
        spec((D, NB), ucol), spec((1, NB), ucol)]
    outs = [spec((n, D), whole, True), spec((n, D), whole, True), spec((n, NB), qcol), spec((n, NB), ucol), spec((n, NB), ucol), spec((n, 128), whole)]
    shapes = [jax.ShapeDtypeStruct(s, BF) for s in ((n, D), (n, D), (n, C), (n, U), (n, U))] + [jax.ShapeDtypeStruct((n, 128), F32)]
    args = [base] + ([] if extra is None else [extra]) + [vec, wq, bq, cos, sin, wu, bu]
    return call(kernel, (nq + nu,), ins, outs, shapes, flops=2 * n * D * (C + U), nbytes=2 * (n * D * 3 + D * (C + U) + n * (C + 2 * U)), name="project")(*args)


def softmax_block(q, k, segq, segk, q0, k0):
    s = lax.dot_general(q, k, (((1,), (1,)), ((), ())), preferred_element_type=F32) * HD ** (-0.5)
    qi = q0 + lax.broadcasted_iota(jnp.int32, s.shape, 0)
    ki = k0 + lax.broadcasted_iota(jnp.int32, s.shape, 1)
    allowed = (segq == segk) & (ki <= qi)
    s = jnp.where(allowed, s, masked_score)
    top = jnp.max(s, axis=1, keepdims=True)
    e = jnp.exp(s - top)
    return e / jnp.sum(e, axis=1, keepdims=True)


def windows(n, qb):
    for i in range(n // qb):
        q0 = i * qb
        yield q0, max(0, q0 - MAXLEN)


def attend_forward(mixed, seg_col, seg_row):
    n, C = mixed.shape
    H = C // (3 * HD)
    qb = 256

    def kernel(q_r, k_r, v_r, sc_r, sr_r, o_r):
        for q0, k0 in windows(n, qb):
            qs, ks = slice(q0, q0 + qb), slice(k0, q0 + qb)
            p = softmax_block(q_r[qs, :], k_r[ks, :], sc_r[qs, :], sr_r[:, ks], q0, k0)
            o_r[qs, :] = jnp.dot(p.astype(BF), v_r[ks, :], preferred_element_type=F32).astype(BF)

    part = lambda t: spec((n, HD), lambda h: (0, 3 * h + t))
    return call(kernel, (H,), [part(0), part(1), part(2), spec((n, 1), lambda h: (0, 0)), spec((1, n), lambda h: (0, 0))],
                spec((n, HD), lambda h: (0, h)), jax.ShapeDtypeStruct((n, H * HD), BF),
                flops=H * n * 640 * HD * 4, nbytes=2 * n * C, name="attend")(mixed, mixed, mixed, seg_col, seg_row)


def attend_backward(mixed, dctx, seg_col, seg_row, cos, sin):
    n, C = mixed.shape
    H = C // (3 * HD)
    qb = 256
    scale = HD ** (-0.5)

    def kernel(q_r, k_r, v_r, do_r, sc_r, sr_r, cos_r, sin_r, o_r, dk_s, dv_s):
        def back(u, rows):
            c, s = cos_r[rows, :], -sin_r[rows, :]
            return jnp.concatenate([turn(u[:, :128], c, s), u[:, 128:]], axis=1).astype(BF)

        dk_s[...] = jnp.zeros_like(dk_s)
        dv_s[...] = jnp.zeros_like(dv_s)
        for q0, k0 in reversed(list(windows(n, qb))):
            qs, ks = slice(q0, q0 + qb), slice(k0, q0 + qb)
            q, k, do = q_r[qs, :], k_r[ks, :], do_r[qs, :]
            p = softmax_block(q, k, sc_r[qs, :], sr_r[:, ks], q0, k0)
            dp = lax.dot_general(do, v_r[ks, :], (((1,), (1,)), ((), ())), preferred_element_type=F32)
            delta = jnp.sum(p * dp, axis=1, keepdims=True)
            ds = (p * (dp - delta)).astype(BF)
            dq = jnp.dot(ds, k, preferred_element_type=F32) * scale
            dk_s[ks, :] += lax.dot_general(ds, q, (((0,), (0,)), ((), ())), preferred_element_type=F32)
            dv_s[ks, :] += lax.dot_general(p.astype(BF), do, (((0,), (0,)), ((), ())), preferred_element_type=F32)
            o_r[qs, :HD] = back(dq, qs)
            o_r[qs, HD:2 * HD] = back(dk_s[qs, :] * scale, qs)
            o_r[qs, 2 * HD:] = dv_s[qs, :].astype(BF)

    part = lambda t: spec((n, HD), lambda h: (0, 3 * h + t))
    whole = lambda h: (0, 0)
    return call(kernel, (H,), [part(0), part(1), part(2), spec((n, HD), lambda h: (0, h)), spec((n, 1), whole), spec((1, n), whole),
                spec((n, 128), whole), spec((n, 128), whole)],
                spec((n, 3 * HD), lambda h: (0, h)), jax.ShapeDtypeStruct((n, C), BF),
                scratch=[pltpu.VMEM((n, HD), F32), pltpu.VMEM((n, HD), F32)],
                flops=H * n * 640 * HD * 10, nbytes=4 * n * C, name="attend_back")(mixed, mixed, mixed, dctx, seg_col, seg_row, cos, sin)


def branch_out(ctx, act, wd, wn):
    n, R = ctx.shape
    U = act.shape[1]
    dp, _, w = wd.shape

    def kernel(c_r, a_r, wd_r, wn_r, o_r):
        o_r[...] = (jnp.dot(c_r[...], wd_r[...], preferred_element_type=F32) + jnp.dot(a_r[...], wn_r[...], preferred_element_type=F32)).astype(BF)

    whole = lambda s: (0, 0)
    pick = lambda s: (s, 0, 0)
    return call(kernel, (dp,), [spec((n, R), whole, True), spec((n, U), whole, True), spec((None, R, w), pick), spec((None, U, w), pick)],
                spec((n, w), lambda s: (0, s)), jax.ShapeDtypeStruct((n, dp * w), BF),
                flops=2 * n * dp * w * (R + U), nbytes=2 * (n * (R + U) + dp * w * (R + U + n)), name="branch")(ctx, act, wd, wn)


def back_in(gr, gp, wd, wn):
    n, D = gr.shape
    dp, R, w = wd.shape
    U = wn.shape[1]
    NB = 256
    nr, nu = R // NB, U // NB

    def kernel(g_r, gp_r, wd_r, wn_r, dc_r, df_r):
        j = pl.program_id(0)

        def times(w_r):
            acc = None
            for s in range(dp):
                t = lax.dot_general(g_r[:, s * w:(s + 1) * w], w_r[s], (((1,), (1,)), ((), ())), preferred_element_type=F32)
                acc = t if acc is None else acc + t
            return acc

        @pl.when(j < nr)
        def _():
            dc_r[...] = times(wd_r).astype(BF)

        @pl.when(j >= nr)
        def _():
            df_r[...] = (times(wn_r) * gp_r[...].astype(F32)).astype(BF)

    rc = lambda j: jnp.minimum(j, nr - 1)
    uc = lambda j: jnp.maximum(j - nr, 0)
    return call(kernel, (nr + nu,), [spec((n, D), lambda j: (0, 0), True), spec((n, NB), lambda j: (0, uc(j))),
                spec((dp, NB, w), lambda j: (0, rc(j), 0)), spec((dp, NB, w), lambda j: (0, uc(j), 0))],
                [spec((n, NB), lambda j: (0, rc(j))), spec((n, NB), lambda j: (0, uc(j)))],
                [jax.ShapeDtypeStruct((n, R), BF), jax.ShapeDtypeStruct((n, U), BF)],
                flops=2 * n * D * (R + U), nbytes=2 * (n * D + D * (R + U) + n * (R + 2 * U)), name="back_in")(gr, gp, wd, wn)


def back_out(dmix, df, wq, wu, base, extra, vec, stats):
    n, C = dmix.shape
    U = df.shape[1]
    D = wq.shape[0]
    NB = 256

    def kernel(*refs):
        if extra is None:
            dm_r, df_r, wq_r, wu_r, base_r, vec_r, st_r, e_r, g_r = refs
        else:
            dm_r, df_r, wq_r, wu_r, base_r, extra_r, vec_r, st_r, e_r, g_r = refs
        nt = (((1,), (1,)), ((), ()))
        d1 = lax.dot_general(dm_r[...], wq_r[...], nt, preferred_element_type=F32)
        d2 = lax.dot_general(df_r[...], wu_r[...], nt, preferred_element_type=F32)
        e_r[...] = (d1 * vec_r[0:1, :] + d2 * vec_r[2:3, :]).astype(BF)
        x = base_r[...].astype(F32)
        if extra is not None:
            x = x + extra_r[...].astype(F32) + vec_r[4:5, :] + vec_r[5:6, :]
        xhat = (x - st_r[:, 0:1]) * st_r[:, 1:2]
        g_r[0:1, :] = jnp.sum(d1 * xhat, axis=0, keepdims=True)
        g_r[1:2, :] = jnp.sum(d1, axis=0, keepdims=True)
        g_r[2:3, :] = jnp.sum(d2 * xhat, axis=0, keepdims=True)
        g_r[3:4, :] = jnp.sum(d2, axis=0, keepdims=True)

    whole = lambda j: (0, 0)
    col = lambda j: (0, j)
    row = lambda j: (j, 0)
    xs = [spec((n, NB), col)] + ([] if extra is None else [spec((n, NB), col)])
    args = [base] + ([] if extra is None else [extra])
    return call(kernel, (D // NB,), [spec((n, C), whole, True), spec((n, U), whole, True), spec((NB, C), row), spec((NB, U), row)] + xs +
                [spec((6, NB), col), spec((n, 128), whole)],
                [spec((n, NB), col), spec((4, NB), col)],
                [jax.ShapeDtypeStruct((n, D), BF), jax.ShapeDtypeStruct((4, D), F32)],
                flops=2 * n * D * (C + U), nbytes=2 * (n * (C + U) + D * (C + U) + n * D * 3), name="back_out")(dmix, df, wq, wu, *args, vec, stats)


def weight_grad(left, right, w=None):
    n, M = left.shape
    N = right.shape[1]
    MB = 256

    def kernel(l_r, r_r, o_r, s_r):
        g = lax.dot_general(l_r[...], r_r[...], (((0,), (0,)), ((), ())), preferred_element_type=F32)
        if w is None:
            o_r[...] = g.astype(BF)
        else:
            for s in range(N // w):
                o_r[s] = g[:, s * w:(s + 1) * w].astype(BF)

        @pl.when(pl.program_id(0) == 0)
        def _():
            s_r[...] = jnp.sum(r_r[...].astype(F32), axis=0, keepdims=True)

    whole = lambda j: (0, 0)
    if w is None:
        out, shape = spec((MB, N), lambda j: (j, 0)), (M, N)
    else:
        out, shape = spec((N // w, MB, w), lambda j: (0, j, 0)), (N // w, M, w)
    return call(kernel, (M // MB,), [spec((n, MB), lambda j: (0, j)), spec((n, N), whole, True)], [out, spec((1, N), whole)],
                [jax.ShapeDtypeStruct(shape, BF), jax.ShapeDtypeStruct((1, N), F32)],
                flops=2 * n * M * N, nbytes=2 * (n * M + n * N + M * N), name="wgrad")(left, right)


def norm_back(gout, e, base, extra, vec, stats, last):
    n, D = base.shape
    RB = 128

    def kernel(*refs):
        g_r, e_r, base_r = refs[:3]
        refs = refs[3:]
        if extra is not None:
            extra_r, refs = refs[0], refs[1:]
        vec_r, st_r, dx_r = refs[:3]
        x = base_r[...].astype(F32)
        if extra is not None:
            x = x + extra_r[...].astype(F32) + vec_r[4:5, :] + vec_r[5:6, :]
        xhat = (x - st_r[:, 0:1]) * st_r[:, 1:2]
        ev = e_r[...].astype(F32)
        me = jnp.mean(ev, axis=1, keepdims=True)
        mx = jnp.mean(ev * xhat, axis=1, keepdims=True)
        dx = g_r[...].astype(F32) + (ev - me - xhat * mx) * st_r[:, 1:2]
        dx_r[...] = dx
        if not last:
            low_r, sum_r = refs[3:]
            low_r[...] = dx.astype(BF)

            @pl.when(pl.program_id(0) == 0)
            def _():
                sum_r[...] = jnp.zeros_like(sum_r)

            sum_r[...] += jnp.sum(dx, axis=0, keepdims=True)

    row = lambda i: (i, 0)
    whole = lambda i: (0, 0)
    rows = spec((RB, D), row)
    ins = [rows, rows, rows] + ([] if extra is None else [rows]) + [spec((6, D), whole), spec((RB, 128), row)]
    args = [gout, e, base] + ([] if extra is None else [extra]) + [vec, stats]
    outs, shapes = [rows], [jax.ShapeDtypeStruct((n, D), F32)]
    if not last:
        outs += [rows, spec((1, D), whole)]
        shapes += [jax.ShapeDtypeStruct((n, D), BF), jax.ShapeDtypeStruct((1, D), F32)]
    return call(kernel, (n // RB,), ins, outs, shapes, flops=10 * n * D, nbytes=16 * n * D, name="norm_back")(*args)


def adam_update(weight, grad, first, second):
    first_new = beta_one * first + (1.0 - beta_one) * grad
    second_new = beta_two * second + (1.0 - beta_two) * grad * grad
    mean_hat = first_new / (1.0 - beta_one**ADAM_STEP)
    square_hat = second_new / (1.0 - beta_two**ADAM_STEP)
    new_weight = weight - rate * (mean_hat / (jnp.sqrt(square_hat) + adam_eps) + decay * weight)
    return grad, first_new, second_new, new_weight - weight


def adam_layer(layer, weights, grads, firsts, seconds, before):
    steps = 8
    blocks = [(w.shape[1] // steps, w.shape[2]) for w in weights]

    def kernel(*refs):
        ins, outs = refs[:16], refs[-16:]
        for i in range(4):
            g = ins[4 + i][...].astype(F32)
            made = adam_update(ins[i][...].astype(F32), g, ins[8 + i][...], ins[12 + i][...])
            for k in range(4):
                outs[4 * i + k][...] = made[k]

    at = lambda b: spec((None,) + b, lambda j: (layer, j, 0))
    ins = [at(b) for b in blocks] + [spec(b, lambda j: (j, 0)) for b in blocks] + [at(b) for b in blocks] * 2
    args = [*weights, *grads, *firsts, *seconds]
    alias = {}
    if before is not None:
        ins += [pl.BlockSpec(memory_space=pl.ANY)] * 16
        args += list(before)
        alias = {16 + i: i for i in range(16)}
    shapes = [jax.ShapeDtypeStruct(w.shape, F32) for w in weights for _ in range(4)]
    count = sum(w.shape[1] * w.shape[2] for w in weights)
    return pl.pallas_call(
        kernel, grid=(steps,), in_specs=ins, out_specs=[at(b) for b in blocks for _ in range(4)], out_shape=shapes,
        input_output_aliases=alias, compiler_params=pltpu.CompilerParams(vmem_limit_bytes=VM),
        cost_estimate=pl.CostEstimate(flops=20 * count, bytes_accessed=30 * count, transcendentals=0), name="adam")(*args)


def layout(lengths_row, rows):
    slots = lengths_row.shape[0]
    number = jnp.arange(slots, dtype=jnp.int32)
    ends = jnp.sum(jnp.where(number[None, :] <= number[:, None], lengths_row[None, :], 0), axis=1)
    starts = ends - lengths_row
    index = jnp.arange(rows, dtype=jnp.int32)
    inside = (index[:, None] >= starts[None, :]) & (index[:, None] < ends[None, :])
    valid = jnp.any(inside, axis=1)
    slot = jnp.sum(jnp.where(inside, number[None, :], 0), axis=1)
    first = jnp.sum(jnp.where(inside, starts[None, :], 0), axis=1)
    segment = jnp.where(valid, slot, slots + index)
    return segment, index - first, valid


def gather_small(parts):
    flat = jnp.concatenate([p.reshape(-1) for p in parts])
    got = lax.all_gather(flat, "dp", axis=0, tiled=False)
    out, at = [], 0
    for p in parts:
        piece = got[:, at:at + p.size].reshape((-1,) + p.shape)
        out.append(jnp.moveaxis(piece, 0, 2).reshape(p.shape[0], p.shape[1], -1))
        at += p.size
    return out


class PlainLinks:
    def gather(self, shards):
        wq, wd, wu, wn = shards
        rows = lambda v: lax.all_gather(v, "dp", axis=0, tiled=True)
        stack = lambda v: lax.all_gather(v, "dp", axis=0, tiled=False)
        return rows(wq), stack(wd), rows(wu), stack(wn)

    def share(self, v):
        return lax.psum(v, "mp")

    def scatter(self, grads):
        cut = lambda g: lax.psum_scatter(g, "dp", scatter_dimension=0, tiled=True)
        gq, gd, gu, gn = grads
        return cut(gq), cut(gd)[0], cut(gu), cut(gn)[0]


def body(links, tokens_in, cotangent, seq_lengths, *params):
    weights, small = params[:4], params[4:7]
    firsts, small_firsts = params[7:11], params[11:14]
    seconds, small_seconds = params[14:18], params[18:21]
    rows, D = tokens_in.shape
    segment, position, valid = layout(seq_lengths[0], rows)
    cos, sin = rope_tables(position)
    seg_col, seg_row = segment[:, None], segment[None, :]
    live = valid[:, None]
    qb, ub, vecs = gather_small(small)
    qb = qb.reshape(LAYERS, 1, -1).astype(F32)
    ub = ub.reshape(LAYERS, 1, -1).astype(F32)
    vecs = vecs.astype(F32)

    held = [jnp.concatenate([vecs[layer, :4], vecs[layer - 1, 4:]]) for layer in range(LAYERS)]

    full, kept, extra = [], [], None
    for layer in range(LAYERS):
        wq, wd, wu, wn = links.gather([w[layer] for w in weights])
        h1, h2, mixed, act, gp, stats = project(tokens_in, extra, held[layer], wq, qb[layer], cos, sin, wu, ub[layer])
        ctx = attend_forward(mixed, seg_col, seg_row)
        branch = links.share(branch_out(ctx, act, wd, wn))
        full.append((wq, wd, wu, wn))
        kept.append((h1, h2, mixed, act, gp, stats, ctx, extra))
        if layer + 1 < LAYERS:
            extra = branch
    x_last = tokens_in.astype(F32) + extra.astype(F32) + vecs[0, 4] + vecs[0, 5] + branch.astype(F32) + vecs[1, 4] + vecs[1, 5]
    output = jnp.where(live, x_last, 0.0).astype(BF)

    gout = gr = jnp.where(live, cotangent, 0).astype(BF)
    sums = jnp.sum(gout.astype(F32), axis=0, keepdims=True)
    big, little = [None] * LAYERS, [None] * LAYERS
    for layer in reversed(range(LAYERS)):
        wq, wd, wu, wn = full[layer]
        h1, h2, mixed, act, gp, stats, ctx, extra = kept[layer]
        dctx, df = back_in(gr, gp, wd, wn)
        dmix = attend_backward(mixed, dctx, seg_col, seg_row, cos, sin)
        e, norm_sums = back_out(dmix, df, wq, wu, tokens_in, extra, held[layer], stats)
        e = links.share(e)
        gd, _ = weight_grad(ctx, gr, w=wd.shape[2])
        gn, _ = weight_grad(act, gr, w=wn.shape[2])
        gq, qsum = weight_grad(h1, dmix)
        gu, usum = weight_grad(h2, df)
        big[layer] = links.scatter((gq, gd, gu, gn))
        little[layer] = (qsum, usum, norm_sums, sums)
        made = norm_back(gout, e, tokens_in, extra, held[layer], stats, layer == 0)
        if layer:
            gout, gr, sums = made
        else:
            input_grad = made[0]

    done = None
    for layer in reversed(range(LAYERS)):
        done = adam_layer(layer, weights, big[layer], firsts, seconds, done)

    norm_sums = lax.psum(jnp.stack([t[2] for t in little]), "mp")
    qsum = jnp.stack([t[0] for t in little]).reshape(-1)
    usum = jnp.stack([t[1] for t in little]).reshape(-1)
    out_sums = jnp.stack([t[3] for t in little])
    vec_sum = jnp.concatenate([norm_sums, out_sums, out_sums], axis=1).reshape(-1)
    total = lax.psum(jnp.concatenate([qsum, usum, vec_sum]), "dp")
    me = lax.axis_index("dp")
    small_out, at = [], 0
    for p, first, second in zip(small, small_firsts, small_seconds):
        width = p.shape[2]
        wide = p.shape[:2] + (lax.axis_size("dp") * width,)
        size = wide[0] * wide[1] * wide[2]
        g = lax.dynamic_slice_in_dim(total[at:at + size].reshape(wide), me * width, width, 2)
        at += size
        small_out += adam_update(p.astype(F32), g, first, second)
    return (output, input_grad, *done, *small_out)


def solution(mesh):
    rows_dp = P("dp", None)
    wide, tall, vec = P(None, "dp", "mp"), P(None, "mp", "dp"), P(None, None, "dp")
    group = (wide, tall, wide, tall, tall, tall, vec)
    return jax.shard_map(
        functools.partial(body, PlainLinks()),
        mesh=mesh,
        in_specs=(rows_dp,) * 3 + group * 3,
        out_specs=(rows_dp,) * 2 + tuple(s for s in group for _ in range(4)),
        check_vma=False,
    )
```

```python
import functools
import jax
import jax.numpy as jnp
from jax import lax
from jax.experimental import pallas as pl
from jax.experimental.pallas import tpu as pltpu
from jax.sharding import PartitionSpec as P

HD = 256
ROT = 64
MAXLEN = 512
norm_eps = 1e-05
masked_score = -1e30
LAYERS = 2
ADAM_STEP = 10
beta_one = 0.9
beta_two = 0.95
adam_eps = 1e-08
rate = 0.02
decay = 0.01
VM = 60 * 1024 * 1024
BF = jnp.bfloat16
F32 = jnp.float32


def call(kernel, grid, in_specs, out_specs, out_shape, scratch=(), flops=0, nbytes=0, name=None):
    return pl.pallas_call(
        kernel,
        grid_spec=pltpu.PrefetchScalarGridSpec(num_scalar_prefetch=0, grid=grid, in_specs=in_specs, out_specs=out_specs, scratch_shapes=list(scratch)),
        out_shape=out_shape,
        compiler_params=pltpu.CompilerParams(vmem_limit_bytes=VM),
        cost_estimate=pl.CostEstimate(flops=flops, bytes_accessed=nbytes, transcendentals=0),
        name=name,
    )


def spec(shape, index, single=False):
    if single:
        return pl.BlockSpec(shape, index, pipeline_mode=pl.Buffered(1))
    return pl.BlockSpec(shape, index)


def rope_tables(position):
    half = ROT // 2
    freq = 10000.0 ** (-(jnp.arange(half, dtype=F32) * 2.0) / ROT)
    angle = position.astype(F32)[:, None] * freq[None, :]
    c, s = jnp.cos(angle), jnp.sin(angle)
    rows = position.shape[0]
    one = jnp.ones((rows, 128 - ROT), F32)
    zero = jnp.zeros((rows, 128 - ROT), F32)
    return jnp.concatenate([c, c, one], axis=1), jnp.concatenate([-s, s, zero], axis=1)


def turn(u, c, s):
    lane = lax.broadcasted_iota(jnp.int32, u.shape, 1)
    other = jnp.where(lane < ROT // 2, pltpu.roll(u, 128 - ROT // 2, 1), pltpu.roll(u, ROT // 2, 1))
    return u * c + other * s


def normed(x):
    mean = jnp.mean(x, axis=1, keepdims=True)
    centred = x - mean
    var = jnp.mean(centred * centred, axis=1, keepdims=True)
    rstd = lax.rsqrt(var + norm_eps)
    return centred * rstd, mean, rstd


def project(base, extra, vec, wq, bq, cos, sin, wu, bu):
    n, D = base.shape
    C, U = wq.shape[1], wu.shape[1]
    NB = 256
    nq, nu = C // NB, U // NB
    RB = min(n, 128)

    def kernel(*refs):
        if extra is None:
            base_r, vec_r, wq_r, bq_r, cos_r, sin_r, wu_r, bu_r, h1_r, h2_r, mix_r, a_r, gp_r, st_r = refs
        else:
            base_r, extra_r, vec_r, wq_r, bq_r, cos_r, sin_r, wu_r, bu_r, h1_r, h2_r, mix_r, a_r, gp_r, st_r = refs
        j = pl.program_id(0)

        @pl.when(j == 0)
        def _():
            @pl.loop(0, n // RB)
            def _(i):
                rows = pl.ds(pl.multiple_of(i * RB, RB), RB)
                x = base_r[rows, :].astype(F32)
                if extra is not None:
                    x = x + extra_r[rows, :].astype(F32) + vec_r[4:5, :] + vec_r[5:6, :]
                xhat, mean, rstd = normed(x)
                st_r[rows, 0:1] = mean
                st_r[rows, 1:2] = rstd
                h1_r[rows, :] = (xhat * vec_r[0:1, :] + vec_r[1:2, :]).astype(BF)
                h2_r[rows, :] = (xhat * vec_r[2:3, :] + vec_r[3:4, :]).astype(BF)

        @pl.when(j < nq)
        def _():
            m = jnp.dot(h1_r[...], wq_r[...], preferred_element_type=F32) + bq_r[...]
            kind = lax.rem(j, 3)

            @pl.when(kind == 2)
            def _():
                mix_r[...] = m.astype(BF)

            @pl.when(kind != 2)
            def _():
                mix_r[:, :128] = turn(m[:, :128], cos_r[...], sin_r[...]).astype(BF)
                mix_r[:, 128:] = m[:, 128:].astype(BF)

        @pl.when(j >= nq)
        def _():
            f = jnp.dot(h2_r[...], wu_r[...], preferred_element_type=F32) + bu_r[...]
            phi = 0.5 * (1.0 + lax.erf(f * 0.7071067811865476))
            a_r[...] = (f * phi).astype(BF)
            gp_r[...] = (phi + f * (jnp.exp(-0.5 * f * f) * 0.3989422804014327)).astype(BF)

    whole = lambda j: (0, 0)
    qcol = lambda j: (0, jnp.minimum(j, nq - 1))
    ucol = lambda j: (0, jnp.maximum(j - nq, 0))
    ins = [spec((n, D), whole, True)] + ([] if extra is None else [spec((n, D), whole, True)]) + [
        spec((6, D), whole), spec((D, NB), qcol), spec((1, NB), qcol), spec((n, 128), whole, True), spec((n, 128), whole, True),
        spec((D, NB), ucol), spec((1, NB), ucol)]
    outs = [spec((n, D), whole, True), spec((n, D), whole, True), spec((n, NB), qcol), spec((n, NB), ucol), spec((n, NB), ucol), spec((n, 128), whole)]
    shapes = [jax.ShapeDtypeStruct(s, BF) for s in ((n, D), (n, D), (n, C), (n, U), (n, U))] + [jax.ShapeDtypeStruct((n, 128), F32)]
    args = [base] + ([] if extra is None else [extra]) + [vec, wq, bq, cos, sin, wu, bu]
    return call(kernel, (nq + nu,), ins, outs, shapes, flops=2 * n * D * (C + U), nbytes=2 * (n * D * 3 + D * (C + U) + n * (C + 2 * U)), name="project")(*args)


def softmax_block(q, k, segq, segk, q0, k0):
    s = lax.dot_general(q, k, (((1,), (1,)), ((), ())), preferred_element_type=F32) * HD ** (-0.5)
    qi = q0 + lax.broadcasted_iota(jnp.int32, s.shape, 0)
    ki = k0 + lax.broadcasted_iota(jnp.int32, s.shape, 1)
    allowed = (segq == segk) & (ki <= qi)
    s = jnp.where(allowed, s, masked_score)
    top = jnp.max(s, axis=1, keepdims=True)
    e = jnp.exp(s - top)
    return e / jnp.sum(e, axis=1, keepdims=True)


def windows(n, qb):
    for i in range(n // qb):
        q0 = i * qb
        yield q0, max(0, q0 - MAXLEN)


def attend_forward(mixed, seg_col, seg_row):
    n, C = mixed.shape
    H = C // (3 * HD)
    qb = 256

    def kernel(q_r, k_r, v_r, sc_r, sr_r, o_r):
        for q0, k0 in windows(n, qb):
            qs, ks = slice(q0, q0 + qb), slice(k0, q0 + qb)
            p = softmax_block(q_r[qs, :], k_r[ks, :], sc_r[qs, :], sr_r[:, ks], q0, k0)
            o_r[qs, :] = jnp.dot(p.astype(BF), v_r[ks, :], preferred_element_type=F32).astype(BF)

    part = lambda t: spec((n, HD), lambda h: (0, 3 * h + t))
    return call(kernel, (H,), [part(0), part(1), part(2), spec((n, 1), lambda h: (0, 0)), spec((1, n), lambda h: (0, 0))],
                spec((n, HD), lambda h: (0, h)), jax.ShapeDtypeStruct((n, H * HD), BF),
                flops=H * n * 640 * HD * 4, nbytes=2 * n * C, name="attend")(mixed, mixed, mixed, seg_col, seg_row)


def attend_backward(mixed, dctx, seg_col, seg_row, cos, sin):
    n, C = mixed.shape
    H = C // (3 * HD)
    qb = 256
    scale = HD ** (-0.5)

    def kernel(q_r, k_r, v_r, do_r, sc_r, sr_r, cos_r, sin_r, o_r, dk_s, dv_s):
        def back(u, rows):
            c, s = cos_r[rows, :], -sin_r[rows, :]
            return jnp.concatenate([turn(u[:, :128], c, s), u[:, 128:]], axis=1).astype(BF)

        dk_s[...] = jnp.zeros_like(dk_s)
        dv_s[...] = jnp.zeros_like(dv_s)
        for q0, k0 in reversed(list(windows(n, qb))):
            qs, ks = slice(q0, q0 + qb), slice(k0, q0 + qb)
            q, k, do = q_r[qs, :], k_r[ks, :], do_r[qs, :]
            p = softmax_block(q, k, sc_r[qs, :], sr_r[:, ks], q0, k0)
            dp = lax.dot_general(do, v_r[ks, :], (((1,), (1,)), ((), ())), preferred_element_type=F32)
            delta = jnp.sum(p * dp, axis=1, keepdims=True)
            ds = (p * (dp - delta)).astype(BF)
            dq = jnp.dot(ds, k, preferred_element_type=F32) * scale
            dk_s[ks, :] += lax.dot_general(ds, q, (((0,), (0,)), ((), ())), preferred_element_type=F32)
            dv_s[ks, :] += lax.dot_general(p.astype(BF), do, (((0,), (0,)), ((), ())), preferred_element_type=F32)
            o_r[qs, :HD] = back(dq, qs)
            o_r[qs, HD:2 * HD] = back(dk_s[qs, :] * scale, qs)
            o_r[qs, 2 * HD:] = dv_s[qs, :].astype(BF)

    part = lambda t: spec((n, HD), lambda h: (0, 3 * h + t))
    whole = lambda h: (0, 0)
    return call(kernel, (H,), [part(0), part(1), part(2), spec((n, HD), lambda h: (0, h)), spec((n, 1), whole), spec((1, n), whole),
                spec((n, 128), whole), spec((n, 128), whole)],
                spec((n, 3 * HD), lambda h: (0, h)), jax.ShapeDtypeStruct((n, C), BF),
                scratch=[pltpu.VMEM((n, HD), F32), pltpu.VMEM((n, HD), F32)],
                flops=H * n * 640 * HD * 10, nbytes=4 * n * C, name="attend_back")(mixed, mixed, mixed, dctx, seg_col, seg_row, cos, sin)


def branch_out(ctx, act, wd, wn):
    n, R = ctx.shape
    U = act.shape[1]
    dp, _, w = wd.shape

    def kernel(c_r, a_r, wd_r, wn_r, o_r):
        o_r[...] = (jnp.dot(c_r[...], wd_r[...], preferred_element_type=F32) + jnp.dot(a_r[...], wn_r[...], preferred_element_type=F32)).astype(BF)

    whole = lambda s: (0, 0)
    pick = lambda s: (s, 0, 0)
    return call(kernel, (dp,), [spec((n, R), whole, True), spec((n, U), whole, True), spec((None, R, w), pick), spec((None, U, w), pick)],
                spec((n, w), lambda s: (0, s)), jax.ShapeDtypeStruct((n, dp * w), BF),
                flops=2 * n * dp * w * (R + U), nbytes=2 * (n * (R + U) + dp * w * (R + U + n)), name="branch")(ctx, act, wd, wn)


def back_in(gr, gp, wd, wn):
    n, D = gr.shape
    dp, R, w = wd.shape
    U = wn.shape[1]
    NB = 256
    nr, nu = R // NB, U // NB

    def kernel(g_r, gp_r, wd_r, wn_r, dc_r, df_r):
        j = pl.program_id(0)

        def times(w_r):
            acc = None
            for s in range(dp):
                t = lax.dot_general(g_r[:, s * w:(s + 1) * w], w_r[s], (((1,), (1,)), ((), ())), preferred_element_type=F32)
                acc = t if acc is None else acc + t
            return acc

        @pl.when(j < nr)
        def _():
            dc_r[...] = times(wd_r).astype(BF)

        @pl.when(j >= nr)
        def _():
            df_r[...] = (times(wn_r) * gp_r[...].astype(F32)).astype(BF)

    rc = lambda j: jnp.minimum(j, nr - 1)
    uc = lambda j: jnp.maximum(j - nr, 0)
    return call(kernel, (nr + nu,), [spec((n, D), lambda j: (0, 0), True), spec((n, NB), lambda j: (0, uc(j))),
                spec((dp, NB, w), lambda j: (0, rc(j), 0)), spec((dp, NB, w), lambda j: (0, uc(j), 0))],
                [spec((n, NB), lambda j: (0, rc(j))), spec((n, NB), lambda j: (0, uc(j)))],
                [jax.ShapeDtypeStruct((n, R), BF), jax.ShapeDtypeStruct((n, U), BF)],
                flops=2 * n * D * (R + U), nbytes=2 * (n * D + D * (R + U) + n * (R + 2 * U)), name="back_in")(gr, gp, wd, wn)


def back_out(dmix, df, wq, wu, base, extra, vec, stats):
    n, C = dmix.shape
    U = df.shape[1]
    D = wq.shape[0]
    NB = 256

    def kernel(*refs):
        if extra is None:
            dm_r, df_r, wq_r, wu_r, base_r, vec_r, st_r, e_r, g_r = refs
        else:
            dm_r, df_r, wq_r, wu_r, base_r, extra_r, vec_r, st_r, e_r, g_r = refs
        nt = (((1,), (1,)), ((), ()))
        d1 = lax.dot_general(dm_r[...], wq_r[...], nt, preferred_element_type=F32)
        d2 = lax.dot_general(df_r[...], wu_r[...], nt, preferred_element_type=F32)
        e_r[...] = (d1 * vec_r[0:1, :] + d2 * vec_r[2:3, :]).astype(BF)
        x = base_r[...].astype(F32)
        if extra is not None:
            x = x + extra_r[...].astype(F32) + vec_r[4:5, :] + vec_r[5:6, :]
        xhat = (x - st_r[:, 0:1]) * st_r[:, 1:2]
        g_r[0:1, :] = jnp.sum(d1 * xhat, axis=0, keepdims=True)
        g_r[1:2, :] = jnp.sum(d1, axis=0, keepdims=True)
        g_r[2:3, :] = jnp.sum(d2 * xhat, axis=0, keepdims=True)
        g_r[3:4, :] = jnp.sum(d2, axis=0, keepdims=True)

    whole = lambda j: (0, 0)
    col = lambda j: (0, j)
    row = lambda j: (j, 0)
    xs = [spec((n, NB), col)] + ([] if extra is None else [spec((n, NB), col)])
    args = [base] + ([] if extra is None else [extra])
    return call(kernel, (D // NB,), [spec((n, C), whole, True), spec((n, U), whole, True), spec((NB, C), row), spec((NB, U), row)] + xs +
                [spec((6, NB), col), spec((n, 128), whole)],
                [spec((n, NB), col), spec((4, NB), col)],
                [jax.ShapeDtypeStruct((n, D), BF), jax.ShapeDtypeStruct((4, D), F32)],
                flops=2 * n * D * (C + U), nbytes=2 * (n * (C + U) + D * (C + U) + n * D * 3), name="back_out")(dmix, df, wq, wu, *args, vec, stats)


def weight_grad(left, right, w=None):
    n, M = left.shape
    N = right.shape[1]
    MB = 256

    def kernel(l_r, r_r, o_r, s_r):
        g = lax.dot_general(l_r[...], r_r[...], (((0,), (0,)), ((), ())), preferred_element_type=F32)
        if w is None:
            o_r[...] = g.astype(BF)
        else:
            for s in range(N // w):
                o_r[s] = g[:, s * w:(s + 1) * w].astype(BF)

        @pl.when(pl.program_id(0) == 0)
        def _():
            s_r[...] = jnp.sum(r_r[...].astype(F32), axis=0, keepdims=True)

    whole = lambda j: (0, 0)
    if w is None:
        out, shape = spec((MB, N), lambda j: (j, 0)), (M, N)
    else:
        out, shape = spec((N // w, MB, w), lambda j: (0, j, 0)), (N // w, M, w)
    return call(kernel, (M // MB,), [spec((n, MB), lambda j: (0, j)), spec((n, N), whole, True)], [out, spec((1, N), whole)],
                [jax.ShapeDtypeStruct(shape, BF), jax.ShapeDtypeStruct((1, N), F32)],
                flops=2 * n * M * N, nbytes=2 * (n * M + n * N + M * N), name="wgrad")(left, right)


def norm_back(gout, e, base, extra, vec, stats, last):
    n, D = base.shape
    RB = 128

    def kernel(*refs):
        g_r, e_r, base_r = refs[:3]
        refs = refs[3:]
        if extra is not None:
            extra_r, refs = refs[0], refs[1:]
        vec_r, st_r, dx_r = refs[:3]
        x = base_r[...].astype(F32)
        if extra is not None:
            x = x + extra_r[...].astype(F32) + vec_r[4:5, :] + vec_r[5:6, :]
        xhat = (x - st_r[:, 0:1]) * st_r[:, 1:2]
        ev = e_r[...].astype(F32)
        me = jnp.mean(ev, axis=1, keepdims=True)
        mx = jnp.mean(ev * xhat, axis=1, keepdims=True)
        dx = g_r[...].astype(F32) + (ev - me - xhat * mx) * st_r[:, 1:2]
        dx_r[...] = dx
        if not last:
            low_r, sum_r = refs[3:]
            low_r[...] = dx.astype(BF)

            @pl.when(pl.program_id(0) == 0)
            def _():
                sum_r[...] = jnp.zeros_like(sum_r)

            sum_r[...] += jnp.sum(dx, axis=0, keepdims=True)

    row = lambda i: (i, 0)
    whole = lambda i: (0, 0)
    rows = spec((RB, D), row)
    ins = [rows, rows, rows] + ([] if extra is None else [rows]) + [spec((6, D), whole), spec((RB, 128), row)]
    args = [gout, e, base] + ([] if extra is None else [extra]) + [vec, stats]
    outs, shapes = [rows], [jax.ShapeDtypeStruct((n, D), F32)]
    if not last:
        outs += [rows, spec((1, D), whole)]
        shapes += [jax.ShapeDtypeStruct((n, D), BF), jax.ShapeDtypeStruct((1, D), F32)]
    return call(kernel, (n // RB,), ins, outs, shapes, flops=10 * n * D, nbytes=16 * n * D, name="norm_back")(*args)


MESH = pl.DeviceIdType.MESH


class Spot:
    def __init__(self):
        i = lax.axis_index("dp")
        c, x, y = lax.rem(i, 2), lax.rem(lax.div(i, 2), 2), lax.div(i, 4)
        self.me = i
        self.dx, self.dy, self.dc = 2 - 4 * x, 4 - 8 * y, 1 - 2 * c
        self.nx, self.ny, self.nc = i + self.dx, i + self.dy, i + self.dc
        self.diag = i + self.dx + self.dy
        z = lax.axis_index("mp")
        self.z = z
        self.outer = (z == 0) | (z == 3)
        self.inner = (z == 1) | (z == 2)
        self.pair = z + 1 - 2 * lax.rem(z, 2)
        self.across = 3 - z

    def meet(self, line):
        barrier = pltpu.get_barrier_semaphore()
        for peer in (self.nx, self.ny, self.nc):
            pl.semaphore_signal(barrier, inc=1, device_id={"dp": peer}, device_id_type=MESH)
        if line:
            pl.semaphore_signal(barrier, inc=1, device_id={"mp": self.pair}, device_id_type=MESH)

            @pl.when(self.inner)
            def _():
                pl.semaphore_signal(barrier, inc=1, device_id={"mp": self.across}, device_id_type=MESH)

            @pl.when(self.inner)
            def _():
                pl.semaphore_wait(barrier, 5)

            @pl.when(self.outer)
            def _():
                pl.semaphore_wait(barrier, 4)
        else:
            pl.semaphore_wait(barrier, 3)


def send_to(axis, peer, src, dst, send, recv):
    return pltpu.make_async_remote_copy(src_ref=src, dst_ref=dst, send_sem=send, recv_sem=recv, device_id={axis: peer}, device_id_type=MESH)


class Gather:
    copies = 9

    def __init__(self, spot, items, send, recv, local):
        self.spot, self.items, self.send, self.recv, self.local = spot, items, send, recv, local
        self.sent = []
        self.own = []

    def go(self, k, n, peer, src, dst):
        copy = send_to("dp", peer, src, dst, self.send.at[k, n], self.recv.at[k, n])
        copy.start()
        self.sent.append(copy)

    def arrived(self, k, n, dst):
        send_to("dp", self.spot.nc, dst, dst, self.send.at[k, n], self.recv.at[k, n]).wait_recv()

    def first(self, k):
        s, (src, out) = self.spot, self.items[k]
        for n, peer in enumerate((s.nx, s.ny, s.nc)):
            self.go(k, n, peer, src, out.at[s.me])
        copy = pltpu.make_async_copy(src, out.at[s.me], self.local.at[k])
        copy.start()
        self.own.append(copy)

    def halves(self, k):
        h = self.items[k][1].shape[1] // 2
        return pl.ds(0, h), pl.ds(h, h)

    def second(self, k):
        s, (_, out) = self.spot, self.items[k]
        low, high = self.halves(k)
        self.arrived(k, 0, out.at[s.nx])
        self.go(k, 3, s.ny, out.at[s.nx, high], out.at[s.nx, high])
        self.go(k, 4, s.nc, out.at[s.nx], out.at[s.nx])
        self.arrived(k, 1, out.at[s.ny])
        self.go(k, 5, s.nx, out.at[s.ny, low], out.at[s.ny, low])
        self.go(k, 6, s.nc, out.at[s.ny], out.at[s.ny])

    def third(self, k):
        s, (_, out) = self.spot, self.items[k]
        low, high = self.halves(k)
        self.arrived(k, 3, out.at[s.diag, high])
        self.go(k, 7, s.nc, out.at[s.diag, high], out.at[s.diag, high])
        self.arrived(k, 5, out.at[s.diag, low])
        self.go(k, 8, s.nc, out.at[s.diag, low], out.at[s.diag, low])

    def last(self, k):
        s, (_, out) = self.spot, self.items[k]
        low, high = self.halves(k)
        self.arrived(k, 2, out.at[s.nc])
        self.arrived(k, 4, out.at[s.nx + s.dc])
        self.arrived(k, 6, out.at[s.ny + s.dc])
        self.arrived(k, 7, out.at[s.diag + s.dc, high])
        self.arrived(k, 8, out.at[s.diag + s.dc, low])

    def close(self):
        for copy in self.own:
            copy.wait()
        for copy in self.sent:
            copy.wait_send()


class LineSum:
    copies = 3

    def __init__(self, spot, part, stage, land, swap, out, send, recv, local, chunks):
        self.spot, self.part, self.stage, self.land, self.swap, self.out = spot, part, stage, land, swap, out
        self.send, self.recv, self.local, self.chunks = send, recv, local, chunks
        self.rows = part.shape[0] // chunks

    def cut(self, k):
        return pl.ds(k * self.rows, self.rows)

    def copy(self, k, n):
        s, rows = self.spot, self.cut(k)
        if n == 0:
            peer, src, dst = s.pair, self.part, self.land
        elif n == 1:
            peer, src, dst = s.across, self.land, self.swap
        else:
            peer, src, dst = s.pair, self.swap, self.swap
        return send_to("mp", peer, src.at[rows], dst.at[rows], self.send.at[k, n], self.recv.at[k, n])

    def keep(self, k):
        rows = self.cut(k)
        return pltpu.make_async_copy(self.swap.at[rows], self.out.at[rows], self.local.at[k])

    def load(self, k):
        return pltpu.make_async_copy(self.part.at[self.cut(k)], self.stage.at[k % 2], self.local.at[self.chunks + k % 2])

    def add(self, k, dst, one, two, base):
        step = 32

        @pl.loop(0, self.rows // step)
        def _(i):
            rows = pl.ds(pl.multiple_of(k * self.rows + i * step, step), step)
            there = pl.ds(pl.multiple_of(base + i * step, step), step)
            dst[rows, :] = (one[there, :].astype(F32) + two[rows, :].astype(F32)).astype(BF)

    def tick(self, t):
        n = self.chunks

        @pl.when(self.spot.outer)
        def _():
            if t < n:
                if t >= 2:
                    self.copy(t - 2, 0).wait_send()
                self.copy(t, 0).start()
            elif t < n + 2:
                self.copy(t - 2, 0).wait_send()
            if 0 <= t - 3 < n:
                self.copy(t - 3, 2).wait_recv()
                self.keep(t - 3).start()

        @pl.when(self.spot.inner)
        def _():
            if t < n:
                if t == 0:
                    self.load(0).start()
                if t + 1 < n:
                    self.load(t + 1).start()
                self.load(t).wait()
                self.copy(t, 0).wait_recv()
                self.add(t, self.land, self.stage.at[t % 2], self.land, 0)
                self.copy(t, 1).start()
            if 0 <= t - 1 < n:
                self.copy(t - 1, 1).wait_recv()
                self.copy(t - 1, 1).wait_send()
                self.add(t - 1, self.swap, self.land, self.swap, (t - 1) * self.rows)
                self.copy(t - 1, 2).start()
                self.keep(t - 1).start()

    def close(self):
        for k in range(self.chunks):
            self.keep(k).wait()

        @pl.when(self.spot.inner)
        def _():
            for k in range(self.chunks):
                self.copy(k, 2).wait_send()


class Scatter:
    copies = 10

    def __init__(self, spot, items, own, sib, fx, fy, gx, gy, send, recv, local):
        self.spot, self.items = spot, items
        self.own, self.sib, self.fx, self.fy, self.gx, self.gy = own, sib, fx, fy, gx, gy
        self.send, self.recv, self.local = send, recv, local
        self.sent, self.loads = [], {}

    def go(self, k, n, peer, src, dst):
        copy = send_to("dp", peer, src, dst, self.send.at[k, n], self.recv.at[k, n])
        copy.start()
        self.sent.append(copy)

    def arrived(self, k, n, dst):
        send_to("dp", self.spot.nc, dst, dst, self.send.at[k, n], self.recv.at[k, n]).wait_recv()

    def first(self, k):
        s, grad = self.spot, self.items[k][0]
        for m, slot in enumerate((s.me, s.nx, s.ny, s.diag)):
            self.go(k, m, s.nc, grad.at[slot + s.dc], self.sib[k].at[m])
        self.loads[k] = []
        for m, slot in enumerate((s.me, s.nx, s.ny, s.diag)):
            copy = pltpu.make_async_copy(grad.at[slot], self.own[k].at[m], self.local.at[k, m])
            copy.start()
            self.loads[k].append(copy)

    def over(self, r, c, body, start=0):
        step = 16
        while step * 2 * c <= 32768 and r % (step * 2) == 0:
            step *= 2

        @pl.loop(0, r // step)
        def _(i):
            body(pl.ds(pl.multiple_of(i * step, step), step), pl.ds(pl.multiple_of(start + i * step, step), step))

    def second(self, k):
        s = self.spot
        own, sib = self.own[k], self.sib[k]
        _, r, c = own.shape
        h = r // 2
        low, high = pl.ds(0, h), pl.ds(h, h)
        for m in (3, 1, 2, 0):
            self.loads[k][m].wait()
            self.arrived(k, m, sib.at[m])

            def add(rows, _, m=m):
                own[m, rows, :] = (own[m, rows, :].astype(F32) + sib[m, rows, :].astype(F32)).astype(BF)

            self.over(r, c, add)
            if m == 3:
                self.go(k, 5, s.nx, own.at[3, low], self.fx[k].at[1])
                self.go(k, 7, s.ny, own.at[3, high], self.fy[k].at[1])
            if m == 1:
                self.go(k, 4, s.nx, own.at[1, low], self.fx[k].at[0])
            if m == 2:
                self.go(k, 6, s.ny, own.at[2, high], self.fy[k].at[0])

    def third(self, k):
        s = self.spot
        own, fx, fy = self.own[k], self.fx[k], self.fy[k]
        _, r, c = own.shape
        h = r // 2
        self.arrived(k, 5, fx.at[1])

        def add_low(rows, _):
            fx[1, rows, :] = (own[2, rows, :].astype(F32) + fx[1, rows, :].astype(F32)).astype(BF)

        self.over(h, c, add_low)
        self.go(k, 8, s.ny, fx.at[1], self.gy[k])
        self.arrived(k, 7, fy.at[1])

        def add_high(rows, there):
            fy[1, rows, :] = (own[1, there, :].astype(F32) + fy[1, rows, :].astype(F32)).astype(BF)

        self.over(h, c, add_high, h)
        self.go(k, 9, s.nx, fy.at[1], self.gx[k])

    def last(self, k):
        own, out = self.own[k], self.items[k][1]
        fx, fy, gx, gy = self.fx[k], self.fy[k], self.gx[k], self.gy[k]
        _, r, c = own.shape
        h = r // 2
        self.arrived(k, 4, fx.at[0])
        self.arrived(k, 8, gy)

        def low(rows, _):
            out[rows, :] = own[0, rows, :].astype(F32) + fx[0, rows, :].astype(F32) + gy[rows, :].astype(F32)

        self.over(h, c, low)
        self.arrived(k, 6, fy.at[0])
        self.arrived(k, 9, gx)

        def high(rows, there):
            out[there, :] = own[0, there, :].astype(F32) + fy[0, rows, :].astype(F32) + gx[rows, :].astype(F32)

        self.over(h, c, high, h)

    def close(self):
        for copy in self.sent:
            copy.wait_send()


def link_kernel(name, ident, gather=None, sums=(), scatter=None, chunks=8, plan=None):
    shards = [] if gather is None else list(gather[0])
    layers = [] if gather is None else list(gather[1])
    sums, grads = list(sums), [] if scatter is None else list(scatter)
    ng, ns, nr = len(shards), len(sums), len(grads)
    HBM = pl.BlockSpec(memory_space=pl.ANY)
    VM_ = pl.BlockSpec(memory_space=pltpu.VMEM)
    shard_shape = lambda v, l: v.shape if l is None else v.shape[1:]
    ins = [HBM] * (ng + ns + nr)
    outs = [HBM] * ng + [HBM] * ns + [VM_] * nr
    shapes = [jax.ShapeDtypeStruct((8,) + shard_shape(v, l), v.dtype) for v, l in zip(shards, layers)]
    shapes += [jax.ShapeDtypeStruct(v.shape, BF) for v in sums]
    shapes += [jax.ShapeDtypeStruct(v.shape[1:], F32) for v in grads]
    scratch = []
    DMA = pltpu.SemaphoreType.DMA
    if ng:
        scratch += [DMA((ng, 9)), DMA((ng, 9)), DMA((ng,))]
    for v in sums:
        scratch += [pltpu.VMEM((2, v.shape[0] // chunks, v.shape[1]), BF), pltpu.VMEM(v.shape, BF), pltpu.VMEM(v.shape, BF), DMA((chunks, 3)), DMA((chunks, 3)), DMA((chunks + 2,))]
    if nr:
        scratch += [DMA((nr, 10)), DMA((nr, 10)), DMA((nr, 4))]
        for v in grads:
            _, r, c = v.shape
            scratch += [pltpu.VMEM((4, r, c), BF), pltpu.VMEM((4, r, c), BF), pltpu.VMEM((2, r // 2, c), BF), pltpu.VMEM((2, r // 2, c), BF),
                        pltpu.VMEM((r // 2, c), BF), pltpu.VMEM((r // 2, c), BF)]

    def kernel(*refs):
        refs = list(refs)
        take = lambda n: [refs.pop(0) for _ in range(n)]
        src, part, grad = take(ng), take(ns), take(nr)
        full, total, owned = take(ng), take(ns), take(nr)
        spot = Spot()
        spot.meet(bool(ns))
        G = S = None
        if ng:
            pick = lambda ref, l: ref if l is None else ref.at[l]
            G = Gather(spot, [(pick(a, l), b) for a, l, b in zip(src, layers, full)], *take(3))
        lines = []
        for k in range(ns):
            stage, land, swap, send, recv, local = take(6)
            lines.append(LineSum(spot, part[k], stage, land, swap, total[k], send, recv, local, chunks))
        if nr:
            send, recv, local = take(3)
            bufs = [take(6) for _ in range(nr)]
            S = Scatter(spot, list(zip(grad, owned)), *[[b[i] for b in bufs] for i in range(6)], send, recv, local)
        plan(G, lines, S)
        for part_ in [G, *lines, S]:
            if part_ is not None:
                part_.close()

    nbytes = sum(v.size * 2 for v in sums + grads) + sum(8 * v.size for v in shards)
    return pl.pallas_call(
        kernel, in_specs=ins, out_specs=outs, out_shape=shapes, scratch_shapes=scratch,
        compiler_params=pltpu.CompilerParams(vmem_limit_bytes=VM, collective_id=ident, has_side_effects=True),
        cost_estimate=pl.CostEstimate(flops=0, bytes_accessed=nbytes, transcendentals=0), name=name)(*shards, *sums, *grads)


def plan_gather(G, lines, S):
    n = len(G.items)
    for k in range(n):
        G.first(k)
    for k in range(n):
        G.second(k)
    for k in range(n):
        G.third(k)
    for k in range(n):
        G.last(k)


def woven(stages):
    def plan(G, lines, S):
        side = G if G is not None else S
        for k in range(len(side.items)):
            side.first(k)
        ticks = [(line, t) for line in lines for t in range(line.chunks + 3)]
        for at, (line, t) in enumerate(ticks):
            line.tick(t)
            for name, k in stages.get(at, ()):
                getattr(side, name)(k)
        for at in sorted(stages):
            if at >= len(ticks):
                for name, k in stages[at]:
                    getattr(side, name)(k)

    return plan


weave_gather = woven({2: [("second", 0), ("second", 1)], 4: [("second", 2)], 6: [("second", 3)], 7: [("third", 0), ("third", 1)], 8: [("third", 2)], 9: [("third", 3)],
                      99: [("last", 0), ("last", 1), ("last", 2), ("last", 3)]})
weave_scatter = woven({1: [("second", 0), ("second", 1)], 2: [("second", 2)], 3: [("second", 3)], 4: [("third", 0), ("third", 1)], 6: [("third", 2)], 8: [("third", 3)],
                       9: [("last", 0), ("last", 1)], 99: [("last", 2), ("last", 3)]})


def adam_update(weight, grad, first, second):
    first_new = beta_one * first + (1.0 - beta_one) * grad
    second_new = beta_two * second + (1.0 - beta_two) * grad * grad
    mean_hat = first_new / (1.0 - beta_one**ADAM_STEP)
    square_hat = second_new / (1.0 - beta_two**ADAM_STEP)
    new_weight = weight - rate * (mean_hat / (jnp.sqrt(square_hat) + adam_eps) + decay * weight)
    return grad, first_new, second_new, new_weight - weight


def adam_layer(layer, weights, grads, firsts, seconds, before):
    steps = 8
    blocks = [(w.shape[1] // steps, w.shape[2]) for w in weights]

    def kernel(*refs):
        ins, outs = refs[:16], refs[-16:]
        for i in range(4):
            g = ins[4 + i][...].astype(F32)
            made = adam_update(ins[i][...].astype(F32), g, ins[8 + i][...], ins[12 + i][...])
            for k in range(4):
                outs[4 * i + k][...] = made[k]

    at = lambda b: spec((None,) + b, lambda j: (layer, j, 0))
    ins = [at(b) for b in blocks] + [spec(b, lambda j: (j, 0)) for b in blocks] + [at(b) for b in blocks] * 2
    args = [*weights, *grads, *firsts, *seconds]
    alias = {}
    if before is not None:
        ins += [pl.BlockSpec(memory_space=pl.ANY)] * 16
        args += list(before)
        alias = {16 + i: i for i in range(16)}
    shapes = [jax.ShapeDtypeStruct(w.shape, F32) for w in weights for _ in range(4)]
    count = sum(w.shape[1] * w.shape[2] for w in weights)
    return pl.pallas_call(
        kernel, grid=(steps,), in_specs=ins, out_specs=[at(b) for b in blocks for _ in range(4)], out_shape=shapes,
        input_output_aliases=alias, compiler_params=pltpu.CompilerParams(vmem_limit_bytes=VM),
        cost_estimate=pl.CostEstimate(flops=20 * count, bytes_accessed=30 * count, transcendentals=0), name="adam")(*args)


def layout(lengths_row, rows):
    slots = lengths_row.shape[0]
    number = jnp.arange(slots, dtype=jnp.int32)
    ends = jnp.sum(jnp.where(number[None, :] <= number[:, None], lengths_row[None, :], 0), axis=1)
    starts = ends - lengths_row
    index = jnp.arange(rows, dtype=jnp.int32)
    inside = (index[:, None] >= starts[None, :]) & (index[:, None] < ends[None, :])
    valid = jnp.any(inside, axis=1)
    slot = jnp.sum(jnp.where(inside, number[None, :], 0), axis=1)
    first = jnp.sum(jnp.where(inside, starts[None, :], 0), axis=1)
    segment = jnp.where(valid, slot, slots + index)
    return segment, index - first, valid


class PlainLinks:
    def weights(self, shards, layer):
        wq, wd, wu, wn = [w[layer] for w in shards]
        rows = lambda v: lax.all_gather(v, "dp", axis=0, tiled=True)
        stack = lambda v: lax.all_gather(v, "dp", axis=0, tiled=False)
        return rows(wq), stack(wd), rows(wu), stack(wn)

    def share(self, v):
        return lax.psum(v, "mp")

    def owned(self, grads):
        cut = lambda g: lax.psum_scatter(g, "dp", scatter_dimension=0, tiled=True)
        gq, gd, gu, gn = grads
        return cut(gq), cut(gd)[0], cut(gu), cut(gn)[0]

    def begin(self, shards, flat):
        return self.weights(shards, 0), lax.all_gather(flat, "dp", axis=0, tiled=False)

    def middle(self, branch, shards):
        return self.share(branch), self.weights(shards, 1)

    def turn(self, e, grads):
        return self.share(e), self.owned(grads)

    def end(self, e, branch, grads):
        return self.share(e), self.share(branch), self.owned(grads)


class ChipLinks:
    def full(self, got):
        wq, wd, wu, wn = got
        return wq.reshape(-1, wq.shape[2]), wd, wu.reshape(-1, wu.shape[2]), wn

    def slots(self, grads):
        gq, gd, gu, gn = grads
        return gq.reshape(8, -1, gq.shape[1]), gd, gu.reshape(8, -1, gu.shape[1]), gn

    def begin(self, shards, flat):
        got = link_kernel("gather", 1, gather=([flat, *shards], [None, 0, 0, 0, 0]), plan=plan_gather)
        return self.full(got[1:]), got[0]

    def middle(self, branch, shards):
        got = link_kernel("sum_gather", 2, gather=(shards, [1] * 4), sums=(branch,), plan=weave_gather)
        return got[4], self.full(got[:4])

    def turn(self, e, grads):
        got = link_kernel("sum_scatter", 3, sums=(e,), scatter=self.slots(grads), plan=weave_scatter)
        return got[0], got[1:]

    def end(self, e, branch, grads):
        got = link_kernel("sums_scatter", 4, sums=(e, branch), scatter=self.slots(grads), plan=weave_scatter)
        return got[0], got[1], got[2:]


def flatten_small(parts):
    flat = jnp.concatenate([p.reshape(-1) for p in parts])
    return jnp.pad(flat, (0, -flat.size % 4096)).reshape(-1, 128)


def unpack_small(got, parts):
    got = got.reshape(got.shape[0], -1)
    out, at = [], 0
    for p in parts:
        piece = got[:, at:at + p.size].reshape((-1,) + p.shape)
        out.append(jnp.moveaxis(piece, 0, 2).reshape(p.shape[0], p.shape[1], -1))
        at += p.size
    return out


def body(links, tokens_in, cotangent, seq_lengths, *params):
    weights, small = params[:4], params[4:7]
    firsts, small_firsts = params[7:11], params[11:14]
    seconds, small_seconds = params[14:18], params[18:21]
    rows, D = tokens_in.shape
    segment, position, valid = layout(seq_lengths[0], rows)
    cos, sin = rope_tables(position)
    seg_col, seg_row = segment[:, None], segment[None, :]
    live = valid[:, None]
    first_full, got = links.begin(weights, flatten_small(small))
    qb, ub, vecs = unpack_small(got, small)
    qb = qb.reshape(LAYERS, 1, -1).astype(F32)
    ub = ub.reshape(LAYERS, 1, -1).astype(F32)
    vecs = vecs.astype(F32)

    held = [jnp.concatenate([vecs[layer, :4], vecs[layer - 1, 4:]]) for layer in range(LAYERS)]

    full, kept, extra = [first_full], [], None
    for layer in range(LAYERS):
        wq, wd, wu, wn = full[layer]
        h1, h2, mixed, act, gp, stats = project(tokens_in, extra, held[layer], wq, qb[layer], cos, sin, wu, ub[layer])
        ctx = attend_forward(mixed, seg_col, seg_row)
        branch = branch_out(ctx, act, wd, wn)
        kept.append((h1, h2, mixed, act, gp, stats, ctx, extra))
        if layer == 0:
            extra, made = links.middle(branch, weights)
            full.append(made)

    gout = gr = jnp.where(live, cotangent, 0).astype(BF)
    sums = jnp.sum(gout.astype(F32), axis=0, keepdims=True)
    big, little = [None] * LAYERS, [None] * LAYERS
    for layer in reversed(range(LAYERS)):
        wq, wd, wu, wn = full[layer]
        h1, h2, mixed, act, gp, stats, ctx, extra = kept[layer]
        dctx, df = back_in(gr, gp, wd, wn)
        dmix = attend_backward(mixed, dctx, seg_col, seg_row, cos, sin)
        e, norm_sums = back_out(dmix, df, wq, wu, tokens_in, extra, held[layer], stats)
        gd, _ = weight_grad(ctx, gr, w=wd.shape[2])
        gn, _ = weight_grad(act, gr, w=wn.shape[2])
        gq, qsum = weight_grad(h1, dmix)
        gu, usum = weight_grad(h2, df)
        if layer:
            e, big[layer] = links.turn(e, (gq, gd, gu, gn))
        else:
            e, branch, big[layer] = links.end(e, branch, (gq, gd, gu, gn))
        little[layer] = (qsum, usum, norm_sums, sums)
        made = norm_back(gout, e, tokens_in, extra, held[layer], stats, layer == 0)
        if layer:
            gout, gr, sums = made
        else:
            input_grad = made[0]
    x_last = tokens_in.astype(F32) + kept[1][-1].astype(F32) + vecs[0, 4] + vecs[0, 5] + branch.astype(F32) + vecs[1, 4] + vecs[1, 5]
    output = jnp.where(live, x_last, 0.0).astype(BF)

    done = None
    for layer in reversed(range(LAYERS)):
        done = adam_layer(layer, weights, big[layer], firsts, seconds, done)

    z, line = lax.axis_index("mp"), lax.axis_size("mp")
    bias = jnp.concatenate([jnp.stack([t[i] for t in little]).reshape(-1) for i in (0, 1)])
    bias = jnp.where(jnp.arange(line)[:, None] == z, bias[None, :], 0.0)
    norm_sums = jnp.stack([t[2] for t in little])
    out_sums = jnp.where(z == 0, jnp.stack([t[3] for t in little]), 0.0)
    vec_sum = jnp.concatenate([norm_sums, out_sums, out_sums], axis=1).reshape(-1)
    total = lax.psum(jnp.concatenate([bias.reshape(-1), vec_sum]), ("dp", "mp"))
    bias = lax.dynamic_slice_in_dim(total[:bias.size].reshape(bias.shape), z, 1, 0)[0]
    total = jnp.concatenate([bias, total[-vec_sum.size:]])
    me = lax.axis_index("dp")
    small_out, at = [], 0
    for p, first, second in zip(small, small_firsts, small_seconds):
        width = p.shape[2]
        wide = p.shape[:2] + (lax.axis_size("dp") * width,)
        size = wide[0] * wide[1] * wide[2]
        g = lax.dynamic_slice_in_dim(total[at:at + size].reshape(wide), me * width, width, 2)
        at += size
        small_out += adam_update(p.astype(F32), g, first, second)
    return (output, input_grad, *done, *small_out)


def solution(mesh):
    rows_dp = P("dp", None)
    wide, tall, vec = P(None, "dp", "mp"), P(None, "mp", "dp"), P(None, None, "dp")
    group = (wide, tall, wide, tall, tall, tall, vec)
    return jax.shard_map(
        functools.partial(body, ChipLinks() if dict(mesh.shape) == {"dp": 8, "mp": 4} else PlainLinks()),
        mesh=mesh,
        in_specs=(rows_dp,) * 3 + group * 3,
        out_specs=(rows_dp,) * 2 + tuple(s for s in group for _ in range(4)),
        check_vma=False,
    )
```

```python
import functools
import jax
import jax.numpy as jnp
from jax import lax
from jax.experimental import pallas as pl
from jax.experimental.pallas import tpu as pltpu
from jax.sharding import PartitionSpec as P

HD = 256
ROT = 64
MAXLEN = 512
norm_eps = 1e-05
masked_score = -1e30
LAYERS = 2
ADAM_STEP = 10
beta_one = 0.9
beta_two = 0.95
adam_eps = 1e-08
rate = 0.02
decay = 0.01
VM = 60 * 1024 * 1024
BF = jnp.bfloat16
ROWS = 256
UPB = 512
F32 = jnp.float32


def call(kernel, grid, in_specs, out_specs, out_shape, scratch=(), flops=0, nbytes=0, name=None, ident=None):
    return pl.pallas_call(
        kernel,
        grid_spec=pltpu.PrefetchScalarGridSpec(num_scalar_prefetch=0, grid=grid, in_specs=in_specs, out_specs=out_specs, scratch_shapes=list(scratch)),
        out_shape=out_shape,
        compiler_params=pltpu.CompilerParams(vmem_limit_bytes=VM, collective_id=ident, has_side_effects=ident is not None),
        cost_estimate=pl.CostEstimate(flops=flops, bytes_accessed=nbytes, transcendentals=0),
        name=name,
    )


def spec(shape, index, single=False):
    if single:
        return pl.BlockSpec(shape, index, pipeline_mode=pl.Buffered(1))
    return pl.BlockSpec(shape, index)


def rope_tables(position):
    half = ROT // 2
    freq = 10000.0 ** (-(jnp.arange(half, dtype=F32) * 2.0) / ROT)
    angle = position.astype(F32)[:, None] * freq[None, :]
    c, s = jnp.cos(angle), jnp.sin(angle)
    rows = position.shape[0]
    one = jnp.ones((rows, 128 - ROT), F32)
    zero = jnp.zeros((rows, 128 - ROT), F32)
    return jnp.concatenate([c, c, one], axis=1), jnp.concatenate([-s, s, zero], axis=1)


def turn(u, c, s):
    lane = lax.broadcasted_iota(jnp.int32, u.shape, 1)
    other = jnp.where(lane < ROT // 2, pltpu.roll(u, 128 - ROT // 2, 1), pltpu.roll(u, ROT // 2, 1))
    return u * c + other * s


def normed(x):
    mean = jnp.mean(x, axis=1, keepdims=True)
    centred = x - mean
    var = jnp.mean(centred * centred, axis=1, keepdims=True)
    rstd = lax.rsqrt(var + norm_eps)
    return centred * rstd, mean, rstd


def row_blocks(n):
    step = min(n, ROWS)
    return [slice(i, i + step) for i in range(0, n, step)]


def project(base, extra, vec, wq, bq, cos, sin, wu, bu, shards=None):
    n, D = base.shape
    C, U = wq.shape[1], wu.shape[1]
    QB, UB = 3 * HD, min(UPB, U)
    nq, nu = C // QB, U // UB
    RB = 128
    nr = n // RB
    ng = 0 if shards is None else len(shards)
    xs = [base] if extra is None else [base, extra]

    def kernel(*refs):
        refs = list(refs)
        take = lambda k: [refs.pop(0) for _ in range(k)]
        x_rs = take(len(xs))
        vec_r, wq_r, bq_r, cos_r, sin_r, wu_r, bu_r = take(7)
        shard_rs = take(ng)
        h1_o, h2_o, mix_r, a_r, gp_r, st_r = take(6)
        full_rs = take(ng)
        h1_r, h2_r = take(2)
        bufs = take(len(xs))
        in_sem, out_sem = take(2)
        j = pl.program_id(0)
        side = None
        if ng:
            spot = Spot()
            side = Gather(spot, [(a.at[0], b) for a, b in zip(shard_rs, full_rs)], *take(3))

            @pl.when(j == 0)
            def _():
                spot.meet(False)
                side.first(0)
                side.first(1)

        def host(step, *stages):
            if side is not None:
                @pl.when(j == min(step, nq + nu - 1))
                def _():
                    for name, *args in stages:
                        getattr(side, name)(*args)
        block = lambda i: pl.ds(i * RB, RB)
        loads = [[pltpu.make_async_copy(x.at[block(i)], buf.at[block(i)], in_sem.at[k, i]) for k, (x, buf) in enumerate(zip(x_rs, bufs))] for i in range(nr)]
        stores = [[pltpu.make_async_copy(h.at[block(i)], o.at[block(i)], out_sem.at[k, i]) for k, (h, o) in enumerate(((h1_r, h1_o), (h2_r, h2_o)))] for i in range(nr)]

        @pl.when(j == 0)
        def _():
            for group in loads:
                for copy in group:
                    copy.start()
            for i in range(nr):
                for copy in loads[i]:
                    copy.wait()
                rows = block(i)
                x = bufs[0][rows, :].astype(F32)
                if extra is not None:
                    x = x + bufs[1][rows, :].astype(F32) + vec_r[4:5, :] + vec_r[5:6, :]
                xhat, mean, rstd = normed(x)
                st_r[rows, 0:1] = mean
                st_r[rows, 1:2] = rstd
                h1_r[rows, :] = (xhat * vec_r[0:1, :] + vec_r[1:2, :]).astype(BF)
                h2_r[rows, :] = (xhat * vec_r[2:3, :] + vec_r[3:4, :]).astype(BF)
                for copy in stores[i]:
                    copy.start()

        @pl.when(j < nq)
        def _():
            for rows in row_blocks(n):
                for part in range(3):
                    at = part * HD
                    m = jnp.dot(h1_r[rows, :], wq_r[:, at:at + HD], preferred_element_type=F32) + bq_r[:, at:at + HD]
                    if part == 2:
                        mix_r[rows, at:at + HD] = m.astype(BF)
                    else:
                        mix_r[rows, at:at + 128] = turn(m[:, :128], cos_r[rows, :], sin_r[rows, :]).astype(BF)
                        mix_r[rows, at + 128:at + HD] = m[:, 128:].astype(BF)

        @pl.when(j >= nq)
        def _():
            for rows in row_blocks(n):
                for at in range(0, UB, 256):
                    cols = slice(at, at + 256)
                    f = jnp.dot(h2_r[rows, :], wu_r[:, cols], preferred_element_type=F32) + bu_r[:, cols]
                    phi = 0.5 * (1.0 + lax.erf(f * 0.7071067811865476))
                    a_r[rows, cols] = (f * phi).astype(BF)
                    gp_r[rows, cols] = (phi + f * (jnp.exp(-0.5 * f * f) * 0.3989422804014327)).astype(BF)

        host(1, ("second", 0))
        host(3, ("second", 1), ("third", 0))
        host(5, ("third", 1), ("last", 0), ("last", 1), ("close",))

        @pl.when(j == nq + nu - 1)
        def _():
            for group in stores:
                for copy in group:
                    copy.wait()

    whole = lambda j: (0, 0)
    qcol = lambda j: (0, jnp.minimum(j, nq - 1))
    ucol = lambda j: (0, jnp.maximum(j - nq, 0))
    far = pl.BlockSpec(memory_space=pl.ANY)
    ins = [far] * len(xs) + [
        spec((6, D), whole), spec((D, QB), qcol), spec((1, QB), qcol), spec((n, 128), whole, True), spec((n, 128), whole, True),
        spec((D, UB), ucol), spec((1, UB), ucol)] + [far] * ng
    outs = [far, far, spec((n, QB), qcol), spec((n, UB), ucol), spec((n, UB), ucol), spec((n, 128), whole)] + [far] * ng
    shapes = [jax.ShapeDtypeStruct(s, BF) for s in ((n, D), (n, D), (n, C), (n, U), (n, U))] + [jax.ShapeDtypeStruct((n, 128), F32)]
    DMA = pltpu.SemaphoreType.DMA
    scratch = [pltpu.VMEM((n, D), BF)] * (2 + len(xs)) + [DMA((len(xs), nr)), DMA((2, nr))]
    if ng:
        scratch += [DMA((ng, 9)), DMA((ng, 9)), DMA((ng,))]
        shapes += [jax.ShapeDtypeStruct((8,) + v.shape[1:], v.dtype) for v in shards]
    return call(kernel, (nq + nu,), ins, outs, shapes, scratch, ident=5 if ng else None, flops=2 * n * D * (C + U), nbytes=2 * (n * D * 3 + D * (C + U) + n * (C + 2 * U)), name="project")(*xs, vec, wq, bq, cos, sin, wu, bu, *(shards or ()))


def softmax_block(q, k, segq, segk, q0, k0):
    s = lax.dot_general(q, k, (((1,), (1,)), ((), ())), preferred_element_type=F32) * HD ** (-0.5)
    qi = q0 + lax.broadcasted_iota(jnp.int32, s.shape, 0)
    ki = k0 + lax.broadcasted_iota(jnp.int32, s.shape, 1)
    allowed = (segq == segk) & (ki <= qi)
    s = jnp.where(allowed, s, masked_score)
    top = jnp.max(s, axis=1, keepdims=True)
    e = jnp.exp(s - top)
    return e / jnp.sum(e, axis=1, keepdims=True)


def windows(n, qb):
    for i in range(n // qb):
        q0 = i * qb
        yield q0, max(0, q0 - MAXLEN)


def attend_forward(mixed, seg_col, seg_row):
    n, C = mixed.shape
    H = C // (3 * HD)
    qb = 256

    def kernel(q_r, k_r, v_r, sc_r, sr_r, o_r):
        for q0, k0 in windows(n, qb):
            qs, ks = slice(q0, q0 + qb), slice(k0, q0 + qb)
            p = softmax_block(q_r[qs, :], k_r[ks, :], sc_r[qs, :], sr_r[:, ks], q0, k0)
            o_r[qs, :] = jnp.dot(p.astype(BF), v_r[ks, :], preferred_element_type=F32).astype(BF)

    part = lambda t: spec((n, HD), lambda h: (0, 3 * h + t))
    return call(kernel, (H,), [part(0), part(1), part(2), spec((n, 1), lambda h: (0, 0)), spec((1, n), lambda h: (0, 0))],
                spec((n, HD), lambda h: (0, h)), jax.ShapeDtypeStruct((n, H * HD), BF),
                flops=H * n * 640 * HD * 4, nbytes=2 * n * C, name="attend")(mixed, mixed, mixed, seg_col, seg_row)


def attend_backward(mixed, dctx, seg_col, seg_row, cos, sin):
    n, C = mixed.shape
    H = C // (3 * HD)
    qb = 256
    scale = HD ** (-0.5)

    def kernel(q_r, k_r, v_r, do_r, sc_r, sr_r, cos_r, sin_r, o_r, dk_s, dv_s):
        def back(u, rows):
            c, s = cos_r[rows, :], -sin_r[rows, :]
            return jnp.concatenate([turn(u[:, :128], c, s), u[:, 128:]], axis=1).astype(BF)

        dk_s[...] = jnp.zeros_like(dk_s)
        dv_s[...] = jnp.zeros_like(dv_s)
        for q0, k0 in reversed(list(windows(n, qb))):
            qs, ks = slice(q0, q0 + qb), slice(k0, q0 + qb)
            q, k, do = q_r[qs, :], k_r[ks, :], do_r[qs, :]
            p = softmax_block(q, k, sc_r[qs, :], sr_r[:, ks], q0, k0)
            dp = lax.dot_general(do, v_r[ks, :], (((1,), (1,)), ((), ())), preferred_element_type=F32)
            delta = jnp.sum(p * dp, axis=1, keepdims=True)
            ds = (p * (dp - delta)).astype(BF)
            dq = jnp.dot(ds, k, preferred_element_type=F32) * scale
            dk_s[ks, :] += lax.dot_general(ds, q, (((0,), (0,)), ((), ())), preferred_element_type=F32)
            dv_s[ks, :] += lax.dot_general(p.astype(BF), do, (((0,), (0,)), ((), ())), preferred_element_type=F32)
            o_r[qs, :HD] = back(dq, qs)
            o_r[qs, HD:2 * HD] = back(dk_s[qs, :] * scale, qs)
            o_r[qs, 2 * HD:] = dv_s[qs, :].astype(BF)

    part = lambda t: spec((n, HD), lambda h: (0, 3 * h + t))
    whole = lambda h: (0, 0)
    return call(kernel, (H,), [part(0), part(1), part(2), spec((n, HD), lambda h: (0, h)), spec((n, 1), whole), spec((1, n), whole),
                spec((n, 128), whole), spec((n, 128), whole)],
                spec((n, 3 * HD), lambda h: (0, h)), jax.ShapeDtypeStruct((n, C), BF),
                scratch=[pltpu.VMEM((n, HD), F32), pltpu.VMEM((n, HD), F32)],
                flops=H * n * 640 * HD * 10, nbytes=4 * n * C, name="attend_back")(mixed, mixed, mixed, dctx, seg_col, seg_row, cos, sin)


def branch_out(ctx, act, wd, wn):
    n, R = ctx.shape
    U = act.shape[1]
    dp, _, w = wd.shape

    def kernel(c_r, a_r, wd_r, wn_r, o_r):
        o_r[...] = (jnp.dot(c_r[...], wd_r[...], preferred_element_type=F32) + jnp.dot(a_r[...], wn_r[...], preferred_element_type=F32)).astype(BF)

    whole = lambda s: (0, 0)
    pick = lambda s: (s, 0, 0)
    return call(kernel, (dp,), [spec((n, R), whole, True), spec((n, U), whole, True), spec((None, R, w), pick), spec((None, U, w), pick)],
                spec((n, w), lambda s: (0, s)), jax.ShapeDtypeStruct((n, dp * w), BF),
                flops=2 * n * dp * w * (R + U), nbytes=2 * (n * (R + U) + dp * w * (R + U + n)), name="branch")(ctx, act, wd, wn)


def back_in(gr, gp, wd, wn):
    n, D = gr.shape
    dp, R, w = wd.shape
    U = wn.shape[1]
    NB = 256
    nr, nu = R // NB, U // NB

    def kernel(g_r, gp_r, wd_r, wn_r, dc_r, df_r):
        j = pl.program_id(0)

        def times(w_r):
            acc = None
            for s in range(dp):
                t = lax.dot_general(g_r[:, s * w:(s + 1) * w], w_r[s], (((1,), (1,)), ((), ())), preferred_element_type=F32)
                acc = t if acc is None else acc + t
            return acc

        @pl.when(j < nr)
        def _():
            dc_r[...] = times(wd_r).astype(BF)

        @pl.when(j >= nr)
        def _():
            df_r[...] = (times(wn_r) * gp_r[...].astype(F32)).astype(BF)

    rc = lambda j: jnp.minimum(j, nr - 1)
    uc = lambda j: jnp.maximum(j - nr, 0)
    return call(kernel, (nr + nu,), [spec((n, D), lambda j: (0, 0), True), spec((n, NB), lambda j: (0, uc(j))),
                spec((dp, NB, w), lambda j: (0, rc(j), 0)), spec((dp, NB, w), lambda j: (0, uc(j), 0))],
                [spec((n, NB), lambda j: (0, rc(j))), spec((n, NB), lambda j: (0, uc(j)))],
                [jax.ShapeDtypeStruct((n, R), BF), jax.ShapeDtypeStruct((n, U), BF)],
                flops=2 * n * D * (R + U), nbytes=2 * (n * D + D * (R + U) + n * (R + 2 * U)), name="back_in")(gr, gp, wd, wn)


def back_out(dmix, df, wq, wu, base, extra, vec, stats):
    n, C = dmix.shape
    U = df.shape[1]
    D = wq.shape[0]
    NB = 256

    def kernel(*refs):
        if extra is None:
            dm_r, df_r, wq_r, wu_r, base_r, vec_r, st_r, e_r, g_r = refs
        else:
            dm_r, df_r, wq_r, wu_r, base_r, extra_r, vec_r, st_r, e_r, g_r = refs
        nt = (((1,), (1,)), ((), ()))
        d1 = lax.dot_general(dm_r[...], wq_r[...], nt, preferred_element_type=F32)
        d2 = lax.dot_general(df_r[...], wu_r[...], nt, preferred_element_type=F32)
        e_r[...] = (d1 * vec_r[0:1, :] + d2 * vec_r[2:3, :]).astype(BF)
        x = base_r[...].astype(F32)
        if extra is not None:
            x = x + extra_r[...].astype(F32) + vec_r[4:5, :] + vec_r[5:6, :]
        xhat = (x - st_r[:, 0:1]) * st_r[:, 1:2]
        g_r[0:1, :] = jnp.sum(d1 * xhat, axis=0, keepdims=True)
        g_r[1:2, :] = jnp.sum(d1, axis=0, keepdims=True)
        g_r[2:3, :] = jnp.sum(d2 * xhat, axis=0, keepdims=True)
        g_r[3:4, :] = jnp.sum(d2, axis=0, keepdims=True)

    whole = lambda j: (0, 0)
    col = lambda j: (0, j)
    row = lambda j: (j, 0)
    xs = [spec((n, NB), col)] + ([] if extra is None else [spec((n, NB), col)])
    args = [base] + ([] if extra is None else [extra])
    return call(kernel, (D // NB,), [spec((n, C), whole, True), spec((n, U), whole, True), spec((NB, C), row), spec((NB, U), row)] + xs +
                [spec((6, NB), col), spec((n, 128), whole)],
                [spec((n, NB), col), spec((4, NB), col)],
                [jax.ShapeDtypeStruct((n, D), BF), jax.ShapeDtypeStruct((4, D), F32)],
                flops=2 * n * D * (C + U), nbytes=2 * (n * (C + U) + D * (C + U) + n * D * 3), name="back_out")(dmix, df, wq, wu, *args, vec, stats)


def weight_grad(left, right, w=None):
    n, M = left.shape
    N = right.shape[1]
    MB = 256

    def kernel(l_r, r_r, o_r, s_r):
        g = lax.dot_general(l_r[...], r_r[...], (((0,), (0,)), ((), ())), preferred_element_type=F32)
        if w is None:
            o_r[...] = g.astype(BF)
        else:
            for s in range(N // w):
                o_r[s] = g[:, s * w:(s + 1) * w].astype(BF)

        @pl.when(pl.program_id(0) == 0)
        def _():
            s_r[...] = jnp.sum(r_r[...].astype(F32), axis=0, keepdims=True)

    whole = lambda j: (0, 0)
    if w is None:
        out, shape = spec((MB, N), lambda j: (j, 0)), (M, N)
    else:
        out, shape = spec((N // w, MB, w), lambda j: (0, j, 0)), (N // w, M, w)
    return call(kernel, (M // MB,), [spec((n, MB), lambda j: (0, j)), spec((n, N), whole, True)], [out, spec((1, N), whole)],
                [jax.ShapeDtypeStruct(shape, BF), jax.ShapeDtypeStruct((1, N), F32)],
                flops=2 * n * M * N, nbytes=2 * (n * M + n * N + M * N), name="wgrad")(left, right)


def norm_back(gout, e, base, extra, vec, stats, last):
    n, D = base.shape
    RB = 128

    def kernel(*refs):
        g_r, e_r, base_r = refs[:3]
        refs = refs[3:]
        if extra is not None:
            extra_r, refs = refs[0], refs[1:]
        vec_r, st_r, dx_r = refs[:3]
        x = base_r[...].astype(F32)
        if extra is not None:
            x = x + extra_r[...].astype(F32) + vec_r[4:5, :] + vec_r[5:6, :]
        xhat = (x - st_r[:, 0:1]) * st_r[:, 1:2]
        ev = e_r[...].astype(F32)
        me = jnp.mean(ev, axis=1, keepdims=True)
        mx = jnp.mean(ev * xhat, axis=1, keepdims=True)
        dx = g_r[...].astype(F32) + (ev - me - xhat * mx) * st_r[:, 1:2]
        dx_r[...] = dx
        if not last:
            low_r, sum_r = refs[3:]
            low_r[...] = dx.astype(BF)

            @pl.when(pl.program_id(0) == 0)
            def _():
                sum_r[...] = jnp.zeros_like(sum_r)

            sum_r[...] += jnp.sum(dx, axis=0, keepdims=True)

    row = lambda i: (i, 0)
    whole = lambda i: (0, 0)
    rows = spec((RB, D), row)
    ins = [rows, rows, rows] + ([] if extra is None else [rows]) + [spec((6, D), whole), spec((RB, 128), row)]
    args = [gout, e, base] + ([] if extra is None else [extra]) + [vec, stats]
    outs, shapes = [rows], [jax.ShapeDtypeStruct((n, D), F32)]
    if not last:
        outs += [rows, spec((1, D), whole)]
        shapes += [jax.ShapeDtypeStruct((n, D), BF), jax.ShapeDtypeStruct((1, D), F32)]
    return call(kernel, (n // RB,), ins, outs, shapes, flops=10 * n * D, nbytes=16 * n * D, name="norm_back")(*args)


MESH = pl.DeviceIdType.MESH


class Spot:
    def __init__(self):
        i = lax.axis_index("dp")
        c, x, y = lax.rem(i, 2), lax.rem(lax.div(i, 2), 2), lax.div(i, 4)
        self.me = i
        self.dx, self.dy, self.dc = 2 - 4 * x, 4 - 8 * y, 1 - 2 * c
        self.nx, self.ny, self.nc = i + self.dx, i + self.dy, i + self.dc
        self.diag = i + self.dx + self.dy
        z = lax.axis_index("mp")
        self.z = z
        self.outer = (z == 0) | (z == 3)
        self.inner = (z == 1) | (z == 2)
        self.pair = z + 1 - 2 * lax.rem(z, 2)
        self.across = 3 - z

    def meet(self, line):
        barrier = pltpu.get_barrier_semaphore()
        for peer in (self.nx, self.ny, self.nc):
            pl.semaphore_signal(barrier, inc=1, device_id={"dp": peer}, device_id_type=MESH)
        if line:
            pl.semaphore_signal(barrier, inc=1, device_id={"mp": self.pair}, device_id_type=MESH)

            @pl.when(self.inner)
            def _():
                pl.semaphore_signal(barrier, inc=1, device_id={"mp": self.across}, device_id_type=MESH)

            @pl.when(self.inner)
            def _():
                pl.semaphore_wait(barrier, 5)

            @pl.when(self.outer)
            def _():
                pl.semaphore_wait(barrier, 4)
        else:
            pl.semaphore_wait(barrier, 3)


def send_to(axis, peer, src, dst, send, recv):
    return pltpu.make_async_remote_copy(src_ref=src, dst_ref=dst, send_sem=send, recv_sem=recv, device_id={axis: peer}, device_id_type=MESH)


class Gather:
    copies = 9

    def __init__(self, spot, items, send, recv, local):
        self.spot, self.items, self.send, self.recv, self.local = spot, items, send, recv, local
        self.sent = []
        self.own = []

    def go(self, k, n, peer, src, dst):
        send_to("dp", peer, src, dst, self.send.at[k, n], self.recv.at[k, n]).start()
        self.sent.append((k, n, peer, src, dst))

    def arrived(self, k, n, dst):
        send_to("dp", self.spot.nc, dst, dst, self.send.at[k, n], self.recv.at[k, n]).wait_recv()

    def first(self, k):
        s, (src, out) = self.spot, self.items[k]
        for n, peer in enumerate((s.nx, s.ny, s.nc)):
            self.go(k, n, peer, src, out.at[s.me])
        pltpu.make_async_copy(src, out.at[s.me], self.local.at[k]).start()
        self.own.append(k)

    def halves(self, k):
        h = self.items[k][1].shape[1] // 2
        return pl.ds(0, h), pl.ds(h, h)

    def second(self, k):
        s, (_, out) = self.spot, self.items[k]
        low, high = self.halves(k)
        self.arrived(k, 0, out.at[s.nx])
        self.go(k, 3, s.ny, out.at[s.nx, high], out.at[s.nx, high])
        self.go(k, 4, s.nc, out.at[s.nx], out.at[s.nx])
        self.arrived(k, 1, out.at[s.ny])
        self.go(k, 5, s.nx, out.at[s.ny, low], out.at[s.ny, low])
        self.go(k, 6, s.nc, out.at[s.ny], out.at[s.ny])

    def third(self, k):
        s, (_, out) = self.spot, self.items[k]
        low, high = self.halves(k)
        self.arrived(k, 3, out.at[s.diag, high])
        self.go(k, 7, s.nc, out.at[s.diag, high], out.at[s.diag, high])
        self.arrived(k, 5, out.at[s.diag, low])
        self.go(k, 8, s.nc, out.at[s.diag, low], out.at[s.diag, low])

    def last(self, k):
        s, (_, out) = self.spot, self.items[k]
        low, high = self.halves(k)
        self.arrived(k, 2, out.at[s.nc])
        self.arrived(k, 4, out.at[s.nx + s.dc])
        self.arrived(k, 6, out.at[s.ny + s.dc])
        self.arrived(k, 7, out.at[s.diag + s.dc, high])
        self.arrived(k, 8, out.at[s.diag + s.dc, low])

    def close(self):
        for k in self.own:
            src, out = self.items[k]
            pltpu.make_async_copy(src, out.at[self.spot.me], self.local.at[k]).wait()
        for k, n, peer, src, dst in self.sent:
            send_to("dp", peer, src, dst, self.send.at[k, n], self.recv.at[k, n]).wait_send()


class LineSum:
    copies = 3

    def __init__(self, spot, part, stage, land, swap, out, send, recv, local, chunks):
        self.spot, self.part, self.stage, self.land, self.swap, self.out = spot, part, stage, land, swap, out
        self.send, self.recv, self.local, self.chunks = send, recv, local, chunks
        self.rows = part.shape[0] // chunks

    def cut(self, k):
        return pl.ds(k * self.rows, self.rows)

    def copy(self, k, n):
        s, rows = self.spot, self.cut(k)
        if n == 0:
            peer, src, dst = s.pair, self.part, self.land
        elif n == 1:
            peer, src, dst = s.across, self.land, self.swap
        else:
            peer, src, dst = s.pair, self.swap, self.swap
        return send_to("mp", peer, src.at[rows], dst.at[rows], self.send.at[k, n], self.recv.at[k, n])

    def keep(self, k):
        rows = self.cut(k)
        return pltpu.make_async_copy(self.swap.at[rows], self.out.at[rows], self.local.at[k])

    def load(self, k):
        return pltpu.make_async_copy(self.part.at[self.cut(k)], self.stage.at[k % 2], self.local.at[self.chunks + k % 2])

    def add(self, k, dst, one, two, base):
        step = 32

        @pl.loop(0, self.rows // step)
        def _(i):
            rows = pl.ds(pl.multiple_of(k * self.rows + i * step, step), step)
            there = pl.ds(pl.multiple_of(base + i * step, step), step)
            dst[rows, :] = (one[there, :].astype(F32) + two[rows, :].astype(F32)).astype(BF)

    def tick(self, t):
        n = self.chunks

        @pl.when(self.spot.outer)
        def _():
            if t < n:
                if t >= 2:
                    self.copy(t - 2, 0).wait_send()
                self.copy(t, 0).start()
            elif t < n + 2:
                self.copy(t - 2, 0).wait_send()
            if 0 <= t - 3 < n:
                self.copy(t - 3, 2).wait_recv()
                self.keep(t - 3).start()

        @pl.when(self.spot.inner)
        def _():
            if t < n:
                if t == 0:
                    self.load(0).start()
                if t + 1 < n:
                    self.load(t + 1).start()
                self.load(t).wait()
                self.copy(t, 0).wait_recv()
                self.add(t, self.land, self.stage.at[t % 2], self.land, 0)
                self.copy(t, 1).start()
            if 0 <= t - 1 < n:
                self.copy(t - 1, 1).wait_recv()
                self.copy(t - 1, 1).wait_send()
                self.add(t - 1, self.swap, self.land, self.swap, (t - 1) * self.rows)
                self.copy(t - 1, 2).start()
                self.keep(t - 1).start()

    def close(self):
        for k in range(self.chunks):
            self.keep(k).wait()

        @pl.when(self.spot.inner)
        def _():
            for k in range(self.chunks):
                self.copy(k, 2).wait_send()


class Scatter:
    copies = 10

    def __init__(self, spot, items, own, sib, fx, fy, gx, gy, send, recv, local):
        self.spot, self.items = spot, items
        self.own, self.sib, self.fx, self.fy, self.gx, self.gy = own, sib, fx, fy, gx, gy
        self.send, self.recv, self.local = send, recv, local
        self.sent, self.loads = [], {}

    def go(self, k, n, peer, src, dst):
        copy = send_to("dp", peer, src, dst, self.send.at[k, n], self.recv.at[k, n])
        copy.start()
        self.sent.append(copy)

    def arrived(self, k, n, dst):
        send_to("dp", self.spot.nc, dst, dst, self.send.at[k, n], self.recv.at[k, n]).wait_recv()

    def first(self, k):
        s, grad = self.spot, self.items[k][0]
        for m, slot in enumerate((s.me, s.nx, s.ny, s.diag)):
            self.go(k, m, s.nc, grad.at[slot + s.dc], self.sib[k].at[m])
        self.loads[k] = []
        for m, slot in enumerate((s.me, s.nx, s.ny, s.diag)):
            copy = pltpu.make_async_copy(grad.at[slot], self.own[k].at[m], self.local.at[k, m])
            copy.start()
            self.loads[k].append(copy)

    def over(self, r, c, body, start=0):
        step = 16
        while step * 2 * c <= 32768 and r % (step * 2) == 0:
            step *= 2

        @pl.loop(0, r // step)
        def _(i):
            body(pl.ds(pl.multiple_of(i * step, step), step), pl.ds(pl.multiple_of(start + i * step, step), step))

    def second(self, k):
        s = self.spot
        own, sib = self.own[k], self.sib[k]
        _, r, c = own.shape
        h = r // 2
        low, high = pl.ds(0, h), pl.ds(h, h)
        for m in (3, 1, 2, 0):
            self.loads[k][m].wait()
            self.arrived(k, m, sib.at[m])

            def add(rows, _, m=m):
                own[m, rows, :] = (own[m, rows, :].astype(F32) + sib[m, rows, :].astype(F32)).astype(BF)

            self.over(r, c, add)
            if m == 3:
                self.go(k, 5, s.nx, own.at[3, low], self.fx[k].at[1])
                self.go(k, 7, s.ny, own.at[3, high], self.fy[k].at[1])
            if m == 1:
                self.go(k, 4, s.nx, own.at[1, low], self.fx[k].at[0])
            if m == 2:
                self.go(k, 6, s.ny, own.at[2, high], self.fy[k].at[0])

    def third(self, k):
        s = self.spot
        own, fx, fy = self.own[k], self.fx[k], self.fy[k]
        _, r, c = own.shape
        h = r // 2
        self.arrived(k, 5, fx.at[1])

        def add_low(rows, _):
            fx[1, rows, :] = (own[2, rows, :].astype(F32) + fx[1, rows, :].astype(F32)).astype(BF)

        self.over(h, c, add_low)
        self.go(k, 8, s.ny, fx.at[1], self.gy[k])
        self.arrived(k, 7, fy.at[1])

        def add_high(rows, there):
            fy[1, rows, :] = (own[1, there, :].astype(F32) + fy[1, rows, :].astype(F32)).astype(BF)

        self.over(h, c, add_high, h)
        self.go(k, 9, s.nx, fy.at[1], self.gx[k])

    def last(self, k):
        own, out = self.own[k], self.items[k][1]
        fx, fy, gx, gy = self.fx[k], self.fy[k], self.gx[k], self.gy[k]
        _, r, c = own.shape
        h = r // 2
        self.arrived(k, 4, fx.at[0])
        self.arrived(k, 8, gy)

        def low(rows, _):
            out[rows, :] = own[0, rows, :].astype(F32) + fx[0, rows, :].astype(F32) + gy[rows, :].astype(F32)

        self.over(h, c, low)
        self.arrived(k, 6, fy.at[0])
        self.arrived(k, 9, gx)

        def high(rows, there):
            out[there, :] = own[0, there, :].astype(F32) + fy[0, rows, :].astype(F32) + gx[rows, :].astype(F32)

        self.over(h, c, high, h)

    def close(self):
        for copy in self.sent:
            copy.wait_send()


def link_kernel(name, ident, gather=None, sums=(), scatter=None, chunks=8, plan=None):
    shards = [] if gather is None else list(gather[0])
    layers = [] if gather is None else list(gather[1])
    sums, grads = list(sums), [] if scatter is None else list(scatter)
    ng, ns, nr = len(shards), len(sums), len(grads)
    HBM = pl.BlockSpec(memory_space=pl.ANY)
    VM_ = pl.BlockSpec(memory_space=pltpu.VMEM)
    shard_shape = lambda v, l: v.shape if l is None else v.shape[1:]
    ins = [HBM] * (ng + ns + nr)
    outs = [HBM] * ng + [HBM] * ns + [VM_] * nr
    shapes = [jax.ShapeDtypeStruct((8,) + shard_shape(v, l), v.dtype) for v, l in zip(shards, layers)]
    shapes += [jax.ShapeDtypeStruct(v.shape, BF) for v in sums]
    shapes += [jax.ShapeDtypeStruct(v.shape[1:], F32) for v in grads]
    scratch = []
    DMA = pltpu.SemaphoreType.DMA
    if ng:
        scratch += [DMA((ng, 9)), DMA((ng, 9)), DMA((ng,))]
    for v in sums:
        scratch += [pltpu.VMEM((2, v.shape[0] // chunks, v.shape[1]), BF), pltpu.VMEM(v.shape, BF), pltpu.VMEM(v.shape, BF), DMA((chunks, 3)), DMA((chunks, 3)), DMA((chunks + 2,))]
    if nr:
        scratch += [DMA((nr, 10)), DMA((nr, 10)), DMA((nr, 4))]
        for v in grads:
            _, r, c = v.shape
            scratch += [pltpu.VMEM((4, r, c), BF), pltpu.VMEM((4, r, c), BF), pltpu.VMEM((2, r // 2, c), BF), pltpu.VMEM((2, r // 2, c), BF),
                        pltpu.VMEM((r // 2, c), BF), pltpu.VMEM((r // 2, c), BF)]

    def kernel(*refs):
        refs = list(refs)
        take = lambda n: [refs.pop(0) for _ in range(n)]
        src, part, grad = take(ng), take(ns), take(nr)
        full, total, owned = take(ng), take(ns), take(nr)
        spot = Spot()
        spot.meet(bool(ns))
        G = S = None
        if ng:
            pick = lambda ref, l: ref if l is None else ref.at[l]
            G = Gather(spot, [(pick(a, l), b) for a, l, b in zip(src, layers, full)], *take(3))
        lines = []
        for k in range(ns):
            stage, land, swap, send, recv, local = take(6)
            lines.append(LineSum(spot, part[k], stage, land, swap, total[k], send, recv, local, chunks))
        if nr:
            send, recv, local = take(3)
            bufs = [take(6) for _ in range(nr)]
            S = Scatter(spot, list(zip(grad, owned)), *[[b[i] for b in bufs] for i in range(6)], send, recv, local)
        plan(G, lines, S)
        for part_ in [G, *lines, S]:
            if part_ is not None:
                part_.close()

    nbytes = sum(v.size * 2 for v in sums + grads) + sum(8 * v.size for v in shards)
    return pl.pallas_call(
        kernel, in_specs=ins, out_specs=outs, out_shape=shapes, scratch_shapes=scratch,
        compiler_params=pltpu.CompilerParams(vmem_limit_bytes=VM, collective_id=ident, has_side_effects=True),
        cost_estimate=pl.CostEstimate(flops=0, bytes_accessed=nbytes, transcendentals=0), name=name)(*shards, *sums, *grads)


def plan_gather(G, lines, S):
    n = len(G.items)
    for k in range(n):
        G.first(k)
    for k in range(n):
        G.second(k)
    for k in range(n):
        G.third(k)
    for k in range(n):
        G.last(k)


def woven(stages):
    def plan(G, lines, S):
        side = G if G is not None else S
        for k in range(len(side.items)):
            side.first(k)
        ticks = [(line, t) for line in lines for t in range(line.chunks + 3)]
        for at, (line, t) in enumerate(ticks):
            line.tick(t)
            for name, k in stages.get(at, ()):
                getattr(side, name)(k)
        for at in sorted(stages):
            if at >= len(ticks):
                for name, k in stages[at]:
                    getattr(side, name)(k)

    return plan


weave_gather = woven({2: [("second", 0), ("second", 1)], 4: [("second", 2)], 6: [("second", 3)], 7: [("third", 0), ("third", 1)], 8: [("third", 2)], 9: [("third", 3)],
                      99: [("last", 0), ("last", 1), ("last", 2), ("last", 3)]})
weave_scatter = woven({1: [("second", 0), ("second", 1)], 2: [("second", 2)], 3: [("second", 3)], 4: [("third", 0), ("third", 1)], 6: [("third", 2)], 8: [("third", 3)],
                       9: [("last", 0), ("last", 1)], 99: [("last", 2), ("last", 3)]})


def adam_update(weight, grad, first, second):
    first_new = beta_one * first + (1.0 - beta_one) * grad
    second_new = beta_two * second + (1.0 - beta_two) * grad * grad
    mean_hat = first_new / (1.0 - beta_one**ADAM_STEP)
    square_hat = second_new / (1.0 - beta_two**ADAM_STEP)
    new_weight = weight - rate * (mean_hat / (jnp.sqrt(square_hat) + adam_eps) + decay * weight)
    return grad, first_new, second_new, new_weight - weight


def adam_layer(layer, weights, grads, firsts, seconds, before):
    steps = 8
    blocks = [(w.shape[1] // steps, w.shape[2]) for w in weights]

    def kernel(*refs):
        ins, outs = refs[:16], refs[-16:]
        for i in range(4):
            g = ins[4 + i][...].astype(F32)
            made = adam_update(ins[i][...].astype(F32), g, ins[8 + i][...], ins[12 + i][...])
            for k in range(4):
                outs[4 * i + k][...] = made[k]

    at = lambda b: spec((None,) + b, lambda j: (layer, j, 0))
    ins = [at(b) for b in blocks] + [spec(b, lambda j: (j, 0)) for b in blocks] + [at(b) for b in blocks] * 2
    args = [*weights, *grads, *firsts, *seconds]
    alias = {}
    if before is not None:
        ins += [pl.BlockSpec(memory_space=pl.ANY)] * 16
        args += list(before)
        alias = {16 + i: i for i in range(16)}
    shapes = [jax.ShapeDtypeStruct(w.shape, F32) for w in weights for _ in range(4)]
    count = sum(w.shape[1] * w.shape[2] for w in weights)
    return pl.pallas_call(
        kernel, grid=(steps,), in_specs=ins, out_specs=[at(b) for b in blocks for _ in range(4)], out_shape=shapes,
        input_output_aliases=alias, compiler_params=pltpu.CompilerParams(vmem_limit_bytes=VM),
        cost_estimate=pl.CostEstimate(flops=20 * count, bytes_accessed=30 * count, transcendentals=0), name="adam")(*args)


def layout(lengths_row, rows):
    slots = lengths_row.shape[0]
    number = jnp.arange(slots, dtype=jnp.int32)
    ends = jnp.sum(jnp.where(number[None, :] <= number[:, None], lengths_row[None, :], 0), axis=1)
    starts = ends - lengths_row
    index = jnp.arange(rows, dtype=jnp.int32)
    inside = (index[:, None] >= starts[None, :]) & (index[:, None] < ends[None, :])
    valid = jnp.any(inside, axis=1)
    slot = jnp.sum(jnp.where(inside, number[None, :], 0), axis=1)
    first = jnp.sum(jnp.where(inside, starts[None, :], 0), axis=1)
    segment = jnp.where(valid, slot, slots + index)
    return segment, index - first, valid


class PlainLinks:
    def weights(self, shards, layer):
        wq, wd, wu, wn = [w[layer] for w in shards]
        rows = lambda v: lax.all_gather(v, "dp", axis=0, tiled=True)
        stack = lambda v: lax.all_gather(v, "dp", axis=0, tiled=False)
        return rows(wq), stack(wd), rows(wu), stack(wn)

    def share(self, v):
        return lax.psum(v, "mp")

    def owned(self, grads):
        cut = lambda g: lax.psum_scatter(g, "dp", scatter_dimension=0, tiled=True)
        gq, gd, gu, gn = grads
        return cut(gq), cut(gd)[0], cut(gu), cut(gn)[0]

    def begin(self, shards, flat):
        return self.weights(shards, 0), lax.all_gather(flat, "dp", axis=0, tiled=False), None

    def middle(self, branch, shards):
        return self.share(branch), self.weights(shards, 1)

    def turn(self, e, grads, ident):
        return self.share(e), self.owned(grads)


class ChipLinks:
    def full(self, got):
        wq, wd, wu, wn = got
        return wq.reshape(-1, wq.shape[2]), wd, wu.reshape(-1, wu.shape[2]), wn

    def slots(self, grads):
        gq, gd, gu, gn = grads
        return gq.reshape(8, -1, gq.shape[1]), gd, gu.reshape(8, -1, gu.shape[1]), gn

    def begin(self, shards, flat):
        wq, wd, wu, wn = shards
        flat, wq, wu = link_kernel("gather", 1, gather=([flat, wq, wu], [None, 0, 0]), plan=plan_gather)
        return (wq.reshape(-1, wq.shape[2]), None, wu.reshape(-1, wu.shape[2]), None), flat, (wd, wn)

    def middle(self, branch, shards):
        got = link_kernel("sum_gather", 2, gather=(shards, [1] * 4), sums=(branch,), plan=weave_gather)
        return got[4], self.full(got[:4])

    def turn(self, e, grads, ident):
        got = link_kernel("sum_scatter", ident, sums=(e,), scatter=self.slots(grads), plan=weave_scatter)
        return got[0], got[1:]


def flatten_small(parts):
    flat = jnp.concatenate([p.reshape(-1) for p in parts])
    return jnp.pad(flat, (0, -flat.size % 4096)).reshape(-1, 128)


def unpack_small(got, parts):
    got = got.reshape(got.shape[0], -1)
    out, at = [], 0
    for p in parts:
        piece = got[:, at:at + p.size].reshape((-1,) + p.shape)
        out.append(jnp.moveaxis(piece, 0, 2).reshape(p.shape[0], p.shape[1], -1))
        at += p.size
    return out


def body(links, tokens_in, cotangent, seq_lengths, *params):
    weights, small = params[:4], params[4:7]
    firsts, small_firsts = params[7:11], params[11:14]
    seconds, small_seconds = params[14:18], params[18:21]
    rows, D = tokens_in.shape
    segment, position, valid = layout(seq_lengths[0], rows)
    cos, sin = rope_tables(position)
    seg_col, seg_row = segment[:, None], segment[None, :]
    live = valid[:, None]
    first_full, got, later = links.begin(weights, flatten_small(small))
    qb, ub, vecs = unpack_small(got, small)
    qb = qb.reshape(LAYERS, 1, -1).astype(F32)
    ub = ub.reshape(LAYERS, 1, -1).astype(F32)
    vecs = vecs.astype(F32)

    held = [jnp.concatenate([vecs[layer, :4], vecs[layer - 1, 4:]]) for layer in range(LAYERS)]

    full, kept, extra = [first_full], [], None
    for layer in range(LAYERS):
        wq, wd, wu, wn = full[layer]
        h1, h2, mixed, act, gp, stats, *more = project(tokens_in, extra, held[layer], wq, qb[layer], cos, sin, wu, ub[layer], later if layer == 0 else None)
        if more:
            wd, wn = more
            full[0] = wq, wd, wu, wn
        ctx = attend_forward(mixed, seg_col, seg_row)
        branch = branch_out(ctx, act, wd, wn)
        kept.append((h1, h2, mixed, act, gp, stats, ctx, extra))
        if layer == 0:
            extra, made = links.middle(branch, weights)
            full.append(made)
        else:
            gout = gr = jnp.where(live, cotangent, 0).astype(BF)
            sums = jnp.sum(gout.astype(F32), axis=0, keepdims=True)
            branch, gr = lax.optimization_barrier((branch, gr))
            branch = lax.psum(branch, "mp")

    big, little = [None] * LAYERS, [None] * LAYERS
    for layer in reversed(range(LAYERS)):
        wq, wd, wu, wn = full[layer]
        h1, h2, mixed, act, gp, stats, ctx, extra = kept[layer]
        dctx, df = back_in(gr, gp, wd, wn)
        dmix = attend_backward(mixed, dctx, seg_col, seg_row, cos, sin)
        e, norm_sums = back_out(dmix, df, wq, wu, tokens_in, extra, held[layer], stats)
        gd, _ = weight_grad(ctx, gr, w=wd.shape[2])
        gn, _ = weight_grad(act, gr, w=wn.shape[2])
        gq, qsum = weight_grad(h1, dmix)
        gu, usum = weight_grad(h2, df)
        if layer:
            e, big[layer] = links.turn(e, (gq, gd, gu, gn), 3)
            branch, e = lax.optimization_barrier((branch, e))
        else:
            e, big[layer] = links.turn(e, (gq, gd, gu, gn), 4)
        little[layer] = (qsum, usum, norm_sums, sums)
        made = norm_back(gout, e, tokens_in, extra, held[layer], stats, layer == 0)
        if layer:
            gout, gr, sums = made
        else:
            input_grad = made[0]
    x_last = tokens_in.astype(F32) + kept[1][-1].astype(F32) + vecs[0, 4] + vecs[0, 5] + branch.astype(F32) + vecs[1, 4] + vecs[1, 5]
    output = jnp.where(live, x_last, 0.0).astype(BF)

    done = None
    for layer in reversed(range(LAYERS)):
        done = adam_layer(layer, weights, big[layer], firsts, seconds, done)

    z, line = lax.axis_index("mp"), lax.axis_size("mp")
    bias = jnp.concatenate([jnp.stack([t[i] for t in little]).reshape(-1) for i in (0, 1)])
    bias = jnp.where(jnp.arange(line)[:, None] == z, bias[None, :], 0.0)
    norm_sums = jnp.stack([t[2] for t in little])
    out_sums = jnp.where(z == 0, jnp.stack([t[3] for t in little]), 0.0)
    vec_sum = jnp.concatenate([norm_sums, out_sums, out_sums], axis=1).reshape(-1)
    total = lax.psum(jnp.concatenate([bias.reshape(-1), vec_sum]), ("dp", "mp"))
    bias = lax.dynamic_slice_in_dim(total[:bias.size].reshape(bias.shape), z, 1, 0)[0]
    total = jnp.concatenate([bias, total[-vec_sum.size:]])
    me = lax.axis_index("dp")
    small_out, at = [], 0
    for p, first, second in zip(small, small_firsts, small_seconds):
        width = p.shape[2]
        wide = p.shape[:2] + (lax.axis_size("dp") * width,)
        size = wide[0] * wide[1] * wide[2]
        g = lax.dynamic_slice_in_dim(total[at:at + size].reshape(wide), me * width, width, 2)
        at += size
        small_out += adam_update(p.astype(F32), g, first, second)
    return (output, input_grad, *done, *small_out)


def solution(mesh):
    rows_dp = P("dp", None)
    wide, tall, vec = P(None, "dp", "mp"), P(None, "mp", "dp"), P(None, None, "dp")
    group = (wide, tall, wide, tall, tall, tall, vec)
    return jax.shard_map(
        functools.partial(body, ChipLinks() if dict(mesh.shape) == {"dp": 8, "mp": 4} else PlainLinks()),
        mesh=mesh,
        in_specs=(rows_dp,) * 3 + group * 3,
        out_specs=(rows_dp,) * 2 + tuple(s for s in group for _ in range(4)),
        check_vma=False,
    )
```

```python
import functools
import jax
import jax.numpy as jnp
from jax import lax
from jax.experimental import pallas as pl
from jax.experimental.pallas import tpu as pltpu
from jax.sharding import PartitionSpec as P

HD = 256
ROT = 64
MAXLEN = 512
norm_eps = 1e-05
masked_score = -1e30
LAYERS = 2
ADAM_STEP = 10
beta_one = 0.9
beta_two = 0.95
adam_eps = 1e-08
rate = 0.02
decay = 0.01
VM = 60 * 1024 * 1024
VM2 = 62 * 1024 * 1024
BF = jnp.bfloat16
ROWS = 256
UPB = 512
F32 = jnp.float32


def call(kernel, grid, in_specs, out_specs, out_shape, scratch=(), flops=0, nbytes=0, name=None, ident=None):
    return pl.pallas_call(
        kernel,
        grid_spec=pltpu.PrefetchScalarGridSpec(num_scalar_prefetch=0, grid=grid, in_specs=in_specs, out_specs=out_specs, scratch_shapes=list(scratch)),
        out_shape=out_shape,
        compiler_params=pltpu.CompilerParams(vmem_limit_bytes=VM, collective_id=ident, has_side_effects=ident is not None),
        cost_estimate=pl.CostEstimate(flops=flops, bytes_accessed=nbytes, transcendentals=0),
        name=name,
    )


def spec(shape, index, single=False):
    if single:
        return pl.BlockSpec(shape, index, pipeline_mode=pl.Buffered(1))
    return pl.BlockSpec(shape, index)


def rope_tables(position):
    half = ROT // 2
    freq = 10000.0 ** (-(jnp.arange(half, dtype=F32) * 2.0) / ROT)
    angle = position.astype(F32)[:, None] * freq[None, :]
    c, s = jnp.cos(angle), jnp.sin(angle)
    rows = position.shape[0]
    one = jnp.ones((rows, 128 - ROT), F32)
    zero = jnp.zeros((rows, 128 - ROT), F32)
    return jnp.concatenate([c, c, one], axis=1), jnp.concatenate([-s, s, zero], axis=1)


def turn(u, c, s):
    lane = lax.broadcasted_iota(jnp.int32, u.shape, 1)
    other = jnp.where(lane < ROT // 2, pltpu.roll(u, 128 - ROT // 2, 1), pltpu.roll(u, ROT // 2, 1))
    return u * c + other * s


def normed(x):
    mean = jnp.mean(x, axis=1, keepdims=True)
    centred = x - mean
    var = jnp.mean(centred * centred, axis=1, keepdims=True)
    rstd = lax.rsqrt(var + norm_eps)
    return centred * rstd, mean, rstd


def row_blocks(n):
    step = min(n, ROWS)
    return [slice(i, i + step) for i in range(0, n, step)]


def project(base, extra, vec, wq, bq, cos, sin, wu, bu, shards=None):
    n, D = base.shape
    C, U = wq.shape[1], wu.shape[1]
    QB, UB = 3 * HD, min(UPB, U)
    nq, nu = C // QB, U // UB
    RB = 128
    nr = n // RB
    ng = 0 if shards is None else len(shards)
    xs = [base] if extra is None else [base, extra]

    def kernel(*refs):
        refs = list(refs)
        take = lambda k: [refs.pop(0) for _ in range(k)]
        x_rs = take(len(xs))
        vec_r, wq_r, bq_r, cos_r, sin_r, wu_r, bu_r = take(7)
        shard_rs = take(ng)
        h1_o, h2_o, mix_r, a_r, gp_r, st_r = take(6)
        full_rs = take(ng)
        h1_r, h2_r = take(2)
        bufs = take(len(xs))
        in_sem, out_sem = take(2)
        j = pl.program_id(0)
        side = None
        if ng:
            spot = Spot()
            side = Gather(spot, [(a.at[0], b) for a, b in zip(shard_rs, full_rs)], *take(3))

            @pl.when(j == 0)
            def _():
                spot.meet(False)
                side.first(0)
                side.first(1)

        def host(step, *stages):
            if side is not None:
                @pl.when(j == min(step, nq + nu - 1))
                def _():
                    for name, *args in stages:
                        getattr(side, name)(*args)
        block = lambda i: pl.ds(i * RB, RB)
        loads = [[pltpu.make_async_copy(x.at[block(i)], buf.at[block(i)], in_sem.at[k, i]) for k, (x, buf) in enumerate(zip(x_rs, bufs))] for i in range(nr)]
        stores = [[pltpu.make_async_copy(h.at[block(i)], o.at[block(i)], out_sem.at[k, i]) for k, (h, o) in enumerate(((h1_r, h1_o), (h2_r, h2_o)))] for i in range(nr)]

        @pl.when(j == 0)
        def _():
            for group in loads:
                for copy in group:
                    copy.start()
            for i in range(nr):
                for copy in loads[i]:
                    copy.wait()
                rows = block(i)
                x = bufs[0][rows, :].astype(F32)
                if extra is not None:
                    x = x + bufs[1][rows, :].astype(F32) + vec_r[4:5, :] + vec_r[5:6, :]
                xhat, mean, rstd = normed(x)
                st_r[rows, 0:1] = mean
                st_r[rows, 1:2] = rstd
                h1_r[rows, :] = (xhat * vec_r[0:1, :] + vec_r[1:2, :]).astype(BF)
                h2_r[rows, :] = (xhat * vec_r[2:3, :] + vec_r[3:4, :]).astype(BF)
                for copy in stores[i]:
                    copy.start()

        @pl.when(j < nq)
        def _():
            for rows in row_blocks(n):
                for part in range(3):
                    at = part * HD
                    m = jnp.dot(h1_r[rows, :], wq_r[:, at:at + HD], preferred_element_type=F32) + bq_r[:, at:at + HD]
                    if part == 2:
                        mix_r[rows, at:at + HD] = m.astype(BF)
                    else:
                        mix_r[rows, at:at + 128] = turn(m[:, :128], cos_r[rows, :], sin_r[rows, :]).astype(BF)
                        mix_r[rows, at + 128:at + HD] = m[:, 128:].astype(BF)

        @pl.when(j >= nq)
        def _():
            for rows in row_blocks(n):
                for at in range(0, UB, 256):
                    cols = slice(at, at + 256)
                    f = jnp.dot(h2_r[rows, :], wu_r[:, cols], preferred_element_type=F32) + bu_r[:, cols]
                    phi = 0.5 * (1.0 + lax.erf(f * 0.7071067811865476))
                    a_r[rows, cols] = (f * phi).astype(BF)
                    gp_r[rows, cols] = (phi + f * (jnp.exp(-0.5 * f * f) * 0.3989422804014327)).astype(BF)

        host(1, ("second", 0))
        host(3, ("second", 1), ("third", 0))
        host(5, ("third", 1), ("last", 0), ("last", 1), ("close",))

        @pl.when(j == nq + nu - 1)
        def _():
            for group in stores:
                for copy in group:
                    copy.wait()

    whole = lambda j: (0, 0)
    qcol = lambda j: (0, jnp.minimum(j, nq - 1))
    ucol = lambda j: (0, jnp.maximum(j - nq, 0))
    far = pl.BlockSpec(memory_space=pl.ANY)
    ins = [far] * len(xs) + [
        spec((6, D), whole), spec((D, QB), qcol), spec((1, QB), qcol), spec((n, 128), whole, True), spec((n, 128), whole, True),
        spec((D, UB), ucol), spec((1, UB), ucol)] + [far] * ng
    outs = [far, far, spec((n, QB), qcol), spec((n, UB), ucol), spec((n, UB), ucol), spec((n, 128), whole)] + [far] * ng
    shapes = [jax.ShapeDtypeStruct(s, BF) for s in ((n, D), (n, D), (n, C), (n, U), (n, U))] + [jax.ShapeDtypeStruct((n, 128), F32)]
    DMA = pltpu.SemaphoreType.DMA
    scratch = [pltpu.VMEM((n, D), BF)] * (2 + len(xs)) + [DMA((len(xs), nr)), DMA((2, nr))]
    if ng:
        scratch += [DMA((ng, 9)), DMA((ng, 9)), DMA((ng,))]
        shapes += [jax.ShapeDtypeStruct((8,) + v.shape[1:], v.dtype) for v in shards]
    return call(kernel, (nq + nu,), ins, outs, shapes, scratch, ident=5 if ng else None, flops=2 * n * D * (C + U), nbytes=2 * (n * D * 3 + D * (C + U) + n * (C + 2 * U)), name="project")(*xs, vec, wq, bq, cos, sin, wu, bu, *(shards or ()))


def softmax_block(q, k, segq, segk, q0, k0):
    s = lax.dot_general(q, k, (((1,), (1,)), ((), ())), preferred_element_type=F32) * HD ** (-0.5)
    qi = q0 + lax.broadcasted_iota(jnp.int32, s.shape, 0)
    ki = k0 + lax.broadcasted_iota(jnp.int32, s.shape, 1)
    allowed = (segq == segk) & (ki <= qi)
    s = jnp.where(allowed, s, masked_score)
    top = jnp.max(s, axis=1, keepdims=True)
    e = jnp.exp(s - top)
    return e / jnp.sum(e, axis=1, keepdims=True)


def windows(n, qb):
    for i in range(n // qb):
        q0 = i * qb
        yield q0, max(0, q0 - MAXLEN)


def attend_forward(mixed, seg_col, seg_row):
    n, C = mixed.shape
    H = C // (3 * HD)
    qb = 256

    def kernel(q_r, k_r, v_r, sc_r, sr_r, o_r):
        for q0, k0 in windows(n, qb):
            qs, ks = slice(q0, q0 + qb), slice(k0, q0 + qb)
            p = softmax_block(q_r[qs, :], k_r[ks, :], sc_r[qs, :], sr_r[:, ks], q0, k0)
            o_r[qs, :] = jnp.dot(p.astype(BF), v_r[ks, :], preferred_element_type=F32).astype(BF)

    part = lambda t: spec((n, HD), lambda h: (0, 3 * h + t))
    return call(kernel, (H,), [part(0), part(1), part(2), spec((n, 1), lambda h: (0, 0)), spec((1, n), lambda h: (0, 0))],
                spec((n, HD), lambda h: (0, h)), jax.ShapeDtypeStruct((n, H * HD), BF),
                flops=H * n * 640 * HD * 4, nbytes=2 * n * C, name="attend")(mixed, mixed, mixed, seg_col, seg_row)


def attend_backward(mixed, dctx, seg_col, seg_row, cos, sin):
    n, C = mixed.shape
    H = C // (3 * HD)
    qb = 256
    scale = HD ** (-0.5)

    def kernel(q_r, k_r, v_r, do_r, sc_r, sr_r, cos_r, sin_r, o_r, dk_s, dv_s):
        def back(u, rows):
            c, s = cos_r[rows, :], -sin_r[rows, :]
            return jnp.concatenate([turn(u[:, :128], c, s), u[:, 128:]], axis=1).astype(BF)

        dk_s[...] = jnp.zeros_like(dk_s)
        dv_s[...] = jnp.zeros_like(dv_s)
        for q0, k0 in reversed(list(windows(n, qb))):
            qs, ks = slice(q0, q0 + qb), slice(k0, q0 + qb)
            q, k, do = q_r[qs, :], k_r[ks, :], do_r[qs, :]
            p = softmax_block(q, k, sc_r[qs, :], sr_r[:, ks], q0, k0)
            dp = lax.dot_general(do, v_r[ks, :], (((1,), (1,)), ((), ())), preferred_element_type=F32)
            delta = jnp.sum(p * dp, axis=1, keepdims=True)
            ds = (p * (dp - delta)).astype(BF)
            dq = jnp.dot(ds, k, preferred_element_type=F32) * scale
            dk_s[ks, :] += lax.dot_general(ds, q, (((0,), (0,)), ((), ())), preferred_element_type=F32)
            dv_s[ks, :] += lax.dot_general(p.astype(BF), do, (((0,), (0,)), ((), ())), preferred_element_type=F32)
            o_r[qs, :HD] = back(dq, qs)
            o_r[qs, HD:2 * HD] = back(dk_s[qs, :] * scale, qs)
            o_r[qs, 2 * HD:] = dv_s[qs, :].astype(BF)

    part = lambda t: spec((n, HD), lambda h: (0, 3 * h + t))
    whole = lambda h: (0, 0)
    return call(kernel, (H,), [part(0), part(1), part(2), spec((n, HD), lambda h: (0, h)), spec((n, 1), whole), spec((1, n), whole),
                spec((n, 128), whole), spec((n, 128), whole)],
                spec((n, 3 * HD), lambda h: (0, h)), jax.ShapeDtypeStruct((n, C), BF),
                scratch=[pltpu.VMEM((n, HD), F32), pltpu.VMEM((n, HD), F32)],
                flops=H * n * 640 * HD * 10, nbytes=4 * n * C, name="attend_back")(mixed, mixed, mixed, dctx, seg_col, seg_row, cos, sin)


def branch_out(ctx, act, wd, wn):
    n, R = ctx.shape
    U = act.shape[1]
    dp, _, w = wd.shape

    def kernel(c_r, a_r, wd_r, wn_r, o_r):
        o_r[...] = (jnp.dot(c_r[...], wd_r[...], preferred_element_type=F32) + jnp.dot(a_r[...], wn_r[...], preferred_element_type=F32)).astype(BF)

    whole = lambda s: (0, 0)
    pick = lambda s: (s, 0, 0)
    return call(kernel, (dp,), [spec((n, R), whole, True), spec((n, U), whole, True), spec((None, R, w), pick), spec((None, U, w), pick)],
                spec((n, w), lambda s: (0, s)), jax.ShapeDtypeStruct((n, dp * w), BF),
                flops=2 * n * dp * w * (R + U), nbytes=2 * (n * (R + U) + dp * w * (R + U + n)), name="branch")(ctx, act, wd, wn)


def back_in(gr, gp, wd, wn):
    n, D = gr.shape
    dp, R, w = wd.shape
    U = wn.shape[1]
    NB = 256
    nr, nu = R // NB, U // NB

    def kernel(g_r, gp_r, wd_r, wn_r, dc_r, df_r):
        j = pl.program_id(0)

        def times(w_r):
            acc = None
            for s in range(dp):
                t = lax.dot_general(g_r[:, s * w:(s + 1) * w], w_r[s], (((1,), (1,)), ((), ())), preferred_element_type=F32)
                acc = t if acc is None else acc + t
            return acc

        @pl.when(j < nr)
        def _():
            dc_r[...] = times(wd_r).astype(BF)

        @pl.when(j >= nr)
        def _():
            df_r[...] = (times(wn_r) * gp_r[...].astype(F32)).astype(BF)

    rc = lambda j: jnp.minimum(j, nr - 1)
    uc = lambda j: jnp.maximum(j - nr, 0)
    return call(kernel, (nr + nu,), [spec((n, D), lambda j: (0, 0), True), spec((n, NB), lambda j: (0, uc(j))),
                spec((dp, NB, w), lambda j: (0, rc(j), 0)), spec((dp, NB, w), lambda j: (0, uc(j), 0))],
                [spec((n, NB), lambda j: (0, rc(j))), spec((n, NB), lambda j: (0, uc(j)))],
                [jax.ShapeDtypeStruct((n, R), BF), jax.ShapeDtypeStruct((n, U), BF)],
                flops=2 * n * D * (R + U), nbytes=2 * (n * D + D * (R + U) + n * (R + 2 * U)), name="back_in")(gr, gp, wd, wn)


def back_out(dmix, df, wq, wu, base, extra, vec, stats):
    n, C = dmix.shape
    U = df.shape[1]
    D = wq.shape[0]
    NB = 256

    def kernel(*refs):
        if extra is None:
            dm_r, df_r, wq_r, wu_r, base_r, vec_r, st_r, e_r, g_r = refs
        else:
            dm_r, df_r, wq_r, wu_r, base_r, extra_r, vec_r, st_r, e_r, g_r = refs
        nt = (((1,), (1,)), ((), ()))
        d1 = lax.dot_general(dm_r[...], wq_r[...], nt, preferred_element_type=F32)
        d2 = lax.dot_general(df_r[...], wu_r[...], nt, preferred_element_type=F32)
        e_r[...] = (d1 * vec_r[0:1, :] + d2 * vec_r[2:3, :]).astype(BF)
        x = base_r[...].astype(F32)
        if extra is not None:
            x = x + extra_r[...].astype(F32) + vec_r[4:5, :] + vec_r[5:6, :]
        xhat = (x - st_r[:, 0:1]) * st_r[:, 1:2]
        g_r[0:1, :] = jnp.sum(d1 * xhat, axis=0, keepdims=True)
        g_r[1:2, :] = jnp.sum(d1, axis=0, keepdims=True)
        g_r[2:3, :] = jnp.sum(d2 * xhat, axis=0, keepdims=True)
        g_r[3:4, :] = jnp.sum(d2, axis=0, keepdims=True)

    whole = lambda j: (0, 0)
    col = lambda j: (0, j)
    row = lambda j: (j, 0)
    xs = [spec((n, NB), col)] + ([] if extra is None else [spec((n, NB), col)])
    args = [base] + ([] if extra is None else [extra])
    return call(kernel, (D // NB,), [spec((n, C), whole, True), spec((n, U), whole, True), spec((NB, C), row), spec((NB, U), row)] + xs +
                [spec((6, NB), col), spec((n, 128), whole)],
                [spec((n, NB), col), spec((4, NB), col)],
                [jax.ShapeDtypeStruct((n, D), BF), jax.ShapeDtypeStruct((4, D), F32)],
                flops=2 * n * D * (C + U), nbytes=2 * (n * (C + U) + D * (C + U) + n * D * 3), name="back_out")(dmix, df, wq, wu, *args, vec, stats)


def weight_grad(left, right, w=None):
    n, M = left.shape
    N = right.shape[1]
    MB = 256

    def kernel(l_r, r_r, o_r, s_r):
        g = lax.dot_general(l_r[...], r_r[...], (((0,), (0,)), ((), ())), preferred_element_type=F32)
        if w is None:
            o_r[...] = g.astype(BF)
        else:
            for s in range(N // w):
                o_r[s] = g[:, s * w:(s + 1) * w].astype(BF)

        @pl.when(pl.program_id(0) == 0)
        def _():
            s_r[...] = jnp.sum(r_r[...].astype(F32), axis=0, keepdims=True)

    whole = lambda j: (0, 0)
    if w is None:
        out, shape = spec((MB, N), lambda j: (j, 0)), (M, N)
    else:
        out, shape = spec((N // w, MB, w), lambda j: (0, j, 0)), (N // w, M, w)
    return call(kernel, (M // MB,), [spec((n, MB), lambda j: (0, j)), spec((n, N), whole, True)], [out, spec((1, N), whole)],
                [jax.ShapeDtypeStruct(shape, BF), jax.ShapeDtypeStruct((1, N), F32)],
                flops=2 * n * M * N, nbytes=2 * (n * M + n * N + M * N), name="wgrad")(left, right)


def norm_back(gout, e, base, extra, vec, stats, last):
    n, D = base.shape
    RB = 128

    def kernel(*refs):
        g_r, e_r, base_r = refs[:3]
        refs = refs[3:]
        if extra is not None:
            extra_r, refs = refs[0], refs[1:]
        vec_r, st_r, dx_r = refs[:3]
        x = base_r[...].astype(F32)
        if extra is not None:
            x = x + extra_r[...].astype(F32) + vec_r[4:5, :] + vec_r[5:6, :]
        xhat = (x - st_r[:, 0:1]) * st_r[:, 1:2]
        ev = e_r[...].astype(F32)
        me = jnp.mean(ev, axis=1, keepdims=True)
        mx = jnp.mean(ev * xhat, axis=1, keepdims=True)
        dx = g_r[...].astype(F32) + (ev - me - xhat * mx) * st_r[:, 1:2]
        dx_r[...] = dx
        if not last:
            low_r, sum_r = refs[3:]
            low_r[...] = dx.astype(BF)

            @pl.when(pl.program_id(0) == 0)
            def _():
                sum_r[...] = jnp.zeros_like(sum_r)

            sum_r[...] += jnp.sum(dx, axis=0, keepdims=True)

    row = lambda i: (i, 0)
    whole = lambda i: (0, 0)
    rows = spec((RB, D), row)
    ins = [rows, rows, rows] + ([] if extra is None else [rows]) + [spec((6, D), whole), spec((RB, 128), row)]
    args = [gout, e, base] + ([] if extra is None else [extra]) + [vec, stats]
    outs, shapes = [rows], [jax.ShapeDtypeStruct((n, D), F32)]
    if not last:
        outs += [rows, spec((1, D), whole)]
        shapes += [jax.ShapeDtypeStruct((n, D), BF), jax.ShapeDtypeStruct((1, D), F32)]
    return call(kernel, (n // RB,), ins, outs, shapes, flops=10 * n * D, nbytes=16 * n * D, name="norm_back")(*args)


MESH = pl.DeviceIdType.MESH


class Spot:
    def __init__(self):
        i = lax.axis_index("dp")
        c, x, y = lax.rem(i, 2), lax.rem(lax.div(i, 2), 2), lax.div(i, 4)
        self.me = i
        self.dx, self.dy, self.dc = 2 - 4 * x, 4 - 8 * y, 1 - 2 * c
        self.nx, self.ny, self.nc = i + self.dx, i + self.dy, i + self.dc
        self.diag = i + self.dx + self.dy
        z = lax.axis_index("mp")
        self.z = z
        self.outer = (z == 0) | (z == 3)
        self.inner = (z == 1) | (z == 2)
        self.pair = z + 1 - 2 * lax.rem(z, 2)
        self.across = 3 - z

    def meet(self, line):
        barrier = pltpu.get_barrier_semaphore()
        for peer in (self.nx, self.ny, self.nc):
            pl.semaphore_signal(barrier, inc=1, device_id={"dp": peer}, device_id_type=MESH)
        if line:
            pl.semaphore_signal(barrier, inc=1, device_id={"mp": self.pair}, device_id_type=MESH)

            @pl.when(self.inner)
            def _():
                pl.semaphore_signal(barrier, inc=1, device_id={"mp": self.across}, device_id_type=MESH)

            @pl.when(self.inner)
            def _():
                pl.semaphore_wait(barrier, 5)

            @pl.when(self.outer)
            def _():
                pl.semaphore_wait(barrier, 4)
        else:
            pl.semaphore_wait(barrier, 3)


def send_to(axis, peer, src, dst, send, recv):
    return pltpu.make_async_remote_copy(src_ref=src, dst_ref=dst, send_sem=send, recv_sem=recv, device_id={axis: peer}, device_id_type=MESH)


class Gather:
    copies = 9

    def __init__(self, spot, items, send, recv, local):
        self.spot, self.items, self.send, self.recv, self.local = spot, items, send, recv, local
        self.sent = []
        self.own = []

    def go(self, k, n, peer, src, dst):
        send_to("dp", peer, src, dst, self.send.at[k, n], self.recv.at[k, n]).start()
        self.sent.append((k, n, peer, src, dst))

    def arrived(self, k, n, dst):
        send_to("dp", self.spot.nc, dst, dst, self.send.at[k, n], self.recv.at[k, n]).wait_recv()

    def first(self, k):
        s, (src, out) = self.spot, self.items[k]
        for n, peer in enumerate((s.nx, s.ny, s.nc)):
            self.go(k, n, peer, src, out.at[s.me])
        pltpu.make_async_copy(src, out.at[s.me], self.local.at[k]).start()
        self.own.append(k)

    def halves(self, k):
        h = self.items[k][1].shape[1] // 2
        return pl.ds(0, h), pl.ds(h, h)

    def second(self, k):
        s, (_, out) = self.spot, self.items[k]
        low, high = self.halves(k)
        self.arrived(k, 0, out.at[s.nx])
        self.go(k, 3, s.ny, out.at[s.nx, high], out.at[s.nx, high])
        self.go(k, 4, s.nc, out.at[s.nx], out.at[s.nx])
        self.arrived(k, 1, out.at[s.ny])
        self.go(k, 5, s.nx, out.at[s.ny, low], out.at[s.ny, low])
        self.go(k, 6, s.nc, out.at[s.ny], out.at[s.ny])

    def third(self, k):
        s, (_, out) = self.spot, self.items[k]
        low, high = self.halves(k)
        self.arrived(k, 3, out.at[s.diag, high])
        self.go(k, 7, s.nc, out.at[s.diag, high], out.at[s.diag, high])
        self.arrived(k, 5, out.at[s.diag, low])
        self.go(k, 8, s.nc, out.at[s.diag, low], out.at[s.diag, low])

    def last(self, k):
        s, (_, out) = self.spot, self.items[k]
        low, high = self.halves(k)
        self.arrived(k, 2, out.at[s.nc])
        self.arrived(k, 4, out.at[s.nx + s.dc])
        self.arrived(k, 6, out.at[s.ny + s.dc])
        self.arrived(k, 7, out.at[s.diag + s.dc, high])
        self.arrived(k, 8, out.at[s.diag + s.dc, low])

    def close(self):
        for k in self.own:
            src, out = self.items[k]
            pltpu.make_async_copy(src, out.at[self.spot.me], self.local.at[k]).wait()
        for k, n, peer, src, dst in self.sent:
            send_to("dp", peer, src, dst, self.send.at[k, n], self.recv.at[k, n]).wait_send()


class LineSum:
    copies = 3

    def __init__(self, spot, part, stage, land, swap, out, send, recv, local, chunks):
        self.spot, self.part, self.stage, self.land, self.swap, self.out = spot, part, stage, land, swap, out
        self.send, self.recv, self.local, self.chunks = send, recv, local, chunks
        self.rows = part.shape[0] // chunks

    def cut(self, k):
        return pl.ds(k * self.rows, self.rows)

    def copy(self, k, n):
        s, rows = self.spot, self.cut(k)
        if n == 0:
            peer, src, dst = s.pair, self.part, self.land
        elif n == 1:
            peer, src, dst = s.across, self.land, self.swap
        else:
            peer, src, dst = s.pair, self.swap, self.swap
        return send_to("mp", peer, src.at[rows], dst.at[rows], self.send.at[k, n], self.recv.at[k, n])

    def keep(self, k):
        rows = self.cut(k)
        return pltpu.make_async_copy(self.swap.at[rows], self.out.at[rows], self.local.at[k])

    def load(self, k):
        return pltpu.make_async_copy(self.part.at[self.cut(k)], self.stage.at[k % 2], self.local.at[self.chunks + k % 2])

    def add(self, k, dst, one, two, base):
        step = 32

        @pl.loop(0, self.rows // step)
        def _(i):
            rows = pl.ds(pl.multiple_of(k * self.rows + i * step, step), step)
            there = pl.ds(pl.multiple_of(base + i * step, step), step)
            dst[rows, :] = (one[there, :].astype(F32) + two[rows, :].astype(F32)).astype(BF)

    def send_step(self, t):
        n = self.chunks

        @pl.when(self.spot.outer)
        def _():
            if 0 <= t - 2 < n:
                self.copy(t - 2, 0).wait_send()
            if t < n:
                self.copy(t, 0).start()
            if 0 <= t - 4 < n:
                self.copy(t - 4, 2).wait_recv()
                self.keep(t - 4).start()

    def add_step(self, t):
        n = self.chunks

        @pl.when(self.spot.inner)
        def _():
            if t < n:
                if t == 0:
                    self.load(0).start()
                if t + 1 < n:
                    self.load(t + 1).start()
                self.load(t).wait()
                self.copy(t, 0).wait_recv()
                self.add(t, self.land, self.stage.at[t % 2], self.land, 0)
                self.copy(t, 1).start()
            if 0 <= t - 1 < n:
                self.copy(t - 1, 1).wait_recv()
                self.copy(t - 1, 1).wait_send()
                self.add(t - 1, self.swap, self.land, self.swap, (t - 1) * self.rows)
                self.copy(t - 1, 2).start()
                self.keep(t - 1).start()

    def close(self):
        for k in range(self.chunks):
            self.keep(k).wait()

        @pl.when(self.spot.inner)
        def _():
            for k in range(self.chunks):
                self.copy(k, 2).wait_send()


class Scatter:
    copies = 10

    def __init__(self, spot, items, own, sib, fx, fy, gx, gy, send, recv, local):
        self.spot, self.items = spot, items
        self.own, self.sib, self.fx, self.fy, self.gx, self.gy = own, sib, fx, fy, gx, gy
        self.send, self.recv, self.local = send, recv, local
        self.sent, self.loads = [], {}

    def go(self, k, n, peer, src, dst):
        copy = send_to("dp", peer, src, dst, self.send.at[k, n], self.recv.at[k, n])
        copy.start()
        self.sent.append(copy)

    def arrived(self, k, n, dst):
        send_to("dp", self.spot.nc, dst, dst, self.send.at[k, n], self.recv.at[k, n]).wait_recv()

    def first(self, k):
        s, grad = self.spot, self.items[k][0]
        for m, slot in enumerate((s.me, s.nx, s.ny, s.diag)):
            self.go(k, m, s.nc, grad.at[slot + s.dc], self.sib[k].at[m])
        self.loads[k] = []
        for m, slot in enumerate((s.me, s.nx, s.ny, s.diag)):
            copy = pltpu.make_async_copy(grad.at[slot], self.own[k].at[m], self.local.at[k, m])
            copy.start()
            self.loads[k].append(copy)

    def over(self, r, c, body, start=0):
        step = 16
        while step * 2 * c <= 32768 and r % (step * 2) == 0:
            step *= 2

        @pl.loop(0, r // step)
        def _(i):
            body(pl.ds(pl.multiple_of(i * step, step), step), pl.ds(pl.multiple_of(start + i * step, step), step))

    def second(self, k):
        s = self.spot
        own, sib = self.own[k], self.sib[k]
        _, r, c = own.shape
        h = r // 2
        low, high = pl.ds(0, h), pl.ds(h, h)
        for m in (3, 1, 2, 0):
            self.loads[k][m].wait()
            self.arrived(k, m, sib.at[m])

            def add(rows, _, m=m):
                own[m, rows, :] = (own[m, rows, :].astype(F32) + sib[m, rows, :].astype(F32)).astype(BF)

            self.over(r, c, add)
            if m == 3:
                self.go(k, 5, s.nx, own.at[3, low], self.fx[k].at[1])
                self.go(k, 7, s.ny, own.at[3, high], self.fy[k].at[1])
            if m == 1:
                self.go(k, 4, s.nx, own.at[1, low], self.fx[k].at[0])
            if m == 2:
                self.go(k, 6, s.ny, own.at[2, high], self.fy[k].at[0])

    def third(self, k):
        s = self.spot
        own, fx, fy = self.own[k], self.fx[k], self.fy[k]
        _, r, c = own.shape
        h = r // 2
        self.arrived(k, 5, fx.at[1])

        def add_low(rows, _):
            fx[1, rows, :] = (own[2, rows, :].astype(F32) + fx[1, rows, :].astype(F32)).astype(BF)

        self.over(h, c, add_low)
        self.go(k, 8, s.ny, fx.at[1], self.gy[k])
        self.arrived(k, 7, fy.at[1])

        def add_high(rows, there):
            fy[1, rows, :] = (own[1, there, :].astype(F32) + fy[1, rows, :].astype(F32)).astype(BF)

        self.over(h, c, add_high, h)
        self.go(k, 9, s.nx, fy.at[1], self.gx[k])

    def last(self, k):
        own, out = self.own[k], self.items[k][1]
        fx, fy, gx, gy = self.fx[k], self.fy[k], self.gx[k], self.gy[k]
        _, r, c = own.shape
        h = r // 2
        self.arrived(k, 4, fx.at[0])
        self.arrived(k, 8, gy)

        def low(rows, _):
            out[rows, :] = own[0, rows, :].astype(F32) + fx[0, rows, :].astype(F32) + gy[rows, :].astype(F32)

        self.over(h, c, low)
        self.arrived(k, 6, fy.at[0])
        self.arrived(k, 9, gx)

        def high(rows, there):
            out[there, :] = own[0, there, :].astype(F32) + fy[0, rows, :].astype(F32) + gx[rows, :].astype(F32)

        self.over(h, c, high, h)

    def close(self):
        for copy in self.sent:
            copy.wait_send()


def link_kernel(name, ident, shards, layers, part=None, chunks=8):
    ng = len(shards)
    HBM = pl.BlockSpec(memory_space=pl.ANY)
    DMA = pltpu.SemaphoreType.DMA
    parts = [] if part is None else [part]
    shapes = [jax.ShapeDtypeStruct((8,) + (v.shape if l is None else v.shape[1:]), v.dtype) for v, l in zip(shards, layers)]
    shapes += [jax.ShapeDtypeStruct(v.shape, BF) for v in parts]
    scratch = [DMA((ng, 9)), DMA((ng, 9)), DMA((ng,))]
    for v in parts:
        scratch += [pltpu.VMEM((2, v.shape[0] // chunks, v.shape[1]), BF), pltpu.VMEM(v.shape, BF), pltpu.VMEM(v.shape, BF), DMA((chunks, 3)), DMA((chunks, 3)), DMA((chunks + 2,))]

    def kernel(*refs):
        refs = list(refs)
        take = lambda n: [refs.pop(0) for _ in range(n)]
        src, ins, full, totals = take(ng), take(len(parts)), take(ng), take(len(parts))
        spot = Spot()
        spot.meet(bool(parts))
        G = Gather(spot, [(a if l is None else a.at[l], b) for a, l, b in zip(src, layers, full)], *take(3))
        if parts:
            stage, land, swap, send, recv, local = take(6)
            line = LineSum(spot, ins[0], stage, land, swap, totals[0], send, recv, local, chunks)
            plan_sum_gather(G, line)
            line.close()
        else:
            plan_gather(G)
        G.close()

    nbytes = sum(v.size * 2 for v in parts) + sum(8 * v.size for v in shards)
    return pl.pallas_call(
        kernel, in_specs=[HBM] * (ng + len(parts)), out_specs=[HBM] * (ng + len(parts)), out_shape=shapes, scratch_shapes=scratch,
        compiler_params=pltpu.CompilerParams(vmem_limit_bytes=VM, collective_id=ident, has_side_effects=True),
        cost_estimate=pl.CostEstimate(flops=0, bytes_accessed=nbytes, transcendentals=0), name=name)(*shards, *parts)


def plan_gather(G):
    n = len(G.items)
    for stage in (G.first, G.second, G.third, G.last):
        for k in range(n):
            stage(k)


class Products:
    def __init__(self, lefts, rights, grads, rhs, lbuf, obuf, rsem, lsem, osem):
        self.lefts, self.rights, self.grads = lefts, rights, grads
        self.rhs, self.lbuf, self.obuf, self.rsem, self.lsem, self.osem = rhs, lbuf, obuf, rsem, lsem, osem

    def right(self, i, slot):
        return pltpu.make_async_copy(self.rights[i], self.rhs[slot], self.rsem.at[i])

    def left(self, k, m):
        cols = pl.ds(pl.multiple_of(m * 256, 256), 256)
        return pltpu.make_async_copy(self.lefts[k].at[:, cols], self.lbuf.at[lax.rem(m, 2)], self.lsem.at[lax.rem(m, 2)])

    def stores(self, k, m):
        grad, o = self.grads[k], self.obuf.at[lax.rem(m, 2)]
        sem = self.osem.at[lax.rem(m, 2)]
        slots, r, c = grad.shape
        if r == 256 and self.lefts[k].shape[1] == slots * r:
            return [pltpu.make_async_copy(o.at[:, pl.ds(0, c)], grad.at[m], sem.at[0])]
        rows = pl.ds(pl.multiple_of(m * 256, 256), 256)
        return [pltpu.make_async_copy(o.at[:, pl.ds(s * c, c)], grad.at[s, rows], sem.at[s]) for s in range(slots)]

    def run(self, k, slot, start, stop):
        count = self.lefts[k].shape[1] // 256
        right = self.rhs[slot]
        width = right.shape[1]
        if start == 0:
            self.left(k, 0).start()

        @pl.loop(start, stop)
        def _(m):
            self.left(k, m).wait()

            @pl.when(m + 1 < count)
            def _():
                self.left(k, m + 1).start()

            @pl.when(m >= 2)
            def _():
                for copy in self.stores(k, m - 2):
                    copy.wait()

            g = lax.dot_general(self.lbuf[lax.rem(m, 2)], right[...], (((0,), (0,)), ((), ())), preferred_element_type=F32)
            self.obuf[lax.rem(m, 2), :, :width] = g.astype(BF)
            for copy in self.stores(k, m):
                copy.start()

        if stop == count:
            for m in (count - 2, count - 1):
                for copy in self.stores(k, jnp.int32(m)):
                    copy.wait()

    def sums(self, slot, out):
        right = self.rhs[slot]
        out[...] = jnp.zeros_like(out)

        @pl.loop(0, right.shape[0] // 64)
        def _(i):
            out[...] += jnp.sum(right[pl.ds(pl.multiple_of(i * 64, 64), 64), :].astype(F32), axis=0, keepdims=True)


def plan_sum_gather(G, line):
    for k in range(4):
        G.first(k)
    stages = {3: [("second", 0), ("second", 1)], 5: [("second", 2)], 7: [("second", 3)], 8: [("third", 0), ("third", 1)], 9: [("third", 2)],
              10: [("third", 3)]}
    line.send_step(0)
    for at in range(1, 12):
        line.send_step(at)
        if at - 1 <= line.chunks:
            line.add_step(at - 1)
        for name, k in stages.get(at, ()):
            getattr(G, name)(k)
    for k in range(4):
        G.last(k)


def sum_scatter(ident, e, lefts, rights, chunks=8):
    n, D = e.shape
    HBM = pl.BlockSpec(memory_space=pl.ANY)
    VM_ = pl.BlockSpec(memory_space=pltpu.VMEM)
    C, U = rights[1].shape[1], rights[2].shape[1]
    w = D // 8
    dims = [(lefts[0].shape[1], w), (lefts[1].shape[1], w), (w, C), (w, U)]
    DMA = pltpu.SemaphoreType.DMA
    outs = [HBM] + [HBM] * 4 + [VM_] * 4 + [VM_] * 2
    shapes = [jax.ShapeDtypeStruct(e.shape, BF)] + [jax.ShapeDtypeStruct((8,) + d, BF) for d in dims] + [jax.ShapeDtypeStruct(d, F32) for d in dims]
    shapes += [jax.ShapeDtypeStruct((1, C), F32), jax.ShapeDtypeStruct((1, U), F32)]
    scratch = [pltpu.VMEM((2, n // chunks, D), BF), pltpu.VMEM((n, D), BF), pltpu.VMEM((n, D), BF), DMA((chunks, 3)), DMA((chunks, 3)), DMA((chunks + 2,))]
    scratch += [DMA((4, 10)), DMA((4, 10)), DMA((4, 4))]
    for r, c in dims:
        scratch += [pltpu.VMEM((4, r, c), BF), pltpu.VMEM((4, r, c), BF), pltpu.VMEM((2, r // 2, c), BF), pltpu.VMEM((2, r // 2, c), BF),
                    pltpu.VMEM((r // 2, c), BF), pltpu.VMEM((r // 2, c), BF)]
    wide = max(D, U)
    scratch += [pltpu.VMEM((n, wide), BF), pltpu.VMEM((n, C), BF), pltpu.VMEM((2, n, 256), BF), pltpu.VMEM((2, 256, wide), BF), DMA((3,)), DMA((2,)), DMA((2, 8))]
    assert D == U

    def kernel(*refs):
        refs = list(refs)
        take = lambda k: [refs.pop(0) for _ in range(k)]
        e_r, left_rs, right_rs = refs.pop(0), take(4), take(3)
        total, grads, owned, sum_rs = refs.pop(0), take(4), take(4), take(2)
        stage, land, swap, send, recv, local = take(6)
        spot = Spot()
        spot.meet(True)
        line = LineSum(spot, e_r, stage, land, swap, total, send, recv, local, chunks)
        send, recv, local = take(3)
        bufs = [take(6) for _ in range(4)]
        S = Scatter(spot, list(zip(grads, owned)), *[[b[i] for b in bufs] for i in range(6)], send, recv, local)
        wide_r, narrow_r, lbuf, obuf, rsem, lsem, osem = take(7)
        W = Products(left_rs, right_rs, grads, (wide_r, narrow_r), lbuf, obuf, rsem, lsem, osem)
        W.right(0, 0).start()
        W.right(1, 1).start()
        line.send_step(0)
        line.send_step(1)
        W.right(0, 0).wait()
        W.run(0, 0, 0, left_rs[0].shape[1] // 256)
        S.first(0)
        half = left_rs[1].shape[1] // 512
        W.run(1, 0, 0, half)
        line.add_step(0)
        line.send_step(2)
        S.second(0)
        W.run(1, 0, half, 2 * half)
        S.first(1)
        W.right(2, 0).start()
        W.right(1, 1).wait()
        W.run(2, 1, 0, 2)
        line.add_step(1)
        line.send_step(3)
        W.run(2, 1, 2, 8)
        S.first(2)
        W.sums(1, sum_rs[0])
        line.add_step(2)
        line.send_step(4)
        S.second(1)
        S.third(0)
        W.right(2, 0).wait()
        W.run(3, 0, 0, 4)
        line.add_step(3)
        line.send_step(5)
        S.second(2)
        W.run(3, 0, 4, 8)
        S.first(3)
        line.add_step(4)
        line.send_step(6)
        W.sums(0, sum_rs[1])
        S.third(1)
        line.add_step(5)
        line.send_step(7)
        S.second(3)
        line.add_step(6)
        line.send_step(8)
        S.third(2)
        line.add_step(7)
        line.send_step(9)
        line.add_step(8)
        line.send_step(10)
        S.third(3)
        S.last(0)
        S.last(1)
        line.send_step(11)
        S.last(2)
        S.last(3)
        line.close()
        S.close()

    flops = 2 * n * D * (lefts[0].shape[1] + lefts[1].shape[1] + C + U)
    got = pl.pallas_call(
        kernel, in_specs=[HBM] * 8, out_specs=outs, out_shape=shapes, scratch_shapes=scratch,
        compiler_params=pltpu.CompilerParams(vmem_limit_bytes=VM2, collective_id=ident, has_side_effects=True),
        cost_estimate=pl.CostEstimate(flops=flops, bytes_accessed=2 * n * D * 12, transcendentals=0), name="sum_scatter")(e, *lefts, *rights)
    gd, gn, gq, gu = got[5:9]
    return got[0], (gq, gd, gu, gn), got[9], got[10]


def adam_update(weight, grad, first, second):
    first_new = beta_one * first + (1.0 - beta_one) * grad
    second_new = beta_two * second + (1.0 - beta_two) * grad * grad
    mean_hat = first_new / (1.0 - beta_one**ADAM_STEP)
    square_hat = second_new / (1.0 - beta_two**ADAM_STEP)
    new_weight = weight - rate * (mean_hat / (jnp.sqrt(square_hat) + adam_eps) + decay * weight)
    return grad, first_new, second_new, new_weight - weight


def adam_layer(layer, weights, grads, firsts, seconds, before):
    steps = 8
    blocks = [(w.shape[1] // steps, w.shape[2]) for w in weights]

    def kernel(*refs):
        ins, outs = refs[:16], refs[-16:]
        for i in range(4):
            g = ins[4 + i][...].astype(F32)
            made = adam_update(ins[i][...].astype(F32), g, ins[8 + i][...], ins[12 + i][...])
            for k in range(4):
                outs[4 * i + k][...] = made[k]

    at = lambda b: spec((None,) + b, lambda j: (layer, j, 0))
    ins = [at(b) for b in blocks] + [spec(b, lambda j: (j, 0)) for b in blocks] + [at(b) for b in blocks] * 2
    args = [*weights, *grads, *firsts, *seconds]
    alias = {}
    if before is not None:
        ins += [pl.BlockSpec(memory_space=pl.ANY)] * 16
        args += list(before)
        alias = {16 + i: i for i in range(16)}
    shapes = [jax.ShapeDtypeStruct(w.shape, F32) for w in weights for _ in range(4)]
    count = sum(w.shape[1] * w.shape[2] for w in weights)
    return pl.pallas_call(
        kernel, grid=(steps,), in_specs=ins, out_specs=[at(b) for b in blocks for _ in range(4)], out_shape=shapes,
        input_output_aliases=alias, compiler_params=pltpu.CompilerParams(vmem_limit_bytes=VM),
        cost_estimate=pl.CostEstimate(flops=20 * count, bytes_accessed=30 * count, transcendentals=0), name="adam")(*args)


def layout(lengths_row, rows):
    slots = lengths_row.shape[0]
    number = jnp.arange(slots, dtype=jnp.int32)
    ends = jnp.sum(jnp.where(number[None, :] <= number[:, None], lengths_row[None, :], 0), axis=1)
    starts = ends - lengths_row
    index = jnp.arange(rows, dtype=jnp.int32)
    inside = (index[:, None] >= starts[None, :]) & (index[:, None] < ends[None, :])
    valid = jnp.any(inside, axis=1)
    slot = jnp.sum(jnp.where(inside, number[None, :], 0), axis=1)
    first = jnp.sum(jnp.where(inside, starts[None, :], 0), axis=1)
    segment = jnp.where(valid, slot, slots + index)
    return segment, index - first, valid


class PlainLinks:
    def weights(self, shards, layer):
        wq, wd, wu, wn = [w[layer] for w in shards]
        rows = lambda v: lax.all_gather(v, "dp", axis=0, tiled=True)
        stack = lambda v: lax.all_gather(v, "dp", axis=0, tiled=False)
        return rows(wq), stack(wd), rows(wu), stack(wn)

    def share(self, v):
        return lax.psum(v, "mp")

    def owned(self, grads):
        cut = lambda g: lax.psum_scatter(g, "dp", scatter_dimension=0, tiled=True)
        gq, gd, gu, gn = grads
        return cut(gq), cut(gd)[0], cut(gu), cut(gn)[0]

    def begin(self, shards, flat):
        return self.weights(shards, 0), lax.all_gather(flat, "dp", axis=0, tiled=False), None

    def middle(self, branch, shards):
        return self.share(branch), self.weights(shards, 1)

    def turn(self, e, lefts, rights, ident):
        ctx, act, h1, h2 = lefts
        gr, dmix, df = rights
        w = gr.shape[1] // lax.axis_size("dp")
        gd, _ = weight_grad(ctx, gr, w=w)
        gn, _ = weight_grad(act, gr, w=w)
        gq, qsum = weight_grad(h1, dmix)
        gu, usum = weight_grad(h2, df)
        return self.share(e), self.owned((gq, gd, gu, gn)), qsum, usum


class ChipLinks:
    def full(self, got):
        wq, wd, wu, wn = got
        return wq.reshape(-1, wq.shape[2]), wd, wu.reshape(-1, wu.shape[2]), wn

    def begin(self, shards, flat):
        wq, wd, wu, wn = shards
        flat, wq, wu = link_kernel("gather", 1, [flat, wq, wu], [None, 0, 0])
        return (wq.reshape(-1, wq.shape[2]), None, wu.reshape(-1, wu.shape[2]), None), flat, (wd, wn)

    def middle(self, branch, shards):
        got = link_kernel("sum_gather", 2, shards, [1] * 4, branch)
        return got[4], self.full(got[:4])

    def turn(self, e, lefts, rights, ident):
        return sum_scatter(ident, e, lefts, rights)


def flatten_small(parts):
    flat = jnp.concatenate([p.reshape(-1) for p in parts])
    return jnp.pad(flat, (0, -flat.size % 4096)).reshape(-1, 128)


def unpack_small(got, parts):
    got = got.reshape(got.shape[0], -1)
    out, at = [], 0
    for p in parts:
        piece = got[:, at:at + p.size].reshape((-1,) + p.shape)
        out.append(jnp.moveaxis(piece, 0, 2).reshape(p.shape[0], p.shape[1], -1))
        at += p.size
    return out


def body(links, tokens_in, cotangent, seq_lengths, *params):
    weights, small = params[:4], params[4:7]
    firsts, small_firsts = params[7:11], params[11:14]
    seconds, small_seconds = params[14:18], params[18:21]
    rows, D = tokens_in.shape
    segment, position, valid = layout(seq_lengths[0], rows)
    cos, sin = rope_tables(position)
    seg_col, seg_row = segment[:, None], segment[None, :]
    live = valid[:, None]
    first_full, got, later = links.begin(weights, flatten_small(small))
    qb, ub, vecs = unpack_small(got, small)
    qb = qb.reshape(LAYERS, 1, -1).astype(F32)
    ub = ub.reshape(LAYERS, 1, -1).astype(F32)
    vecs = vecs.astype(F32)

    held = [jnp.concatenate([vecs[layer, :4], vecs[layer - 1, 4:]]) for layer in range(LAYERS)]

    full, kept, extra = [first_full], [], None
    for layer in range(LAYERS):
        wq, wd, wu, wn = full[layer]
        h1, h2, mixed, act, gp, stats, *more = project(tokens_in, extra, held[layer], wq, qb[layer], cos, sin, wu, ub[layer], later if layer == 0 else None)
        if more:
            wd, wn = more
            full[0] = wq, wd, wu, wn
        ctx = attend_forward(mixed, seg_col, seg_row)
        branch = branch_out(ctx, act, wd, wn)
        kept.append((h1, h2, mixed, act, gp, stats, ctx, extra))
        if layer == 0:
            extra, made = links.middle(branch, weights)
            full.append(made)
        else:
            gout = gr = jnp.where(live, cotangent, 0).astype(BF)
            sums = jnp.sum(gout.astype(F32), axis=0, keepdims=True)
            branch, gr = lax.optimization_barrier((branch, gr))
            half = rows // 2
            tops, bottom = lax.psum(branch[:half], "mp"), branch[half:]

    big, little = [None] * LAYERS, [None] * LAYERS
    for layer in reversed(range(LAYERS)):
        wq, wd, wu, wn = full[layer]
        h1, h2, mixed, act, gp, stats, ctx, extra = kept[layer]
        dctx, df = back_in(gr, gp, wd, wn)
        dmix = attend_backward(mixed, dctx, seg_col, seg_row, cos, sin)
        e, norm_sums = back_out(dmix, df, wq, wu, tokens_in, extra, held[layer], stats)
        if layer == 0:
            bottom, e = lax.optimization_barrier((bottom, e))
        e, big[layer], qsum, usum = links.turn(e, (ctx, act, h1, h2), (gr, dmix, df), 3 + layer)
        little[layer] = (qsum, usum, norm_sums, sums)
        if layer:
            tops, e, bottom = lax.optimization_barrier((tops, e, bottom))
            bottom = lax.psum(bottom, "mp")
        made = norm_back(gout, e, tokens_in, extra, held[layer], stats, layer == 0)
        if layer:
            gout, gr, sums = made
        else:
            input_grad = made[0]
    branch = jnp.concatenate([tops, bottom])
    x_last = tokens_in.astype(F32) + kept[1][-1].astype(F32) + vecs[0, 4] + vecs[0, 5] + branch.astype(F32) + vecs[1, 4] + vecs[1, 5]
    output = jnp.where(live, x_last, 0.0).astype(BF)

    done = None
    for layer in reversed(range(LAYERS)):
        done = adam_layer(layer, weights, big[layer], firsts, seconds, done)

    z, line = lax.axis_index("mp"), lax.axis_size("mp")
    bias = jnp.concatenate([jnp.stack([t[i] for t in little]).reshape(-1) for i in (0, 1)])
    bias = jnp.where(jnp.arange(line)[:, None] == z, bias[None, :], 0.0)
    norm_sums = jnp.stack([t[2] for t in little])
    out_sums = jnp.where(z == 0, jnp.stack([t[3] for t in little]), 0.0)
    vec_sum = jnp.concatenate([norm_sums, out_sums, out_sums], axis=1).reshape(-1)
    total = lax.psum(jnp.concatenate([bias.reshape(-1), vec_sum]), ("dp", "mp"))
    bias = lax.dynamic_slice_in_dim(total[:bias.size].reshape(bias.shape), z, 1, 0)[0]
    total = jnp.concatenate([bias, total[-vec_sum.size:]])
    me = lax.axis_index("dp")
    small_out, at = [], 0
    for p, first, second in zip(small, small_firsts, small_seconds):
        width = p.shape[2]
        wide = p.shape[:2] + (lax.axis_size("dp") * width,)
        size = wide[0] * wide[1] * wide[2]
        g = lax.dynamic_slice_in_dim(total[at:at + size].reshape(wide), me * width, width, 2)
        at += size
        small_out += adam_update(p.astype(F32), g, first, second)
    return (output, input_grad, *done, *small_out)


def solution(mesh):
    rows_dp = P("dp", None)
    wide, tall, vec = P(None, "dp", "mp"), P(None, "mp", "dp"), P(None, None, "dp")
    group = (wide, tall, wide, tall, tall, tall, vec)
    return jax.shard_map(
        functools.partial(body, ChipLinks() if dict(mesh.shape) == {"dp": 8, "mp": 4} else PlainLinks()),
        mesh=mesh,
        in_specs=(rows_dp,) * 3 + group * 3,
        out_specs=(rows_dp,) * 2 + tuple(s for s in group for _ in range(4)),
        check_vma=False,
    )
```

```python
import functools
import jax
import jax.numpy as jnp
from jax import lax
from jax.experimental import pallas as pl
from jax.experimental.pallas import tpu as pltpu
from jax.sharding import PartitionSpec as P

HD = 256
ROT = 64
MAXLEN = 512
norm_eps = 1e-05
masked_score = -1e30
LAYERS = 2
BROW = 128
ADAM_STEP = 10
beta_one = 0.9
beta_two = 0.95
adam_eps = 1e-08
rate = 0.02
decay = 0.01
VM = 60 * 1024 * 1024
VM2 = 62 * 1024 * 1024
BF = jnp.bfloat16
ROWS = 256
UPB = 512
F32 = jnp.float32


def call(kernel, grid, in_specs, out_specs, out_shape, scratch=(), flops=0, nbytes=0, name=None, ident=None):
    return pl.pallas_call(
        kernel,
        grid_spec=pltpu.PrefetchScalarGridSpec(num_scalar_prefetch=0, grid=grid, in_specs=in_specs, out_specs=out_specs, scratch_shapes=list(scratch)),
        out_shape=out_shape,
        compiler_params=pltpu.CompilerParams(vmem_limit_bytes=VM, collective_id=ident, has_side_effects=ident is not None),
        cost_estimate=pl.CostEstimate(flops=flops, bytes_accessed=nbytes, transcendentals=0),
        name=name,
    )


def spec(shape, index, single=False):
    if single:
        return pl.BlockSpec(shape, index, pipeline_mode=pl.Buffered(1))
    return pl.BlockSpec(shape, index)


def rope_tables(position):
    half = ROT // 2
    freq = 10000.0 ** (-(jnp.arange(half, dtype=F32) * 2.0) / ROT)
    angle = position.astype(F32)[:, None] * freq[None, :]
    c, s = jnp.cos(angle), jnp.sin(angle)
    rows = position.shape[0]
    one = jnp.ones((rows, 128 - ROT), F32)
    zero = jnp.zeros((rows, 128 - ROT), F32)
    return jnp.concatenate([c, c, one], axis=1), jnp.concatenate([-s, s, zero], axis=1)


def turn(u, c, s):
    lane = lax.broadcasted_iota(jnp.int32, u.shape, 1)
    other = jnp.where(lane < ROT // 2, pltpu.roll(u, 128 - ROT // 2, 1), pltpu.roll(u, ROT // 2, 1))
    return u * c + other * s


def normed(x):
    mean = jnp.mean(x, axis=1, keepdims=True)
    centred = x - mean
    var = jnp.mean(centred * centred, axis=1, keepdims=True)
    rstd = lax.rsqrt(var + norm_eps)
    return centred * rstd, mean, rstd


def row_blocks(n):
    step = min(n, ROWS)
    return [slice(i, i + step) for i in range(0, n, step)]


def project(base, extra, vec, wq, bq, cos, sin, wu, bu, shards=None):
    n, D = base.shape
    C, U = wq.shape[1], wu.shape[1]
    QB, UB = 3 * HD, min(UPB, U)
    nq, nu = C // QB, U // UB
    RB = 128
    nr = n // RB
    ng = 0 if shards is None else len(shards)
    xs = [base] if extra is None else [base, extra]

    def kernel(*refs):
        refs = list(refs)
        take = lambda k: [refs.pop(0) for _ in range(k)]
        x_rs = take(len(xs))
        vec_r, wq_r, bq_r, cos_r, sin_r, wu_r, bu_r = take(7)
        shard_rs = take(ng)
        h1_o, h2_o, mix_r, a_r, gp_r, st_r = take(6)
        full_rs = take(ng)
        h1_r, h2_r = take(2)
        bufs = take(len(xs))
        in_sem, out_sem = take(2)
        j = pl.program_id(0)
        side = None
        if ng:
            spot = Spot()
            side = Gather(spot, [(a.at[0], b) for a, b in zip(shard_rs, full_rs)], *take(3))

            @pl.when(j == 0)
            def _():
                spot.meet(False)
                side.first(0)
                side.first(1)

        def host(step, *stages):
            if side is not None:
                @pl.when(j == min(step, nq + nu - 1))
                def _():
                    for name, *args in stages:
                        getattr(side, name)(*args)
        block = lambda i: pl.ds(i * RB, RB)
        loads = [[pltpu.make_async_copy(x.at[block(i)], buf.at[block(i)], in_sem.at[k, i]) for k, (x, buf) in enumerate(zip(x_rs, bufs))] for i in range(nr)]
        stores = [[pltpu.make_async_copy(h.at[block(i)], o.at[block(i)], out_sem.at[k, i]) for k, (h, o) in enumerate(((h1_r, h1_o), (h2_r, h2_o)))] for i in range(nr)]

        @pl.when(j == 0)
        def _():
            for group in loads:
                for copy in group:
                    copy.start()
            for i in range(nr):
                for copy in loads[i]:
                    copy.wait()
                rows = block(i)
                x = bufs[0][rows, :].astype(F32)
                if extra is not None:
                    x = x + bufs[1][rows, :].astype(F32) + vec_r[4:5, :] + vec_r[5:6, :]
                xhat, mean, rstd = normed(x)
                st_r[rows, 0:1] = mean
                st_r[rows, 1:2] = rstd
                h1_r[rows, :] = (xhat * vec_r[0:1, :] + vec_r[1:2, :]).astype(BF)
                h2_r[rows, :] = (xhat * vec_r[2:3, :] + vec_r[3:4, :]).astype(BF)
                for copy in stores[i]:
                    copy.start()

        @pl.when(j < nq)
        def _():
            for rows in row_blocks(n):
                for part in range(3):
                    at = part * HD
                    m = jnp.dot(h1_r[rows, :], wq_r[:, at:at + HD], preferred_element_type=F32) + bq_r[:, at:at + HD]
                    if part == 2:
                        mix_r[rows, at:at + HD] = m.astype(BF)
                    else:
                        mix_r[rows, at:at + 128] = turn(m[:, :128], cos_r[rows, :], sin_r[rows, :]).astype(BF)
                        mix_r[rows, at + 128:at + HD] = m[:, 128:].astype(BF)

        @pl.when(j >= nq)
        def _():
            for rows in row_blocks(n):
                for at in range(0, UB, 256):
                    cols = slice(at, at + 256)
                    f = jnp.dot(h2_r[rows, :], wu_r[:, cols], preferred_element_type=F32) + bu_r[:, cols]
                    phi = 0.5 * (1.0 + lax.erf(f * 0.7071067811865476))
                    a_r[rows, cols] = (f * phi).astype(BF)
                    gp_r[rows, cols] = (phi + f * (jnp.exp(-0.5 * f * f) * 0.3989422804014327)).astype(BF)

        host(1, ("second", 0))
        host(3, ("second", 1), ("third", 0))
        host(5, ("third", 1), ("last", 0), ("last", 1), ("close",))

        @pl.when(j == nq + nu - 1)
        def _():
            for group in stores:
                for copy in group:
                    copy.wait()

    whole = lambda j: (0, 0)
    qcol = lambda j: (0, jnp.minimum(j, nq - 1))
    ucol = lambda j: (0, jnp.maximum(j - nq, 0))
    far = pl.BlockSpec(memory_space=pl.ANY)
    ins = [far] * len(xs) + [
        spec((6, D), whole), spec((D, QB), qcol), spec((1, QB), qcol), spec((n, 128), whole, True), spec((n, 128), whole, True),
        spec((D, UB), ucol), spec((1, UB), ucol)] + [far] * ng
    outs = [far, far, spec((n, QB), qcol), spec((n, UB), ucol), spec((n, UB), ucol), spec((n, 128), whole)] + [far] * ng
    shapes = [jax.ShapeDtypeStruct(s, BF) for s in ((n, D), (n, D), (n, C), (n, U), (n, U))] + [jax.ShapeDtypeStruct((n, 128), F32)]
    DMA = pltpu.SemaphoreType.DMA
    scratch = [pltpu.VMEM((n, D), BF)] * (2 + len(xs)) + [DMA((len(xs), nr)), DMA((2, nr))]
    if ng:
        scratch += [DMA((ng, 9)), DMA((ng, 9)), DMA((ng,))]
        shapes += [jax.ShapeDtypeStruct((8,) + v.shape[1:], v.dtype) for v in shards]
    return call(kernel, (nq + nu,), ins, outs, shapes, scratch, ident=5 if ng else None, flops=2 * n * D * (C + U), nbytes=2 * (n * D * 3 + D * (C + U) + n * (C + 2 * U)), name="project")(*xs, vec, wq, bq, cos, sin, wu, bu, *(shards or ()))


def softmax_block(q, k, segq, segk, q0, k0):
    s = lax.dot_general(q, k, (((1,), (1,)), ((), ())), preferred_element_type=F32) * HD ** (-0.5)
    qi = q0 + lax.broadcasted_iota(jnp.int32, s.shape, 0)
    ki = k0 + lax.broadcasted_iota(jnp.int32, s.shape, 1)
    allowed = (segq == segk) & (ki <= qi)
    s = jnp.where(allowed, s, masked_score)
    top = jnp.max(s, axis=1, keepdims=True)
    e = jnp.exp(s - top)
    return e / jnp.sum(e, axis=1, keepdims=True)


def windows(n, qb):
    for i in range(n // qb):
        q0 = i * qb
        yield q0, max(0, q0 - MAXLEN)


def attend_forward(mixed, seg_col, seg_row):
    n, C = mixed.shape
    H = C // (3 * HD)
    qb = 256

    def kernel(q_r, k_r, v_r, sc_r, sr_r, o_r):
        for q0, k0 in windows(n, qb):
            qs, ks = slice(q0, q0 + qb), slice(k0, q0 + qb)
            p = softmax_block(q_r[qs, :], k_r[ks, :], sc_r[qs, :], sr_r[:, ks], q0, k0)
            o_r[qs, :] = jnp.dot(p.astype(BF), v_r[ks, :], preferred_element_type=F32).astype(BF)

    part = lambda t: spec((n, HD), lambda h: (0, 3 * h + t))
    return call(kernel, (H,), [part(0), part(1), part(2), spec((n, 1), lambda h: (0, 0)), spec((1, n), lambda h: (0, 0))],
                spec((n, HD), lambda h: (0, h)), jax.ShapeDtypeStruct((n, H * HD), BF),
                flops=H * n * 640 * HD * 4, nbytes=2 * n * C, name="attend")(mixed, mixed, mixed, seg_col, seg_row)


def attend_backward(mixed, dctx, seg_col, seg_row, cos, sin):
    n, C = mixed.shape
    H = C // (3 * HD)
    qb = 256
    scale = HD ** (-0.5)

    def kernel(q_r, k_r, v_r, do_r, sc_r, sr_r, cos_r, sin_r, o_r, dk_s, dv_s):
        def back(u, rows):
            c, s = cos_r[rows, :], -sin_r[rows, :]
            return jnp.concatenate([turn(u[:, :128], c, s), u[:, 128:]], axis=1).astype(BF)

        dk_s[...] = jnp.zeros_like(dk_s)
        dv_s[...] = jnp.zeros_like(dv_s)
        for q0, k0 in reversed(list(windows(n, qb))):
            qs, ks = slice(q0, q0 + qb), slice(k0, q0 + qb)
            q, k, do = q_r[qs, :], k_r[ks, :], do_r[qs, :]
            p = softmax_block(q, k, sc_r[qs, :], sr_r[:, ks], q0, k0)
            dp = lax.dot_general(do, v_r[ks, :], (((1,), (1,)), ((), ())), preferred_element_type=F32)
            delta = jnp.sum(p * dp, axis=1, keepdims=True)
            ds = (p * (dp - delta)).astype(BF)
            dq = jnp.dot(ds, k, preferred_element_type=F32) * scale
            dk_s[ks, :] += lax.dot_general(ds, q, (((0,), (0,)), ((), ())), preferred_element_type=F32)
            dv_s[ks, :] += lax.dot_general(p.astype(BF), do, (((0,), (0,)), ((), ())), preferred_element_type=F32)
            o_r[qs, :HD] = back(dq, qs)
            o_r[qs, HD:2 * HD] = back(dk_s[qs, :] * scale, qs)
            o_r[qs, 2 * HD:] = dv_s[qs, :].astype(BF)

    part = lambda t: spec((n, HD), lambda h: (0, 3 * h + t))
    whole = lambda h: (0, 0)
    return call(kernel, (H,), [part(0), part(1), part(2), spec((n, HD), lambda h: (0, h)), spec((n, 1), whole), spec((1, n), whole),
                spec((n, 128), whole), spec((n, 128), whole)],
                spec((n, 3 * HD), lambda h: (0, h)), jax.ShapeDtypeStruct((n, C), BF),
                scratch=[pltpu.VMEM((n, HD), F32), pltpu.VMEM((n, HD), F32)],
                flops=H * n * 640 * HD * 10, nbytes=4 * n * C, name="attend_back")(mixed, mixed, mixed, dctx, seg_col, seg_row, cos, sin)


def branch_out(ctx, act, wd, wn):
    n, R = ctx.shape
    U = act.shape[1]
    dp, _, w = wd.shape

    def kernel(c_r, a_r, wd_r, wn_r, o_r):
        o_r[...] = (jnp.dot(c_r[...], wd_r[...], preferred_element_type=F32) + jnp.dot(a_r[...], wn_r[...], preferred_element_type=F32)).astype(BF)

    whole = lambda s: (0, 0)
    pick = lambda s: (s, 0, 0)
    return call(kernel, (dp,), [spec((n, R), whole, True), spec((n, U), whole, True), spec((None, R, w), pick), spec((None, U, w), pick)],
                spec((n, w), lambda s: (0, s)), jax.ShapeDtypeStruct((n, dp * w), BF),
                flops=2 * n * dp * w * (R + U), nbytes=2 * (n * (R + U) + dp * w * (R + U + n)), name="branch")(ctx, act, wd, wn)


def back_in(gr, gp, wd, wn):
    n, D = gr.shape
    dp, R, w = wd.shape
    U = wn.shape[1]
    NB = 256
    nr, nu = R // NB, U // NB

    def kernel(g_r, gp_r, wd_r, wn_r, dc_r, df_r):
        j = pl.program_id(0)

        def times(w_r):
            acc = None
            for s in range(dp):
                t = lax.dot_general(g_r[:, s * w:(s + 1) * w], w_r[s], (((1,), (1,)), ((), ())), preferred_element_type=F32)
                acc = t if acc is None else acc + t
            return acc

        @pl.when(j < nr)
        def _():
            dc_r[...] = times(wd_r).astype(BF)

        @pl.when(j >= nr)
        def _():
            df_r[...] = (times(wn_r) * gp_r[...].astype(F32)).astype(BF)

    rc = lambda j: jnp.minimum(j, nr - 1)
    uc = lambda j: jnp.maximum(j - nr, 0)
    return call(kernel, (nr + nu,), [spec((n, D), lambda j: (0, 0), True), spec((n, NB), lambda j: (0, uc(j))),
                spec((dp, NB, w), lambda j: (0, rc(j), 0)), spec((dp, NB, w), lambda j: (0, uc(j), 0))],
                [spec((n, NB), lambda j: (0, rc(j))), spec((n, NB), lambda j: (0, uc(j)))],
                [jax.ShapeDtypeStruct((n, R), BF), jax.ShapeDtypeStruct((n, U), BF)],
                flops=2 * n * D * (R + U), nbytes=2 * (n * D + D * (R + U) + n * (R + 2 * U)), name="back_in")(gr, gp, wd, wn)


def back_out(dmix, df, wq, wu, base, extra, vec, stats):
    n, C = dmix.shape
    U = df.shape[1]
    D = wq.shape[0]
    NB = 256

    def kernel(*refs):
        if extra is None:
            dm_r, df_r, wq_r, wu_r, base_r, vec_r, st_r, e_r, g_r = refs
        else:
            dm_r, df_r, wq_r, wu_r, base_r, extra_r, vec_r, st_r, e_r, g_r = refs
        nt = (((1,), (1,)), ((), ()))
        d1 = lax.dot_general(dm_r[...], wq_r[...], nt, preferred_element_type=F32)
        d2 = lax.dot_general(df_r[...], wu_r[...], nt, preferred_element_type=F32)
        e_r[...] = (d1 * vec_r[0:1, :] + d2 * vec_r[2:3, :]).astype(BF)
        x = base_r[...].astype(F32)
        if extra is not None:
            x = x + extra_r[...].astype(F32) + vec_r[4:5, :] + vec_r[5:6, :]
        xhat = (x - st_r[:, 0:1]) * st_r[:, 1:2]
        g_r[0:1, :] = jnp.sum(d1 * xhat, axis=0, keepdims=True)
        g_r[1:2, :] = jnp.sum(d1, axis=0, keepdims=True)
        g_r[2:3, :] = jnp.sum(d2 * xhat, axis=0, keepdims=True)
        g_r[3:4, :] = jnp.sum(d2, axis=0, keepdims=True)

    whole = lambda j: (0, 0)
    col = lambda j: (0, j)
    row = lambda j: (j, 0)
    xs = [spec((n, NB), col)] + ([] if extra is None else [spec((n, NB), col)])
    args = [base] + ([] if extra is None else [extra])
    return call(kernel, (D // NB,), [spec((n, C), whole, True), spec((n, U), whole, True), spec((NB, C), row), spec((NB, U), row)] + xs +
                [spec((6, NB), col), spec((n, 128), whole)],
                [spec((n, NB), col), spec((4, NB), col)],
                [jax.ShapeDtypeStruct((n, D), BF), jax.ShapeDtypeStruct((4, D), F32)],
                flops=2 * n * D * (C + U), nbytes=2 * (n * (C + U) + D * (C + U) + n * D * 3), name="back_out")(dmix, df, wq, wu, *args, vec, stats)


def weight_grad(left, right, w=None):
    n, M = left.shape
    N = right.shape[1]
    MB = 256

    def kernel(l_r, r_r, o_r, s_r):
        g = lax.dot_general(l_r[...], r_r[...], (((0,), (0,)), ((), ())), preferred_element_type=F32)
        if w is None:
            o_r[...] = g.astype(BF)
        else:
            for s in range(N // w):
                o_r[s] = g[:, s * w:(s + 1) * w].astype(BF)

        @pl.when(pl.program_id(0) == 0)
        def _():
            s_r[...] = jnp.sum(r_r[...].astype(F32), axis=0, keepdims=True)

    whole = lambda j: (0, 0)
    if w is None:
        out, shape = spec((MB, N), lambda j: (j, 0)), (M, N)
    else:
        out, shape = spec((N // w, MB, w), lambda j: (0, j, 0)), (N // w, M, w)
    return call(kernel, (M // MB,), [spec((n, MB), lambda j: (0, j)), spec((n, N), whole, True)], [out, spec((1, N), whole)],
                [jax.ShapeDtypeStruct(shape, BF), jax.ShapeDtypeStruct((1, N), F32)],
                flops=2 * n * M * N, nbytes=2 * (n * M + n * N + M * N), name="wgrad")(left, right)


def norm_back(gout, e, base, extra, vec, stats, last):
    n, D = base.shape
    RB = 128

    def kernel(*refs):
        g_r, e_r, base_r = refs[:3]
        refs = refs[3:]
        if extra is not None:
            extra_r, refs = refs[0], refs[1:]
        vec_r, st_r, dx_r = refs[:3]
        x = base_r[...].astype(F32)
        if extra is not None:
            x = x + extra_r[...].astype(F32) + vec_r[4:5, :] + vec_r[5:6, :]
        xhat = (x - st_r[:, 0:1]) * st_r[:, 1:2]
        ev = e_r[...].astype(F32)
        me = jnp.mean(ev, axis=1, keepdims=True)
        mx = jnp.mean(ev * xhat, axis=1, keepdims=True)
        dx = g_r[...].astype(F32) + (ev - me - xhat * mx) * st_r[:, 1:2]
        dx_r[...] = dx
        if not last:
            low_r, sum_r = refs[3:]
            low_r[...] = dx.astype(BF)

            @pl.when(pl.program_id(0) == 0)
            def _():
                sum_r[...] = jnp.zeros_like(sum_r)

            sum_r[...] += jnp.sum(dx, axis=0, keepdims=True)

    row = lambda i: (i, 0)
    whole = lambda i: (0, 0)
    rows = spec((RB, D), row)
    ins = [rows, rows, rows] + ([] if extra is None else [rows]) + [spec((6, D), whole), spec((RB, 128), row)]
    args = [gout, e, base] + ([] if extra is None else [extra]) + [vec, stats]
    outs, shapes = [rows], [jax.ShapeDtypeStruct((n, D), F32)]
    if not last:
        outs += [rows, spec((1, D), whole)]
        shapes += [jax.ShapeDtypeStruct((n, D), BF), jax.ShapeDtypeStruct((1, D), F32)]
    return call(kernel, (n // RB,), ins, outs, shapes, flops=10 * n * D, nbytes=16 * n * D, name="norm_back")(*args)


MESH = pl.DeviceIdType.MESH


class Spot:
    def __init__(self):
        i = lax.axis_index("dp")
        c, x, y = lax.rem(i, 2), lax.rem(lax.div(i, 2), 2), lax.div(i, 4)
        self.me = i
        self.dx, self.dy, self.dc = 2 - 4 * x, 4 - 8 * y, 1 - 2 * c
        self.nx, self.ny, self.nc = i + self.dx, i + self.dy, i + self.dc
        self.diag = i + self.dx + self.dy
        z = lax.axis_index("mp")
        self.z = z
        self.outer = (z == 0) | (z == 3)
        self.inner = (z == 1) | (z == 2)
        self.pair = z + 1 - 2 * lax.rem(z, 2)
        self.across = 3 - z

    def meet(self, line):
        barrier = pltpu.get_barrier_semaphore()
        for peer in (self.nx, self.ny, self.nc):
            pl.semaphore_signal(barrier, inc=1, device_id={"dp": peer}, device_id_type=MESH)
        if line:
            pl.semaphore_signal(barrier, inc=1, device_id={"mp": self.pair}, device_id_type=MESH)

            @pl.when(self.inner)
            def _():
                pl.semaphore_signal(barrier, inc=1, device_id={"mp": self.across}, device_id_type=MESH)

            @pl.when(self.inner)
            def _():
                pl.semaphore_wait(barrier, 5)

            @pl.when(self.outer)
            def _():
                pl.semaphore_wait(barrier, 4)
        else:
            pl.semaphore_wait(barrier, 3)


def send_to(axis, peer, src, dst, send, recv):
    return pltpu.make_async_remote_copy(src_ref=src, dst_ref=dst, send_sem=send, recv_sem=recv, device_id={axis: peer}, device_id_type=MESH)


class Gather:
    copies = 9

    def __init__(self, spot, items, send, recv, local):
        self.spot, self.items, self.send, self.recv, self.local = spot, items, send, recv, local
        self.sent = []
        self.own = []

    def go(self, k, n, peer, src, dst):
        send_to("dp", peer, src, dst, self.send.at[k, n], self.recv.at[k, n]).start()
        self.sent.append((k, n, peer, src, dst))

    def arrived(self, k, n, dst):
        send_to("dp", self.spot.nc, dst, dst, self.send.at[k, n], self.recv.at[k, n]).wait_recv()

    def first(self, k):
        s, (src, out) = self.spot, self.items[k]
        for n, peer in enumerate((s.nx, s.ny, s.nc)):
            self.go(k, n, peer, src, out.at[s.me])
        pltpu.make_async_copy(src, out.at[s.me], self.local.at[k]).start()
        self.own.append(k)

    def halves(self, k):
        h = self.items[k][1].shape[1] // 2
        return pl.ds(0, h), pl.ds(h, h)

    def second(self, k):
        s, (_, out) = self.spot, self.items[k]
        low, high = self.halves(k)
        self.arrived(k, 0, out.at[s.nx])
        self.go(k, 3, s.ny, out.at[s.nx, high], out.at[s.nx, high])
        self.go(k, 4, s.nc, out.at[s.nx], out.at[s.nx])
        self.arrived(k, 1, out.at[s.ny])
        self.go(k, 5, s.nx, out.at[s.ny, low], out.at[s.ny, low])
        self.go(k, 6, s.nc, out.at[s.ny], out.at[s.ny])

    def third(self, k):
        s, (_, out) = self.spot, self.items[k]
        low, high = self.halves(k)
        self.arrived(k, 3, out.at[s.diag, high])
        self.go(k, 7, s.nc, out.at[s.diag, high], out.at[s.diag, high])
        self.arrived(k, 5, out.at[s.diag, low])
        self.go(k, 8, s.nc, out.at[s.diag, low], out.at[s.diag, low])

    def last(self, k):
        s, (_, out) = self.spot, self.items[k]
        low, high = self.halves(k)
        self.arrived(k, 2, out.at[s.nc])
        self.arrived(k, 4, out.at[s.nx + s.dc])
        self.arrived(k, 6, out.at[s.ny + s.dc])
        self.arrived(k, 7, out.at[s.diag + s.dc, high])
        self.arrived(k, 8, out.at[s.diag + s.dc, low])

    def close(self):
        for k in self.own:
            src, out = self.items[k]
            pltpu.make_async_copy(src, out.at[self.spot.me], self.local.at[k]).wait()
        for k, n, peer, src, dst in self.sent:
            send_to("dp", peer, src, dst, self.send.at[k, n], self.recv.at[k, n]).wait_send()


class LineSum:
    copies = 3

    def __init__(self, spot, pairs, stage, land, swap, send, recv, local):
        self.spot, self.stage, self.land, self.swap = spot, stage, land, swap
        self.send, self.recv, self.local = send, recv, local
        self.rows = stage.shape[1]
        self.parts, self.outs = [], []
        for part, start, out, rows in pairs:
            for at in range(0, rows, self.rows):
                self.parts.append(part.at[pl.ds(start + at, self.rows)])
                self.outs.append(out.at[pl.ds(at, self.rows)])
        self.chunks = len(self.parts)

    def cut(self, k):
        return pl.ds(k * self.rows, self.rows)

    def copy(self, k, n):
        s, rows = self.spot, self.cut(k)
        if n == 0:
            peer, src, dst = s.pair, self.parts[k], self.land
        elif n == 1:
            peer, src, dst = s.across, self.land.at[rows], self.swap
        else:
            peer, src, dst = s.pair, self.swap.at[rows], self.swap
        return send_to("mp", peer, src, dst.at[rows], self.send.at[k, n], self.recv.at[k, n])

    def keep(self, k):
        rows = self.cut(k)
        return pltpu.make_async_copy(self.swap.at[rows], self.outs[k], self.local.at[k])

    def load(self, k):
        return pltpu.make_async_copy(self.parts[k], self.stage.at[k % 2], self.local.at[self.chunks + k % 2])

    def add(self, k, dst, one, two, base):
        step = 32

        @pl.loop(0, self.rows // step)
        def _(i):
            rows = pl.ds(pl.multiple_of(k * self.rows + i * step, step), step)
            there = pl.ds(pl.multiple_of(base + i * step, step), step)
            dst[rows, :] = (one[there, :].astype(F32) + two[rows, :].astype(F32)).astype(BF)

    def send_step(self, t):
        n = self.chunks

        @pl.when(self.spot.outer)
        def _():
            if 0 <= t - 2 < n:
                self.copy(t - 2, 0).wait_send()
            if t < n:
                self.copy(t, 0).start()
            if 0 <= t - 4 < n:
                self.copy(t - 4, 2).wait_recv()
                self.keep(t - 4).start()

    def add_step(self, t):
        n = self.chunks

        @pl.when(self.spot.inner)
        def _():
            if t < n:
                if t == 0:
                    self.load(0).start()
                if t + 1 < n:
                    self.load(t + 1).start()
                self.load(t).wait()
                self.copy(t, 0).wait_recv()
                self.add(t, self.land, self.stage.at[t % 2], self.land, 0)
                self.copy(t, 1).start()
            if 0 <= t - 1 < n:
                self.copy(t - 1, 1).wait_recv()
                self.copy(t - 1, 1).wait_send()
                self.add(t - 1, self.swap, self.land, self.swap, (t - 1) * self.rows)
                self.copy(t - 1, 2).start()
                self.keep(t - 1).start()

    def close(self):
        for k in range(self.chunks):
            self.keep(k).wait()

        @pl.when(self.spot.inner)
        def _():
            for k in range(self.chunks):
                self.copy(k, 2).wait_send()


class Scatter:
    copies = 10

    def __init__(self, spot, items, own, sib, fx, fy, gx, gy, send, recv, local):
        self.spot, self.items = spot, items
        self.own, self.sib, self.fx, self.fy, self.gx, self.gy = own, sib, fx, fy, gx, gy
        self.send, self.recv, self.local = send, recv, local
        self.sent, self.loads = [], {}

    def go(self, k, n, peer, src, dst):
        copy = send_to("dp", peer, src, dst, self.send.at[k, n], self.recv.at[k, n])
        copy.start()
        self.sent.append(copy)

    def arrived(self, k, n, dst):
        send_to("dp", self.spot.nc, dst, dst, self.send.at[k, n], self.recv.at[k, n]).wait_recv()

    def first(self, k):
        s, grad = self.spot, self.items[k][0]
        for m, slot in enumerate((s.me, s.nx, s.ny, s.diag)):
            self.go(k, m, s.nc, grad.at[slot + s.dc], self.sib[k].at[m])
        self.loads[k] = []
        for m, slot in enumerate((s.me, s.nx, s.ny, s.diag)):
            copy = pltpu.make_async_copy(grad.at[slot], self.own[k].at[m], self.local.at[k, m])
            copy.start()
            self.loads[k].append(copy)

    def over(self, r, c, body, start=0):
        step = 16
        while step * 2 * c <= 32768 and r % (step * 2) == 0:
            step *= 2

        @pl.loop(0, r // step)
        def _(i):
            body(pl.ds(pl.multiple_of(i * step, step), step), pl.ds(pl.multiple_of(start + i * step, step), step))

    def second(self, k):
        s = self.spot
        own, sib = self.own[k], self.sib[k]
        _, r, c = own.shape
        h = r // 2
        low, high = pl.ds(0, h), pl.ds(h, h)
        for m in (3, 1, 2, 0):
            self.loads[k][m].wait()
            self.arrived(k, m, sib.at[m])

            def add(rows, _, m=m):
                own[m, rows, :] = (own[m, rows, :].astype(F32) + sib[m, rows, :].astype(F32)).astype(BF)

            self.over(r, c, add)
            if m == 3:
                self.go(k, 5, s.nx, own.at[3, low], self.fx[k].at[1])
                self.go(k, 7, s.ny, own.at[3, high], self.fy[k].at[1])
            if m == 1:
                self.go(k, 4, s.nx, own.at[1, low], self.fx[k].at[0])
            if m == 2:
                self.go(k, 6, s.ny, own.at[2, high], self.fy[k].at[0])

    def third(self, k):
        s = self.spot
        own, fx, fy = self.own[k], self.fx[k], self.fy[k]
        _, r, c = own.shape
        h = r // 2
        self.arrived(k, 5, fx.at[1])

        def add_low(rows, _):
            fx[1, rows, :] = (own[2, rows, :].astype(F32) + fx[1, rows, :].astype(F32)).astype(BF)

        self.over(h, c, add_low)
        self.go(k, 8, s.ny, fx.at[1], self.gy[k])
        self.arrived(k, 7, fy.at[1])

        def add_high(rows, there):
            fy[1, rows, :] = (own[1, there, :].astype(F32) + fy[1, rows, :].astype(F32)).astype(BF)

        self.over(h, c, add_high, h)
        self.go(k, 9, s.nx, fy.at[1], self.gx[k])

    def last(self, k):
        own, out = self.own[k], self.items[k][1]
        fx, fy, gx, gy = self.fx[k], self.fy[k], self.gx[k], self.gy[k]
        _, r, c = own.shape
        h = r // 2
        self.arrived(k, 4, fx.at[0])
        self.arrived(k, 8, gy)

        def low(rows, _):
            out[rows, :] = own[0, rows, :].astype(F32) + fx[0, rows, :].astype(F32) + gy[rows, :].astype(F32)

        self.over(h, c, low)
        self.arrived(k, 6, fy.at[0])
        self.arrived(k, 9, gx)

        def high(rows, there):
            out[there, :] = own[0, there, :].astype(F32) + fy[0, rows, :].astype(F32) + gx[rows, :].astype(F32)

        self.over(h, c, high, h)

    def close(self):
        for copy in self.sent:
            copy.wait_send()


def link_kernel(name, ident, shards, layers, part=None, chunks=8):
    ng = len(shards)
    HBM = pl.BlockSpec(memory_space=pl.ANY)
    DMA = pltpu.SemaphoreType.DMA
    parts = [] if part is None else [part]
    shapes = [jax.ShapeDtypeStruct((8,) + (v.shape if l is None else v.shape[1:]), v.dtype) for v, l in zip(shards, layers)]
    shapes += [jax.ShapeDtypeStruct(v.shape, BF) for v in parts]
    scratch = [DMA((ng, 9)), DMA((ng, 9)), DMA((ng,))]
    for v in parts:
        scratch += [pltpu.VMEM((2, v.shape[0] // chunks, v.shape[1]), BF), pltpu.VMEM(v.shape, BF), pltpu.VMEM(v.shape, BF), DMA((chunks, 3)), DMA((chunks, 3)), DMA((chunks + 2,))]

    def kernel(*refs):
        refs = list(refs)
        take = lambda n: [refs.pop(0) for _ in range(n)]
        src, ins, full, totals = take(ng), take(len(parts)), take(ng), take(len(parts))
        spot = Spot()
        spot.meet(bool(parts))
        G = Gather(spot, [(a if l is None else a.at[l], b) for a, l, b in zip(src, layers, full)], *take(3))
        if parts:
            stage, land, swap, send, recv, local = take(6)
            line = LineSum(spot, [(ins[0], 0, totals[0], ins[0].shape[0])], stage, land, swap, send, recv, local)
            plan_sum_gather(G, line)
            line.close()
        else:
            plan_gather(G)
        G.close()

    nbytes = sum(v.size * 2 for v in parts) + sum(8 * v.size for v in shards)
    return pl.pallas_call(
        kernel, in_specs=[HBM] * (ng + len(parts)), out_specs=[HBM] * (ng + len(parts)), out_shape=shapes, scratch_shapes=scratch,
        compiler_params=pltpu.CompilerParams(vmem_limit_bytes=VM, collective_id=ident, has_side_effects=True),
        cost_estimate=pl.CostEstimate(flops=0, bytes_accessed=nbytes, transcendentals=0), name=name)(*shards, *parts)


def plan_gather(G):
    n = len(G.items)
    for stage in (G.first, G.second, G.third, G.last):
        for k in range(n):
            stage(k)


class Products:
    def __init__(self, lefts, rights, grads, rhs, lbuf, obuf, rsem, lsem, osem):
        self.lefts, self.rights, self.grads = lefts, rights, grads
        self.rhs, self.lbuf, self.obuf, self.rsem, self.lsem, self.osem = rhs, lbuf, obuf, rsem, lsem, osem

    def right(self, i, slot):
        return pltpu.make_async_copy(self.rights[i], self.rhs[slot], self.rsem.at[i])

    def left(self, k, m):
        cols = pl.ds(pl.multiple_of(m * 256, 256), 256)
        return pltpu.make_async_copy(self.lefts[k].at[:, cols], self.lbuf.at[lax.rem(m, 2)], self.lsem.at[lax.rem(m, 2)])

    def stores(self, k, m):
        grad, o = self.grads[k], self.obuf.at[lax.rem(m, 2)]
        sem = self.osem.at[lax.rem(m, 2)]
        slots, r, c = grad.shape
        if r == 256 and self.lefts[k].shape[1] == slots * r:
            return [pltpu.make_async_copy(o.at[:, pl.ds(0, c)], grad.at[m], sem.at[0])]
        rows = pl.ds(pl.multiple_of(m * 256, 256), 256)
        return [pltpu.make_async_copy(o.at[:, pl.ds(s * c, c)], grad.at[s, rows], sem.at[s]) for s in range(slots)]

    def run(self, k, slot, start, stop):
        count = self.lefts[k].shape[1] // 256
        right = self.rhs[slot]
        width = right.shape[1]
        if start == 0:
            self.left(k, 0).start()

        @pl.loop(start, stop)
        def _(m):
            self.left(k, m).wait()

            @pl.when(m + 1 < count)
            def _():
                self.left(k, m + 1).start()

            @pl.when(m >= 2)
            def _():
                for copy in self.stores(k, m - 2):
                    copy.wait()

            g = lax.dot_general(self.lbuf[lax.rem(m, 2)], right[...], (((0,), (0,)), ((), ())), preferred_element_type=F32)
            self.obuf[lax.rem(m, 2), :, :width] = g.astype(BF)
            for copy in self.stores(k, m):
                copy.start()

        if stop == count:
            for m in (count - 2, count - 1):
                for copy in self.stores(k, jnp.int32(m)):
                    copy.wait()

    def sums(self, slot, out):
        right = self.rhs[slot]
        out[...] = jnp.zeros_like(out)

        @pl.loop(0, right.shape[0] // 64)
        def _(i):
            out[...] += jnp.sum(right[pl.ds(pl.multiple_of(i * 64, 64), 64), :].astype(F32), axis=0, keepdims=True)


def plan_sum_gather(G, line):
    for k in range(4):
        G.first(k)
    stages = {3: [("second", 0), ("second", 1)], 5: [("second", 2)], 7: [("second", 3)], 8: [("third", 0), ("third", 1)], 9: [("third", 2)],
              10: [("third", 3)]}
    line.send_step(0)
    for at in range(1, 12):
        line.send_step(at)
        if at - 1 <= line.chunks:
            line.add_step(at - 1)
        for name, k in stages.get(at, ()):
            getattr(G, name)(k)
    for k in range(4):
        G.last(k)


def sum_scatter(ident, e, more, first_row, more_rows, lefts, rights, step=128):
    n, D = e.shape
    HBM = pl.BlockSpec(memory_space=pl.ANY)
    VM_ = pl.BlockSpec(memory_space=pltpu.VMEM)
    C, U = rights[1].shape[1], rights[2].shape[1]
    w = D // 8
    dims = [(lefts[0].shape[1], w), (lefts[1].shape[1], w), (w, C), (w, U)]
    DMA = pltpu.SemaphoreType.DMA
    chunks = (n + more_rows) // step
    outs = [HBM] * 2 + [HBM] * 4 + [VM_] * 4 + [VM_] * 2
    shapes = [jax.ShapeDtypeStruct(e.shape, BF), jax.ShapeDtypeStruct((more_rows, D), BF)] + [jax.ShapeDtypeStruct((8,) + d, BF) for d in dims] + [jax.ShapeDtypeStruct(d, F32) for d in dims]
    shapes += [jax.ShapeDtypeStruct((1, C), F32), jax.ShapeDtypeStruct((1, U), F32)]
    scratch = [pltpu.VMEM((2, step, D), BF)] + [pltpu.VMEM((n + more_rows, D), BF)] * 2 + [DMA((chunks, 3)), DMA((chunks, 3)), DMA((chunks + 2,))]
    scratch += [DMA((4, 10)), DMA((4, 10)), DMA((4, 4))]
    for r, c in dims:
        scratch += [pltpu.VMEM((4, r, c), BF), pltpu.VMEM((4, r, c), BF), pltpu.VMEM((2, r // 2, c), BF), pltpu.VMEM((2, r // 2, c), BF),
                    pltpu.VMEM((r // 2, c), BF), pltpu.VMEM((r // 2, c), BF)]
    wide = max(D, U)
    scratch += [pltpu.VMEM((n, wide), BF), pltpu.VMEM((n, C), BF), pltpu.VMEM((2, n, 256), BF), pltpu.VMEM((2, 256, wide), BF), DMA((3,)), DMA((2,)), DMA((2, 8))]
    assert D == U

    def kernel(*refs):
        refs = list(refs)
        take = lambda k: [refs.pop(0) for _ in range(k)]
        (e_r, more_r), left_rs, right_rs = take(2), take(4), take(3)
        (total, more_total), grads, owned, sum_rs = take(2), take(4), take(4), take(2)
        stage, land, swap, send, recv, local = take(6)
        spot = Spot()
        spot.meet(True)
        line = LineSum(spot, [(e_r, 0, total, n), (more_r, first_row, more_total, more_rows)], stage, land, swap, send, recv, local)
        send, recv, local = take(3)
        bufs = [take(6) for _ in range(4)]
        S = Scatter(spot, list(zip(grads, owned)), *[[b[i] for b in bufs] for i in range(6)], send, recv, local)
        wide_r, narrow_r, lbuf, obuf, rsem, lsem, osem = take(7)
        W = Products(left_rs, right_rs, grads, (wide_r, narrow_r), lbuf, obuf, rsem, lsem, osem)
        W.right(0, 0).start()
        W.right(1, 1).start()
        half = left_rs[1].shape[1] // 512
        state = [2, 0]

        def slot():
            send_at, add_at = state
            if add_at <= chunks:
                line.add_step(add_at)
            if send_at < chunks + 4:
                line.send_step(send_at)
            state[:] = send_at + 1, add_at + 1

        line.send_step(0)
        line.send_step(1)
        W.right(0, 0).wait()
        W.run(0, 0, 0, left_rs[0].shape[1] // 256)
        S.first(0)
        W.run(1, 0, 0, half)
        slot()
        S.second(0)
        W.run(1, 0, half, 2 * half)
        S.first(1)
        W.right(2, 0).start()
        W.right(1, 1).wait()
        W.run(2, 1, 0, 2)
        slot()
        W.run(2, 1, 2, 8)
        S.first(2)
        S.second(1)
        slot()
        W.right(2, 0).wait()
        W.run(3, 0, 0, 4)
        S.third(0)
        slot()
        S.second(2)
        W.run(3, 0, 4, 8)
        S.first(3)
        W.sums(1, sum_rs[0])
        slot()
        S.third(1)
        S.second(3)
        slot()
        W.sums(0, sum_rs[1])
        S.last(0)
        slot()
        S.third(2)
        S.last(1)
        slot()
        slot()
        S.third(3)
        S.last(2)
        while state[0] < chunks + 4:
            slot()
        S.last(3)
        line.close()
        S.close()

    flops = 2 * n * D * (lefts[0].shape[1] + lefts[1].shape[1] + C + U)
    got = pl.pallas_call(
        kernel, in_specs=[HBM] * 9, out_specs=outs, out_shape=shapes, scratch_shapes=scratch,
        compiler_params=pltpu.CompilerParams(vmem_limit_bytes=VM2, collective_id=ident, has_side_effects=True),
        cost_estimate=pl.CostEstimate(flops=flops, bytes_accessed=2 * n * D * 12, transcendentals=0), name="sum_scatter")(e, more, *lefts, *rights)
    gd, gn, gq, gu = got[6:10]
    return got[0], got[1], (gq, gd, gu, gn), got[10], got[11]


def small_sum(pieces, shared):
    ndp, r, _ = pieces.shape
    nmp = lax.axis_size("mp")

    def kernel(x_r, o_r, land, line, send, recv, send2, recv2):
        i, z = lax.axis_index("dp"), lax.axis_index("mp")
        barrier = pltpu.get_barrier_semaphore()
        for s in range(1, ndp):
            pl.semaphore_signal(barrier, inc=1, device_id={"dp": lax.rem(i + s, ndp)}, device_id_type=MESH)
        for s in range(1, nmp):
            pl.semaphore_signal(barrier, inc=1, device_id={"mp": lax.rem(z + s, nmp)}, device_id_type=MESH)
        pl.semaphore_wait(barrier, ndp + nmp - 2)
        first = [send_to("dp", lax.rem(i + s, ndp), x_r.at[lax.rem(i + s, ndp)], land.at[i], send.at[s], recv.at[s]) for s in range(1, ndp)]
        for copy in first:
            copy.start()
        land[pl.ds(i, 1)] = x_r[pl.ds(i, 1)]
        for s in range(1, ndp):
            there = land.at[lax.rem(i - s + ndp, ndp)]
            send_to("dp", i, there, there, send.at[s], recv.at[s]).wait_recv()
        acc = land[0]
        for j in range(1, ndp):
            acc = acc + land[j]
        o_r[...] = acc
        line[pl.ds(z, 1)] = acc[None, :shared]
        second = [send_to("mp", lax.rem(z + s, nmp), line.at[z], line.at[z], send2.at[s], recv2.at[s]) for s in range(1, nmp)]
        for copy in second:
            copy.start()
        for s in range(1, nmp):
            there = line.at[lax.rem(z - s + nmp, nmp)]
            send_to("mp", z, there, there, send2.at[s], recv2.at[s]).wait_recv()
        acc = line[0]
        for j in range(1, nmp):
            acc = acc + line[j]
        o_r[:shared] = acc
        for copy in first + second:
            copy.wait_send()

    VM_ = pl.BlockSpec(memory_space=pltpu.VMEM)
    DMA = pltpu.SemaphoreType.DMA
    return pl.pallas_call(
        kernel, in_specs=[VM_], out_specs=VM_, out_shape=jax.ShapeDtypeStruct((r, 128), F32),
        scratch_shapes=[pltpu.VMEM(pieces.shape, F32), pltpu.VMEM((nmp, shared, 128), F32), DMA((ndp,)), DMA((ndp,)), DMA((nmp,)), DMA((nmp,))],
        compiler_params=pltpu.CompilerParams(vmem_limit_bytes=VM // 4, collective_id=6, has_side_effects=True), name="small_sum")(pieces)


def adam_update(weight, grad, first, second):
    first_new = beta_one * first + (1.0 - beta_one) * grad
    second_new = beta_two * second + (1.0 - beta_two) * grad * grad
    mean_hat = first_new / (1.0 - beta_one**ADAM_STEP)
    square_hat = second_new / (1.0 - beta_two**ADAM_STEP)
    new_weight = weight - rate * (mean_hat / (jnp.sqrt(square_hat) + adam_eps) + decay * weight)
    return grad, first_new, second_new, new_weight - weight


def adam_layer(layer, weights, grads, firsts, seconds, before):
    steps = 8
    blocks = [(w.shape[1] // steps, w.shape[2]) for w in weights]

    def kernel(*refs):
        ins, outs = refs[:16], refs[-16:]
        for i in range(4):
            g = ins[4 + i][...].astype(F32)
            made = adam_update(ins[i][...].astype(F32), g, ins[8 + i][...], ins[12 + i][...])
            for k in range(4):
                outs[4 * i + k][...] = made[k]

    at = lambda b: spec((None,) + b, lambda j: (layer, j, 0))
    ins = [at(b) for b in blocks] + [spec(b, lambda j: (j, 0)) for b in blocks] + [at(b) for b in blocks] * 2
    args = [*weights, *grads, *firsts, *seconds]
    alias = {}
    if before is not None:
        ins += [pl.BlockSpec(memory_space=pl.ANY)] * 16
        args += list(before)
        alias = {16 + i: i for i in range(16)}
    shapes = [jax.ShapeDtypeStruct(w.shape, F32) for w in weights for _ in range(4)]
    count = sum(w.shape[1] * w.shape[2] for w in weights)
    return pl.pallas_call(
        kernel, grid=(steps,), in_specs=ins, out_specs=[at(b) for b in blocks for _ in range(4)], out_shape=shapes,
        input_output_aliases=alias, compiler_params=pltpu.CompilerParams(vmem_limit_bytes=VM),
        cost_estimate=pl.CostEstimate(flops=20 * count, bytes_accessed=30 * count, transcendentals=0), name="adam")(*args)


def layout(lengths_row, rows):
    slots = lengths_row.shape[0]
    number = jnp.arange(slots, dtype=jnp.int32)
    ends = jnp.sum(jnp.where(number[None, :] <= number[:, None], lengths_row[None, :], 0), axis=1)
    starts = ends - lengths_row
    index = jnp.arange(rows, dtype=jnp.int32)
    inside = (index[:, None] >= starts[None, :]) & (index[:, None] < ends[None, :])
    valid = jnp.any(inside, axis=1)
    slot = jnp.sum(jnp.where(inside, number[None, :], 0), axis=1)
    first = jnp.sum(jnp.where(inside, starts[None, :], 0), axis=1)
    segment = jnp.where(valid, slot, slots + index)
    return segment, index - first, valid


class PlainLinks:
    def weights(self, shards, layer):
        wq, wd, wu, wn = [w[layer] for w in shards]
        rows = lambda v: lax.all_gather(v, "dp", axis=0, tiled=True)
        stack = lambda v: lax.all_gather(v, "dp", axis=0, tiled=False)
        return rows(wq), stack(wd), rows(wu), stack(wn)

    def share(self, v):
        return lax.psum(v, "mp")

    def owned(self, grads):
        cut = lambda g: lax.psum_scatter(g, "dp", scatter_dimension=0, tiled=True)
        gq, gd, gu, gn = grads
        return cut(gq), cut(gd)[0], cut(gu), cut(gn)[0]

    def small(self, pieces, shared):
        total = lax.psum(pieces, "dp")[lax.axis_index("dp")]
        return jnp.concatenate([lax.psum(total[:shared], "mp"), total[shared:]])

    def begin(self, shards, flat):
        return self.weights(shards, 0), lax.all_gather(flat, "dp", axis=0, tiled=False), None

    def middle(self, branch, shards):
        return self.share(branch), self.weights(shards, 1)

    def turn(self, e, more, first_row, more_rows, lefts, rights, ident):
        ctx, act, h1, h2 = lefts
        gr, dmix, df = rights
        w = gr.shape[1] // lax.axis_size("dp")
        gd, _ = weight_grad(ctx, gr, w=w)
        gn, _ = weight_grad(act, gr, w=w)
        gq, qsum = weight_grad(h1, dmix)
        gu, usum = weight_grad(h2, df)
        more = self.share(more[first_row:first_row + more_rows])
        return self.share(e), more, self.owned((gq, gd, gu, gn)), qsum, usum


class ChipLinks:
    def full(self, got):
        wq, wd, wu, wn = got
        return wq.reshape(-1, wq.shape[2]), wd, wu.reshape(-1, wu.shape[2]), wn

    def begin(self, shards, flat):
        wq, wd, wu, wn = shards
        flat, wq, wu = link_kernel("gather", 1, [flat, wq, wu], [None, 0, 0])
        return (wq.reshape(-1, wq.shape[2]), None, wu.reshape(-1, wu.shape[2]), None), flat, (wd, wn)

    def middle(self, branch, shards):
        got = link_kernel("sum_gather", 2, shards, [1] * 4, branch)
        return got[4], self.full(got[:4])

    def turn(self, e, more, first_row, more_rows, lefts, rights, ident):
        return sum_scatter(ident, e, more, first_row, more_rows, lefts, rights)

    def small(self, pieces, shared):
        return small_sum(pieces, shared)


def flatten_small(parts):
    flat = jnp.concatenate([p.reshape(-1) for p in parts])
    return jnp.pad(flat, (0, -flat.size % 4096)).reshape(-1, 128)


def unpack_small(got, parts):
    got = got.reshape(got.shape[0], -1)
    out, at = [], 0
    for p in parts:
        piece = got[:, at:at + p.size].reshape((-1,) + p.shape)
        out.append(jnp.moveaxis(piece, 0, 2).reshape(p.shape[0], p.shape[1], -1))
        at += p.size
    return out


def body(links, tokens_in, cotangent, seq_lengths, *params):
    weights, small = params[:4], params[4:7]
    firsts, small_firsts = params[7:11], params[11:14]
    seconds, small_seconds = params[14:18], params[18:21]
    rows, D = tokens_in.shape
    segment, position, valid = layout(seq_lengths[0], rows)
    cos, sin = rope_tables(position)
    seg_col, seg_row = segment[:, None], segment[None, :]
    live = valid[:, None]
    first_full, got, later = links.begin(weights, flatten_small(small))
    qb, ub, vecs = unpack_small(got, small)
    qb = qb.reshape(LAYERS, 1, -1).astype(F32)
    ub = ub.reshape(LAYERS, 1, -1).astype(F32)
    vecs = vecs.astype(F32)

    held = [jnp.concatenate([vecs[layer, :4], vecs[layer - 1, 4:]]) for layer in range(LAYERS)]

    full, kept, extra = [first_full], [], None
    for layer in range(LAYERS):
        wq, wd, wu, wn = full[layer]
        h1, h2, mixed, act, gp, stats, *more = project(tokens_in, extra, held[layer], wq, qb[layer], cos, sin, wu, ub[layer], later if layer == 0 else None)
        if more:
            wd, wn = more
            full[0] = wq, wd, wu, wn
        ctx = attend_forward(mixed, seg_col, seg_row)
        branch = branch_out(ctx, act, wd, wn)
        kept.append((h1, h2, mixed, act, gp, stats, ctx, extra))
        if layer == 0:
            extra, made = links.middle(branch, weights)
            full.append(made)
        else:
            gout = gr = jnp.where(live, cotangent, 0).astype(BF)
            sums = jnp.sum(gout.astype(F32), axis=0, keepdims=True)
            branch, gr = lax.optimization_barrier((branch, gr))
            branch_sum = [None] * 4
            quarter = rows // 4
            branch_sum[0] = lax.psum(branch[:quarter], "mp")
    big, little = [None] * LAYERS, [None] * LAYERS
    for layer in reversed(range(LAYERS)):
        wq, wd, wu, wn = full[layer]
        h1, h2, mixed, act, gp, stats, ctx, extra = kept[layer]
        dctx, df = back_in(gr, gp, wd, wn)
        dmix = attend_backward(mixed, dctx, seg_col, seg_row, cos, sin)
        e, norm_sums = back_out(dmix, df, wq, wu, tokens_in, extra, held[layer], stats)
        if layer == 0:
            branch_sum[2], e = lax.optimization_barrier((branch_sum[2], e))
        at = 1 if layer else 3
        e, branch_sum[at], big[layer], qsum, usum = links.turn(e, branch, at * quarter, quarter, (ctx, act, h1, h2), (gr, dmix, df), 3 + layer)
        little[layer] = (qsum, usum, norm_sums, sums)
        if layer:
            branch_sum[0], e, third = lax.optimization_barrier((branch_sum[0], e, branch[2 * quarter:3 * quarter]))
            branch_sum[2] = lax.psum(third, "mp")
        made = norm_back(gout, e, tokens_in, extra, held[layer], stats, layer == 0)
        if layer:
            gout, gr, sums = made
        else:
            input_grad = made[0]
    branch = jnp.concatenate(branch_sum)
    x_last = tokens_in.astype(F32) + kept[1][-1].astype(F32) + vecs[0, 4] + vecs[0, 5] + branch.astype(F32) + vecs[1, 4] + vecs[1, 5]
    output = jnp.where(live, x_last, 0.0).astype(BF)

    done = None
    for layer in reversed(range(LAYERS)):
        done = adam_layer(layer, weights, big[layer], firsts, seconds, done)

    ndp = lax.axis_size("dp")

    def pieces(v, width):
        v = v.reshape(-1, ndp, width // ndp)
        return jnp.moveaxis(v, 1, 0).reshape(ndp, -1)

    norms = jnp.concatenate([pieces(t[2], D) for t in little], axis=1)
    rest = [pieces(t[i], BROW) for i in (0, 1) for t in little] + [pieces(t[3], D) for t in little]
    rest = jnp.concatenate(rest, axis=1)
    shared, count = norms.shape[1] // 128, rest.shape[1]
    rest = jnp.pad(rest, ((0, 0), (0, -count % 1024)))
    total = links.small(jnp.concatenate([norms, rest], axis=1).reshape(ndp, -1, 128), shared)
    norms, rest = total[:shared].reshape(LAYERS, 4, -1), total[shared:].reshape(-1)
    small_grads, at = [], 0
    for p in small[:2]:
        small_grads.append(rest[at:at + p.size].reshape(p.shape))
        at += p.size
    tops_sum = rest[at:count].reshape(LAYERS, 1, -1)
    small_grads.append(jnp.concatenate([norms, tops_sum, tops_sum], axis=1))
    small_out = []
    for p, g, first, second in zip(small, small_grads, small_firsts, small_seconds):
        small_out += adam_update(p.astype(F32), g, first, second)
    return (output, input_grad, *done, *small_out)


def solution(mesh):
    rows_dp = P("dp", None)
    wide, tall, vec = P(None, "dp", "mp"), P(None, "mp", "dp"), P(None, None, "dp")
    group = (wide, tall, wide, tall, tall, tall, vec)
    return jax.shard_map(
        functools.partial(body, ChipLinks() if dict(mesh.shape) == {"dp": 8, "mp": 4} else PlainLinks()),
        mesh=mesh,
        in_specs=(rows_dp,) * 3 + group * 3,
        out_specs=(rows_dp,) * 2 + tuple(s for s in group for _ in range(4)),
        check_vma=False,
    )
```

```python
import functools
import jax
import jax.numpy as jnp
from jax import lax
from jax.experimental import pallas as pl
from jax.experimental.pallas import tpu as pltpu
from jax.sharding import PartitionSpec as P

HD = 256
ROT = 64
MAXLEN = 512
norm_eps = 1e-05
masked_score = -1e30
LAYERS = 2
BROW = 128
ADAM_STEP = 10
beta_one = 0.9
beta_two = 0.95
adam_eps = 1e-08
rate = 0.02
decay = 0.01
VM = 60 * 1024 * 1024
VM2 = 62 * 1024 * 1024
BF = jnp.bfloat16
ROWS = 256
UPB = 512
F32 = jnp.float32


def call(kernel, grid, in_specs, out_specs, out_shape, scratch=(), flops=0, nbytes=0, name=None, ident=None):
    return pl.pallas_call(
        kernel,
        grid_spec=pltpu.PrefetchScalarGridSpec(num_scalar_prefetch=0, grid=grid, in_specs=in_specs, out_specs=out_specs, scratch_shapes=list(scratch)),
        out_shape=out_shape,
        compiler_params=pltpu.CompilerParams(vmem_limit_bytes=VM, collective_id=ident, has_side_effects=ident is not None),
        cost_estimate=pl.CostEstimate(flops=flops, bytes_accessed=nbytes, transcendentals=0),
        name=name,
    )


def spec(shape, index, single=False):
    if single:
        return pl.BlockSpec(shape, index, pipeline_mode=pl.Buffered(1))
    return pl.BlockSpec(shape, index)


def rope_tables(position):
    half = ROT // 2
    freq = 10000.0 ** (-(jnp.arange(half, dtype=F32) * 2.0) / ROT)
    angle = position.astype(F32)[:, None] * freq[None, :]
    c, s = jnp.cos(angle), jnp.sin(angle)
    rows = position.shape[0]
    one = jnp.ones((rows, 128 - ROT), F32)
    zero = jnp.zeros((rows, 128 - ROT), F32)
    return jnp.concatenate([c, c, one], axis=1), jnp.concatenate([-s, s, zero], axis=1)


def turn(u, c, s):
    lane = lax.broadcasted_iota(jnp.int32, u.shape, 1)
    other = jnp.where(lane < ROT // 2, pltpu.roll(u, 128 - ROT // 2, 1), pltpu.roll(u, ROT // 2, 1))
    return u * c + other * s


def normed(x):
    mean = jnp.mean(x, axis=1, keepdims=True)
    centred = x - mean
    var = jnp.mean(centred * centred, axis=1, keepdims=True)
    rstd = lax.rsqrt(var + norm_eps)
    return centred * rstd, mean, rstd


def row_blocks(n):
    step = min(n, ROWS)
    return [slice(i, i + step) for i in range(0, n, step)]


def project(base, extra, vec, wq, bq, cos, sin, wu, bu, shards=None):
    n, D = base.shape
    C, U = wq.shape[1], wu.shape[1]
    QB, UB = 3 * HD, min(UPB, U)
    nq, nu = C // QB, U // UB
    RB = 128
    nr = n // RB
    ng = 0 if shards is None else len(shards)
    xs = [base] if extra is None else [base, extra]

    def kernel(*refs):
        refs = list(refs)
        take = lambda k: [refs.pop(0) for _ in range(k)]
        x_rs = take(len(xs))
        vec_r, wq_r, bq_r, cos_r, sin_r, wu_r, bu_r = take(7)
        shard_rs = take(ng)
        h1_o, h2_o, mix_r, a_r, gp_r, st_r = take(6)
        full_rs = take(ng)
        h1_r, h2_r = take(2)
        bufs = take(len(xs))
        in_sem, out_sem = take(2)
        j = pl.program_id(0)
        side = None
        if ng:
            spot = Spot()
            side = Gather(spot, [(a.at[0], b) for a, b in zip(shard_rs, full_rs)], *take(3))

            @pl.when(j == 0)
            def _():
                spot.meet(False)
                side.first(0)
                side.first(1)

        def host(step, *stages):
            if side is not None:
                @pl.when(j == min(step, nq + nu - 1))
                def _():
                    for name, *args in stages:
                        getattr(side, name)(*args)
        block = lambda i: pl.ds(i * RB, RB)
        loads = [[pltpu.make_async_copy(x.at[block(i)], buf.at[block(i)], in_sem.at[k, i]) for k, (x, buf) in enumerate(zip(x_rs, bufs))] for i in range(nr)]
        stores = [[pltpu.make_async_copy(h.at[block(i)], o.at[block(i)], out_sem.at[k, i]) for k, (h, o) in enumerate(((h1_r, h1_o), (h2_r, h2_o)))] for i in range(nr)]

        @pl.when(j == 0)
        def _():
            for group in loads:
                for copy in group:
                    copy.start()
            for i in range(nr):
                for copy in loads[i]:
                    copy.wait()
                rows = block(i)
                x = bufs[0][rows, :].astype(F32)
                if extra is not None:
                    x = x + bufs[1][rows, :].astype(F32) + vec_r[4:5, :] + vec_r[5:6, :]
                xhat, mean, rstd = normed(x)
                st_r[rows, 0:1] = mean
                st_r[rows, 1:2] = rstd
                h1_r[rows, :] = (xhat * vec_r[0:1, :] + vec_r[1:2, :]).astype(BF)
                h2_r[rows, :] = (xhat * vec_r[2:3, :] + vec_r[3:4, :]).astype(BF)
                for copy in stores[i]:
                    copy.start()

        @pl.when(j < nq)
        def _():
            for rows in row_blocks(n):
                for part in range(3):
                    at = part * HD
                    m = jnp.dot(h1_r[rows, :], wq_r[:, at:at + HD], preferred_element_type=F32) + bq_r[:, at:at + HD]
                    if part == 2:
                        mix_r[rows, at:at + HD] = m.astype(BF)
                    else:
                        mix_r[rows, at:at + 128] = turn(m[:, :128], cos_r[rows, :], sin_r[rows, :]).astype(BF)
                        mix_r[rows, at + 128:at + HD] = m[:, 128:].astype(BF)

        @pl.when(j >= nq)
        def _():
            for rows in row_blocks(n):
                for at in range(0, UB, 256):
                    cols = slice(at, at + 256)
                    f = jnp.dot(h2_r[rows, :], wu_r[:, cols], preferred_element_type=F32) + bu_r[:, cols]
                    phi = 0.5 * (1.0 + lax.erf(f * 0.7071067811865476))
                    a_r[rows, cols] = (f * phi).astype(BF)
                    gp_r[rows, cols] = (phi + f * (jnp.exp(-0.5 * f * f) * 0.3989422804014327)).astype(BF)

        host(2, ("second", 0))
        host(4, ("second", 1), ("third", 0))
        host(5, ("third", 1), ("last", 0), ("last", 1), ("close",))

        @pl.when(j == nq + nu - 1)
        def _():
            for group in stores:
                for copy in group:
                    copy.wait()

    whole = lambda j: (0, 0)
    qcol = lambda j: (0, jnp.minimum(j, nq - 1))
    ucol = lambda j: (0, jnp.maximum(j - nq, 0))
    far = pl.BlockSpec(memory_space=pl.ANY)
    ins = [far] * len(xs) + [
        spec((6, D), whole), spec((D, QB), qcol), spec((1, QB), qcol), spec((n, 128), whole, True), spec((n, 128), whole, True),
        spec((D, UB), ucol), spec((1, UB), ucol)] + [far] * ng
    outs = [far, far, spec((n, QB), qcol), spec((n, UB), ucol), spec((n, UB), ucol), spec((n, 128), whole)] + [far] * ng
    shapes = [jax.ShapeDtypeStruct(s, BF) for s in ((n, D), (n, D), (n, C), (n, U), (n, U))] + [jax.ShapeDtypeStruct((n, 128), F32)]
    DMA = pltpu.SemaphoreType.DMA
    scratch = [pltpu.VMEM((n, D), BF)] * (2 + len(xs)) + [DMA((len(xs), nr)), DMA((2, nr))]
    if ng:
        scratch += [DMA((ng, 9)), DMA((ng, 9)), DMA((ng,))]
        shapes += [jax.ShapeDtypeStruct((8,) + v.shape[1:], v.dtype) for v in shards]
    return call(kernel, (nq + nu,), ins, outs, shapes, scratch, ident=5 if ng else None, flops=2 * n * D * (C + U), nbytes=2 * (n * D * 3 + D * (C + U) + n * (C + 2 * U)), name="project")(*xs, vec, wq, bq, cos, sin, wu, bu, *(shards or ()))


def softmax_block(q, k, segq, segk, q0, k0):
    s = lax.dot_general(q, k, (((1,), (1,)), ((), ())), preferred_element_type=F32) * HD ** (-0.5)
    qi = q0 + lax.broadcasted_iota(jnp.int32, s.shape, 0)
    ki = k0 + lax.broadcasted_iota(jnp.int32, s.shape, 1)
    allowed = (segq == segk) & (ki <= qi)
    s = jnp.where(allowed, s, masked_score)
    top = jnp.max(s, axis=1, keepdims=True)
    e = jnp.exp(s - top)
    return e / jnp.sum(e, axis=1, keepdims=True)


def windows(n, qb):
    for i in range(n // qb):
        q0 = i * qb
        yield q0, max(0, q0 - MAXLEN)


def attend_forward(mixed, seg_col, seg_row):
    n, C = mixed.shape
    H = C // (3 * HD)
    qb = 256

    def kernel(q_r, k_r, v_r, sc_r, sr_r, o_r):
        for q0, k0 in windows(n, qb):
            qs, ks = slice(q0, q0 + qb), slice(k0, q0 + qb)
            p = softmax_block(q_r[qs, :], k_r[ks, :], sc_r[qs, :], sr_r[:, ks], q0, k0)
            o_r[qs, :] = jnp.dot(p.astype(BF), v_r[ks, :], preferred_element_type=F32).astype(BF)

    part = lambda t: spec((n, HD), lambda h: (0, 3 * h + t))
    return call(kernel, (H,), [part(0), part(1), part(2), spec((n, 1), lambda h: (0, 0)), spec((1, n), lambda h: (0, 0))],
                spec((n, HD), lambda h: (0, h)), jax.ShapeDtypeStruct((n, H * HD), BF),
                flops=H * n * 640 * HD * 4, nbytes=2 * n * C, name="attend")(mixed, mixed, mixed, seg_col, seg_row)


def attend_backward(mixed, dctx, seg_col, seg_row, cos, sin):
    n, C = mixed.shape
    H = C // (3 * HD)
    qb = 256
    scale = HD ** (-0.5)

    def kernel(q_r, k_r, v_r, do_r, sc_r, sr_r, cos_r, sin_r, o_r, dk_s, dv_s):
        def back(u, rows):
            c, s = cos_r[rows, :], -sin_r[rows, :]
            return jnp.concatenate([turn(u[:, :128], c, s), u[:, 128:]], axis=1).astype(BF)

        dk_s[...] = jnp.zeros_like(dk_s)
        dv_s[...] = jnp.zeros_like(dv_s)
        for q0, k0 in reversed(list(windows(n, qb))):
            qs, ks = slice(q0, q0 + qb), slice(k0, q0 + qb)
            q, k, do = q_r[qs, :], k_r[ks, :], do_r[qs, :]
            p = softmax_block(q, k, sc_r[qs, :], sr_r[:, ks], q0, k0)
            dp = lax.dot_general(do, v_r[ks, :], (((1,), (1,)), ((), ())), preferred_element_type=F32)
            delta = jnp.sum(p * dp, axis=1, keepdims=True)
            ds = (p * (dp - delta)).astype(BF)
            dq = jnp.dot(ds, k, preferred_element_type=F32) * scale
            dk_s[ks, :] += lax.dot_general(ds, q, (((0,), (0,)), ((), ())), preferred_element_type=F32)
            dv_s[ks, :] += lax.dot_general(p.astype(BF), do, (((0,), (0,)), ((), ())), preferred_element_type=F32)
            o_r[qs, :HD] = back(dq, qs)
            o_r[qs, HD:2 * HD] = back(dk_s[qs, :] * scale, qs)
            o_r[qs, 2 * HD:] = dv_s[qs, :].astype(BF)

    part = lambda t: spec((n, HD), lambda h: (0, 3 * h + t))
    whole = lambda h: (0, 0)
    return call(kernel, (H,), [part(0), part(1), part(2), spec((n, HD), lambda h: (0, h)), spec((n, 1), whole), spec((1, n), whole),
                spec((n, 128), whole), spec((n, 128), whole)],
                spec((n, 3 * HD), lambda h: (0, h)), jax.ShapeDtypeStruct((n, C), BF),
                scratch=[pltpu.VMEM((n, HD), F32), pltpu.VMEM((n, HD), F32)],
                flops=H * n * 640 * HD * 10, nbytes=4 * n * C, name="attend_back")(mixed, mixed, mixed, dctx, seg_col, seg_row, cos, sin)


def branch_out(ctx, act, wd, wn):
    n, R = ctx.shape
    U = act.shape[1]
    dp, _, w = wd.shape

    def kernel(c_r, a_r, wd_r, wn_r, o_r):
        o_r[...] = (jnp.dot(c_r[...], wd_r[...], preferred_element_type=F32) + jnp.dot(a_r[...], wn_r[...], preferred_element_type=F32)).astype(BF)

    whole = lambda s: (0, 0)
    pick = lambda s: (s, 0, 0)
    return call(kernel, (dp,), [spec((n, R), whole, True), spec((n, U), whole, True), spec((None, R, w), pick), spec((None, U, w), pick)],
                spec((n, w), lambda s: (0, s)), jax.ShapeDtypeStruct((n, dp * w), BF),
                flops=2 * n * dp * w * (R + U), nbytes=2 * (n * (R + U) + dp * w * (R + U + n)), name="branch")(ctx, act, wd, wn)


def back_in(gr, gp, wd, wn):
    n, D = gr.shape
    dp, R, w = wd.shape
    U = wn.shape[1]
    NB = 256
    nr, nu = R // NB, U // NB

    def kernel(g_r, gp_r, wd_r, wn_r, dc_r, df_r):
        j = pl.program_id(0)

        def times(w_r):
            acc = None
            for s in range(dp):
                t = lax.dot_general(g_r[:, s * w:(s + 1) * w], w_r[s], (((1,), (1,)), ((), ())), preferred_element_type=F32)
                acc = t if acc is None else acc + t
            return acc

        @pl.when(j < nr)
        def _():
            dc_r[...] = times(wd_r).astype(BF)

        @pl.when(j >= nr)
        def _():
            df_r[...] = (times(wn_r) * gp_r[...].astype(F32)).astype(BF)

    rc = lambda j: jnp.minimum(j, nr - 1)
    uc = lambda j: jnp.maximum(j - nr, 0)
    return call(kernel, (nr + nu,), [spec((n, D), lambda j: (0, 0), True), spec((n, NB), lambda j: (0, uc(j))),
                spec((dp, NB, w), lambda j: (0, rc(j), 0)), spec((dp, NB, w), lambda j: (0, uc(j), 0))],
                [spec((n, NB), lambda j: (0, rc(j))), spec((n, NB), lambda j: (0, uc(j)))],
                [jax.ShapeDtypeStruct((n, R), BF), jax.ShapeDtypeStruct((n, U), BF)],
                flops=2 * n * D * (R + U), nbytes=2 * (n * D + D * (R + U) + n * (R + 2 * U)), name="back_in")(gr, gp, wd, wn)


def back_out(dmix, df, wq, wu, base, extra, vec, stats):
    n, C = dmix.shape
    U = df.shape[1]
    D = wq.shape[0]
    NB = 256

    def kernel(*refs):
        if extra is None:
            dm_r, df_r, wq_r, wu_r, base_r, vec_r, st_r, e_r, g_r = refs
        else:
            dm_r, df_r, wq_r, wu_r, base_r, extra_r, vec_r, st_r, e_r, g_r = refs
        nt = (((1,), (1,)), ((), ()))
        d1 = lax.dot_general(dm_r[...], wq_r[...], nt, preferred_element_type=F32)
        d2 = lax.dot_general(df_r[...], wu_r[...], nt, preferred_element_type=F32)
        e_r[...] = (d1 * vec_r[0:1, :] + d2 * vec_r[2:3, :]).astype(BF)
        x = base_r[...].astype(F32)
        if extra is not None:
            x = x + extra_r[...].astype(F32) + vec_r[4:5, :] + vec_r[5:6, :]
        xhat = (x - st_r[:, 0:1]) * st_r[:, 1:2]
        g_r[0:1, :] = jnp.sum(d1 * xhat, axis=0, keepdims=True)
        g_r[1:2, :] = jnp.sum(d1, axis=0, keepdims=True)
        g_r[2:3, :] = jnp.sum(d2 * xhat, axis=0, keepdims=True)
        g_r[3:4, :] = jnp.sum(d2, axis=0, keepdims=True)

    whole = lambda j: (0, 0)
    col = lambda j: (0, j)
    row = lambda j: (j, 0)
    xs = [spec((n, NB), col)] + ([] if extra is None else [spec((n, NB), col)])
    args = [base] + ([] if extra is None else [extra])
    return call(kernel, (D // NB,), [spec((n, C), whole, True), spec((n, U), whole, True), spec((NB, C), row), spec((NB, U), row)] + xs +
                [spec((6, NB), col), spec((n, 128), whole)],
                [spec((n, NB), col), spec((4, NB), col)],
                [jax.ShapeDtypeStruct((n, D), BF), jax.ShapeDtypeStruct((4, D), F32)],
                flops=2 * n * D * (C + U), nbytes=2 * (n * (C + U) + D * (C + U) + n * D * 3), name="back_out")(dmix, df, wq, wu, *args, vec, stats)


def weight_grad(left, right, w=None):
    n, M = left.shape
    N = right.shape[1]
    MB = 256

    def kernel(l_r, r_r, o_r, s_r):
        g = lax.dot_general(l_r[...], r_r[...], (((0,), (0,)), ((), ())), preferred_element_type=F32)
        if w is None:
            o_r[...] = g.astype(BF)
        else:
            for s in range(N // w):
                o_r[s] = g[:, s * w:(s + 1) * w].astype(BF)

        @pl.when(pl.program_id(0) == 0)
        def _():
            s_r[...] = jnp.sum(r_r[...].astype(F32), axis=0, keepdims=True)

    whole = lambda j: (0, 0)
    if w is None:
        out, shape = spec((MB, N), lambda j: (j, 0)), (M, N)
    else:
        out, shape = spec((N // w, MB, w), lambda j: (0, j, 0)), (N // w, M, w)
    return call(kernel, (M // MB,), [spec((n, MB), lambda j: (0, j)), spec((n, N), whole, True)], [out, spec((1, N), whole)],
                [jax.ShapeDtypeStruct(shape, BF), jax.ShapeDtypeStruct((1, N), F32)],
                flops=2 * n * M * N, nbytes=2 * (n * M + n * N + M * N), name="wgrad")(left, right)


def norm_back(gout, e, base, extra, vec, stats):
    n, D = base.shape
    RB = 128

    def kernel(g_r, e_r, base_r, extra_r, vec_r, st_r, dx_r, low_r, sum_r):
        x = base_r[...].astype(F32) + extra_r[...].astype(F32) + vec_r[4:5, :] + vec_r[5:6, :]
        dx = g_r[...].astype(F32) + norm_pullback(x, e_r, st_r)
        dx_r[...] = dx
        low_r[...] = dx.astype(BF)

        @pl.when(pl.program_id(0) == 0)
        def _():
            sum_r[...] = jnp.zeros_like(sum_r)

        sum_r[...] += jnp.sum(dx, axis=0, keepdims=True)

    row = lambda i: (i, 0)
    whole = lambda i: (0, 0)
    rows = spec((RB, D), row)
    shapes = [jax.ShapeDtypeStruct((n, D), F32), jax.ShapeDtypeStruct((n, D), BF), jax.ShapeDtypeStruct((1, D), F32)]
    return call(kernel, (n // RB,), [rows] * 4 + [spec((6, D), whole), spec((RB, 128), row)], [rows, rows, spec((1, D), whole)], shapes,
                flops=10 * n * D, nbytes=16 * n * D, name="norm_back")(gout, e, base, extra, vec, stats)


def norm_pullback(x, e_r, st_r):
    xhat = (x - st_r[:, 0:1]) * st_r[:, 1:2]
    ev = e_r[...].astype(F32)
    me = jnp.mean(ev, axis=1, keepdims=True)
    mx = jnp.mean(ev * xhat, axis=1, keepdims=True)
    return (ev - me - xhat * mx) * st_r[:, 1:2]


def finish(gout, e, base, extra, branches, held, live, stats):
    n, D = base.shape
    RB = 128
    each = n // len(branches) // RB

    def kernel(g_r, e_r, base_r, extra_r, *refs):
        branch_rs, (held_r, live_r, st_r, dx_r, out_r) = refs[:len(branches)], refs[len(branches):]
        i = pl.program_id(0)
        x = base_r[...].astype(F32)
        dx_r[...] = g_r[...] + norm_pullback(x, e_r, st_r)
        for k, b_r in enumerate(branch_rs):
            @pl.when(lax.div(i, each) == k)
            def _(b_r=b_r):
                last = base_r[...].astype(F32) + extra_r[...].astype(F32) + b_r[...].astype(F32) + held_r[...]
                out_r[...] = jnp.where(live_r[...] > 0.0, last, 0.0).astype(BF)

    row = lambda i: (i, 0)
    whole = lambda i: (0, 0)
    rows = spec((RB, D), row)
    part = lambda k: spec((RB, D), lambda i: (jnp.clip(i - k * each, 0, each - 1), 0))
    ins = [rows] * 4 + [part(k) for k in range(len(branches))] + [spec((1, D), whole), spec((RB, 1), row), spec((RB, 128), row)]
    return call(kernel, (n // RB,), ins, [rows, rows], [jax.ShapeDtypeStruct((n, D), F32), jax.ShapeDtypeStruct((n, D), BF)],
                flops=10 * n * D, nbytes=18 * n * D, name="finish")(gout, e, base, extra, *branches, held, live, stats)


MESH = pl.DeviceIdType.MESH


class Spot:
    def __init__(self):
        i = lax.axis_index("dp")
        c, x, y = lax.rem(i, 2), lax.rem(lax.div(i, 2), 2), lax.div(i, 4)
        self.me = i
        self.dx, self.dy, self.dc = 2 - 4 * x, 4 - 8 * y, 1 - 2 * c
        self.nx, self.ny, self.nc = i + self.dx, i + self.dy, i + self.dc
        self.diag = i + self.dx + self.dy
        z = lax.axis_index("mp")
        self.z = z
        self.outer = (z == 0) | (z == 3)
        self.inner = (z == 1) | (z == 2)
        self.pair = z + 1 - 2 * lax.rem(z, 2)
        self.across = 3 - z

    def meet(self, line):
        barrier = pltpu.get_barrier_semaphore()
        for peer in (self.nx, self.ny, self.nc):
            pl.semaphore_signal(barrier, inc=1, device_id={"dp": peer}, device_id_type=MESH)
        if line:
            pl.semaphore_signal(barrier, inc=1, device_id={"mp": self.pair}, device_id_type=MESH)

            @pl.when(self.inner)
            def _():
                pl.semaphore_signal(barrier, inc=1, device_id={"mp": self.across}, device_id_type=MESH)

            @pl.when(self.inner)
            def _():
                pl.semaphore_wait(barrier, 5)

            @pl.when(self.outer)
            def _():
                pl.semaphore_wait(barrier, 4)
        else:
            pl.semaphore_wait(barrier, 3)


def send_to(axis, peer, src, dst, send, recv):
    return pltpu.make_async_remote_copy(src_ref=src, dst_ref=dst, send_sem=send, recv_sem=recv, device_id={axis: peer}, device_id_type=MESH)


class Gather:
    copies = 9

    def __init__(self, spot, items, send, recv, local):
        self.spot, self.items, self.send, self.recv, self.local = spot, items, send, recv, local
        self.sent = []
        self.own = []

    def go(self, k, n, peer, src, dst):
        send_to("dp", peer, src, dst, self.send.at[k, n], self.recv.at[k, n]).start()
        self.sent.append((k, n, peer, src, dst))

    def arrived(self, k, n, dst):
        send_to("dp", self.spot.nc, dst, dst, self.send.at[k, n], self.recv.at[k, n]).wait_recv()

    def first(self, k):
        s, (src, out) = self.spot, self.items[k]
        for n, peer in enumerate((s.nx, s.ny, s.nc)):
            self.go(k, n, peer, src, out.at[s.me])
        pltpu.make_async_copy(src, out.at[s.me], self.local.at[k]).start()
        self.own.append(k)

    def halves(self, k):
        h = self.items[k][1].shape[1] // 2
        return pl.ds(0, h), pl.ds(h, h)

    def second(self, k):
        s, (_, out) = self.spot, self.items[k]
        low, high = self.halves(k)
        self.arrived(k, 0, out.at[s.nx])
        self.go(k, 3, s.ny, out.at[s.nx, high], out.at[s.nx, high])
        self.go(k, 4, s.nc, out.at[s.nx], out.at[s.nx])
        self.arrived(k, 1, out.at[s.ny])
        self.go(k, 5, s.nx, out.at[s.ny, low], out.at[s.ny, low])
        self.go(k, 6, s.nc, out.at[s.ny], out.at[s.ny])

    def third(self, k):
        s, (_, out) = self.spot, self.items[k]
        low, high = self.halves(k)
        self.arrived(k, 3, out.at[s.diag, high])
        self.go(k, 7, s.nc, out.at[s.diag, high], out.at[s.diag, high])
        self.arrived(k, 5, out.at[s.diag, low])
        self.go(k, 8, s.nc, out.at[s.diag, low], out.at[s.diag, low])

    def last(self, k):
        s, (_, out) = self.spot, self.items[k]
        low, high = self.halves(k)
        self.arrived(k, 2, out.at[s.nc])
        self.arrived(k, 4, out.at[s.nx + s.dc])
        self.arrived(k, 6, out.at[s.ny + s.dc])
        self.arrived(k, 7, out.at[s.diag + s.dc, high])
        self.arrived(k, 8, out.at[s.diag + s.dc, low])

    def close(self):
        for k in self.own:
            src, out = self.items[k]
            pltpu.make_async_copy(src, out.at[self.spot.me], self.local.at[k]).wait()
        for k, n, peer, src, dst in self.sent:
            send_to("dp", peer, src, dst, self.send.at[k, n], self.recv.at[k, n]).wait_send()


AHEAD, LAG, BACK = 3, 2, 7


class LineSum:
    copies = 3

    def __init__(self, spot, pairs, stage, land, swap, send, recv, local):
        self.spot, self.stage, self.land, self.swap = spot, stage, land, swap
        self.send, self.recv, self.local = send, recv, local
        self.rows = stage.shape[1]
        self.parts, self.outs = [], []
        for part, start, out, rows in pairs:
            for at in range(0, rows, self.rows):
                self.parts.append(part.at[pl.ds(start + at, self.rows)])
                self.outs.append(out.at[pl.ds(at, self.rows)])
        self.chunks = len(self.parts)

    def cut(self, k):
        return pl.ds(k * self.rows, self.rows)

    def copy(self, k, n):
        s, rows = self.spot, self.cut(k)
        if n == 0:
            peer, src, dst = s.pair, self.parts[k], self.land
        elif n == 1:
            peer, src, dst = s.across, self.land.at[rows], self.swap
        else:
            peer, src, dst = s.pair, self.swap.at[rows], self.swap
        return send_to("mp", peer, src, dst.at[rows], self.send.at[k, n], self.recv.at[k, n])

    def keep(self, k):
        rows = self.cut(k)
        return pltpu.make_async_copy(self.swap.at[rows], self.outs[k], self.local.at[k])

    def load(self, k):
        return pltpu.make_async_copy(self.parts[k], self.stage.at[k % 2], self.local.at[self.chunks + k % 2])

    def add(self, k, dst, one, two, base):
        step = 32

        @pl.loop(0, self.rows // step)
        def _(i):
            rows = pl.ds(pl.multiple_of(k * self.rows + i * step, step), step)
            there = pl.ds(pl.multiple_of(base + i * step, step), step)
            dst[rows, :] = (one[there, :].astype(F32) + two[rows, :].astype(F32)).astype(BF)

    def send_step(self, t):
        n = self.chunks

        @pl.when(self.spot.outer)
        def _():
            if 0 <= t - AHEAD < n:
                self.copy(t - AHEAD, 0).wait_send()
            if t < n:
                self.copy(t, 0).start()
            if 0 <= t - BACK < n:
                self.copy(t - BACK, 2).wait_recv()
                self.keep(t - BACK).start()

    def add_step(self, t):
        n = self.chunks

        @pl.when(self.spot.inner)
        def _():
            if t < n:
                if t == 0:
                    self.load(0).start()
                if t + 1 < n:
                    self.load(t + 1).start()
                self.load(t).wait()
                self.copy(t, 0).wait_recv()
                self.add(t, self.land, self.stage.at[t % 2], self.land, 0)
                self.copy(t, 1).start()
            if 0 <= t - LAG < n:
                self.copy(t - LAG, 1).wait_recv()
                self.copy(t - LAG, 1).wait_send()
                self.add(t - LAG, self.swap, self.land, self.swap, (t - LAG) * self.rows)
                self.copy(t - LAG, 2).start()
                self.keep(t - LAG).start()

    def begin(self):
        self.sent_to, self.added_to = 0, 0
        for _ in range(AHEAD):
            self.send_step(self.sent_to)
            self.sent_to += 1

    def slot(self):
        if self.added_to < self.chunks + LAG:
            self.add_step(self.added_to)
            self.added_to += 1
        if self.sent_to < self.chunks + BACK:
            self.send_step(self.sent_to)
            self.sent_to += 1

    def finish(self):
        while self.added_to < self.chunks + LAG or self.sent_to < self.chunks + BACK:
            self.slot()

    def close(self):
        for k in range(self.chunks):
            self.keep(k).wait()

        @pl.when(self.spot.inner)
        def _():
            for k in range(self.chunks):
                self.copy(k, 2).wait_send()


class Scatter:
    copies = 10

    def __init__(self, spot, items, own, sib, fx, fy, gx, gy, send, recv, local):
        self.spot, self.items = spot, items
        self.own, self.sib, self.fx, self.fy, self.gx, self.gy = own, sib, fx, fy, gx, gy
        self.send, self.recv, self.local = send, recv, local
        self.sent = []

    def go(self, k, n, peer, src, dst):
        send_to("dp", peer(), src(), dst(), self.send.at[k, n], self.recv.at[k, n]).start()
        self.sent.append((k, n, src))

    def arrived(self, k, n, dst):
        send_to("dp", self.spot.nc, dst, dst, self.send.at[k, n], self.recv.at[k, n]).wait_recv()

    def first(self, k):
        s, grad = self.spot, self.items[k][0]
        for m, slot in enumerate((s.me, s.nx, s.ny, s.diag)):
            self.go(k, m, lambda: s.nc, lambda slot=slot: grad.at[slot + s.dc], lambda m=m: self.sib[k].at[m])
        for m in range(4):
            self.load(k, m).start()

    def load(self, k, m):
        s = self.spot
        slot = (s.me, s.nx, s.ny, s.diag)[m]
        return pltpu.make_async_copy(self.items[k][0].at[slot], self.own[k].at[m], self.local.at[k, m])

    def over(self, r, c, body, start=0):
        step = 16
        while step * 2 * c <= 32768 and r % (step * 2) == 0:
            step *= 2

        @pl.loop(0, r // step)
        def _(i):
            body(pl.ds(pl.multiple_of(i * step, step), step), pl.ds(pl.multiple_of(start + i * step, step), step))

    def second(self, k):
        s = self.spot
        own, sib = self.own[k], self.sib[k]
        _, r, c = own.shape
        h = r // 2
        low, high = pl.ds(0, h), pl.ds(h, h)
        for m in (3, 1, 2, 0):
            self.load(k, m).wait()
            self.arrived(k, m, sib.at[m])

            def add(rows, _, m=m):
                own[m, rows, :] = (own[m, rows, :].astype(F32) + sib[m, rows, :].astype(F32)).astype(BF)

            self.over(r, c, add)
            if m == 3:
                self.go(k, 5, lambda: s.nx, lambda: own.at[3, low], lambda: self.fx[k].at[1])
                self.go(k, 7, lambda: s.ny, lambda: own.at[3, high], lambda: self.fy[k].at[1])
            if m == 1:
                self.go(k, 4, lambda: s.nx, lambda: own.at[1, low], lambda: self.fx[k].at[0])
            if m == 2:
                self.go(k, 6, lambda: s.ny, lambda: own.at[2, high], lambda: self.fy[k].at[0])

    def third(self, k):
        s = self.spot
        own, fx, fy = self.own[k], self.fx[k], self.fy[k]
        _, r, c = own.shape
        h = r // 2
        self.arrived(k, 5, fx.at[1])

        def add_low(rows, _):
            fx[1, rows, :] = (own[2, rows, :].astype(F32) + fx[1, rows, :].astype(F32)).astype(BF)

        self.over(h, c, add_low)
        self.go(k, 8, lambda: s.ny, lambda: fx.at[1], lambda: self.gy[k])
        self.arrived(k, 7, fy.at[1])

        def add_high(rows, there):
            fy[1, rows, :] = (own[1, there, :].astype(F32) + fy[1, rows, :].astype(F32)).astype(BF)

        self.over(h, c, add_high, h)
        self.go(k, 9, lambda: s.nx, lambda: fy.at[1], lambda: self.gx[k])

    def last(self, k):
        own, out = self.own[k], self.items[k][1]
        fx, fy, gx, gy = self.fx[k], self.fy[k], self.gx[k], self.gy[k]
        _, r, c = own.shape
        h = r // 2
        self.arrived(k, 4, fx.at[0])
        self.arrived(k, 8, gy)

        def low(rows, _):
            out[rows, :] = own[0, rows, :].astype(F32) + fx[0, rows, :].astype(F32) + gy[rows, :].astype(F32)

        self.over(h, c, low)
        self.arrived(k, 6, fy.at[0])
        self.arrived(k, 9, gx)

        def high(rows, there):
            out[there, :] = own[0, there, :].astype(F32) + fy[0, rows, :].astype(F32) + gx[rows, :].astype(F32)

        self.over(h, c, high, h)

    def close(self):
        for k, n, src in self.sent:
            send_to("dp", self.spot.nc, src(), src(), self.send.at[k, n], self.recv.at[k, n]).wait_send()


def link_kernel(name, ident, shards, layers, part=None, chunks=16):
    ng = len(shards)
    HBM = pl.BlockSpec(memory_space=pl.ANY)
    DMA = pltpu.SemaphoreType.DMA
    parts = [] if part is None else [part]
    shapes = [jax.ShapeDtypeStruct((8,) + (v.shape if l is None else v.shape[1:]), v.dtype) for v, l in zip(shards, layers)]
    shapes += [jax.ShapeDtypeStruct(v.shape, BF) for v in parts]
    scratch = [DMA((ng, 9)), DMA((ng, 9)), DMA((ng,))]
    for v in parts:
        scratch += [pltpu.VMEM((2, v.shape[0] // chunks, v.shape[1]), BF), pltpu.VMEM(v.shape, BF), pltpu.VMEM(v.shape, BF), DMA((chunks, 3)), DMA((chunks, 3)), DMA((chunks + 2,))]

    def kernel(*refs):
        refs = list(refs)
        take = lambda n: [refs.pop(0) for _ in range(n)]
        src, ins, full, totals = take(ng), take(len(parts)), take(ng), take(len(parts))
        spot = Spot()
        spot.meet(bool(parts))
        G = Gather(spot, [(a if l is None else a.at[l], b) for a, l, b in zip(src, layers, full)], *take(3))
        if parts:
            stage, land, swap, send, recv, local = take(6)
            line = LineSum(spot, [(ins[0], 0, totals[0], ins[0].shape[0])], stage, land, swap, send, recv, local)
            plan_sum_gather(G, line)
            line.close()
        else:
            plan_gather(G)
        G.close()

    nbytes = sum(v.size * 2 for v in parts) + sum(8 * v.size for v in shards)
    return pl.pallas_call(
        kernel, in_specs=[HBM] * (ng + len(parts)), out_specs=[HBM] * (ng + len(parts)), out_shape=shapes, scratch_shapes=scratch,
        compiler_params=pltpu.CompilerParams(vmem_limit_bytes=VM, collective_id=ident, has_side_effects=True),
        cost_estimate=pl.CostEstimate(flops=0, bytes_accessed=nbytes, transcendentals=0), name=name)(*shards, *parts)


def plan_gather(G):
    n = len(G.items)
    for stage in (G.first, G.second, G.third, G.last):
        for k in range(n):
            stage(k)


class Products:
    def __init__(self, lefts, rights, grads, rhs, lbuf, obuf, rsem, lsem, osem):
        self.lefts, self.rights, self.grads = lefts, rights, grads
        self.rhs, self.lbuf, self.obuf, self.rsem, self.lsem, self.osem = rhs, lbuf, obuf, rsem, lsem, osem

    def right(self, i, slot):
        return pltpu.make_async_copy(self.rights[i], self.rhs[slot], self.rsem.at[i])

    def left(self, k, m):
        odd = m % 2 if isinstance(m, int) else lax.rem(m, 2)
        cols = pl.ds(m * 256 if isinstance(m, int) else pl.multiple_of(m * 256, 256), 256)
        return pltpu.make_async_copy(self.lefts[k].at[:, cols], self.lbuf.at[odd], self.lsem.at[odd])

    def stores(self, k, m):
        odd = m % 2 if isinstance(m, int) else lax.rem(m, 2)
        grad, o, sem = self.grads[k], self.obuf.at[odd], self.osem.at[odd]
        slots, r, c = grad.shape
        if r == 256 and self.lefts[k].shape[1] == slots * r:
            return [pltpu.make_async_copy(o.at[:, pl.ds(0, c)], grad.at[m], sem.at[0])]
        rows = pl.ds(m * 256 if isinstance(m, int) else pl.multiple_of(m * 256, 256), 256)
        return [pltpu.make_async_copy(o.at[:, pl.ds(s * c, c)], grad.at[s, rows], sem.at[s]) for s in range(slots)]

    def run(self, k, slot, hooks):
        count = self.lefts[k].shape[1] // 256
        right = self.rhs[slot]
        width = right.shape[1]
        self.left(k, 0).start()

        @pl.loop(0, count)
        def _(m):
            self.left(k, m).wait()

            @pl.when(m + 1 < count)
            def _():
                self.left(k, m + 1).start()

            @pl.when(m >= 2)
            def _():
                for copy in self.stores(k, m - 2):
                    copy.wait()

            g = lax.dot_general(self.lbuf[lax.rem(m, 2)], right[...], (((0,), (0,)), ((), ())), preferred_element_type=F32)
            self.obuf[lax.rem(m, 2), :, :width] = g.astype(BF)
            for copy in self.stores(k, m):
                copy.start()
            for at in sorted(hooks):
                pl.when(m == at)(hooks[at])

        for m in (count - 2, count - 1):
            for copy in self.stores(k, m):
                copy.wait()

    def sums(self, slot, out):
        right = self.rhs[slot]
        out[...] = jnp.zeros_like(out)

        @pl.loop(0, right.shape[0] // 64)
        def _(i):
            out[...] += jnp.sum(right[pl.ds(pl.multiple_of(i * 64, 64), 64), :].astype(F32), axis=0, keepdims=True)


def plan_sum_gather(G, line):
    for k in range(4):
        G.first(k)
    stages = {5: [("second", 0), ("second", 1)], 9: [("second", 2)], 12: [("second", 3)], 14: [("third", 0), ("third", 1)], 15: [("third", 2)],
              17: [("third", 3)]}
    line.begin()
    for at in range(18):
        line.slot()
        for name, k in stages.get(at, ()):
            getattr(G, name)(k)
    line.finish()
    for k in range(4):
        G.last(k)


def sum_scatter(ident, e, more, first_row, more_rows, lefts, rights, step=64):
    n, D = e.shape
    HBM = pl.BlockSpec(memory_space=pl.ANY)
    VM_ = pl.BlockSpec(memory_space=pltpu.VMEM)
    C, U = rights[1].shape[1], rights[2].shape[1]
    w = D // 8
    dims = [(lefts[0].shape[1], w), (lefts[1].shape[1], w), (w, C), (w, U)]
    DMA = pltpu.SemaphoreType.DMA
    chunks = (n + more_rows) // step
    outs = [HBM] * 2 + [HBM] * 4 + [VM_] * 4 + [VM_] * 3
    shapes = [jax.ShapeDtypeStruct(e.shape, BF), jax.ShapeDtypeStruct((more_rows, D), BF)] + [jax.ShapeDtypeStruct((8,) + d, BF) for d in dims] + [jax.ShapeDtypeStruct(d, F32) for d in dims]
    shapes += [jax.ShapeDtypeStruct((1, C), F32), jax.ShapeDtypeStruct((1, U), F32), jax.ShapeDtypeStruct((1, D), F32)]
    scratch = [pltpu.VMEM((2, step, D), BF)] + [pltpu.VMEM((n + more_rows, D), BF)] * 2 + [DMA((chunks, 3)), DMA((chunks, 3)), DMA((chunks + 2,))]
    scratch += [DMA((4, 10)), DMA((4, 10)), DMA((4, 4))]
    for r, c in dims:
        scratch += [pltpu.VMEM((4, r, c), BF), pltpu.VMEM((4, r, c), BF), pltpu.VMEM((2, r // 2, c), BF), pltpu.VMEM((2, r // 2, c), BF),
                    pltpu.VMEM((r // 2, c), BF), pltpu.VMEM((r // 2, c), BF)]
    wide = max(D, U)
    scratch += [pltpu.VMEM((n, wide), BF), pltpu.VMEM((n, C), BF), pltpu.VMEM((2, n, 256), BF), pltpu.VMEM((2, 256, wide), BF), DMA((3,)), DMA((2,)), DMA((2, 8))]
    assert D == U

    def kernel(*refs):
        refs = list(refs)
        take = lambda k: [refs.pop(0) for _ in range(k)]
        (e_r, more_r), left_rs, right_rs = take(2), take(4), take(3)
        (total, more_total), grads, owned, sum_rs = take(2), take(4), take(4), take(3)
        stage, land, swap, send, recv, local = take(6)
        spot = Spot()
        spot.meet(True)
        line = LineSum(spot, [(e_r, 0, total, n), (more_r, first_row, more_total, more_rows)], stage, land, swap, send, recv, local)
        send, recv, local = take(3)
        bufs = [take(6) for _ in range(4)]
        S = Scatter(spot, list(zip(grads, owned)), *[[b[i] for b in bufs] for i in range(6)], send, recv, local)
        wide_r, narrow_r, lbuf, obuf, rsem, lsem, osem = take(7)
        W = Products(left_rs, right_rs, grads, (wide_r, narrow_r), lbuf, obuf, rsem, lsem, osem)
        W.right(0, 0).start()
        W.right(1, 1).start()
        def steps(*what):
            def go():
                for step, *args in what:
                    step(*args)

            return go

        slot = (line.slot,)
        line.begin()
        W.right(0, 0).wait()
        W.run(0, 0, {})
        S.first(0)
        W.run(1, 0, {1: steps(slot), 3: steps(slot), 5: steps(slot, (S.second, 0)), 7: steps(slot)})
        S.first(1)
        W.sums(0, sum_rs[2])
        W.right(2, 0).start()
        W.right(1, 1).wait()
        W.run(2, 1, {2: steps(slot), 5: steps(slot, (S.second, 1))})
        S.first(2)
        line.slot()
        W.right(2, 0).wait()
        W.run(3, 0, {1: steps(slot), 2: steps((S.third, 0)), 4: steps(slot, (S.second, 2)), 7: steps(slot)})
        S.first(3)
        line.slot()
        W.sums(1, sum_rs[0])
        S.third(1)
        line.slot()
        S.second(3)
        line.slot()
        W.sums(0, sum_rs[1])
        S.last(0)
        line.slot()
        line.slot()
        S.third(2)
        line.slot()
        S.last(1)
        line.slot()
        line.slot()
        S.third(3)
        line.slot()
        S.last(2)
        line.finish()
        S.last(3)
        line.close()
        S.close()

    flops = 2 * n * D * (lefts[0].shape[1] + lefts[1].shape[1] + C + U)
    got = pl.pallas_call(
        kernel, in_specs=[HBM] * 9, out_specs=outs, out_shape=shapes, scratch_shapes=scratch,
        compiler_params=pltpu.CompilerParams(vmem_limit_bytes=VM2, collective_id=ident, has_side_effects=True),
        cost_estimate=pl.CostEstimate(flops=flops, bytes_accessed=2 * n * D * 12, transcendentals=0), name="sum_scatter")(e, more, *lefts, *rights)
    gd, gn, gq, gu = got[6:10]
    return got[0], got[1], (gq, gd, gu, gn), got[10], got[11], got[12]


def small_sum(pieces, shared):
    ndp, r, _ = pieces.shape
    nmp = lax.axis_size("mp")

    def kernel(x_r, o_r, land, line, send, recv, send2, recv2):
        i, z = lax.axis_index("dp"), lax.axis_index("mp")
        barrier = pltpu.get_barrier_semaphore()
        for s in range(1, ndp):
            pl.semaphore_signal(barrier, inc=1, device_id={"dp": lax.rem(i + s, ndp)}, device_id_type=MESH)
        for s in range(1, nmp):
            pl.semaphore_signal(barrier, inc=1, device_id={"mp": lax.rem(z + s, nmp)}, device_id_type=MESH)
        pl.semaphore_wait(barrier, ndp + nmp - 2)
        first = [send_to("dp", lax.rem(i + s, ndp), x_r.at[lax.rem(i + s, ndp)], land.at[i], send.at[s], recv.at[s]) for s in range(1, ndp)]
        for copy in first:
            copy.start()
        land[pl.ds(i, 1)] = x_r[pl.ds(i, 1)]
        for s in range(1, ndp):
            there = land.at[lax.rem(i - s + ndp, ndp)]
            send_to("dp", i, there, there, send.at[s], recv.at[s]).wait_recv()
        acc = land[0]
        for j in range(1, ndp):
            acc = acc + land[j]
        o_r[...] = acc
        line[pl.ds(z, 1)] = acc[None, :shared]
        second = [send_to("mp", lax.rem(z + s, nmp), line.at[z], line.at[z], send2.at[s], recv2.at[s]) for s in range(1, nmp)]
        for copy in second:
            copy.start()
        for s in range(1, nmp):
            there = line.at[lax.rem(z - s + nmp, nmp)]
            send_to("mp", z, there, there, send2.at[s], recv2.at[s]).wait_recv()
        acc = line[0]
        for j in range(1, nmp):
            acc = acc + line[j]
        o_r[:shared] = acc
        for copy in first + second:
            copy.wait_send()

    VM_ = pl.BlockSpec(memory_space=pltpu.VMEM)
    DMA = pltpu.SemaphoreType.DMA
    return pl.pallas_call(
        kernel, in_specs=[VM_], out_specs=VM_, out_shape=jax.ShapeDtypeStruct((r, 128), F32),
        scratch_shapes=[pltpu.VMEM(pieces.shape, F32), pltpu.VMEM((nmp, shared, 128), F32), DMA((ndp,)), DMA((ndp,)), DMA((nmp,)), DMA((nmp,))],
        compiler_params=pltpu.CompilerParams(vmem_limit_bytes=VM // 4, collective_id=6, has_side_effects=True), name="small_sum")(pieces)


def adam_update(weight, grad, first, second):
    first_new = beta_one * first + (1.0 - beta_one) * grad
    second_new = beta_two * second + (1.0 - beta_two) * grad * grad
    mean_hat = first_new / (1.0 - beta_one**ADAM_STEP)
    square_hat = second_new / (1.0 - beta_two**ADAM_STEP)
    new_weight = weight - rate * (mean_hat / (jnp.sqrt(square_hat) + adam_eps) + decay * weight)
    return grad, first_new, second_new, new_weight - weight


def adam_layer(layer, weights, grads, firsts, seconds, before):
    steps = 8
    blocks = [(w.shape[1] // steps, w.shape[2]) for w in weights]

    def kernel(*refs):
        ins, outs = refs[:16], refs[-16:]
        for i in range(4):
            g = ins[4 + i][...].astype(F32)
            made = adam_update(ins[i][...].astype(F32), g, ins[8 + i][...], ins[12 + i][...])
            for k in range(4):
                outs[4 * i + k][...] = made[k]

    at = lambda b: spec((None,) + b, lambda j: (layer, j, 0))
    ins = [at(b) for b in blocks] + [spec(b, lambda j: (j, 0)) for b in blocks] + [at(b) for b in blocks] * 2
    args = [*weights, *grads, *firsts, *seconds]
    alias = {}
    if before is not None:
        ins += [pl.BlockSpec(memory_space=pl.ANY)] * 16
        args += list(before)
        alias = {16 + i: i for i in range(16)}
    shapes = [jax.ShapeDtypeStruct(w.shape, F32) for w in weights for _ in range(4)]
    count = sum(w.shape[1] * w.shape[2] for w in weights)
    return pl.pallas_call(
        kernel, grid=(steps,), in_specs=ins, out_specs=[at(b) for b in blocks for _ in range(4)], out_shape=shapes,
        input_output_aliases=alias, compiler_params=pltpu.CompilerParams(vmem_limit_bytes=VM),
        cost_estimate=pl.CostEstimate(flops=20 * count, bytes_accessed=30 * count, transcendentals=0), name="adam")(*args)


def layout(lengths_row, rows):
    slots = lengths_row.shape[0]
    number = jnp.arange(slots, dtype=jnp.int32)
    ends = jnp.sum(jnp.where(number[None, :] <= number[:, None], lengths_row[None, :], 0), axis=1)
    starts = ends - lengths_row
    index = jnp.arange(rows, dtype=jnp.int32)
    inside = (index[:, None] >= starts[None, :]) & (index[:, None] < ends[None, :])
    valid = jnp.any(inside, axis=1)
    slot = jnp.sum(jnp.where(inside, number[None, :], 0), axis=1)
    first = jnp.sum(jnp.where(inside, starts[None, :], 0), axis=1)
    segment = jnp.where(valid, slot, slots + index)
    return segment, index - first, valid


class PlainLinks:
    def weights(self, shards, layer):
        wq, wd, wu, wn = [w[layer] for w in shards]
        rows = lambda v: lax.all_gather(v, "dp", axis=0, tiled=True)
        stack = lambda v: lax.all_gather(v, "dp", axis=0, tiled=False)
        return rows(wq), stack(wd), rows(wu), stack(wn)

    def share(self, v):
        return lax.psum(v, "mp")

    def owned(self, grads):
        cut = lambda g: lax.psum_scatter(g, "dp", scatter_dimension=0, tiled=True)
        gq, gd, gu, gn = grads
        return cut(gq), cut(gd)[0], cut(gu), cut(gn)[0]

    def small(self, pieces, shared):
        total = lax.psum(pieces, "dp")[lax.axis_index("dp")]
        return jnp.concatenate([lax.psum(total[:shared], "mp"), total[shared:]])

    def begin(self, shards, flat):
        return self.weights(shards, 0), lax.all_gather(flat, "dp", axis=0, tiled=False), None

    def middle(self, branch, shards):
        return self.share(branch), self.weights(shards, 1)

    def turn(self, e, more, first_row, more_rows, lefts, rights, ident):
        ctx, act, h1, h2 = lefts
        gr, dmix, df = rights
        w = gr.shape[1] // lax.axis_size("dp")
        gd, low_sums = weight_grad(ctx, gr, w=w)
        gn, _ = weight_grad(act, gr, w=w)
        gq, qsum = weight_grad(h1, dmix)
        gu, usum = weight_grad(h2, df)
        more = self.share(more[first_row:first_row + more_rows])
        return self.share(e), more, self.owned((gq, gd, gu, gn)), qsum, usum, low_sums


class ChipLinks:
    def full(self, got):
        wq, wd, wu, wn = got
        return wq.reshape(-1, wq.shape[2]), wd, wu.reshape(-1, wu.shape[2]), wn

    def begin(self, shards, flat):
        wq, wd, wu, wn = shards
        flat, wq, wu = link_kernel("gather", 1, [flat, wq, wu], [None, 0, 0])
        return (wq.reshape(-1, wq.shape[2]), None, wu.reshape(-1, wu.shape[2]), None), flat, (wd, wn)

    def middle(self, branch, shards):
        got = link_kernel("sum_gather", 2, shards, [1] * 4, branch)
        return got[4], self.full(got[:4])

    def turn(self, e, more, first_row, more_rows, lefts, rights, ident):
        return sum_scatter(ident, e, more, first_row, more_rows, lefts, rights)

    def small(self, pieces, shared):
        return small_sum(pieces, shared)


def flatten_small(parts):
    flat = jnp.concatenate([p.reshape(-1) for p in parts])
    return jnp.pad(flat, (0, -flat.size % 4096)).reshape(-1, 128)


def unpack_small(got, parts):
    got = got.reshape(got.shape[0], -1)
    out, at = [], 0
    for p in parts:
        piece = got[:, at:at + p.size].reshape((-1,) + p.shape)
        out.append(jnp.moveaxis(piece, 0, 2).reshape(p.shape[0], p.shape[1], -1))
        at += p.size
    return out


def body(links, tokens_in, cotangent, seq_lengths, *params):
    weights, small = params[:4], params[4:7]
    firsts, small_firsts = params[7:11], params[11:14]
    seconds, small_seconds = params[14:18], params[18:21]
    rows, D = tokens_in.shape
    segment, position, valid = layout(seq_lengths[0], rows)
    cos, sin = rope_tables(position)
    seg_col, seg_row = segment[:, None], segment[None, :]
    live = valid[:, None]
    first_full, got, later = links.begin(weights, flatten_small(small))
    qb, ub, vecs = unpack_small(got, small)
    qb = qb.reshape(LAYERS, 1, -1).astype(F32)
    ub = ub.reshape(LAYERS, 1, -1).astype(F32)
    vecs = vecs.astype(F32)

    held = [jnp.concatenate([vecs[layer, :4], vecs[layer - 1, 4:]]) for layer in range(LAYERS)]

    full, kept, extra = [first_full], [], None
    for layer in range(LAYERS):
        wq, wd, wu, wn = full[layer]
        h1, h2, mixed, act, gp, stats, *more = project(tokens_in, extra, held[layer], wq, qb[layer], cos, sin, wu, ub[layer], later if layer == 0 else None)
        if more:
            wd, wn = more
            full[0] = wq, wd, wu, wn
        ctx = attend_forward(mixed, seg_col, seg_row)
        branch = branch_out(ctx, act, wd, wn)
        kept.append((h1, h2, mixed, act, gp, stats, ctx, extra))
        if layer == 0:
            extra, made = links.middle(branch, weights)
            full.append(made)
        else:
            gout = gr = jnp.where(live, cotangent, 0).astype(BF)
            sums = None
            branch, gr = lax.optimization_barrier((branch, gr))
            branch_sum = [None] * 4
            quarter = rows // 4
            branch_sum[0] = lax.psum(branch[:quarter], "mp")
    big, little = [None] * LAYERS, [None] * LAYERS
    for layer in reversed(range(LAYERS)):
        wq, wd, wu, wn = full[layer]
        h1, h2, mixed, act, gp, stats, ctx, extra = kept[layer]
        dctx, df = back_in(gr, gp, wd, wn)
        dmix = attend_backward(mixed, dctx, seg_col, seg_row, cos, sin)
        e, norm_sums = back_out(dmix, df, wq, wu, tokens_in, extra, held[layer], stats)
        if layer == 0:
            branch_sum[2], e = lax.optimization_barrier((branch_sum[2], e))
        at = 1 if layer else 3
        e, branch_sum[at], big[layer], qsum, usum, low_sums = links.turn(e, branch, at * quarter, quarter, (ctx, act, h1, h2), (gr, dmix, df), 3 + layer)
        little[layer] = (qsum, usum, norm_sums, low_sums if sums is None else sums)
        if layer:
            branch_sum[0], e, third = lax.optimization_barrier((branch_sum[0], e, branch[2 * quarter:3 * quarter]))
            branch_sum[2] = lax.psum(third, "mp")
        if layer:
            gout, gr, sums = norm_back(gout, e, tokens_in, extra, held[layer], stats)
    every = (vecs[0, 4:5] + vecs[0, 5:6]) + (vecs[1, 4:5] + vecs[1, 5:6])
    input_grad, output = finish(gout, e, tokens_in, kept[1][-1], branch_sum, every, live.astype(F32), stats)

    done = None
    for layer in reversed(range(LAYERS)):
        done = adam_layer(layer, weights, big[layer], firsts, seconds, done)

    ndp = lax.axis_size("dp")

    def pieces(v, width):
        v = v.reshape(-1, ndp, width // ndp)
        return jnp.moveaxis(v, 1, 0).reshape(ndp, -1)

    norms = jnp.concatenate([pieces(t[2], D) for t in little], axis=1)
    rest = [pieces(t[i], BROW) for i in (0, 1) for t in little] + [pieces(t[3], D) for t in little]
    rest = jnp.concatenate(rest, axis=1)
    shared, count = norms.shape[1] // 128, rest.shape[1]
    rest = jnp.pad(rest, ((0, 0), (0, -count % 1024)))
    total = links.small(jnp.concatenate([norms, rest], axis=1).reshape(ndp, -1, 128), shared)
    norms, rest = total[:shared].reshape(LAYERS, 4, -1), total[shared:].reshape(-1)
    small_grads, at = [], 0
    for p in small[:2]:
        small_grads.append(rest[at:at + p.size].reshape(p.shape))
        at += p.size
    tops_sum = rest[at:count].reshape(LAYERS, 1, -1)
    small_grads.append(jnp.concatenate([norms, tops_sum, tops_sum], axis=1))
    small_out = []
    for p, g, first, second in zip(small, small_grads, small_firsts, small_seconds):
        small_out += adam_update(p.astype(F32), g, first, second)
    return (output, input_grad, *done, *small_out)


def solution(mesh):
    rows_dp = P("dp", None)
    wide, tall, vec = P(None, "dp", "mp"), P(None, "mp", "dp"), P(None, None, "dp")
    group = (wide, tall, wide, tall, tall, tall, vec)
    return jax.shard_map(
        functools.partial(body, ChipLinks() if dict(mesh.shape) == {"dp": 8, "mp": 4} else PlainLinks()),
        mesh=mesh,
        in_specs=(rows_dp,) * 3 + group * 3,
        out_specs=(rows_dp,) * 2 + tuple(s for s in group for _ in range(4)),
        check_vma=False,
    )
```

```python
import functools
import jax
import jax.numpy as jnp
from jax import lax
from jax.experimental import pallas as pl
from jax.experimental.pallas import tpu as pltpu
from jax.sharding import PartitionSpec as P

HD = 256
ROT = 64
MAXLEN = 512
norm_eps = 1e-05
masked_score = -1e30
LAYERS = 2
BROW = 128
ADAM_STEP = 10
beta_one = 0.9
beta_two = 0.95
adam_eps = 1e-08
rate = 0.02
decay = 0.01
VM = 60 * 1024 * 1024
VM2 = 62 * 1024 * 1024
BF = jnp.bfloat16
ROWS = 256
UPB = 512
F32 = jnp.float32


def call(kernel, grid, in_specs, out_specs, out_shape, scratch=(), flops=0, nbytes=0, name=None, ident=None):
    return pl.pallas_call(
        kernel,
        grid_spec=pltpu.PrefetchScalarGridSpec(num_scalar_prefetch=0, grid=grid, in_specs=in_specs, out_specs=out_specs, scratch_shapes=list(scratch)),
        out_shape=out_shape,
        compiler_params=pltpu.CompilerParams(vmem_limit_bytes=VM, collective_id=ident, has_side_effects=ident is not None),
        cost_estimate=pl.CostEstimate(flops=flops, bytes_accessed=nbytes, transcendentals=0),
        name=name,
    )


def spec(shape, index, single=False):
    if single:
        return pl.BlockSpec(shape, index, pipeline_mode=pl.Buffered(1))
    return pl.BlockSpec(shape, index)


def rope_tables(position):
    half = ROT // 2
    freq = 10000.0 ** (-(jnp.arange(half, dtype=F32) * 2.0) / ROT)
    angle = position.astype(F32)[:, None] * freq[None, :]
    c, s = jnp.cos(angle), jnp.sin(angle)
    rows = position.shape[0]
    one = jnp.ones((rows, 128 - ROT), F32)
    zero = jnp.zeros((rows, 128 - ROT), F32)
    return jnp.concatenate([c, c, one], axis=1), jnp.concatenate([-s, s, zero], axis=1)


def turn(u, c, s):
    lane = lax.broadcasted_iota(jnp.int32, u.shape, 1)
    other = jnp.where(lane < ROT // 2, pltpu.roll(u, 128 - ROT // 2, 1), pltpu.roll(u, ROT // 2, 1))
    return u * c + other * s


def normed(x):
    mean = jnp.mean(x, axis=1, keepdims=True)
    centred = x - mean
    var = jnp.mean(centred * centred, axis=1, keepdims=True)
    rstd = lax.rsqrt(var + norm_eps)
    return centred * rstd, mean, rstd


def row_blocks(n):
    step = min(n, ROWS)
    return [slice(i, i + step) for i in range(0, n, step)]


def project(base, extra, vec, wq, bq, cos, sin, wu, bu, shards=None):
    n, D = base.shape
    C, U = wq.shape[1], wu.shape[1]
    QB, UB = 3 * HD, min(UPB, U)
    nq, nu = C // QB, U // UB
    RB = 128
    nr = n // RB
    ng = 0 if shards is None else len(shards)
    xs = [base] if extra is None else [base, extra]

    def kernel(*refs):
        refs = list(refs)
        take = lambda k: [refs.pop(0) for _ in range(k)]
        x_rs = take(len(xs))
        vec_r, wq_r, bq_r, cos_r, sin_r, wu_r, bu_r = take(7)
        shard_rs = take(ng)
        h1_o, h2_o, mix_r, a_r, gp_r, st_r = take(6)
        full_rs = take(ng)
        h1_r, h2_r = take(2)
        bufs = take(len(xs))
        in_sem, out_sem = take(2)
        j = pl.program_id(0)
        side = None
        if ng:
            spot = Spot()
            side = Gather(spot, [(a.at[0], b) for a, b in zip(shard_rs, full_rs)], *take(3))

            @pl.when(j == 0)
            def _():
                spot.meet(False)
                side.first(0)
                side.first(1)

        def host(step, *stages):
            if side is not None:
                @pl.when(j == min(step, nq + nu - 1))
                def _():
                    for name, *args in stages:
                        getattr(side, name)(*args)
        block = lambda i: pl.ds(i * RB, RB)
        loads = [[pltpu.make_async_copy(x.at[block(i)], buf.at[block(i)], in_sem.at[k, i]) for k, (x, buf) in enumerate(zip(x_rs, bufs))] for i in range(nr)]
        stores = [[pltpu.make_async_copy(h.at[block(i)], o.at[block(i)], out_sem.at[k, i]) for k, (h, o) in enumerate(((h1_r, h1_o), (h2_r, h2_o)))] for i in range(nr)]

        @pl.when(j == 0)
        def _():
            for group in loads:
                for copy in group:
                    copy.start()
            for i in range(nr):
                for copy in loads[i]:
                    copy.wait()
                rows = block(i)
                x = bufs[0][rows, :].astype(F32)
                if extra is not None:
                    x = x + bufs[1][rows, :].astype(F32) + vec_r[4:5, :] + vec_r[5:6, :]
                xhat, mean, rstd = normed(x)
                st_r[rows, 0:1] = mean
                st_r[rows, 1:2] = rstd
                h1_r[rows, :] = (xhat * vec_r[0:1, :] + vec_r[1:2, :]).astype(BF)
                h2_r[rows, :] = (xhat * vec_r[2:3, :] + vec_r[3:4, :]).astype(BF)
                for copy in stores[i]:
                    copy.start()

        @pl.when(j < nq)
        def _():
            for rows in row_blocks(n):
                for part in range(3):
                    at = part * HD
                    m = jnp.dot(h1_r[rows, :], wq_r[:, at:at + HD], preferred_element_type=F32) + bq_r[:, at:at + HD]
                    if part == 2:
                        mix_r[rows, at:at + HD] = m.astype(BF)
                    else:
                        mix_r[rows, at:at + 128] = turn(m[:, :128], cos_r[rows, :], sin_r[rows, :]).astype(BF)
                        mix_r[rows, at + 128:at + HD] = m[:, 128:].astype(BF)

        @pl.when(j >= nq)
        def _():
            for rows in row_blocks(n):
                for at in range(0, UB, 256):
                    cols = slice(at, at + 256)
                    f = jnp.dot(h2_r[rows, :], wu_r[:, cols], preferred_element_type=F32) + bu_r[:, cols]
                    phi = 0.5 * (1.0 + lax.erf(f * 0.7071067811865476))
                    a_r[rows, cols] = (f * phi).astype(BF)
                    gp_r[rows, cols] = (phi + f * (jnp.exp(-0.5 * f * f) * 0.3989422804014327)).astype(BF)

        host(2, ("second", 0))
        host(4, ("second", 1), ("third", 0))
        host(5, ("third", 1), ("last", 0), ("last", 1), ("close",))

        @pl.when(j == nq + nu - 1)
        def _():
            for group in stores:
                for copy in group:
                    copy.wait()

    whole = lambda j: (0, 0)
    qcol = lambda j: (0, jnp.minimum(j, nq - 1))
    ucol = lambda j: (0, jnp.maximum(j - nq, 0))
    far = pl.BlockSpec(memory_space=pl.ANY)
    ins = [far] * len(xs) + [
        spec((6, D), whole), spec((D, QB), qcol), spec((1, QB), qcol), spec((n, 128), whole, True), spec((n, 128), whole, True),
        spec((D, UB), ucol), spec((1, UB), ucol)] + [far] * ng
    outs = [far, far, spec((n, QB), qcol), spec((n, UB), ucol), spec((n, UB), ucol), spec((n, 128), whole)] + [far] * ng
    shapes = [jax.ShapeDtypeStruct(s, BF) for s in ((n, D), (n, D), (n, C), (n, U), (n, U))] + [jax.ShapeDtypeStruct((n, 128), F32)]
    DMA = pltpu.SemaphoreType.DMA
    scratch = [pltpu.VMEM((n, D), BF)] * (2 + len(xs)) + [DMA((len(xs), nr)), DMA((2, nr))]
    if ng:
        scratch += [DMA((ng, 9)), DMA((ng, 9)), DMA((ng,))]
        shapes += [jax.ShapeDtypeStruct((8,) + v.shape[1:], v.dtype) for v in shards]
    return call(kernel, (nq + nu,), ins, outs, shapes, scratch, ident=5 if ng else None, flops=2 * n * D * (C + U), nbytes=2 * (n * D * 3 + D * (C + U) + n * (C + 2 * U)), name="project")(*xs, vec, wq, bq, cos, sin, wu, bu, *(shards or ()))


def softmax_block(q, k, segq, segk, q0, k0):
    s = lax.dot_general(q, k, (((1,), (1,)), ((), ())), preferred_element_type=F32) * HD ** (-0.5)
    qi = q0 + lax.broadcasted_iota(jnp.int32, s.shape, 0)
    ki = k0 + lax.broadcasted_iota(jnp.int32, s.shape, 1)
    allowed = (segq == segk) & (ki <= qi)
    s = jnp.where(allowed, s, masked_score)
    top = jnp.max(s, axis=1, keepdims=True)
    e = jnp.exp(s - top)
    return e / jnp.sum(e, axis=1, keepdims=True)


def windows(n, qb):
    for i in range(n // qb):
        q0 = i * qb
        yield q0, max(0, q0 - MAXLEN)


def attend_forward(mixed, seg_col, seg_row):
    n, C = mixed.shape
    H = C // (3 * HD)
    qb = 256

    def kernel(q_r, k_r, v_r, sc_r, sr_r, o_r):
        for q0, k0 in windows(n, qb):
            qs, ks = slice(q0, q0 + qb), slice(k0, q0 + qb)
            p = softmax_block(q_r[qs, :], k_r[ks, :], sc_r[qs, :], sr_r[:, ks], q0, k0)
            o_r[qs, :] = jnp.dot(p.astype(BF), v_r[ks, :], preferred_element_type=F32).astype(BF)

    part = lambda t: spec((n, HD), lambda h: (0, 3 * h + t))
    return call(kernel, (H,), [part(0), part(1), part(2), spec((n, 1), lambda h: (0, 0)), spec((1, n), lambda h: (0, 0))],
                spec((n, HD), lambda h: (0, h)), jax.ShapeDtypeStruct((n, H * HD), BF),
                flops=H * n * 640 * HD * 4, nbytes=2 * n * C, name="attend")(mixed, mixed, mixed, seg_col, seg_row)


def attend_backward(mixed, dctx, seg_col, seg_row, cos, sin):
    n, C = mixed.shape
    H = C // (3 * HD)
    qb = 256
    scale = HD ** (-0.5)

    def kernel(q_r, k_r, v_r, do_r, sc_r, sr_r, cos_r, sin_r, o_r, dk_s, dv_s):
        def back(u, rows):
            c, s = cos_r[rows, :], -sin_r[rows, :]
            return jnp.concatenate([turn(u[:, :128], c, s), u[:, 128:]], axis=1).astype(BF)

        dk_s[...] = jnp.zeros_like(dk_s)
        dv_s[...] = jnp.zeros_like(dv_s)
        for q0, k0 in reversed(list(windows(n, qb))):
            qs, ks = slice(q0, q0 + qb), slice(k0, q0 + qb)
            q, k, do = q_r[qs, :], k_r[ks, :], do_r[qs, :]
            p = softmax_block(q, k, sc_r[qs, :], sr_r[:, ks], q0, k0)
            dp = lax.dot_general(do, v_r[ks, :], (((1,), (1,)), ((), ())), preferred_element_type=F32)
            delta = jnp.sum(p * dp, axis=1, keepdims=True)
            ds = (p * (dp - delta)).astype(BF)
            dq = jnp.dot(ds, k, preferred_element_type=F32) * scale
            dk_s[ks, :] += lax.dot_general(ds, q, (((0,), (0,)), ((), ())), preferred_element_type=F32)
            dv_s[ks, :] += lax.dot_general(p.astype(BF), do, (((0,), (0,)), ((), ())), preferred_element_type=F32)
            o_r[qs, :HD] = back(dq, qs)
            o_r[qs, HD:2 * HD] = back(dk_s[qs, :] * scale, qs)
            o_r[qs, 2 * HD:] = dv_s[qs, :].astype(BF)

    part = lambda t: spec((n, HD), lambda h: (0, 3 * h + t))
    whole = lambda h: (0, 0)
    return call(kernel, (H,), [part(0), part(1), part(2), spec((n, HD), lambda h: (0, h)), spec((n, 1), whole), spec((1, n), whole),
                spec((n, 128), whole), spec((n, 128), whole)],
                spec((n, 3 * HD), lambda h: (0, h)), jax.ShapeDtypeStruct((n, C), BF),
                scratch=[pltpu.VMEM((n, HD), F32), pltpu.VMEM((n, HD), F32)],
                flops=H * n * 640 * HD * 10, nbytes=4 * n * C, name="attend_back")(mixed, mixed, mixed, dctx, seg_col, seg_row, cos, sin)


def branch_out(ctx, act, wd, wn):
    n, R = ctx.shape
    U = act.shape[1]
    dp, _, w = wd.shape

    def kernel(c_r, a_r, wd_r, wn_r, o_r):
        o_r[...] = (jnp.dot(c_r[...], wd_r[...], preferred_element_type=F32) + jnp.dot(a_r[...], wn_r[...], preferred_element_type=F32)).astype(BF)

    whole = lambda s: (0, 0)
    pick = lambda s: (s, 0, 0)
    return call(kernel, (dp,), [spec((n, R), whole, True), spec((n, U), whole, True), spec((None, R, w), pick), spec((None, U, w), pick)],
                spec((n, w), lambda s: (0, s)), jax.ShapeDtypeStruct((n, dp * w), BF),
                flops=2 * n * dp * w * (R + U), nbytes=2 * (n * (R + U) + dp * w * (R + U + n)), name="branch")(ctx, act, wd, wn)


def back_in(gr, gp, wd, wn):
    n, D = gr.shape
    dp, R, w = wd.shape
    U = wn.shape[1]
    NB = 256
    nr, nu = R // NB, U // NB

    def kernel(g_r, gp_r, wd_r, wn_r, dc_r, df_r):
        j = pl.program_id(0)

        def times(w_r):
            acc = None
            for s in range(dp):
                t = lax.dot_general(g_r[:, s * w:(s + 1) * w], w_r[s], (((1,), (1,)), ((), ())), preferred_element_type=F32)
                acc = t if acc is None else acc + t
            return acc

        @pl.when(j < nr)
        def _():
            dc_r[...] = times(wd_r).astype(BF)

        @pl.when(j >= nr)
        def _():
            df_r[...] = (times(wn_r) * gp_r[...].astype(F32)).astype(BF)

    rc = lambda j: jnp.minimum(j, nr - 1)
    uc = lambda j: jnp.maximum(j - nr, 0)
    return call(kernel, (nr + nu,), [spec((n, D), lambda j: (0, 0), True), spec((n, NB), lambda j: (0, uc(j))),
                spec((dp, NB, w), lambda j: (0, rc(j), 0)), spec((dp, NB, w), lambda j: (0, uc(j), 0))],
                [spec((n, NB), lambda j: (0, rc(j))), spec((n, NB), lambda j: (0, uc(j)))],
                [jax.ShapeDtypeStruct((n, R), BF), jax.ShapeDtypeStruct((n, U), BF)],
                flops=2 * n * D * (R + U), nbytes=2 * (n * D + D * (R + U) + n * (R + 2 * U)), name="back_in")(gr, gp, wd, wn)


def back_out(dmix, df, wq, wu, base, extra, vec, stats):
    n, C = dmix.shape
    U = df.shape[1]
    D = wq.shape[0]
    NB = 256

    def kernel(*refs):
        if extra is None:
            dm_r, df_r, wq_r, wu_r, base_r, vec_r, st_r, e_r, g_r = refs
        else:
            dm_r, df_r, wq_r, wu_r, base_r, extra_r, vec_r, st_r, e_r, g_r = refs
        nt = (((1,), (1,)), ((), ()))
        d1 = lax.dot_general(dm_r[...], wq_r[...], nt, preferred_element_type=F32)
        d2 = lax.dot_general(df_r[...], wu_r[...], nt, preferred_element_type=F32)
        e_r[...] = (d1 * vec_r[0:1, :] + d2 * vec_r[2:3, :]).astype(BF)
        x = base_r[...].astype(F32)
        if extra is not None:
            x = x + extra_r[...].astype(F32) + vec_r[4:5, :] + vec_r[5:6, :]
        xhat = (x - st_r[:, 0:1]) * st_r[:, 1:2]
        g_r[0:1, :] = jnp.sum(d1 * xhat, axis=0, keepdims=True)
        g_r[1:2, :] = jnp.sum(d1, axis=0, keepdims=True)
        g_r[2:3, :] = jnp.sum(d2 * xhat, axis=0, keepdims=True)
        g_r[3:4, :] = jnp.sum(d2, axis=0, keepdims=True)

    whole = lambda j: (0, 0)
    col = lambda j: (0, j)
    row = lambda j: (j, 0)
    xs = [spec((n, NB), col)] + ([] if extra is None else [spec((n, NB), col)])
    args = [base] + ([] if extra is None else [extra])
    return call(kernel, (D // NB,), [spec((n, C), whole, True), spec((n, U), whole, True), spec((NB, C), row), spec((NB, U), row)] + xs +
                [spec((6, NB), col), spec((n, 128), whole)],
                [spec((n, NB), col), spec((4, NB), col)],
                [jax.ShapeDtypeStruct((n, D), BF), jax.ShapeDtypeStruct((4, D), F32)],
                flops=2 * n * D * (C + U), nbytes=2 * (n * (C + U) + D * (C + U) + n * D * 3), name="back_out")(dmix, df, wq, wu, *args, vec, stats)


def weight_grad(left, right, w=None):
    n, M = left.shape
    N = right.shape[1]
    MB = 256

    def kernel(l_r, r_r, o_r, s_r):
        g = lax.dot_general(l_r[...], r_r[...], (((0,), (0,)), ((), ())), preferred_element_type=F32)
        if w is None:
            o_r[...] = g.astype(BF)
        else:
            for s in range(N // w):
                o_r[s] = g[:, s * w:(s + 1) * w].astype(BF)

        @pl.when(pl.program_id(0) == 0)
        def _():
            s_r[...] = jnp.sum(r_r[...].astype(F32), axis=0, keepdims=True)

    whole = lambda j: (0, 0)
    if w is None:
        out, shape = spec((MB, N), lambda j: (j, 0)), (M, N)
    else:
        out, shape = spec((N // w, MB, w), lambda j: (0, j, 0)), (N // w, M, w)
    return call(kernel, (M // MB,), [spec((n, MB), lambda j: (0, j)), spec((n, N), whole, True)], [out, spec((1, N), whole)],
                [jax.ShapeDtypeStruct(shape, BF), jax.ShapeDtypeStruct((1, N), F32)],
                flops=2 * n * M * N, nbytes=2 * (n * M + n * N + M * N), name="wgrad")(left, right)


def norm_back(gout, e, base, extra, vec, stats):
    n, D = base.shape
    RB = 128

    def kernel(g_r, e_r, base_r, extra_r, vec_r, st_r, dx_r, low_r, sum_r):
        x = base_r[...].astype(F32) + extra_r[...].astype(F32) + vec_r[4:5, :] + vec_r[5:6, :]
        dx = g_r[...].astype(F32) + norm_pullback(x, e_r, st_r)
        dx_r[...] = dx
        low_r[...] = dx.astype(BF)

        @pl.when(pl.program_id(0) == 0)
        def _():
            sum_r[...] = jnp.zeros_like(sum_r)

        sum_r[...] += jnp.sum(dx, axis=0, keepdims=True)

    row = lambda i: (i, 0)
    whole = lambda i: (0, 0)
    rows = spec((RB, D), row)
    shapes = [jax.ShapeDtypeStruct((n, D), F32), jax.ShapeDtypeStruct((n, D), BF), jax.ShapeDtypeStruct((1, D), F32)]
    return call(kernel, (n // RB,), [rows] * 4 + [spec((6, D), whole), spec((RB, 128), row)], [rows, rows, spec((1, D), whole)], shapes,
                flops=10 * n * D, nbytes=16 * n * D, name="norm_back")(gout, e, base, extra, vec, stats)


def norm_pullback(x, e_r, st_r):
    xhat = (x - st_r[:, 0:1]) * st_r[:, 1:2]
    ev = e_r[...].astype(F32)
    me = jnp.mean(ev, axis=1, keepdims=True)
    mx = jnp.mean(ev * xhat, axis=1, keepdims=True)
    return (ev - me - xhat * mx) * st_r[:, 1:2]


def finish(gout, e, base, extra, branches, held, live, stats):
    n, D = base.shape
    RB = 64
    counts = [b.shape[0] // RB for b in branches]
    starts = [sum(counts[:k]) for k in range(len(counts))]

    def kernel(g_r, e_r, base_r, extra_r, *refs):
        branch_rs, (held_r, live_r, st_r, dx_r, out_r) = refs[:len(branches)], refs[len(branches):]
        i = pl.program_id(0)
        x = base_r[...].astype(F32)
        dx_r[...] = g_r[...] + norm_pullback(x, e_r, st_r)
        for k, b_r in enumerate(branch_rs):
            @pl.when((i >= starts[k]) & (i < starts[k] + counts[k]))
            def _(b_r=b_r):
                last = base_r[...].astype(F32) + extra_r[...].astype(F32) + b_r[...].astype(F32) + held_r[...]
                out_r[...] = jnp.where(live_r[...] > 0.0, last, 0.0).astype(BF)

    row = lambda i: (i, 0)
    whole = lambda i: (0, 0)
    rows = spec((RB, D), row)
    part = lambda k: spec((RB, D), lambda i: (jnp.clip(i - starts[k], 0, counts[k] - 1), 0))
    ins = [rows] * 4 + [part(k) for k in range(len(branches))] + [spec((1, D), whole), spec((RB, 1), row), spec((RB, 128), row)]
    return call(kernel, (n // RB,), ins, [rows, rows], [jax.ShapeDtypeStruct((n, D), F32), jax.ShapeDtypeStruct((n, D), BF)],
                flops=10 * n * D, nbytes=18 * n * D, name="finish")(gout, e, base, extra, *branches, held, live, stats)


MESH = pl.DeviceIdType.MESH


class Spot:
    def __init__(self):
        i = lax.axis_index("dp")
        c, x, y = lax.rem(i, 2), lax.rem(lax.div(i, 2), 2), lax.div(i, 4)
        self.me, self.core = i, c
        self.dx, self.dy, self.dc = 2 - 4 * x, 4 - 8 * y, 1 - 2 * c
        self.nx, self.ny, self.nc = i + self.dx, i + self.dy, i + self.dc
        self.diag = i + self.dx + self.dy
        z = lax.axis_index("mp")
        self.z = z
        self.outer = (z == 0) | (z == 3)
        self.inner = (z == 1) | (z == 2)
        self.pair = z + 1 - 2 * lax.rem(z, 2)
        self.across = 3 - z

    def meet(self, line):
        barrier = pltpu.get_barrier_semaphore()
        for peer in (self.nx, self.ny, self.nc):
            pl.semaphore_signal(barrier, inc=1, device_id={"dp": peer}, device_id_type=MESH)
        if line:
            pl.semaphore_signal(barrier, inc=1, device_id={"mp": self.pair}, device_id_type=MESH)

            @pl.when(self.inner)
            def _():
                pl.semaphore_signal(barrier, inc=1, device_id={"mp": self.across}, device_id_type=MESH)

            @pl.when(self.inner)
            def _():
                pl.semaphore_wait(barrier, 5)

            @pl.when(self.outer)
            def _():
                pl.semaphore_wait(barrier, 4)
        else:
            pl.semaphore_wait(barrier, 3)


def send_to(axis, peer, src, dst, send, recv):
    return pltpu.make_async_remote_copy(src_ref=src, dst_ref=dst, send_sem=send, recv_sem=recv, device_id={axis: peer}, device_id_type=MESH)


class Gather:
    copies = 9

    def __init__(self, spot, items, send, recv, local):
        self.spot, self.items, self.send, self.recv, self.local = spot, items, send, recv, local
        self.sent = []
        self.own = []

    def go(self, k, n, peer, src, dst):
        send_to("dp", peer, src, dst, self.send.at[k, n], self.recv.at[k, n]).start()
        self.sent.append((k, n, peer, src, dst))

    def arrived(self, k, n, dst):
        send_to("dp", self.spot.nc, dst, dst, self.send.at[k, n], self.recv.at[k, n]).wait_recv()

    def first(self, k):
        s, (src, out) = self.spot, self.items[k]
        for n, peer in enumerate((s.nx, s.ny, s.nc)):
            self.go(k, n, peer, src, out.at[s.me])
        pltpu.make_async_copy(src, out.at[s.me], self.local.at[k]).start()
        self.own.append(k)

    def halves(self, k):
        h = self.items[k][1].shape[1] // 2
        return pl.ds(0, h), pl.ds(h, h)

    def second(self, k):
        s, (_, out) = self.spot, self.items[k]
        low, high = self.halves(k)
        self.arrived(k, 0, out.at[s.nx])
        self.go(k, 3, s.ny, out.at[s.nx, high], out.at[s.nx, high])
        self.go(k, 4, s.nc, out.at[s.nx], out.at[s.nx])
        self.arrived(k, 1, out.at[s.ny])
        self.go(k, 5, s.nx, out.at[s.ny, low], out.at[s.ny, low])
        self.go(k, 6, s.nc, out.at[s.ny], out.at[s.ny])

    def third(self, k):
        s, (_, out) = self.spot, self.items[k]
        low, high = self.halves(k)
        self.arrived(k, 3, out.at[s.diag, high])
        self.go(k, 7, s.nc, out.at[s.diag, high], out.at[s.diag, high])
        self.arrived(k, 5, out.at[s.diag, low])
        self.go(k, 8, s.nc, out.at[s.diag, low], out.at[s.diag, low])

    def last(self, k):
        s, (_, out) = self.spot, self.items[k]
        low, high = self.halves(k)
        self.arrived(k, 2, out.at[s.nc])
        self.arrived(k, 4, out.at[s.nx + s.dc])
        self.arrived(k, 6, out.at[s.ny + s.dc])
        self.arrived(k, 7, out.at[s.diag + s.dc, high])
        self.arrived(k, 8, out.at[s.diag + s.dc, low])

    def close(self):
        for k in self.own:
            src, out = self.items[k]
            pltpu.make_async_copy(src, out.at[self.spot.me], self.local.at[k]).wait()
        for k, n, peer, src, dst in self.sent:
            send_to("dp", peer, src, dst, self.send.at[k, n], self.recv.at[k, n]).wait_send()


AHEAD, LAG, BACK = 3, 1, 5


class LineSum:
    copies = 3

    def __init__(self, spot, pairs, stage, land, swap, send, recv, local):
        self.spot, self.stage, self.land, self.swap = spot, stage, land, swap
        self.send, self.recv, self.local = send, recv, local
        self.rows = stage.shape[1]
        self.parts, self.outs = [], []
        for part, start, out, rows in pairs:
            for at in range(0, rows, self.rows):
                self.parts.append(part.at[pl.ds(start + at, self.rows)])
                self.outs.append(out.at[pl.ds(at, self.rows)])
        self.chunks = len(self.parts)

    def cut(self, k):
        return pl.ds(k * self.rows, self.rows)

    def copy(self, k, n):
        s, rows = self.spot, self.cut(k)
        if n == 0:
            peer, src, dst = s.pair, self.parts[k], self.land
        elif n == 1:
            peer, src, dst = s.across, self.land.at[rows], self.swap
        else:
            peer, src, dst = s.pair, self.swap.at[rows], self.swap
        return send_to("mp", peer, src, dst.at[rows], self.send.at[k, n], self.recv.at[k, n])

    def keep(self, k):
        rows = self.cut(k)
        return pltpu.make_async_copy(self.swap.at[rows], self.outs[k], self.local.at[k])

    def load(self, k):
        return pltpu.make_async_copy(self.parts[k], self.stage.at[k % 2], self.local.at[self.chunks + k % 2])

    def add(self, k, dst, one, two, base):
        step = 32

        @pl.loop(0, self.rows // step)
        def _(i):
            rows = pl.ds(pl.multiple_of(k * self.rows + i * step, step), step)
            there = pl.ds(pl.multiple_of(base + i * step, step), step)
            dst[rows, :] = (one[there, :].astype(F32) + two[rows, :].astype(F32)).astype(BF)

    def send_step(self, t):
        n = self.chunks

        @pl.when(self.spot.outer)
        def _():
            if 0 <= t - AHEAD < n:
                self.copy(t - AHEAD, 0).wait_send()
            if t < n:
                self.copy(t, 0).start()
            if 0 <= t - BACK < n:
                self.copy(t - BACK, 2).wait_recv()
                self.keep(t - BACK).start()

    def add_step(self, t):
        n = self.chunks

        @pl.when(self.spot.inner)
        def _():
            if t < n:
                if t == 0:
                    self.load(0).start()
                if t + 1 < n:
                    self.load(t + 1).start()
                self.load(t).wait()
                self.copy(t, 0).wait_recv()
                self.add(t, self.land, self.stage.at[t % 2], self.land, 0)
                self.copy(t, 1).start()
            if 0 <= t - LAG < n:
                self.copy(t - LAG, 1).wait_recv()
                self.copy(t - LAG, 1).wait_send()
                self.add(t - LAG, self.swap, self.land, self.swap, (t - LAG) * self.rows)
                self.copy(t - LAG, 2).start()
                self.keep(t - LAG).start()

    def begin(self):
        self.sent_to, self.added_to = 0, 0
        for _ in range(AHEAD):
            self.send_step(self.sent_to)
            self.sent_to += 1

    def slot(self):
        if self.added_to < self.chunks + LAG:
            self.add_step(self.added_to)
            self.added_to += 1
        if self.sent_to < self.chunks + BACK:
            self.send_step(self.sent_to)
            self.sent_to += 1

    def finish(self):
        while self.added_to < self.chunks + LAG or self.sent_to < self.chunks + BACK:
            self.slot()

    def close(self):
        for k in range(self.chunks):
            self.keep(k).wait()

        @pl.when(self.spot.inner)
        def _():
            for k in range(self.chunks):
                self.copy(k, 2).wait_send()


class Scatter:
    copies = 10

    def __init__(self, spot, items, own, sib, fx, fy, gx, gy, send, recv, local):
        self.spot, self.items = spot, items
        self.own, self.sib, self.fx, self.fy, self.gx, self.gy = own, sib, fx, fy, gx, gy
        self.send, self.recv, self.local = send, recv, local
        self.sent = []

    def go(self, k, n, peer, src, dst):
        send_to("dp", peer(), src(), dst(), self.send.at[k, n], self.recv.at[k, n]).start()
        self.sent.append((k, n, src))

    def arrived(self, k, n, dst):
        send_to("dp", self.spot.nc, dst, dst, self.send.at[k, n], self.recv.at[k, n]).wait_recv()

    def hand(self, k):
        s, grad = self.spot, self.items[k][0]
        for m, slot in enumerate((s.me, s.nx, s.ny, s.diag)):
            self.go(k, m, lambda: s.nc, lambda slot=slot: grad.at[slot + s.dc], lambda m=m: self.sib[k].at[m])

    def hold(self, k):
        for m in range(4):
            self.load(k, m).start()

    def first(self, k):
        self.hand(k)
        self.hold(k)

    def load(self, k, m):
        s = self.spot
        slot = (s.me, s.nx, s.ny, s.diag)[m]
        return pltpu.make_async_copy(self.items[k][0].at[slot], self.own[k].at[m], self.local.at[k, m])

    def over(self, r, c, body, start=0):
        step = 16
        while step * 2 * c <= 32768 and r % (step * 2) == 0:
            step *= 2

        @pl.loop(0, r // step)
        def _(i):
            body(pl.ds(pl.multiple_of(i * step, step), step), pl.ds(pl.multiple_of(start + i * step, step), step))

    def second(self, k):
        s = self.spot
        own, sib = self.own[k], self.sib[k]
        _, r, c = own.shape
        h = r // 2
        low, high = pl.ds(0, h), pl.ds(h, h)
        for m in (3, 1, 2, 0):
            self.load(k, m).wait()
            self.arrived(k, m, sib.at[m])

            def add(rows, _, m=m):
                own[m, rows, :] = (own[m, rows, :].astype(F32) + sib[m, rows, :].astype(F32)).astype(BF)

            self.over(r, c, add)
            if m == 3:
                self.go(k, 5, lambda: s.nx, lambda: own.at[3, low], lambda: self.fx[k].at[1])
                self.go(k, 7, lambda: s.ny, lambda: own.at[3, high], lambda: self.fy[k].at[1])
            if m == 1:
                self.go(k, 4, lambda: s.nx, lambda: own.at[1, low], lambda: self.fx[k].at[0])
            if m == 2:
                self.go(k, 6, lambda: s.ny, lambda: own.at[2, high], lambda: self.fy[k].at[0])

    def third(self, k):
        s = self.spot
        own, fx, fy = self.own[k], self.fx[k], self.fy[k]
        _, r, c = own.shape
        h = r // 2
        self.arrived(k, 5, fx.at[1])

        def add_low(rows, _):
            fx[1, rows, :] = (own[2, rows, :].astype(F32) + fx[1, rows, :].astype(F32)).astype(BF)

        self.over(h, c, add_low)
        self.go(k, 8, lambda: s.ny, lambda: fx.at[1], lambda: self.gy[k])
        self.arrived(k, 7, fy.at[1])

        def add_high(rows, there):
            fy[1, rows, :] = (own[1, there, :].astype(F32) + fy[1, rows, :].astype(F32)).astype(BF)

        self.over(h, c, add_high, h)
        self.go(k, 9, lambda: s.nx, lambda: fy.at[1], lambda: self.gx[k])

    def last(self, k):
        own, out = self.own[k], self.items[k][1]
        fx, fy, gx, gy = self.fx[k], self.fy[k], self.gx[k], self.gy[k]
        _, r, c = own.shape
        h = r // 2
        self.arrived(k, 4, fx.at[0])
        self.arrived(k, 8, gy)

        def low(rows, _):
            out[rows, :] = own[0, rows, :].astype(F32) + fx[0, rows, :].astype(F32) + gy[rows, :].astype(F32)

        self.over(h, c, low)
        self.arrived(k, 6, fy.at[0])
        self.arrived(k, 9, gx)

        def high(rows, there):
            out[there, :] = own[0, there, :].astype(F32) + fy[0, rows, :].astype(F32) + gx[rows, :].astype(F32)

        self.over(h, c, high, h)

    def close(self):
        for k, n, src in self.sent:
            send_to("dp", self.spot.nc, src(), src(), self.send.at[k, n], self.recv.at[k, n]).wait_send()


def link_kernel(name, ident, shards, layers, part=None, chunks=16):
    ng = len(shards)
    HBM = pl.BlockSpec(memory_space=pl.ANY)
    DMA = pltpu.SemaphoreType.DMA
    parts = [] if part is None else [part]
    shapes = [jax.ShapeDtypeStruct((8,) + (v.shape if l is None else v.shape[1:]), v.dtype) for v, l in zip(shards, layers)]
    shapes += [jax.ShapeDtypeStruct(v.shape, BF) for v in parts]
    scratch = [DMA((ng, 9)), DMA((ng, 9)), DMA((ng,))]
    for v in parts:
        scratch += [pltpu.VMEM((2, v.shape[0] // chunks, v.shape[1]), BF), pltpu.VMEM(v.shape, BF), pltpu.VMEM(v.shape, BF), DMA((chunks, 3)), DMA((chunks, 3)), DMA((chunks + 2,))]

    def kernel(*refs):
        refs = list(refs)
        take = lambda n: [refs.pop(0) for _ in range(n)]
        src, ins, full, totals = take(ng), take(len(parts)), take(ng), take(len(parts))
        spot = Spot()
        spot.meet(bool(parts))
        G = Gather(spot, [(a if l is None else a.at[l], b) for a, l, b in zip(src, layers, full)], *take(3))
        if parts:
            stage, land, swap, send, recv, local = take(6)
            line = LineSum(spot, [(ins[0], 0, totals[0], ins[0].shape[0])], stage, land, swap, send, recv, local)
            plan_sum_gather(G, line)
            line.close()
        else:
            plan_gather(G)
        G.close()

    nbytes = sum(v.size * 2 for v in parts) + sum(8 * v.size for v in shards)
    return pl.pallas_call(
        kernel, in_specs=[HBM] * (ng + len(parts)), out_specs=[HBM] * (ng + len(parts)), out_shape=shapes, scratch_shapes=scratch,
        compiler_params=pltpu.CompilerParams(vmem_limit_bytes=VM, collective_id=ident, has_side_effects=True),
        cost_estimate=pl.CostEstimate(flops=0, bytes_accessed=nbytes, transcendentals=0), name=name)(*shards, *parts)


def plan_gather(G):
    n = len(G.items)
    for stage in (G.first, G.second, G.third, G.last):
        for k in range(n):
            stage(k)


class Products:
    def __init__(self, core, lefts, rights, grads, rhs, lbuf, obuf, rsem, lsem, osem):
        self.core = core
        self.lefts, self.rights, self.grads = lefts, rights, grads
        self.rhs, self.lbuf, self.obuf, self.rsem, self.lsem, self.osem = rhs, lbuf, obuf, rsem, lsem, osem

    def right(self, i, slot):
        return pltpu.make_async_copy(self.rights[i], self.rhs[slot], self.rsem.at[i])

    def split(self, k):
        slots, r, _ = self.grads[k].shape
        return r == 256 and self.lefts[k].shape[1] == slots * r

    def block(self, k, m):
        if self.split(k):
            late = m // 4 if isinstance(m, int) else lax.div(m, 4)
            return 2 * (m - 4 * late) + 1 - self.core - late + 2 * late * self.core
        return m

    def columns(self, block):
        return pl.ds(block * 256 if isinstance(block, int) else pl.multiple_of(block * 256, 256), 256)

    def left(self, k, m):
        odd = m % 2 if isinstance(m, int) else lax.rem(m, 2)
        return pltpu.make_async_copy(self.lefts[k].at[:, self.columns(self.block(k, m))], self.lbuf.at[odd], self.lsem.at[odd])

    def stores(self, k, m):
        odd = m % 2 if isinstance(m, int) else lax.rem(m, 2)
        grad, o, sem = self.grads[k], self.obuf.at[odd], self.osem.at[odd]
        slots, _, c = grad.shape
        block = self.block(k, m)
        if self.split(k):
            return [pltpu.make_async_copy(o.at[:, pl.ds(0, c)], grad.at[block], sem.at[0])]
        return [pltpu.make_async_copy(o.at[:, pl.ds(s * c, c)], grad.at[s, self.columns(block)], sem.at[s]) for s in range(slots)]

    def run(self, k, slot, start, stop, hooks):
        right = self.rhs[slot]
        width = right.shape[1]
        self.left(k, start).start()

        @pl.loop(start, stop)
        def _(m):
            self.left(k, m).wait()

            @pl.when(m + 1 < stop)
            def _():
                self.left(k, m + 1).start()

            @pl.when(m >= start + 2)
            def _():
                for copy in self.stores(k, m - 2):
                    copy.wait()

            g = lax.dot_general(self.lbuf[lax.rem(m, 2)], right[...], (((0,), (0,)), ((), ())), preferred_element_type=F32)
            self.obuf[lax.rem(m, 2), :, :width] = g.astype(BF)
            for copy in self.stores(k, m):
                copy.start()
            for at in sorted(hooks):
                pl.when(m == at)(hooks[at])

        for m in (stop - 2, stop - 1):
            for copy in self.stores(k, m):
                copy.wait()

    def sums(self, slot, out):
        right = self.rhs[slot]
        out[...] = jnp.zeros_like(out)

        @pl.loop(0, right.shape[0] // 64)
        def _(i):
            out[...] += jnp.sum(right[pl.ds(pl.multiple_of(i * 64, 64), 64), :].astype(F32), axis=0, keepdims=True)


def plan_sum_gather(G, line):
    for k in range(4):
        G.first(k)
    stages = {5: [("second", 0), ("second", 1)], 9: [("second", 2)], 12: [("second", 3)], 14: [("third", 0), ("third", 1)], 15: [("third", 2)],
              17: [("third", 3)]}
    line.begin()
    for at in range(18):
        line.slot()
        for name, k in stages.get(at, ()):
            getattr(G, name)(k)
    line.finish()
    for k in range(4):
        G.last(k)


def sum_scatter(ident, e, more, first_row, more_rows, lefts, rights, step=64):
    n, D = e.shape
    HBM = pl.BlockSpec(memory_space=pl.ANY)
    VM_ = pl.BlockSpec(memory_space=pltpu.VMEM)
    C, U = rights[1].shape[1], rights[2].shape[1]
    w = D // 8
    dims = [(lefts[0].shape[1], w), (lefts[1].shape[1], w), (w, C), (w, U)]
    DMA = pltpu.SemaphoreType.DMA
    chunks = (n + more_rows) // step
    outs = [HBM] * 2 + [HBM] * 4 + [VM_] * 4 + [VM_] * 3
    shapes = [jax.ShapeDtypeStruct(e.shape, BF), jax.ShapeDtypeStruct((more_rows, D), BF)] + [jax.ShapeDtypeStruct((8,) + d, BF) for d in dims] + [jax.ShapeDtypeStruct(d, F32) for d in dims]
    shapes += [jax.ShapeDtypeStruct((1, C), F32), jax.ShapeDtypeStruct((1, U), F32), jax.ShapeDtypeStruct((1, D), F32)]
    scratch = [pltpu.VMEM((2, step, D), BF)] + [pltpu.VMEM((n + more_rows, D), BF)] * 2 + [DMA((chunks, 3)), DMA((chunks, 3)), DMA((chunks + 2,))]
    cut = [dims[0], (dims[1][0] // 2, w), (dims[1][0] // 2, w), dims[2], dims[3]]
    scratch += [DMA((5, 10)), DMA((5, 10)), DMA((5, 4))]
    for r, c in cut:
        scratch += [pltpu.VMEM((4, r, c), BF), pltpu.VMEM((4, r, c), BF), pltpu.VMEM((2, r // 2, c), BF), pltpu.VMEM((2, r // 2, c), BF),
                    pltpu.VMEM((r // 2, c), BF), pltpu.VMEM((r // 2, c), BF)]
    wide = max(D, U)
    scratch += [pltpu.VMEM((n, wide), BF), pltpu.VMEM((n, C), BF), pltpu.VMEM((2, n, 256), BF), pltpu.VMEM((2, 256, wide), BF), DMA((3,)), DMA((2,)), DMA((2, 8))]
    assert D == U

    def kernel(*refs):
        refs = list(refs)
        take = lambda k: [refs.pop(0) for _ in range(k)]
        (e_r, more_r), left_rs, right_rs = take(2), take(4), take(3)
        (total, more_total), grads, owned, sum_rs = take(2), take(4), take(4), take(3)
        stage, land, swap, send, recv, local = take(6)
        spot = Spot()
        spot.meet(True)
        line = LineSum(spot, [(e_r, 0, total, n), (more_r, first_row, more_total, more_rows)], stage, land, swap, send, recv, local)
        send, recv, local = take(3)
        bufs = [take(6) for _ in range(5)]
        half = cut[1][0]
        low, high = pl.ds(0, half), pl.ds(half, half)
        items = [(grads[0], owned[0]), (grads[1].at[:, low], owned[1].at[low]), (grads[1].at[:, high], owned[1].at[high])]
        items += [(grads[2], owned[2]), (grads[3], owned[3])]
        S = Scatter(spot, items, *[[b[i] for b in bufs] for i in range(6)], send, recv, local)
        wide_r, narrow_r, lbuf, obuf, rsem, lsem, osem = take(7)
        W = Products(spot.core, left_rs, right_rs, grads, (wide_r, narrow_r), lbuf, obuf, rsem, lsem, osem)
        W.right(0, 0).start()
        W.right(1, 1).start()
        def steps(*what):
            def go():
                for step, *args in what:
                    step(*args)

            return go

        slot = (line.slot,)
        line.begin()
        W.right(0, 0).wait()
        W.run(1, 0, 0, 4, {1: steps(slot)})
        S.first(1)
        line.slot()
        W.run(0, 0, 0, left_rs[0].shape[1] // 256, {})
        S.first(0)
        S.second(1)
        line.slot()
        W.run(1, 0, 4, 8, {5: steps(slot)})
        S.first(2)
        W.sums(0, sum_rs[2])
        W.right(2, 0).start()
        S.second(0)
        line.slot()
        W.right(1, 1).wait()
        W.run(2, 1, 0, 8, {0: steps((S.second, 2), (S.third, 1)), 2: steps(slot), 5: steps((S.hand, 3), slot)})
        S.hold(3)
        line.slot()
        S.third(0)
        S.second(3)
        W.right(2, 0).wait()
        W.run(3, 0, 0, 8, {1: steps(slot), 3: steps((S.third, 2)), 4: steps(slot), 5: steps((S.hand, 4)), 6: steps(slot)})
        S.hold(4)
        line.slot()
        S.second(4)
        W.sums(1, sum_rs[0])
        line.slot()
        S.third(3)
        line.slot()
        W.sums(0, sum_rs[1])
        line.slot()
        S.last(0)
        S.last(1)
        line.slot()
        S.last(2)
        line.slot()
        line.slot()
        S.third(4)
        line.slot()
        S.last(3)
        line.finish()
        S.last(4)
        line.close()
        S.close()

    flops = 2 * n * D * (lefts[0].shape[1] + lefts[1].shape[1] + C + U)
    got = pl.pallas_call(
        kernel, in_specs=[HBM] * 9, out_specs=outs, out_shape=shapes, scratch_shapes=scratch,
        compiler_params=pltpu.CompilerParams(vmem_limit_bytes=VM2, collective_id=ident, has_side_effects=True),
        cost_estimate=pl.CostEstimate(flops=flops, bytes_accessed=2 * n * D * 12, transcendentals=0), name="sum_scatter")(e, more, *lefts, *rights)
    gd, gn, gq, gu = got[6:10]
    return got[0], got[1], (gq, gd, gu, gn), got[10], got[11], got[12]


def small_sum(pieces, shared):
    ndp, r, _ = pieces.shape
    nmp = lax.axis_size("mp")

    def kernel(x_r, o_r, land, line, send, recv, send2, recv2):
        i, z = lax.axis_index("dp"), lax.axis_index("mp")
        barrier = pltpu.get_barrier_semaphore()
        for s in range(1, ndp):
            pl.semaphore_signal(barrier, inc=1, device_id={"dp": lax.rem(i + s, ndp)}, device_id_type=MESH)
        for s in range(1, nmp):
            pl.semaphore_signal(barrier, inc=1, device_id={"mp": lax.rem(z + s, nmp)}, device_id_type=MESH)
        pl.semaphore_wait(barrier, ndp + nmp - 2)
        first = [send_to("dp", lax.rem(i + s, ndp), x_r.at[lax.rem(i + s, ndp)], land.at[i], send.at[s], recv.at[s]) for s in range(1, ndp)]
        for copy in first:
            copy.start()
        land[pl.ds(i, 1)] = x_r[pl.ds(i, 1)]
        for s in range(1, ndp):
            there = land.at[lax.rem(i - s + ndp, ndp)]
            send_to("dp", i, there, there, send.at[s], recv.at[s]).wait_recv()
        acc = land[0]
        for j in range(1, ndp):
            acc = acc + land[j]
        o_r[...] = acc
        line[pl.ds(z, 1)] = acc[None, :shared]
        second = [send_to("mp", lax.rem(z + s, nmp), line.at[z], line.at[z], send2.at[s], recv2.at[s]) for s in range(1, nmp)]
        for copy in second:
            copy.start()
        for s in range(1, nmp):
            there = line.at[lax.rem(z - s + nmp, nmp)]
            send_to("mp", z, there, there, send2.at[s], recv2.at[s]).wait_recv()
        acc = line[0]
        for j in range(1, nmp):
            acc = acc + line[j]
        o_r[:shared] = acc
        for copy in first + second:
            copy.wait_send()

    VM_ = pl.BlockSpec(memory_space=pltpu.VMEM)
    DMA = pltpu.SemaphoreType.DMA
    return pl.pallas_call(
        kernel, in_specs=[VM_], out_specs=VM_, out_shape=jax.ShapeDtypeStruct((r, 128), F32),
        scratch_shapes=[pltpu.VMEM(pieces.shape, F32), pltpu.VMEM((nmp, shared, 128), F32), DMA((ndp,)), DMA((ndp,)), DMA((nmp,)), DMA((nmp,))],
        compiler_params=pltpu.CompilerParams(vmem_limit_bytes=VM // 4, collective_id=6, has_side_effects=True), name="small_sum")(pieces)


def adam_update(weight, grad, first, second):
    first_new = beta_one * first + (1.0 - beta_one) * grad
    second_new = beta_two * second + (1.0 - beta_two) * grad * grad
    mean_hat = first_new / (1.0 - beta_one**ADAM_STEP)
    square_hat = second_new / (1.0 - beta_two**ADAM_STEP)
    new_weight = weight - rate * (mean_hat / (jnp.sqrt(square_hat) + adam_eps) + decay * weight)
    return grad, first_new, second_new, new_weight - weight


def adam_layer(layer, weights, grads, firsts, seconds, before):
    steps = 8
    blocks = [(w.shape[1] // steps, w.shape[2]) for w in weights]

    def kernel(*refs):
        ins, outs = refs[:16], refs[-16:]
        for i in range(4):
            g = ins[4 + i][...].astype(F32)
            made = adam_update(ins[i][...].astype(F32), g, ins[8 + i][...], ins[12 + i][...])
            for k in range(4):
                outs[4 * i + k][...] = made[k]

    at = lambda b: spec((None,) + b, lambda j: (layer, j, 0))
    ins = [at(b) for b in blocks] + [spec(b, lambda j: (j, 0)) for b in blocks] + [at(b) for b in blocks] * 2
    args = [*weights, *grads, *firsts, *seconds]
    alias = {}
    if before is not None:
        ins += [pl.BlockSpec(memory_space=pl.ANY)] * 16
        args += list(before)
        alias = {16 + i: i for i in range(16)}
    shapes = [jax.ShapeDtypeStruct(w.shape, F32) for w in weights for _ in range(4)]
    count = sum(w.shape[1] * w.shape[2] for w in weights)
    return pl.pallas_call(
        kernel, grid=(steps,), in_specs=ins, out_specs=[at(b) for b in blocks for _ in range(4)], out_shape=shapes,
        input_output_aliases=alias, compiler_params=pltpu.CompilerParams(vmem_limit_bytes=VM),
        cost_estimate=pl.CostEstimate(flops=20 * count, bytes_accessed=30 * count, transcendentals=0), name="adam")(*args)


def layout(lengths_row, rows):
    slots = lengths_row.shape[0]
    number = jnp.arange(slots, dtype=jnp.int32)
    ends = jnp.sum(jnp.where(number[None, :] <= number[:, None], lengths_row[None, :], 0), axis=1)
    starts = ends - lengths_row
    index = jnp.arange(rows, dtype=jnp.int32)
    inside = (index[:, None] >= starts[None, :]) & (index[:, None] < ends[None, :])
    valid = jnp.any(inside, axis=1)
    slot = jnp.sum(jnp.where(inside, number[None, :], 0), axis=1)
    first = jnp.sum(jnp.where(inside, starts[None, :], 0), axis=1)
    segment = jnp.where(valid, slot, slots + index)
    return segment, index - first, valid


class PlainLinks:
    def weights(self, shards, layer):
        wq, wd, wu, wn = [w[layer] for w in shards]
        rows = lambda v: lax.all_gather(v, "dp", axis=0, tiled=True)
        stack = lambda v: lax.all_gather(v, "dp", axis=0, tiled=False)
        return rows(wq), stack(wd), rows(wu), stack(wn)

    def share(self, v):
        return lax.psum(v, "mp")

    def owned(self, grads):
        cut = lambda g: lax.psum_scatter(g, "dp", scatter_dimension=0, tiled=True)
        gq, gd, gu, gn = grads
        return cut(gq), cut(gd)[0], cut(gu), cut(gn)[0]

    def small(self, pieces, shared):
        total = lax.psum(pieces, "dp")[lax.axis_index("dp")]
        return jnp.concatenate([lax.psum(total[:shared], "mp"), total[shared:]])

    def begin(self, shards, flat):
        return self.weights(shards, 0), lax.all_gather(flat, "dp", axis=0, tiled=False), None

    def middle(self, branch, shards):
        return self.share(branch), self.weights(shards, 1)

    def turn(self, e, more, first_row, more_rows, lefts, rights, ident):
        ctx, act, h1, h2 = lefts
        gr, dmix, df = rights
        w = gr.shape[1] // lax.axis_size("dp")
        gd, low_sums = weight_grad(ctx, gr, w=w)
        gn, _ = weight_grad(act, gr, w=w)
        gq, qsum = weight_grad(h1, dmix)
        gu, usum = weight_grad(h2, df)
        more = self.share(more[first_row:first_row + more_rows])
        return self.share(e), more, self.owned((gq, gd, gu, gn)), qsum, usum, low_sums


class ChipLinks:
    def full(self, got):
        wq, wd, wu, wn = got
        return wq.reshape(-1, wq.shape[2]), wd, wu.reshape(-1, wu.shape[2]), wn

    def begin(self, shards, flat):
        wq, wd, wu, wn = shards
        flat, wq, wu = link_kernel("gather", 1, [flat, wq, wu], [None, 0, 0])
        return (wq.reshape(-1, wq.shape[2]), None, wu.reshape(-1, wu.shape[2]), None), flat, (wd, wn)

    def middle(self, branch, shards):
        got = link_kernel("sum_gather", 2, shards, [1] * 4, branch)
        return got[4], self.full(got[:4])

    def turn(self, e, more, first_row, more_rows, lefts, rights, ident):
        return sum_scatter(ident, e, more, first_row, more_rows, lefts, rights)

    def small(self, pieces, shared):
        return small_sum(pieces, shared)


def flatten_small(parts):
    flat = jnp.concatenate([p.reshape(-1) for p in parts])
    return jnp.pad(flat, (0, -flat.size % 4096)).reshape(-1, 128)


def unpack_small(got, parts):
    got = got.reshape(got.shape[0], -1)
    out, at = [], 0
    for p in parts:
        piece = got[:, at:at + p.size].reshape((-1,) + p.shape)
        out.append(jnp.moveaxis(piece, 0, 2).reshape(p.shape[0], p.shape[1], -1))
        at += p.size
    return out


def body(links, tokens_in, cotangent, seq_lengths, *params):
    weights, small = params[:4], params[4:7]
    firsts, small_firsts = params[7:11], params[11:14]
    seconds, small_seconds = params[14:18], params[18:21]
    rows, D = tokens_in.shape
    segment, position, valid = layout(seq_lengths[0], rows)
    cos, sin = rope_tables(position)
    seg_col, seg_row = segment[:, None], segment[None, :]
    live = valid[:, None]
    first_full, got, later = links.begin(weights, flatten_small(small))
    qb, ub, vecs = unpack_small(got, small)
    qb = qb.reshape(LAYERS, 1, -1).astype(F32)
    ub = ub.reshape(LAYERS, 1, -1).astype(F32)
    vecs = vecs.astype(F32)

    held = [jnp.concatenate([vecs[layer, :4], vecs[layer - 1, 4:]]) for layer in range(LAYERS)]

    full, kept, extra = [first_full], [], None
    for layer in range(LAYERS):
        wq, wd, wu, wn = full[layer]
        h1, h2, mixed, act, gp, stats, *more = project(tokens_in, extra, held[layer], wq, qb[layer], cos, sin, wu, ub[layer], later if layer == 0 else None)
        if more:
            wd, wn = more
            full[0] = wq, wd, wu, wn
        ctx = attend_forward(mixed, seg_col, seg_row)
        branch = branch_out(ctx, act, wd, wn)
        kept.append((h1, h2, mixed, act, gp, stats, ctx, extra))
        if layer == 0:
            extra, made = links.middle(branch, weights)
            full.append(made)
        else:
            gout = gr = jnp.where(live, cotangent, 0).astype(BF)
            sums = None
            branch, gr = lax.optimization_barrier((branch, gr))
            branch_sum = [None] * 4
            cuts = [0, rows // 4, rows * 7 // 16, rows * 13 // 16, rows]
            branch_sum[0] = lax.psum(branch[:cuts[1]], "mp")
    big, little = [None] * LAYERS, [None] * LAYERS
    for layer in reversed(range(LAYERS)):
        wq, wd, wu, wn = full[layer]
        h1, h2, mixed, act, gp, stats, ctx, extra = kept[layer]
        dctx, df = back_in(gr, gp, wd, wn)
        dmix = attend_backward(mixed, dctx, seg_col, seg_row, cos, sin)
        e, norm_sums = back_out(dmix, df, wq, wu, tokens_in, extra, held[layer], stats)
        before = 0 if layer else 2
        branch_sum[before], e = lax.optimization_barrier((branch_sum[before], e))
        at = 1 if layer else 3
        e, branch_sum[at], big[layer], qsum, usum, low_sums = links.turn(e, branch, cuts[at], cuts[at + 1] - cuts[at], (ctx, act, h1, h2), (gr, dmix, df), 3 + layer)
        little[layer] = (qsum, usum, norm_sums, low_sums if sums is None else sums)
        if layer:
            e, third = lax.optimization_barrier((e, branch[cuts[2]:cuts[3]]))
            branch_sum[2] = lax.psum(third, "mp")
        if layer:
            gout, gr, sums = norm_back(gout, e, tokens_in, extra, held[layer], stats)
    every = (vecs[0, 4:5] + vecs[0, 5:6]) + (vecs[1, 4:5] + vecs[1, 5:6])
    input_grad, output = finish(gout, e, tokens_in, kept[1][-1], branch_sum, every, live.astype(F32), stats)

    done = None
    for layer in reversed(range(LAYERS)):
        done = adam_layer(layer, weights, big[layer], firsts, seconds, done)

    ndp = lax.axis_size("dp")

    def pieces(v, width):
        v = v.reshape(-1, ndp, width // ndp)
        return jnp.moveaxis(v, 1, 0).reshape(ndp, -1)

    norms = jnp.concatenate([pieces(t[2], D) for t in little], axis=1)
    rest = [pieces(t[i], BROW) for i in (0, 1) for t in little] + [pieces(t[3], D) for t in little]
    rest = jnp.concatenate(rest, axis=1)
    shared, count = norms.shape[1] // 128, rest.shape[1]
    rest = jnp.pad(rest, ((0, 0), (0, -count % 1024)))
    total = links.small(jnp.concatenate([norms, rest], axis=1).reshape(ndp, -1, 128), shared)
    norms, rest = total[:shared].reshape(LAYERS, 4, -1), total[shared:].reshape(-1)
    small_grads, at = [], 0
    for p in small[:2]:
        small_grads.append(rest[at:at + p.size].reshape(p.shape))
        at += p.size
    tops_sum = rest[at:count].reshape(LAYERS, 1, -1)
    small_grads.append(jnp.concatenate([norms, tops_sum, tops_sum], axis=1))
    small_out = []
    for p, g, first, second in zip(small, small_grads, small_firsts, small_seconds):
        small_out += adam_update(p.astype(F32), g, first, second)
    return (output, input_grad, *done, *small_out)


def solution(mesh):
    rows_dp = P("dp", None)
    wide, tall, vec = P(None, "dp", "mp"), P(None, "mp", "dp"), P(None, None, "dp")
    group = (wide, tall, wide, tall, tall, tall, vec)
    return jax.shard_map(
        functools.partial(body, ChipLinks() if dict(mesh.shape) == {"dp": 8, "mp": 4} else PlainLinks()),
        mesh=mesh,
        in_specs=(rows_dp,) * 3 + group * 3,
        out_specs=(rows_dp,) * 2 + tuple(s for s in group for _ in range(4)),
        check_vma=False,
    )
```

```python
import functools
import jax
import jax.numpy as jnp
from jax import lax
from jax.experimental import pallas as pl
from jax.experimental.pallas import tpu as pltpu
from jax.sharding import PartitionSpec as P

HD = 256
ROT = 64
MAXLEN = 512
norm_eps = 1e-05
masked_score = -1e30
LAYERS = 2
BROW = 128
ADAM_STEP = 10
beta_one = 0.9
beta_two = 0.95
adam_eps = 1e-08
rate = 0.02
decay = 0.01
VM = 60 * 1024 * 1024
VM2 = 62 * 1024 * 1024
BF = jnp.bfloat16
ROWS = 256
UPB = 512
F32 = jnp.float32


def call(kernel, grid, in_specs, out_specs, out_shape, scratch=(), flops=0, nbytes=0, name=None, ident=None):
    return pl.pallas_call(
        kernel,
        grid_spec=pltpu.PrefetchScalarGridSpec(num_scalar_prefetch=0, grid=grid, in_specs=in_specs, out_specs=out_specs, scratch_shapes=list(scratch)),
        out_shape=out_shape,
        compiler_params=pltpu.CompilerParams(vmem_limit_bytes=VM, collective_id=ident, has_side_effects=ident is not None),
        cost_estimate=pl.CostEstimate(flops=flops, bytes_accessed=nbytes, transcendentals=0),
        name=name,
    )


def spec(shape, index, single=False):
    if single:
        return pl.BlockSpec(shape, index, pipeline_mode=pl.Buffered(1))
    return pl.BlockSpec(shape, index)


def rope_tables(position):
    half = ROT // 2
    freq = 10000.0 ** (-(jnp.arange(half, dtype=F32) * 2.0) / ROT)
    angle = position.astype(F32)[:, None] * freq[None, :]
    c, s = jnp.cos(angle), jnp.sin(angle)
    rows = position.shape[0]
    one = jnp.ones((rows, 128 - ROT), F32)
    zero = jnp.zeros((rows, 128 - ROT), F32)
    return jnp.concatenate([c, c, one], axis=1), jnp.concatenate([-s, s, zero], axis=1)


def turn(u, c, s):
    lane = lax.broadcasted_iota(jnp.int32, u.shape, 1)
    other = jnp.where(lane < ROT // 2, pltpu.roll(u, 128 - ROT // 2, 1), pltpu.roll(u, ROT // 2, 1))
    return u * c + other * s


def normed(x):
    mean = jnp.mean(x, axis=1, keepdims=True)
    centred = x - mean
    var = jnp.mean(centred * centred, axis=1, keepdims=True)
    rstd = lax.rsqrt(var + norm_eps)
    return centred * rstd, mean, rstd


def row_blocks(n):
    step = min(n, ROWS)
    return [slice(i, i + step) for i in range(0, n, step)]


def project(base, extra, vec, wq, bq, cos, sin, wu, bu, shards=None):
    n, D = base.shape
    C, U = wq.shape[1], wu.shape[1]
    QB, UB = 3 * HD, min(UPB, U)
    nq, nu = C // QB, U // UB
    RB = 128
    nr = n // RB
    ng = 0 if shards is None else len(shards)
    xs = [base] if extra is None else [base, extra]

    def kernel(*refs):
        refs = list(refs)
        take = lambda k: [refs.pop(0) for _ in range(k)]
        x_rs = take(len(xs))
        vec_r, wq_r, bq_r, cos_r, sin_r, wu_r, bu_r = take(7)
        shard_rs = take(ng)
        h1_o, h2_o, mix_r, a_r, gp_r, st_r = take(6)
        full_rs = take(ng)
        h1_r, h2_r = take(2)
        bufs = take(len(xs))
        in_sem, out_sem = take(2)
        j = pl.program_id(0)
        side = None
        if ng:
            spot = Spot()
            side = Gather(spot, [(a.at[0], b) for a, b in zip(shard_rs, full_rs)], *take(3))

            @pl.when(j == 0)
            def _():
                spot.meet(False)
                side.first(0)
                side.first(1)

        def host(step, *stages):
            if side is not None:
                @pl.when(j == min(step, nq + nu - 1))
                def _():
                    for name, *args in stages:
                        getattr(side, name)(*args)
        block = lambda i: pl.ds(i * RB, RB)
        loads = [[pltpu.make_async_copy(x.at[block(i)], buf.at[block(i)], in_sem.at[k, i]) for k, (x, buf) in enumerate(zip(x_rs, bufs))] for i in range(nr)]
        stores = [[pltpu.make_async_copy(h.at[block(i)], o.at[block(i)], out_sem.at[k, i]) for k, (h, o) in enumerate(((h1_r, h1_o), (h2_r, h2_o)))] for i in range(nr)]

        @pl.when(j == 0)
        def _():
            for group in loads:
                for copy in group:
                    copy.start()
            for i in range(nr):
                for copy in loads[i]:
                    copy.wait()
                rows = block(i)
                x = bufs[0][rows, :].astype(F32)
                if extra is not None:
                    x = x + bufs[1][rows, :].astype(F32) + vec_r[4:5, :] + vec_r[5:6, :]
                xhat, mean, rstd = normed(x)
                st_r[rows, 0:1] = mean
                st_r[rows, 1:2] = rstd
                h1_r[rows, :] = (xhat * vec_r[0:1, :] + vec_r[1:2, :]).astype(BF)
                h2_r[rows, :] = (xhat * vec_r[2:3, :] + vec_r[3:4, :]).astype(BF)
                for copy in stores[i]:
                    copy.start()

        @pl.when(j < nq)
        def _():
            for rows in row_blocks(n):
                for part in range(3):
                    at = part * HD
                    m = jnp.dot(h1_r[rows, :], wq_r[:, at:at + HD], preferred_element_type=F32) + bq_r[:, at:at + HD]
                    if part == 2:
                        mix_r[rows, at:at + HD] = m.astype(BF)
                    else:
                        mix_r[rows, at:at + 128] = turn(m[:, :128], cos_r[rows, :], sin_r[rows, :]).astype(BF)
                        mix_r[rows, at + 128:at + HD] = m[:, 128:].astype(BF)

        @pl.when(j >= nq)
        def _():
            for rows in row_blocks(n):
                for at in range(0, UB, 256):
                    cols = slice(at, at + 256)
                    f = jnp.dot(h2_r[rows, :], wu_r[:, cols], preferred_element_type=F32) + bu_r[:, cols]
                    phi = 0.5 * (1.0 + lax.erf(f * 0.7071067811865476))
                    a_r[rows, cols] = (f * phi).astype(BF)
                    gp_r[rows, cols] = (phi + f * (jnp.exp(-0.5 * f * f) * 0.3989422804014327)).astype(BF)

        host(2, ("second", 0))
        host(4, ("second", 1), ("third", 0))
        host(5, ("third", 1), ("last", 0), ("last", 1), ("close",))

        @pl.when(j == nq + nu - 1)
        def _():
            for group in stores:
                for copy in group:
                    copy.wait()

    whole = lambda j: (0, 0)
    qcol = lambda j: (0, jnp.minimum(j, nq - 1))
    ucol = lambda j: (0, jnp.maximum(j - nq, 0))
    far = pl.BlockSpec(memory_space=pl.ANY)
    ins = [far] * len(xs) + [
        spec((6, D), whole), spec((D, QB), qcol), spec((1, QB), qcol), spec((n, 128), whole, True), spec((n, 128), whole, True),
        spec((D, UB), ucol), spec((1, UB), ucol)] + [far] * ng
    outs = [far, far, spec((n, QB), qcol), spec((n, UB), ucol), spec((n, UB), ucol), spec((n, 128), whole)] + [far] * ng
    shapes = [jax.ShapeDtypeStruct(s, BF) for s in ((n, D), (n, D), (n, C), (n, U), (n, U))] + [jax.ShapeDtypeStruct((n, 128), F32)]
    DMA = pltpu.SemaphoreType.DMA
    scratch = [pltpu.VMEM((n, D), BF)] * (2 + len(xs)) + [DMA((len(xs), nr)), DMA((2, nr))]
    if ng:
        scratch += [DMA((ng, 9)), DMA((ng, 9)), DMA((ng,))]
        shapes += [jax.ShapeDtypeStruct((8,) + v.shape[1:], v.dtype) for v in shards]
    return call(kernel, (nq + nu,), ins, outs, shapes, scratch, ident=5 if ng else None, flops=2 * n * D * (C + U), nbytes=2 * (n * D * 3 + D * (C + U) + n * (C + 2 * U)), name="project")(*xs, vec, wq, bq, cos, sin, wu, bu, *(shards or ()))


def softmax_block(q, k, segq, segk, q0, k0):
    s = lax.dot_general(q, k, (((1,), (1,)), ((), ())), preferred_element_type=F32) * HD ** (-0.5)
    qi = q0 + lax.broadcasted_iota(jnp.int32, s.shape, 0)
    ki = k0 + lax.broadcasted_iota(jnp.int32, s.shape, 1)
    allowed = (segq == segk) & (ki <= qi)
    s = jnp.where(allowed, s, masked_score)
    top = jnp.max(s, axis=1, keepdims=True)
    e = jnp.exp(s - top)
    return e / jnp.sum(e, axis=1, keepdims=True)


def windows(n, qb):
    for i in range(n // qb):
        q0 = i * qb
        yield q0, max(0, q0 - MAXLEN)


def attend_forward(mixed, seg_col, seg_row):
    n, C = mixed.shape
    H = C // (3 * HD)
    qb = 256

    def kernel(q_r, k_r, v_r, sc_r, sr_r, o_r):
        for q0, k0 in windows(n, qb):
            qs, ks = slice(q0, q0 + qb), slice(k0, q0 + qb)
            p = softmax_block(q_r[qs, :], k_r[ks, :], sc_r[qs, :], sr_r[:, ks], q0, k0)
            o_r[qs, :] = jnp.dot(p.astype(BF), v_r[ks, :], preferred_element_type=F32).astype(BF)

    part = lambda t: spec((n, HD), lambda h: (0, 3 * h + t))
    return call(kernel, (H,), [part(0), part(1), part(2), spec((n, 1), lambda h: (0, 0)), spec((1, n), lambda h: (0, 0))],
                spec((n, HD), lambda h: (0, h)), jax.ShapeDtypeStruct((n, H * HD), BF),
                flops=H * n * 640 * HD * 4, nbytes=2 * n * C, name="attend")(mixed, mixed, mixed, seg_col, seg_row)


def attend_backward(mixed, dctx, seg_col, seg_row, cos, sin):
    n, C = mixed.shape
    H = C // (3 * HD)
    qb = 256
    scale = HD ** (-0.5)

    def kernel(q_r, k_r, v_r, do_r, sc_r, sr_r, cos_r, sin_r, o_r, dk_s, dv_s):
        def back(u, rows):
            c, s = cos_r[rows, :], -sin_r[rows, :]
            return jnp.concatenate([turn(u[:, :128], c, s), u[:, 128:]], axis=1).astype(BF)

        dk_s[...] = jnp.zeros_like(dk_s)
        dv_s[...] = jnp.zeros_like(dv_s)
        for q0, k0 in reversed(list(windows(n, qb))):
            qs, ks = slice(q0, q0 + qb), slice(k0, q0 + qb)
            q, k, do = q_r[qs, :], k_r[ks, :], do_r[qs, :]
            p = softmax_block(q, k, sc_r[qs, :], sr_r[:, ks], q0, k0)
            dp = lax.dot_general(do, v_r[ks, :], (((1,), (1,)), ((), ())), preferred_element_type=F32)
            delta = jnp.sum(p * dp, axis=1, keepdims=True)
            ds = (p * (dp - delta)).astype(BF)
            dq = jnp.dot(ds, k, preferred_element_type=F32) * scale
            dk_s[ks, :] += lax.dot_general(ds, q, (((0,), (0,)), ((), ())), preferred_element_type=F32)
            dv_s[ks, :] += lax.dot_general(p.astype(BF), do, (((0,), (0,)), ((), ())), preferred_element_type=F32)
            o_r[qs, :HD] = back(dq, qs)
            o_r[qs, HD:2 * HD] = back(dk_s[qs, :] * scale, qs)
            o_r[qs, 2 * HD:] = dv_s[qs, :].astype(BF)

    part = lambda t: spec((n, HD), lambda h: (0, 3 * h + t))
    whole = lambda h: (0, 0)
    return call(kernel, (H,), [part(0), part(1), part(2), spec((n, HD), lambda h: (0, h)), spec((n, 1), whole), spec((1, n), whole),
                spec((n, 128), whole), spec((n, 128), whole)],
                spec((n, 3 * HD), lambda h: (0, h)), jax.ShapeDtypeStruct((n, C), BF),
                scratch=[pltpu.VMEM((n, HD), F32), pltpu.VMEM((n, HD), F32)],
                flops=H * n * 640 * HD * 10, nbytes=4 * n * C, name="attend_back")(mixed, mixed, mixed, dctx, seg_col, seg_row, cos, sin)


def branch_out(ctx, act, wd, wn, cuts=None):
    n, R = ctx.shape
    U = act.shape[1]
    dp, _, w = wd.shape
    cuts = cuts or [0, n]
    parts = list(zip(cuts, cuts[1:]))

    def kernel(c_r, a_r, wd_r, wn_r, *o_rs):
        out = (jnp.dot(c_r[...], wd_r[...], preferred_element_type=F32) + jnp.dot(a_r[...], wn_r[...], preferred_element_type=F32)).astype(BF)
        for (low, high), o_r in zip(parts, o_rs):
            o_r[...] = out[low:high]

    whole = lambda s: (0, 0)
    pick = lambda s: (s, 0, 0)
    return call(kernel, (dp,), [spec((n, R), whole, True), spec((n, U), whole, True), spec((None, R, w), pick), spec((None, U, w), pick)],
                [spec((high - low, w), lambda s: (0, s)) for low, high in parts], [jax.ShapeDtypeStruct((high - low, dp * w), BF) for low, high in parts],
                flops=2 * n * dp * w * (R + U), nbytes=2 * (n * (R + U) + dp * w * (R + U + n)), name="branch")(ctx, act, wd, wn)


def back_in(gr, gp, wd, wn):
    n, D = gr.shape
    dp, R, w = wd.shape
    U = wn.shape[1]
    NB = 256
    nr, nu = R // NB, U // NB

    def kernel(g_r, gp_r, wd_r, wn_r, dc_r, df_r):
        j = pl.program_id(0)

        def times(w_r):
            acc = None
            for s in range(dp):
                t = lax.dot_general(g_r[:, s * w:(s + 1) * w], w_r[s], (((1,), (1,)), ((), ())), preferred_element_type=F32)
                acc = t if acc is None else acc + t
            return acc

        @pl.when(j < nr)
        def _():
            dc_r[...] = times(wd_r).astype(BF)

        @pl.when(j >= nr)
        def _():
            df_r[...] = (times(wn_r) * gp_r[...].astype(F32)).astype(BF)

    rc = lambda j: jnp.minimum(j, nr - 1)
    uc = lambda j: jnp.maximum(j - nr, 0)
    return call(kernel, (nr + nu,), [spec((n, D), lambda j: (0, 0), True), spec((n, NB), lambda j: (0, uc(j))),
                spec((dp, NB, w), lambda j: (0, rc(j), 0)), spec((dp, NB, w), lambda j: (0, uc(j), 0))],
                [spec((n, NB), lambda j: (0, rc(j))), spec((n, NB), lambda j: (0, uc(j)))],
                [jax.ShapeDtypeStruct((n, R), BF), jax.ShapeDtypeStruct((n, U), BF)],
                flops=2 * n * D * (R + U), nbytes=2 * (n * D + D * (R + U) + n * (R + 2 * U)), name="back_in")(gr, gp, wd, wn)


def back_out(dmix, df, wq, wu, base, extra, vec, stats):
    n, C = dmix.shape
    U = df.shape[1]
    D = wq.shape[0]
    NB = 256

    def kernel(*refs):
        if extra is None:
            dm_r, df_r, wq_r, wu_r, base_r, vec_r, st_r, e_r, g_r = refs
        else:
            dm_r, df_r, wq_r, wu_r, base_r, extra_r, vec_r, st_r, e_r, g_r = refs
        nt = (((1,), (1,)), ((), ()))
        d1 = lax.dot_general(dm_r[...], wq_r[...], nt, preferred_element_type=F32)
        d2 = lax.dot_general(df_r[...], wu_r[...], nt, preferred_element_type=F32)
        e_r[...] = (d1 * vec_r[0:1, :] + d2 * vec_r[2:3, :]).astype(BF)
        x = base_r[...].astype(F32)
        if extra is not None:
            x = x + extra_r[...].astype(F32) + vec_r[4:5, :] + vec_r[5:6, :]
        xhat = (x - st_r[:, 0:1]) * st_r[:, 1:2]
        g_r[0:1, :] = jnp.sum(d1 * xhat, axis=0, keepdims=True)
        g_r[1:2, :] = jnp.sum(d1, axis=0, keepdims=True)
        g_r[2:3, :] = jnp.sum(d2 * xhat, axis=0, keepdims=True)
        g_r[3:4, :] = jnp.sum(d2, axis=0, keepdims=True)

    whole = lambda j: (0, 0)
    col = lambda j: (0, j)
    row = lambda j: (j, 0)
    xs = [spec((n, NB), col)] + ([] if extra is None else [spec((n, NB), col)])
    args = [base] + ([] if extra is None else [extra])
    return call(kernel, (D // NB,), [spec((n, C), whole, True), spec((n, U), whole, True), spec((NB, C), row), spec((NB, U), row)] + xs +
                [spec((6, NB), col), spec((n, 128), whole)],
                [spec((n, NB), col), spec((4, NB), col)],
                [jax.ShapeDtypeStruct((n, D), BF), jax.ShapeDtypeStruct((4, D), F32)],
                flops=2 * n * D * (C + U), nbytes=2 * (n * (C + U) + D * (C + U) + n * D * 3), name="back_out")(dmix, df, wq, wu, *args, vec, stats)


def weight_grad(left, right, w=None):
    n, M = left.shape
    N = right.shape[1]
    MB = 256

    def kernel(l_r, r_r, o_r, s_r):
        g = lax.dot_general(l_r[...], r_r[...], (((0,), (0,)), ((), ())), preferred_element_type=F32)
        if w is None:
            o_r[...] = g.astype(BF)
        else:
            for s in range(N // w):
                o_r[s] = g[:, s * w:(s + 1) * w].astype(BF)

        @pl.when(pl.program_id(0) == 0)
        def _():
            s_r[...] = jnp.sum(r_r[...].astype(F32), axis=0, keepdims=True)

    whole = lambda j: (0, 0)
    if w is None:
        out, shape = spec((MB, N), lambda j: (j, 0)), (M, N)
    else:
        out, shape = spec((N // w, MB, w), lambda j: (0, j, 0)), (N // w, M, w)
    return call(kernel, (M // MB,), [spec((n, MB), lambda j: (0, j)), spec((n, N), whole, True)], [out, spec((1, N), whole)],
                [jax.ShapeDtypeStruct(shape, BF), jax.ShapeDtypeStruct((1, N), F32)],
                flops=2 * n * M * N, nbytes=2 * (n * M + n * N + M * N), name="wgrad")(left, right)


def norm_back(gout, e, base, extra, vec, stats):
    n, D = base.shape
    RB = 256

    def kernel(g_r, e_r, base_r, extra_r, vec_r, st_r, dx_r, low_r, sum_r):
        x = base_r[...].astype(F32) + extra_r[...].astype(F32) + vec_r[4:5, :] + vec_r[5:6, :]
        dx = g_r[...].astype(F32) + norm_pullback(x, e_r, st_r)
        dx_r[...] = dx
        low_r[...] = dx.astype(BF)

        @pl.when(pl.program_id(0) == 0)
        def _():
            sum_r[...] = jnp.zeros_like(sum_r)

        sum_r[...] += jnp.sum(dx, axis=0, keepdims=True)

    row = lambda i: (i, 0)
    whole = lambda i: (0, 0)
    rows = spec((RB, D), row)
    shapes = [jax.ShapeDtypeStruct((n, D), F32), jax.ShapeDtypeStruct((n, D), BF), jax.ShapeDtypeStruct((1, D), F32)]
    return call(kernel, (n // RB,), [rows] * 4 + [spec((6, D), whole), spec((RB, 128), row)], [rows, rows, spec((1, D), whole)], shapes,
                flops=10 * n * D, nbytes=16 * n * D, name="norm_back")(gout, e, base, extra, vec, stats)


def norm_pullback(x, e_r, st_r):
    xhat = (x - st_r[:, 0:1]) * st_r[:, 1:2]
    ev = e_r[...].astype(F32)
    me = jnp.mean(ev, axis=1, keepdims=True)
    mx = jnp.mean(ev * xhat, axis=1, keepdims=True)
    return (ev - me - xhat * mx) * st_r[:, 1:2]


def finish(gout, e, base, extra, branches, held, live, stats):
    n, D = base.shape
    RB = 128
    counts = [b.shape[0] // RB for b in branches]
    starts = [sum(counts[:k]) for k in range(len(counts))]

    def kernel(g_r, e_r, base_r, extra_r, *refs):
        branch_rs, (held_r, live_r, st_r, dx_r, out_r) = refs[:len(branches)], refs[len(branches):]
        i = pl.program_id(0)
        x = base_r[...].astype(F32)
        dx_r[...] = g_r[...] + norm_pullback(x, e_r, st_r)
        for k, b_r in enumerate(branch_rs):
            @pl.when((i >= starts[k]) & (i < starts[k] + counts[k]))
            def _(b_r=b_r):
                last = base_r[...].astype(F32) + extra_r[...].astype(F32) + b_r[...].astype(F32) + held_r[...]
                out_r[...] = jnp.where(live_r[...] > 0.0, last, 0.0).astype(BF)

    row = lambda i: (i, 0)
    whole = lambda i: (0, 0)
    rows = spec((RB, D), row)
    part = lambda k: spec((RB, D), lambda i: (jnp.clip(i - starts[k], 0, counts[k] - 1), 0))
    ins = [rows] * 4 + [part(k) for k in range(len(branches))] + [spec((1, D), whole), spec((RB, 1), row), spec((RB, 128), row)]
    return call(kernel, (n // RB,), ins, [rows, rows], [jax.ShapeDtypeStruct((n, D), F32), jax.ShapeDtypeStruct((n, D), BF)],
                flops=10 * n * D, nbytes=18 * n * D, name="finish")(gout, e, base, extra, *branches, held, live, stats)


MESH = pl.DeviceIdType.MESH


class Spot:
    def __init__(self):
        i = lax.axis_index("dp")
        c, x, y = lax.rem(i, 2), lax.rem(lax.div(i, 2), 2), lax.div(i, 4)
        self.me, self.core = i, c
        self.dx, self.dy, self.dc = 2 - 4 * x, 4 - 8 * y, 1 - 2 * c
        self.nx, self.ny, self.nc = i + self.dx, i + self.dy, i + self.dc
        self.diag = i + self.dx + self.dy
        z = lax.axis_index("mp")
        self.z = z
        self.outer = (z == 0) | (z == 3)
        self.inner = (z == 1) | (z == 2)
        self.pair = z + 1 - 2 * lax.rem(z, 2)
        self.across = 3 - z

    def meet(self, line):
        barrier = pltpu.get_barrier_semaphore()
        for peer in (self.nx, self.ny, self.nc):
            pl.semaphore_signal(barrier, inc=1, device_id={"dp": peer}, device_id_type=MESH)
        if line:
            pl.semaphore_signal(barrier, inc=1, device_id={"mp": self.pair}, device_id_type=MESH)

            @pl.when(self.inner)
            def _():
                pl.semaphore_signal(barrier, inc=1, device_id={"mp": self.across}, device_id_type=MESH)

            @pl.when(self.inner)
            def _():
                pl.semaphore_wait(barrier, 5)

            @pl.when(self.outer)
            def _():
                pl.semaphore_wait(barrier, 4)
        else:
            pl.semaphore_wait(barrier, 3)


def send_to(axis, peer, src, dst, send, recv):
    return pltpu.make_async_remote_copy(src_ref=src, dst_ref=dst, send_sem=send, recv_sem=recv, device_id={axis: peer}, device_id_type=MESH)


class Gather:
    copies = 9

    def __init__(self, spot, items, send, recv, local):
        self.spot, self.items, self.send, self.recv, self.local = spot, items, send, recv, local
        self.sent = []
        self.own = []

    def go(self, k, n, peer, src, dst):
        send_to("dp", peer, src, dst, self.send.at[k, n], self.recv.at[k, n]).start()
        self.sent.append((k, n, peer, src, dst))

    def arrived(self, k, n, dst):
        send_to("dp", self.spot.nc, dst, dst, self.send.at[k, n], self.recv.at[k, n]).wait_recv()

    def first(self, k):
        s, (src, out) = self.spot, self.items[k]
        for n, peer in enumerate((s.nx, s.ny, s.nc)):
            self.go(k, n, peer, src, out.at[s.me])
        pltpu.make_async_copy(src, out.at[s.me], self.local.at[k]).start()
        self.own.append(k)

    def halves(self, k):
        h = self.items[k][1].shape[1] // 2
        return pl.ds(0, h), pl.ds(h, h)

    def second(self, k):
        s, (_, out) = self.spot, self.items[k]
        low, high = self.halves(k)
        self.arrived(k, 0, out.at[s.nx])
        self.go(k, 3, s.ny, out.at[s.nx, high], out.at[s.nx, high])
        self.go(k, 4, s.nc, out.at[s.nx], out.at[s.nx])
        self.arrived(k, 1, out.at[s.ny])
        self.go(k, 5, s.nx, out.at[s.ny, low], out.at[s.ny, low])
        self.go(k, 6, s.nc, out.at[s.ny], out.at[s.ny])

    def third(self, k):
        s, (_, out) = self.spot, self.items[k]
        low, high = self.halves(k)
        self.arrived(k, 3, out.at[s.diag, high])
        self.go(k, 7, s.nc, out.at[s.diag, high], out.at[s.diag, high])
        self.arrived(k, 5, out.at[s.diag, low])
        self.go(k, 8, s.nc, out.at[s.diag, low], out.at[s.diag, low])

    def last(self, k):
        s, (_, out) = self.spot, self.items[k]
        low, high = self.halves(k)
        self.arrived(k, 2, out.at[s.nc])
        self.arrived(k, 4, out.at[s.nx + s.dc])
        self.arrived(k, 6, out.at[s.ny + s.dc])
        self.arrived(k, 7, out.at[s.diag + s.dc, high])
        self.arrived(k, 8, out.at[s.diag + s.dc, low])

    def close(self):
        for k in self.own:
            src, out = self.items[k]
            pltpu.make_async_copy(src, out.at[self.spot.me], self.local.at[k]).wait()
        for k, n, peer, src, dst in self.sent:
            send_to("dp", peer, src, dst, self.send.at[k, n], self.recv.at[k, n]).wait_send()


AHEAD, LAG, BACK = 3, 1, 5


class LineSum:
    copies = 3

    def __init__(self, spot, pairs, stage, land, swap, send, recv, local):
        self.spot, self.stage, self.land, self.swap = spot, stage, land, swap
        self.send, self.recv, self.local = send, recv, local
        self.rows = stage.shape[1]
        self.parts, self.outs = [], []
        for part, start, out, rows in pairs:
            for at in range(0, rows, self.rows):
                self.parts.append(part.at[pl.ds(start + at, self.rows)])
                self.outs.append(out.at[pl.ds(at, self.rows)])
        self.chunks = len(self.parts)

    def cut(self, k):
        return pl.ds(k * self.rows, self.rows)

    def copy(self, k, n):
        s, rows = self.spot, self.cut(k)
        if n == 0:
            peer, src, dst = s.pair, self.parts[k], self.land
        elif n == 1:
            peer, src, dst = s.across, self.land.at[rows], self.swap
        else:
            peer, src, dst = s.pair, self.swap.at[rows], self.swap
        return send_to("mp", peer, src, dst.at[rows], self.send.at[k, n], self.recv.at[k, n])

    def keep(self, k):
        rows = self.cut(k)
        return pltpu.make_async_copy(self.swap.at[rows], self.outs[k], self.local.at[k])

    def load(self, k):
        return pltpu.make_async_copy(self.parts[k], self.stage.at[k % 2], self.local.at[self.chunks + k % 2])

    def add(self, k, dst, one, two, base):
        step = 32

        @pl.loop(0, self.rows // step)
        def _(i):
            rows = pl.ds(pl.multiple_of(k * self.rows + i * step, step), step)
            there = pl.ds(pl.multiple_of(base + i * step, step), step)
            dst[rows, :] = (one[there, :].astype(F32) + two[rows, :].astype(F32)).astype(BF)

    def send_step(self, t):
        n = self.chunks

        @pl.when(self.spot.outer)
        def _():
            if 0 <= t - AHEAD < n:
                self.copy(t - AHEAD, 0).wait_send()
            if t < n:
                self.copy(t, 0).start()
            if 0 <= t - BACK < n:
                self.copy(t - BACK, 2).wait_recv()
                self.keep(t - BACK).start()

    def add_step(self, t):
        n = self.chunks

        @pl.when(self.spot.inner)
        def _():
            if t < n:
                if t == 0:
                    self.load(0).start()
                if t + 1 < n:
                    self.load(t + 1).start()
                self.load(t).wait()
                self.copy(t, 0).wait_recv()
                self.add(t, self.land, self.stage.at[t % 2], self.land, 0)
                self.copy(t, 1).start()
            if 0 <= t - LAG < n:
                self.copy(t - LAG, 1).wait_recv()
                self.copy(t - LAG, 1).wait_send()
                self.add(t - LAG, self.swap, self.land, self.swap, (t - LAG) * self.rows)
                self.copy(t - LAG, 2).start()
                self.keep(t - LAG).start()

    def begin(self):
        self.sent_to, self.added_to = 0, 0
        for _ in range(AHEAD):
            self.send_step(self.sent_to)
            self.sent_to += 1

    def slot(self):
        if self.added_to < self.chunks + LAG:
            self.add_step(self.added_to)
            self.added_to += 1
        if self.sent_to < self.chunks + BACK:
            self.send_step(self.sent_to)
            self.sent_to += 1

    def finish(self):
        while self.added_to < self.chunks + LAG or self.sent_to < self.chunks + BACK:
            self.slot()

    def close(self):
        for k in range(self.chunks):
            self.keep(k).wait()

        @pl.when(self.spot.inner)
        def _():
            for k in range(self.chunks):
                self.copy(k, 2).wait_send()


class Scatter:
    copies = 10

    def __init__(self, spot, items, own, sib, fx, fy, gx, gy, send, recv, local):
        self.spot, self.items = spot, items
        self.own, self.sib, self.fx, self.fy, self.gx, self.gy = own, sib, fx, fy, gx, gy
        self.send, self.recv, self.local = send, recv, local
        self.sent = []

    def go(self, k, n, peer, src, dst):
        send_to("dp", peer(), src(), dst(), self.send.at[k, n], self.recv.at[k, n]).start()
        self.sent.append((k, n, src))

    def arrived(self, k, n, dst):
        send_to("dp", self.spot.nc, dst, dst, self.send.at[k, n], self.recv.at[k, n]).wait_recv()

    def hand(self, k):
        s, grad = self.spot, self.items[k][0]
        for m, slot in enumerate((s.me, s.nx, s.ny, s.diag)):
            self.go(k, m, lambda: s.nc, lambda slot=slot: grad.at[slot + s.dc], lambda m=m: self.sib[k].at[m])

    def hold(self, k):
        for m in range(4):
            self.load(k, m).start()

    def first(self, k):
        self.hand(k)
        self.hold(k)

    def load(self, k, m):
        s = self.spot
        slot = (s.me, s.nx, s.ny, s.diag)[m]
        return pltpu.make_async_copy(self.items[k][0].at[slot], self.own[k].at[m], self.local.at[k, m])

    def over(self, r, c, body, start=0):
        step = 16
        while step * 2 * c <= 32768 and r % (step * 2) == 0:
            step *= 2

        @pl.loop(0, r // step)
        def _(i):
            body(pl.ds(pl.multiple_of(i * step, step), step), pl.ds(pl.multiple_of(start + i * step, step), step))

    def second(self, k):
        s = self.spot
        own, sib = self.own[k], self.sib[k]
        _, r, c = own.shape
        h = r // 2
        low, high = pl.ds(0, h), pl.ds(h, h)
        for m in (3, 1, 2, 0):
            self.load(k, m).wait()
            self.arrived(k, m, sib.at[m])

            def add(rows, _, m=m):
                own[m, rows, :] = (own[m, rows, :].astype(F32) + sib[m, rows, :].astype(F32)).astype(BF)

            self.over(r, c, add)
            if m == 3:
                self.go(k, 5, lambda: s.nx, lambda: own.at[3, low], lambda: self.fx[k].at[1])
                self.go(k, 7, lambda: s.ny, lambda: own.at[3, high], lambda: self.fy[k].at[1])
            if m == 1:
                self.go(k, 4, lambda: s.nx, lambda: own.at[1, low], lambda: self.fx[k].at[0])
            if m == 2:
                self.go(k, 6, lambda: s.ny, lambda: own.at[2, high], lambda: self.fy[k].at[0])

    def third(self, k):
        s = self.spot
        own, fx, fy = self.own[k], self.fx[k], self.fy[k]
        _, r, c = own.shape
        h = r // 2
        self.arrived(k, 5, fx.at[1])

        def add_low(rows, _):
            fx[1, rows, :] = (own[2, rows, :].astype(F32) + fx[1, rows, :].astype(F32)).astype(BF)

        self.over(h, c, add_low)
        self.go(k, 8, lambda: s.ny, lambda: fx.at[1], lambda: self.gy[k])
        self.arrived(k, 7, fy.at[1])

        def add_high(rows, there):
            fy[1, rows, :] = (own[1, there, :].astype(F32) + fy[1, rows, :].astype(F32)).astype(BF)

        self.over(h, c, add_high, h)
        self.go(k, 9, lambda: s.nx, lambda: fy.at[1], lambda: self.gx[k])

    def last(self, k):
        own, out = self.own[k], self.items[k][1]
        fx, fy, gx, gy = self.fx[k], self.fy[k], self.gx[k], self.gy[k]
        _, r, c = own.shape
        h = r // 2
        self.arrived(k, 4, fx.at[0])
        self.arrived(k, 8, gy)

        def low(rows, _):
            out[rows, :] = own[0, rows, :].astype(F32) + fx[0, rows, :].astype(F32) + gy[rows, :].astype(F32)

        self.over(h, c, low)
        self.arrived(k, 6, fy.at[0])
        self.arrived(k, 9, gx)

        def high(rows, there):
            out[there, :] = own[0, there, :].astype(F32) + fy[0, rows, :].astype(F32) + gx[rows, :].astype(F32)

        self.over(h, c, high, h)

    def close(self):
        for k, n, src in self.sent:
            send_to("dp", self.spot.nc, src(), src(), self.send.at[k, n], self.recv.at[k, n]).wait_send()


def link_kernel(name, ident, shards, layers, part=None, chunks=16):
    ng = len(shards)
    HBM = pl.BlockSpec(memory_space=pl.ANY)
    DMA = pltpu.SemaphoreType.DMA
    parts = [] if part is None else [part]
    shapes = [jax.ShapeDtypeStruct((8,) + (v.shape if l is None else v.shape[1:]), v.dtype) for v, l in zip(shards, layers)]
    shapes += [jax.ShapeDtypeStruct(v.shape, BF) for v in parts]
    scratch = [DMA((ng, 9)), DMA((ng, 9)), DMA((ng,))]
    for v in parts:
        scratch += [pltpu.VMEM((2, v.shape[0] // chunks, v.shape[1]), BF), pltpu.VMEM(v.shape, BF), pltpu.VMEM(v.shape, BF), DMA((chunks, 3)), DMA((chunks, 3)), DMA((chunks + 2,))]

    def kernel(*refs):
        refs = list(refs)
        take = lambda n: [refs.pop(0) for _ in range(n)]
        src, ins, full, totals = take(ng), take(len(parts)), take(ng), take(len(parts))
        spot = Spot()
        spot.meet(bool(parts))
        G = Gather(spot, [(a if l is None else a.at[l], b) for a, l, b in zip(src, layers, full)], *take(3))
        if parts:
            stage, land, swap, send, recv, local = take(6)
            line = LineSum(spot, [(ins[0], 0, totals[0], ins[0].shape[0])], stage, land, swap, send, recv, local)
            plan_sum_gather(G, line)
            line.close()
        else:
            plan_gather(G)
        G.close()

    nbytes = sum(v.size * 2 for v in parts) + sum(8 * v.size for v in shards)
    return pl.pallas_call(
        kernel, in_specs=[HBM] * (ng + len(parts)), out_specs=[HBM] * (ng + len(parts)), out_shape=shapes, scratch_shapes=scratch,
        compiler_params=pltpu.CompilerParams(vmem_limit_bytes=VM, collective_id=ident, has_side_effects=True),
        cost_estimate=pl.CostEstimate(flops=0, bytes_accessed=nbytes, transcendentals=0), name=name)(*shards, *parts)


def plan_gather(G):
    n = len(G.items)
    for stage in (G.first, G.second, G.third, G.last):
        for k in range(n):
            stage(k)


class Products:
    def __init__(self, core, lefts, rights, grads, rhs, lbuf, obuf, rsem, lsem, osem):
        self.core = core
        self.lefts, self.rights, self.grads = lefts, rights, grads
        self.rhs, self.lbuf, self.obuf, self.rsem, self.lsem, self.osem = rhs, lbuf, obuf, rsem, lsem, osem

    def right(self, i, slot):
        return pltpu.make_async_copy(self.rights[i], self.rhs[slot], self.rsem.at[i])

    def split(self, k):
        slots, r, _ = self.grads[k].shape
        return r == 256 and self.lefts[k].shape[1] == slots * r

    def block(self, k, m):
        if self.split(k):
            late = m // 4 if isinstance(m, int) else lax.div(m, 4)
            return 2 * (m - 4 * late) + 1 - self.core - late + 2 * late * self.core
        return m

    def columns(self, block):
        return pl.ds(block * 256 if isinstance(block, int) else pl.multiple_of(block * 256, 256), 256)

    def left(self, k, m):
        odd = m % 2 if isinstance(m, int) else lax.rem(m, 2)
        return pltpu.make_async_copy(self.lefts[k].at[:, self.columns(self.block(k, m))], self.lbuf.at[odd], self.lsem.at[odd])

    def stores(self, k, m):
        odd = m % 2 if isinstance(m, int) else lax.rem(m, 2)
        grad, o, sem = self.grads[k], self.obuf.at[odd], self.osem.at[odd]
        slots, _, c = grad.shape
        block = self.block(k, m)
        if self.split(k):
            return [pltpu.make_async_copy(o.at[:, pl.ds(0, c)], grad.at[block], sem.at[0])]
        return [pltpu.make_async_copy(o.at[:, pl.ds(s * c, c)], grad.at[s, self.columns(block)], sem.at[s]) for s in range(slots)]

    def run(self, k, slot, start, stop, hooks):
        right = self.rhs[slot]
        width = right.shape[1]
        self.left(k, start).start()

        @pl.loop(start, stop)
        def _(m):
            self.left(k, m).wait()

            @pl.when(m + 1 < stop)
            def _():
                self.left(k, m + 1).start()

            @pl.when(m >= start + 2)
            def _():
                for copy in self.stores(k, m - 2):
                    copy.wait()

            g = lax.dot_general(self.lbuf[lax.rem(m, 2)], right[...], (((0,), (0,)), ((), ())), preferred_element_type=F32)
            self.obuf[lax.rem(m, 2), :, :width] = g.astype(BF)
            for copy in self.stores(k, m):
                copy.start()
            for at in sorted(hooks):
                pl.when(m == at)(hooks[at])

        for m in (stop - 2, stop - 1):
            for copy in self.stores(k, m):
                copy.wait()

    def sums(self, slot, out):
        right = self.rhs[slot]
        out[...] = jnp.zeros_like(out)

        @pl.loop(0, right.shape[0] // 64)
        def _(i):
            out[...] += jnp.sum(right[pl.ds(pl.multiple_of(i * 64, 64), 64), :].astype(F32), axis=0, keepdims=True)


def plan_sum_gather(G, line):
    for k in range(4):
        G.first(k)
    stages = {5: [("second", 0), ("second", 1)], 9: [("second", 2)], 12: [("second", 3)], 14: [("third", 0), ("third", 1)], 15: [("third", 2)],
              17: [("third", 3)]}
    line.begin()
    for at in range(18):
        line.slot()
        for name, k in stages.get(at, ()):
            getattr(G, name)(k)
    line.finish()
    for k in range(4):
        G.last(k)


def sum_scatter(ident, e, more, lefts, rights, step=64):
    n, D = e.shape
    HBM = pl.BlockSpec(memory_space=pl.ANY)
    VM_ = pl.BlockSpec(memory_space=pltpu.VMEM)
    C, U = rights[1].shape[1], rights[2].shape[1]
    w = D // 8
    dims = [(lefts[0].shape[1], w), (lefts[1].shape[1], w), (w, C), (w, U)]
    DMA = pltpu.SemaphoreType.DMA
    more_rows = more.shape[0]
    chunks = (n + more_rows) // step
    outs = [HBM] * 2 + [HBM] * 4 + [VM_] * 4 + [VM_] * 3
    shapes = [jax.ShapeDtypeStruct(e.shape, BF), jax.ShapeDtypeStruct((more_rows, D), BF)] + [jax.ShapeDtypeStruct((8,) + d, BF) for d in dims] + [jax.ShapeDtypeStruct(d, F32) for d in dims]
    shapes += [jax.ShapeDtypeStruct((1, C), F32), jax.ShapeDtypeStruct((1, U), F32), jax.ShapeDtypeStruct((1, D), F32)]
    scratch = [pltpu.VMEM((2, step, D), BF)] + [pltpu.VMEM((n + more_rows, D), BF)] * 2 + [DMA((chunks, 3)), DMA((chunks, 3)), DMA((chunks + 2,))]
    cut = [dims[0], (dims[1][0] // 2, w), (dims[1][0] // 2, w), dims[2], dims[3]]
    scratch += [DMA((5, 10)), DMA((5, 10)), DMA((5, 4))]
    for r, c in cut:
        scratch += [pltpu.VMEM((4, r, c), BF), pltpu.VMEM((4, r, c), BF), pltpu.VMEM((2, r // 2, c), BF), pltpu.VMEM((2, r // 2, c), BF),
                    pltpu.VMEM((r // 2, c), BF), pltpu.VMEM((r // 2, c), BF)]
    wide = max(D, U)
    scratch += [pltpu.VMEM((n, wide), BF), pltpu.VMEM((n, C), BF), pltpu.VMEM((2, n, 256), BF), pltpu.VMEM((2, 256, wide), BF), DMA((3,)), DMA((2,)), DMA((2, 8))]
    assert D == U

    def kernel(*refs):
        refs = list(refs)
        take = lambda k: [refs.pop(0) for _ in range(k)]
        (e_r, more_r), left_rs, right_rs = take(2), take(4), take(3)
        (total, more_total), grads, owned, sum_rs = take(2), take(4), take(4), take(3)
        stage, land, swap, send, recv, local = take(6)
        spot = Spot()
        spot.meet(True)
        line = LineSum(spot, [(e_r, 0, total, n), (more_r, 0, more_total, more_rows)], stage, land, swap, send, recv, local)
        send, recv, local = take(3)
        bufs = [take(6) for _ in range(5)]
        half = cut[1][0]
        low, high = pl.ds(0, half), pl.ds(half, half)
        items = [(grads[0], owned[0]), (grads[1].at[:, low], owned[1].at[low]), (grads[1].at[:, high], owned[1].at[high])]
        items += [(grads[2], owned[2]), (grads[3], owned[3])]
        S = Scatter(spot, items, *[[b[i] for b in bufs] for i in range(6)], send, recv, local)
        wide_r, narrow_r, lbuf, obuf, rsem, lsem, osem = take(7)
        W = Products(spot.core, left_rs, right_rs, grads, (wide_r, narrow_r), lbuf, obuf, rsem, lsem, osem)
        W.right(0, 0).start()
        W.right(1, 1).start()
        def steps(*what):
            def go():
                for step, *args in what:
                    step(*args)

            return go

        slot = (line.slot,)
        line.begin()
        W.right(0, 0).wait()
        W.run(1, 0, 0, 4, {1: steps(slot)})
        S.first(1)
        line.slot()
        W.run(0, 0, 0, left_rs[0].shape[1] // 256, {})
        S.first(0)
        S.second(1)
        line.slot()
        W.run(1, 0, 4, 8, {5: steps(slot)})
        S.first(2)
        W.sums(0, sum_rs[2])
        W.right(2, 0).start()
        S.second(0)
        line.slot()
        W.right(1, 1).wait()
        W.run(2, 1, 0, 8, {0: steps((S.second, 2), (S.third, 1)), 2: steps(slot), 5: steps((S.hand, 3), slot)})
        S.hold(3)
        line.slot()
        S.third(0)
        S.second(3)
        W.right(2, 0).wait()
        W.run(3, 0, 0, 8, {1: steps(slot), 3: steps((S.third, 2)), 4: steps(slot), 5: steps((S.hand, 4)), 6: steps(slot)})
        S.hold(4)
        line.slot()
        S.second(4)
        W.sums(1, sum_rs[0])
        line.slot()
        S.third(3)
        line.slot()
        W.sums(0, sum_rs[1])
        line.slot()
        S.last(0)
        S.last(1)
        line.slot()
        S.last(2)
        line.slot()
        line.slot()
        S.third(4)
        line.slot()
        S.last(3)
        line.finish()
        S.last(4)
        line.close()
        S.close()

    flops = 2 * n * D * (lefts[0].shape[1] + lefts[1].shape[1] + C + U)
    got = pl.pallas_call(
        kernel, in_specs=[HBM] * 9, out_specs=outs, out_shape=shapes, scratch_shapes=scratch,
        compiler_params=pltpu.CompilerParams(vmem_limit_bytes=VM2, collective_id=ident, has_side_effects=True),
        cost_estimate=pl.CostEstimate(flops=flops, bytes_accessed=2 * n * D * 12, transcendentals=0), name="sum_scatter")(e, more, *lefts, *rights)
    gd, gn, gq, gu = got[6:10]
    return got[0], got[1], (gq, gd, gu, gn), got[10], got[11], got[12]


def small_sum(pieces, shared):
    ndp, r, _ = pieces.shape
    nmp = lax.axis_size("mp")

    def kernel(x_r, o_r, land, line, send, recv, send2, recv2):
        i, z = lax.axis_index("dp"), lax.axis_index("mp")
        barrier = pltpu.get_barrier_semaphore()
        for s in range(1, ndp):
            pl.semaphore_signal(barrier, inc=1, device_id={"dp": lax.rem(i + s, ndp)}, device_id_type=MESH)
        for s in range(1, nmp):
            pl.semaphore_signal(barrier, inc=1, device_id={"mp": lax.rem(z + s, nmp)}, device_id_type=MESH)
        pl.semaphore_wait(barrier, ndp + nmp - 2)
        first = [send_to("dp", lax.rem(i + s, ndp), x_r.at[lax.rem(i + s, ndp)], land.at[i], send.at[s], recv.at[s]) for s in range(1, ndp)]
        for copy in first:
            copy.start()
        land[pl.ds(i, 1)] = x_r[pl.ds(i, 1)]
        for s in range(1, ndp):
            there = land.at[lax.rem(i - s + ndp, ndp)]
            send_to("dp", i, there, there, send.at[s], recv.at[s]).wait_recv()
        acc = land[0]
        for j in range(1, ndp):
            acc = acc + land[j]
        o_r[...] = acc
        line[pl.ds(z, 1)] = acc[None, :shared]
        second = [send_to("mp", lax.rem(z + s, nmp), line.at[z], line.at[z], send2.at[s], recv2.at[s]) for s in range(1, nmp)]
        for copy in second:
            copy.start()
        for s in range(1, nmp):
            there = line.at[lax.rem(z - s + nmp, nmp)]
            send_to("mp", z, there, there, send2.at[s], recv2.at[s]).wait_recv()
        acc = line[0]
        for j in range(1, nmp):
            acc = acc + line[j]
        o_r[:shared] = acc
        for copy in first + second:
            copy.wait_send()

    VM_ = pl.BlockSpec(memory_space=pltpu.VMEM)
    DMA = pltpu.SemaphoreType.DMA
    return pl.pallas_call(
        kernel, in_specs=[VM_], out_specs=VM_, out_shape=jax.ShapeDtypeStruct((r, 128), F32),
        scratch_shapes=[pltpu.VMEM(pieces.shape, F32), pltpu.VMEM((nmp, shared, 128), F32), DMA((ndp,)), DMA((ndp,)), DMA((nmp,)), DMA((nmp,))],
        compiler_params=pltpu.CompilerParams(vmem_limit_bytes=VM // 4, collective_id=6, has_side_effects=True), name="small_sum")(pieces)


def adam_update(weight, grad, first, second):
    first_new = beta_one * first + (1.0 - beta_one) * grad
    second_new = beta_two * second + (1.0 - beta_two) * grad * grad
    mean_hat = first_new / (1.0 - beta_one**ADAM_STEP)
    square_hat = second_new / (1.0 - beta_two**ADAM_STEP)
    new_weight = weight - rate * (mean_hat / (jnp.sqrt(square_hat) + adam_eps) + decay * weight)
    return grad, first_new, second_new, new_weight - weight


def adam_layer(layer, weights, grads, firsts, seconds, before):
    steps = 4
    blocks = [(w.shape[1] // steps, w.shape[2]) for w in weights]

    def kernel(*refs):
        ins, outs = refs[:16], refs[-16:]
        for i in range(4):
            g = ins[4 + i][...].astype(F32)
            made = adam_update(ins[i][...].astype(F32), g, ins[8 + i][...], ins[12 + i][...])
            for k in range(4):
                outs[4 * i + k][...] = made[k]

    at = lambda b: spec((None,) + b, lambda j: (layer, j, 0))
    ins = [at(b) for b in blocks] + [spec(b, lambda j: (j, 0)) for b in blocks] + [at(b) for b in blocks] * 2
    args = [*weights, *grads, *firsts, *seconds]
    alias = {}
    if before is not None:
        ins += [pl.BlockSpec(memory_space=pl.ANY)] * 16
        args += list(before)
        alias = {16 + i: i for i in range(16)}
    shapes = [jax.ShapeDtypeStruct(w.shape, F32) for w in weights for _ in range(4)]
    count = sum(w.shape[1] * w.shape[2] for w in weights)
    return pl.pallas_call(
        kernel, grid=(steps,), in_specs=ins, out_specs=[at(b) for b in blocks for _ in range(4)], out_shape=shapes,
        input_output_aliases=alias, compiler_params=pltpu.CompilerParams(vmem_limit_bytes=VM),
        cost_estimate=pl.CostEstimate(flops=20 * count, bytes_accessed=30 * count, transcendentals=0), name="adam")(*args)


def layout(lengths_row, rows):
    slots = lengths_row.shape[0]
    number = jnp.arange(slots, dtype=jnp.int32)
    ends = jnp.sum(jnp.where(number[None, :] <= number[:, None], lengths_row[None, :], 0), axis=1)
    starts = ends - lengths_row
    index = jnp.arange(rows, dtype=jnp.int32)
    inside = (index[:, None] >= starts[None, :]) & (index[:, None] < ends[None, :])
    valid = jnp.any(inside, axis=1)
    slot = jnp.sum(jnp.where(inside, number[None, :], 0), axis=1)
    first = jnp.sum(jnp.where(inside, starts[None, :], 0), axis=1)
    segment = jnp.where(valid, slot, slots + index)
    return segment, index - first, valid


class PlainLinks:
    def weights(self, shards, layer):
        wq, wd, wu, wn = [w[layer] for w in shards]
        rows = lambda v: lax.all_gather(v, "dp", axis=0, tiled=True)
        stack = lambda v: lax.all_gather(v, "dp", axis=0, tiled=False)
        return rows(wq), stack(wd), rows(wu), stack(wn)

    def share(self, v):
        return lax.psum(v, "mp")

    def owned(self, grads):
        cut = lambda g: lax.psum_scatter(g, "dp", scatter_dimension=0, tiled=True)
        gq, gd, gu, gn = grads
        return cut(gq), cut(gd)[0], cut(gu), cut(gn)[0]

    def small(self, pieces, shared):
        total = lax.psum(pieces, "dp")[lax.axis_index("dp")]
        return jnp.concatenate([lax.psum(total[:shared], "mp"), total[shared:]])

    def begin(self, shards, flat):
        return self.weights(shards, 0), lax.all_gather(flat, "dp", axis=0, tiled=False), None

    def middle(self, branch, shards):
        return self.share(branch), self.weights(shards, 1)

    def turn(self, e, more, lefts, rights, ident):
        ctx, act, h1, h2 = lefts
        gr, dmix, df = rights
        w = gr.shape[1] // lax.axis_size("dp")
        gd, low_sums = weight_grad(ctx, gr, w=w)
        gn, _ = weight_grad(act, gr, w=w)
        gq, qsum = weight_grad(h1, dmix)
        gu, usum = weight_grad(h2, df)
        return self.share(e), self.share(more), self.owned((gq, gd, gu, gn)), qsum, usum, low_sums


class ChipLinks:
    def full(self, got):
        wq, wd, wu, wn = got
        return wq.reshape(-1, wq.shape[2]), wd, wu.reshape(-1, wu.shape[2]), wn

    def begin(self, shards, flat):
        wq, wd, wu, wn = shards
        flat, wq, wu = link_kernel("gather", 1, [flat, wq, wu], [None, 0, 0])
        return (wq.reshape(-1, wq.shape[2]), None, wu.reshape(-1, wu.shape[2]), None), flat, (wd, wn)

    def middle(self, branch, shards):
        got = link_kernel("sum_gather", 2, shards, [1] * 4, branch)
        return got[4], self.full(got[:4])

    def turn(self, e, more, lefts, rights, ident):
        return sum_scatter(ident, e, more, lefts, rights)

    def small(self, pieces, shared):
        return small_sum(pieces, shared)


def flatten_small(parts):
    flat = jnp.concatenate([p.reshape(-1) for p in parts])
    return jnp.pad(flat, (0, -flat.size % 4096)).reshape(-1, 128)


def unpack_small(got, parts):
    got = got.reshape(got.shape[0], -1)
    out, at = [], 0
    for p in parts:
        piece = got[:, at:at + p.size].reshape((-1,) + p.shape)
        out.append(jnp.moveaxis(piece, 0, 2).reshape(p.shape[0], p.shape[1], -1))
        at += p.size
    return out


def body(links, tokens_in, cotangent, seq_lengths, *params):
    weights, small = params[:4], params[4:7]
    firsts, small_firsts = params[7:11], params[11:14]
    seconds, small_seconds = params[14:18], params[18:21]
    rows, D = tokens_in.shape
    segment, position, valid = layout(seq_lengths[0], rows)
    cos, sin = rope_tables(position)
    seg_col, seg_row = segment[:, None], segment[None, :]
    live = valid[:, None]
    first_full, got, later = links.begin(weights, flatten_small(small))
    qb, ub, vecs = unpack_small(got, small)
    qb = qb.reshape(LAYERS, 1, -1).astype(F32)
    ub = ub.reshape(LAYERS, 1, -1).astype(F32)
    vecs = vecs.astype(F32)

    held = [jnp.concatenate([vecs[layer, :4], vecs[layer - 1, 4:]]) for layer in range(LAYERS)]

    full, kept, extra = [first_full], [], None
    for layer in range(LAYERS):
        wq, wd, wu, wn = full[layer]
        h1, h2, mixed, act, gp, stats, *more = project(tokens_in, extra, held[layer], wq, qb[layer], cos, sin, wu, ub[layer], later if layer == 0 else None)
        if more:
            wd, wn = more
            full[0] = wq, wd, wu, wn
        ctx = attend_forward(mixed, seg_col, seg_row)
        branch = branch_out(ctx, act, wd, wn, [0, rows // 4, rows * 3 // 8, rows * 3 // 4, rows] if layer else None)
        kept.append((h1, h2, mixed, act, gp, stats, ctx, extra))
        if layer == 0:
            extra, made = links.middle(branch[0], weights)
            full.append(made)
        else:
            gout = gr = jnp.where(live, cotangent, 0).astype(BF)
            sums = None
            branch, gr = lax.optimization_barrier((branch, gr))
            branch_sum = [lax.psum(branch[0], "mp"), None, None, None]
    big, little = [None] * LAYERS, [None] * LAYERS
    for layer in reversed(range(LAYERS)):
        wq, wd, wu, wn = full[layer]
        h1, h2, mixed, act, gp, stats, ctx, extra = kept[layer]
        dctx, df = back_in(gr, gp, wd, wn)
        dmix = attend_backward(mixed, dctx, seg_col, seg_row, cos, sin)
        e, norm_sums = back_out(dmix, df, wq, wu, tokens_in, extra, held[layer], stats)
        before = 0 if layer else 2
        branch_sum[before], e = lax.optimization_barrier((branch_sum[before], e))
        at = 1 if layer else 3
        e, branch_sum[at], big[layer], qsum, usum, low_sums = links.turn(e, branch[at], (ctx, act, h1, h2), (gr, dmix, df), 3 + layer)
        little[layer] = (qsum, usum, norm_sums, low_sums if sums is None else sums)
        if layer:
            e, third = lax.optimization_barrier((e, branch[2]))
            branch_sum[2] = lax.psum(third, "mp")
        if layer:
            gout, gr, sums = norm_back(gout, e, tokens_in, extra, held[layer], stats)
    every = (vecs[0, 4:5] + vecs[0, 5:6]) + (vecs[1, 4:5] + vecs[1, 5:6])
    input_grad, output = finish(gout, e, tokens_in, kept[1][-1], branch_sum, every, live.astype(F32), stats)

    done = None
    for layer in reversed(range(LAYERS)):
        done = adam_layer(layer, weights, big[layer], firsts, seconds, done)

    ndp = lax.axis_size("dp")

    def pieces(v, width):
        v = v.reshape(-1, ndp, width // ndp)
        return jnp.moveaxis(v, 1, 0).reshape(ndp, -1)

    norms = jnp.concatenate([pieces(t[2], D) for t in little], axis=1)
    rest = [pieces(t[i], BROW) for i in (0, 1) for t in little] + [pieces(t[3], D) for t in little]
    rest = jnp.concatenate(rest, axis=1)
    shared, count = norms.shape[1] // 128, rest.shape[1]
    rest = jnp.pad(rest, ((0, 0), (0, -count % 1024)))
    total = links.small(jnp.concatenate([norms, rest], axis=1).reshape(ndp, -1, 128), shared)
    norms, rest = total[:shared].reshape(LAYERS, 4, -1), total[shared:].reshape(-1)
    small_grads, at = [], 0
    for p in small[:2]:
        small_grads.append(rest[at:at + p.size].reshape(p.shape))
        at += p.size
    tops_sum = rest[at:count].reshape(LAYERS, 1, -1)
    small_grads.append(jnp.concatenate([norms, tops_sum, tops_sum], axis=1))
    small_out = []
    for p, g, first, second in zip(small, small_grads, small_firsts, small_seconds):
        small_out += adam_update(p.astype(F32), g, first, second)
    return (output, input_grad, *done, *small_out)


def solution(mesh):
    rows_dp = P("dp", None)
    wide, tall, vec = P(None, "dp", "mp"), P(None, "mp", "dp"), P(None, None, "dp")
    group = (wide, tall, wide, tall, tall, tall, vec)
    return jax.shard_map(
        functools.partial(body, ChipLinks() if dict(mesh.shape) == {"dp": 8, "mp": 4} else PlainLinks()),
        mesh=mesh,
        in_specs=(rows_dp,) * 3 + group * 3,
        out_specs=(rows_dp,) * 2 + tuple(s for s in group for _ in range(4)),
        check_vma=False,
    )
```

```python
import functools
import jax
import jax.numpy as jnp
from jax import lax
from jax.experimental import pallas as pl
from jax.experimental.pallas import tpu as pltpu
from jax.sharding import PartitionSpec as P

HD = 256
ROT = 64
MAXLEN = 512
norm_eps = 1e-05
masked_score = -1e30
LAYERS = 2
BROW = 128
ADAM_STEP = 10
beta_one = 0.9
beta_two = 0.95
adam_eps = 1e-08
rate = 0.02
decay = 0.01
VM = 60 * 1024 * 1024
VM2 = 62 * 1024 * 1024
BF = jnp.bfloat16
ROWS = 256
UPB = 512
F32 = jnp.float32


def call(kernel, grid, in_specs, out_specs, out_shape, scratch=(), flops=0, nbytes=0, name=None, ident=None):
    return pl.pallas_call(
        kernel,
        grid_spec=pltpu.PrefetchScalarGridSpec(num_scalar_prefetch=0, grid=grid, in_specs=in_specs, out_specs=out_specs, scratch_shapes=list(scratch)),
        out_shape=out_shape,
        compiler_params=pltpu.CompilerParams(vmem_limit_bytes=VM, collective_id=ident, has_side_effects=ident is not None),
        cost_estimate=pl.CostEstimate(flops=flops, bytes_accessed=nbytes, transcendentals=0),
        name=name,
    )


def spec(shape, index, single=False):
    if single:
        return pl.BlockSpec(shape, index, pipeline_mode=pl.Buffered(1))
    return pl.BlockSpec(shape, index)


def rope_tables(position):
    half = ROT // 2
    freq = 10000.0 ** (-(jnp.arange(half, dtype=F32) * 2.0) / ROT)
    angle = position.astype(F32)[:, None] * freq[None, :]
    c, s = jnp.cos(angle), jnp.sin(angle)
    rows = position.shape[0]
    one = jnp.ones((rows, 128 - ROT), F32)
    zero = jnp.zeros((rows, 128 - ROT), F32)
    return jnp.concatenate([c, c, one], axis=1), jnp.concatenate([-s, s, zero], axis=1)


def turn(u, c, s):
    lane = lax.broadcasted_iota(jnp.int32, u.shape, 1)
    other = jnp.where(lane < ROT // 2, pltpu.roll(u, 128 - ROT // 2, 1), pltpu.roll(u, ROT // 2, 1))
    return u * c + other * s


def normed(x):
    mean = jnp.mean(x, axis=1, keepdims=True)
    centred = x - mean
    var = jnp.mean(centred * centred, axis=1, keepdims=True)
    rstd = lax.rsqrt(var + norm_eps)
    return centred * rstd, mean, rstd


def row_blocks(n):
    step = min(n, ROWS)
    return [slice(i, i + step) for i in range(0, n, step)]


def project(base, extra, vec, wq, bq, cos, sin, wu, bu, shards=None):
    n, D = base.shape
    C, U = wq.shape[1], wu.shape[1]
    QB, UB = 3 * HD, min(UPB, U)
    nq, nu = C // QB, U // UB
    RB = 128
    nr = n // RB
    ng = 0 if shards is None else len(shards)
    xs = [base] if extra is None else [base, extra]

    def kernel(*refs):
        refs = list(refs)
        take = lambda k: [refs.pop(0) for _ in range(k)]
        x_rs = take(len(xs))
        vec_r, wq_r, bq_r, cos_r, sin_r, wu_r, bu_r = take(7)
        shard_rs = take(ng)
        h1_o, h2_o, mix_r, a_r, gp_r, st_r = take(6)
        full_rs = take(ng)
        h1_r, h2_r = take(2)
        bufs = take(len(xs))
        in_sem, out_sem = take(2)
        j = pl.program_id(0)
        side = None
        if ng:
            spot = Spot()
            half = full_rs[0].shape[1] // 2
            pieces = [pl.ds(0, half), pl.ds(half, half)]
            side = Gather(spot, [(shard_rs[0].at[0, p], full_rs[0].at[:, p]) for p in pieces], *take(3))

            @pl.when(j == 0)
            def _():
                spot.meet(False)
                side.first(0)
                side.first(1)

        def host(step, *stages):
            if side is not None:
                @pl.when(j == min(step, nq + nu - 1))
                def _():
                    for name, *args in stages:
                        getattr(side, name)(*args)
        block = lambda i: pl.ds(i * RB, RB)
        loads = [[pltpu.make_async_copy(x.at[block(i)], buf.at[block(i)], in_sem.at[k, i]) for k, (x, buf) in enumerate(zip(x_rs, bufs))] for i in range(nr)]
        stores = [[pltpu.make_async_copy(h.at[block(i)], o.at[block(i)], out_sem.at[k, i]) for k, (h, o) in enumerate(((h1_r, h1_o), (h2_r, h2_o)))] for i in range(nr)]

        @pl.when(j == 0)
        def _():
            for group in loads:
                for copy in group:
                    copy.start()
            for i in range(nr):
                for copy in loads[i]:
                    copy.wait()
                rows = block(i)
                x = bufs[0][rows, :].astype(F32)
                if extra is not None:
                    x = x + bufs[1][rows, :].astype(F32) + vec_r[4:5, :] + vec_r[5:6, :]
                xhat, mean, rstd = normed(x)
                st_r[rows, 0:1] = mean
                st_r[rows, 1:2] = rstd
                h1_r[rows, :] = (xhat * vec_r[0:1, :] + vec_r[1:2, :]).astype(BF)
                h2_r[rows, :] = (xhat * vec_r[2:3, :] + vec_r[3:4, :]).astype(BF)
                for copy in stores[i]:
                    copy.start()

        @pl.when(j < nq)
        def _():
            for rows in row_blocks(n):
                for part in range(3):
                    at = part * HD
                    m = jnp.dot(h1_r[rows, :], wq_r[:, at:at + HD], preferred_element_type=F32) + bq_r[:, at:at + HD]
                    if part == 2:
                        mix_r[rows, at:at + HD] = m.astype(BF)
                    else:
                        mix_r[rows, at:at + 128] = turn(m[:, :128], cos_r[rows, :], sin_r[rows, :]).astype(BF)
                        mix_r[rows, at + 128:at + HD] = m[:, 128:].astype(BF)

        @pl.when(j >= nq)
        def _():
            for rows in row_blocks(n):
                for at in range(0, UB, 256):
                    cols = slice(at, at + 256)
                    f = jnp.dot(h2_r[rows, :], wu_r[:, cols], preferred_element_type=F32) + bu_r[:, cols]
                    phi = 0.5 * (1.0 + lax.erf(f * 0.7071067811865476))
                    a_r[rows, cols] = (f * phi).astype(BF)
                    gp_r[rows, cols] = (phi + f * (jnp.exp(-0.5 * f * f) * 0.3989422804014327)).astype(BF)

        host(2, ("second", 0))
        host(4, ("second", 1), ("third", 0))
        host(5, ("third", 1), ("last", 0), ("last", 1), ("close",))

        @pl.when(j == nq + nu - 1)
        def _():
            for group in stores:
                for copy in group:
                    copy.wait()

    whole = lambda j: (0, 0)
    qcol = lambda j: (0, jnp.minimum(j, nq - 1))
    ucol = lambda j: (0, jnp.maximum(j - nq, 0))
    far = pl.BlockSpec(memory_space=pl.ANY)
    ins = [far] * len(xs) + [
        spec((6, D), whole), spec((D, QB), qcol), spec((1, QB), qcol), spec((n, 128), whole, True), spec((n, 128), whole, True),
        spec((D, UB), ucol), spec((1, UB), ucol)] + [far] * ng
    outs = [far, far, spec((n, QB), qcol), spec((n, UB), ucol), spec((n, UB), ucol), spec((n, 128), whole)] + [far] * ng
    shapes = [jax.ShapeDtypeStruct(s, BF) for s in ((n, D), (n, D), (n, C), (n, U), (n, U))] + [jax.ShapeDtypeStruct((n, 128), F32)]
    DMA = pltpu.SemaphoreType.DMA
    scratch = [pltpu.VMEM((n, D), BF)] * (2 + len(xs)) + [DMA((len(xs), nr)), DMA((2, nr))]
    if ng:
        scratch += [DMA((2, 9)), DMA((2, 9)), DMA((2,))]
        shapes += [jax.ShapeDtypeStruct((8,) + v.shape[1:], v.dtype) for v in shards]
    return call(kernel, (nq + nu,), ins, outs, shapes, scratch, ident=5 if ng else None, flops=2 * n * D * (C + U), nbytes=2 * (n * D * 3 + D * (C + U) + n * (C + 2 * U)), name="project")(*xs, vec, wq, bq, cos, sin, wu, bu, *(shards or ()))


def softmax_block(q, k, segq, segk, q0, k0):
    s = lax.dot_general(q, k, (((1,), (1,)), ((), ())), preferred_element_type=F32) * HD ** (-0.5)
    qi = q0 + lax.broadcasted_iota(jnp.int32, s.shape, 0)
    ki = k0 + lax.broadcasted_iota(jnp.int32, s.shape, 1)
    allowed = (segq == segk) & (ki <= qi)
    s = jnp.where(allowed, s, masked_score)
    top = jnp.max(s, axis=1, keepdims=True)
    e = jnp.exp(s - top)
    return e / jnp.sum(e, axis=1, keepdims=True)


def windows(n, qb):
    for i in range(n // qb):
        q0 = i * qb
        yield q0, max(0, q0 - MAXLEN)


def attend_forward(mixed, seg_col, seg_row):
    n, C = mixed.shape
    H = C // (3 * HD)
    qb = 256

    def kernel(q_r, k_r, v_r, sc_r, sr_r, o_r):
        for q0, k0 in windows(n, qb):
            qs, ks = slice(q0, q0 + qb), slice(k0, q0 + qb)
            p = softmax_block(q_r[qs, :], k_r[ks, :], sc_r[qs, :], sr_r[:, ks], q0, k0)
            o_r[qs, :] = jnp.dot(p.astype(BF), v_r[ks, :], preferred_element_type=F32).astype(BF)

    part = lambda t: spec((n, HD), lambda h: (0, 3 * h + t))
    return call(kernel, (H,), [part(0), part(1), part(2), spec((n, 1), lambda h: (0, 0)), spec((1, n), lambda h: (0, 0))],
                spec((n, HD), lambda h: (0, h)), jax.ShapeDtypeStruct((n, H * HD), BF),
                flops=H * n * 640 * HD * 4, nbytes=2 * n * C, name="attend")(mixed, mixed, mixed, seg_col, seg_row)


def attend_backward(mixed, dctx, seg_col, seg_row, cos, sin):
    n, C = mixed.shape
    H = C // (3 * HD)
    qb = 256
    scale = HD ** (-0.5)

    def kernel(q_r, k_r, v_r, do_r, sc_r, sr_r, cos_r, sin_r, o_r, dk_s, dv_s):
        def back(u, rows):
            c, s = cos_r[rows, :], -sin_r[rows, :]
            return jnp.concatenate([turn(u[:, :128], c, s), u[:, 128:]], axis=1).astype(BF)

        dk_s[...] = jnp.zeros_like(dk_s)
        dv_s[...] = jnp.zeros_like(dv_s)
        for q0, k0 in reversed(list(windows(n, qb))):
            qs, ks = slice(q0, q0 + qb), slice(k0, q0 + qb)
            q, k, do = q_r[qs, :], k_r[ks, :], do_r[qs, :]
            p = softmax_block(q, k, sc_r[qs, :], sr_r[:, ks], q0, k0)
            dp = lax.dot_general(do, v_r[ks, :], (((1,), (1,)), ((), ())), preferred_element_type=F32)
            delta = jnp.sum(p * dp, axis=1, keepdims=True)
            ds = (p * (dp - delta)).astype(BF)
            dq = jnp.dot(ds, k, preferred_element_type=F32) * scale
            dk_s[ks, :] += lax.dot_general(ds, q, (((0,), (0,)), ((), ())), preferred_element_type=F32)
            dv_s[ks, :] += lax.dot_general(p.astype(BF), do, (((0,), (0,)), ((), ())), preferred_element_type=F32)
            o_r[qs, :HD] = back(dq, qs)
            o_r[qs, HD:2 * HD] = back(dk_s[qs, :] * scale, qs)
            o_r[qs, 2 * HD:] = dv_s[qs, :].astype(BF)

    part = lambda t: spec((n, HD), lambda h: (0, 3 * h + t))
    whole = lambda h: (0, 0)
    return call(kernel, (H,), [part(0), part(1), part(2), spec((n, HD), lambda h: (0, h)), spec((n, 1), whole), spec((1, n), whole),
                spec((n, 128), whole), spec((n, 128), whole)],
                spec((n, 3 * HD), lambda h: (0, h)), jax.ShapeDtypeStruct((n, C), BF),
                scratch=[pltpu.VMEM((n, HD), F32), pltpu.VMEM((n, HD), F32)],
                flops=H * n * 640 * HD * 10, nbytes=4 * n * C, name="attend_back")(mixed, mixed, mixed, dctx, seg_col, seg_row, cos, sin)


def branch_out(ctx, act, wd, wn, cuts=None):
    n, R = ctx.shape
    U = act.shape[1]
    dp, _, w = wd.shape
    cuts = cuts or [0, n]
    parts = list(zip(cuts, cuts[1:]))

    def kernel(c_r, a_r, wd_r, wn_r, *o_rs):
        out = (jnp.dot(c_r[...], wd_r[...], preferred_element_type=F32) + jnp.dot(a_r[...], wn_r[...], preferred_element_type=F32)).astype(BF)
        for (low, high), o_r in zip(parts, o_rs):
            o_r[...] = out[low:high]

    whole = lambda s: (0, 0)
    pick = lambda s: (s, 0, 0)
    return call(kernel, (dp,), [spec((n, R), whole, True), spec((n, U), whole, True), spec((None, R, w), pick), spec((None, U, w), pick)],
                [spec((high - low, w), lambda s: (0, s)) for low, high in parts], [jax.ShapeDtypeStruct((high - low, dp * w), BF) for low, high in parts],
                flops=2 * n * dp * w * (R + U), nbytes=2 * (n * (R + U) + dp * w * (R + U + n)), name="branch")(ctx, act, wd, wn)


def back_in(gr, gp, wd, wn):
    n, D = gr.shape
    dp, R, w = wd.shape
    U = wn.shape[1]
    NB = 256
    nr, nu = R // NB, U // NB

    def kernel(g_r, gp_r, wd_r, wn_r, dc_r, df_r):
        j = pl.program_id(0)

        def times(w_r):
            acc = None
            for s in range(dp):
                t = lax.dot_general(g_r[:, s * w:(s + 1) * w], w_r[s], (((1,), (1,)), ((), ())), preferred_element_type=F32)
                acc = t if acc is None else acc + t
            return acc

        @pl.when(j < nr)
        def _():
            dc_r[...] = times(wd_r).astype(BF)

        @pl.when(j >= nr)
        def _():
            df_r[...] = (times(wn_r) * gp_r[...].astype(F32)).astype(BF)

    rc = lambda j: jnp.minimum(j, nr - 1)
    uc = lambda j: jnp.maximum(j - nr, 0)
    return call(kernel, (nr + nu,), [spec((n, D), lambda j: (0, 0), True), spec((n, NB), lambda j: (0, uc(j))),
                spec((dp, NB, w), lambda j: (0, rc(j), 0)), spec((dp, NB, w), lambda j: (0, uc(j), 0))],
                [spec((n, NB), lambda j: (0, rc(j))), spec((n, NB), lambda j: (0, uc(j)))],
                [jax.ShapeDtypeStruct((n, R), BF), jax.ShapeDtypeStruct((n, U), BF)],
                flops=2 * n * D * (R + U), nbytes=2 * (n * D + D * (R + U) + n * (R + 2 * U)), name="back_in")(gr, gp, wd, wn)


def back_out(dmix, df, wq, wu, base, extra, vec, stats):
    n, C = dmix.shape
    U = df.shape[1]
    D = wq.shape[0]
    NB = 256

    def kernel(*refs):
        if extra is None:
            dm_r, df_r, wq_r, wu_r, base_r, vec_r, st_r, e_r, g_r = refs
        else:
            dm_r, df_r, wq_r, wu_r, base_r, extra_r, vec_r, st_r, e_r, g_r = refs
        nt = (((1,), (1,)), ((), ()))
        d1 = lax.dot_general(dm_r[...], wq_r[...], nt, preferred_element_type=F32)
        d2 = lax.dot_general(df_r[...], wu_r[...], nt, preferred_element_type=F32)
        e_r[...] = (d1 * vec_r[0:1, :] + d2 * vec_r[2:3, :]).astype(BF)
        x = base_r[...].astype(F32)
        if extra is not None:
            x = x + extra_r[...].astype(F32) + vec_r[4:5, :] + vec_r[5:6, :]
        xhat = (x - st_r[:, 0:1]) * st_r[:, 1:2]
        g_r[0:1, :] = jnp.sum(d1 * xhat, axis=0, keepdims=True)
        g_r[1:2, :] = jnp.sum(d1, axis=0, keepdims=True)
        g_r[2:3, :] = jnp.sum(d2 * xhat, axis=0, keepdims=True)
        g_r[3:4, :] = jnp.sum(d2, axis=0, keepdims=True)

    whole = lambda j: (0, 0)
    col = lambda j: (0, j)
    row = lambda j: (j, 0)
    xs = [spec((n, NB), col)] + ([] if extra is None else [spec((n, NB), col)])
    args = [base] + ([] if extra is None else [extra])
    return call(kernel, (D // NB,), [spec((n, C), whole, True), spec((n, U), whole, True), spec((NB, C), row), spec((NB, U), row)] + xs +
                [spec((6, NB), col), spec((n, 128), whole)],
                [spec((n, NB), col), spec((4, NB), col)],
                [jax.ShapeDtypeStruct((n, D), BF), jax.ShapeDtypeStruct((4, D), F32)],
                flops=2 * n * D * (C + U), nbytes=2 * (n * (C + U) + D * (C + U) + n * D * 3), name="back_out")(dmix, df, wq, wu, *args, vec, stats)


def weight_grad(left, right, w=None):
    n, M = left.shape
    N = right.shape[1]
    MB = 256

    def kernel(l_r, r_r, o_r, s_r):
        g = lax.dot_general(l_r[...], r_r[...], (((0,), (0,)), ((), ())), preferred_element_type=F32)
        if w is None:
            o_r[...] = g.astype(BF)
        else:
            for s in range(N // w):
                o_r[s] = g[:, s * w:(s + 1) * w].astype(BF)

        @pl.when(pl.program_id(0) == 0)
        def _():
            s_r[...] = jnp.sum(r_r[...].astype(F32), axis=0, keepdims=True)

    whole = lambda j: (0, 0)
    if w is None:
        out, shape = spec((MB, N), lambda j: (j, 0)), (M, N)
    else:
        out, shape = spec((N // w, MB, w), lambda j: (0, j, 0)), (N // w, M, w)
    return call(kernel, (M // MB,), [spec((n, MB), lambda j: (0, j)), spec((n, N), whole, True)], [out, spec((1, N), whole)],
                [jax.ShapeDtypeStruct(shape, BF), jax.ShapeDtypeStruct((1, N), F32)],
                flops=2 * n * M * N, nbytes=2 * (n * M + n * N + M * N), name="wgrad")(left, right)


def norm_back(gout, e, base, extra, vec, stats):
    n, D = base.shape
    RB = 256

    def kernel(g_r, e_r, base_r, extra_r, vec_r, st_r, dx_r, low_r, sum_r):
        x = base_r[...].astype(F32) + extra_r[...].astype(F32) + vec_r[4:5, :] + vec_r[5:6, :]
        dx = g_r[...].astype(F32) + norm_pullback(x, e_r, st_r)
        dx_r[...] = dx
        low_r[...] = dx.astype(BF)

        @pl.when(pl.program_id(0) == 0)
        def _():
            sum_r[...] = jnp.zeros_like(sum_r)

        sum_r[...] += jnp.sum(dx, axis=0, keepdims=True)

    row = lambda i: (i, 0)
    whole = lambda i: (0, 0)
    rows = spec((RB, D), row)
    shapes = [jax.ShapeDtypeStruct((n, D), F32), jax.ShapeDtypeStruct((n, D), BF), jax.ShapeDtypeStruct((1, D), F32)]
    return call(kernel, (n // RB,), [rows] * 4 + [spec((6, D), whole), spec((RB, 128), row)], [rows, rows, spec((1, D), whole)], shapes,
                flops=10 * n * D, nbytes=16 * n * D, name="norm_back")(gout, e, base, extra, vec, stats)


def norm_pullback(x, e_r, st_r):
    xhat = (x - st_r[:, 0:1]) * st_r[:, 1:2]
    ev = e_r[...].astype(F32)
    me = jnp.mean(ev, axis=1, keepdims=True)
    mx = jnp.mean(ev * xhat, axis=1, keepdims=True)
    return (ev - me - xhat * mx) * st_r[:, 1:2]


def finish(gout, e, base, extra, branches, held, live, stats):
    n, D = base.shape
    RB = 128
    counts = [b.shape[0] // RB for b in branches]
    starts = [sum(counts[:k]) for k in range(len(counts))]

    def kernel(g_r, e_r, base_r, extra_r, *refs):
        branch_rs, (held_r, live_r, st_r, dx_r, out_r) = refs[:len(branches)], refs[len(branches):]
        i = pl.program_id(0)
        x = base_r[...].astype(F32)
        dx_r[...] = g_r[...] + norm_pullback(x, e_r, st_r)
        for k, b_r in enumerate(branch_rs):
            @pl.when((i >= starts[k]) & (i < starts[k] + counts[k]))
            def _(b_r=b_r):
                last = base_r[...].astype(F32) + extra_r[...].astype(F32) + b_r[...].astype(F32) + held_r[...]
                out_r[...] = jnp.where(live_r[...] > 0.0, last, 0.0).astype(BF)

    row = lambda i: (i, 0)
    whole = lambda i: (0, 0)
    rows = spec((RB, D), row)
    part = lambda k: spec((RB, D), lambda i: (jnp.clip(i - starts[k], 0, counts[k] - 1), 0))
    ins = [rows] * 4 + [part(k) for k in range(len(branches))] + [spec((1, D), whole), spec((RB, 1), row), spec((RB, 128), row)]
    return call(kernel, (n // RB,), ins, [rows, rows], [jax.ShapeDtypeStruct((n, D), F32), jax.ShapeDtypeStruct((n, D), BF)],
                flops=10 * n * D, nbytes=18 * n * D, name="finish")(gout, e, base, extra, *branches, held, live, stats)


MESH = pl.DeviceIdType.MESH


class Spot:
    def __init__(self):
        i = lax.axis_index("dp")
        c, x, y = lax.rem(i, 2), lax.rem(lax.div(i, 2), 2), lax.div(i, 4)
        self.me, self.core = i, c
        self.dx, self.dy, self.dc = 2 - 4 * x, 4 - 8 * y, 1 - 2 * c
        self.nx, self.ny, self.nc = i + self.dx, i + self.dy, i + self.dc
        self.diag = i + self.dx + self.dy
        z = lax.axis_index("mp")
        self.z = z
        self.outer = (z == 0) | (z == 3)
        self.inner = (z == 1) | (z == 2)
        self.pair = z + 1 - 2 * lax.rem(z, 2)
        self.across = 3 - z

    def meet(self, line):
        barrier = pltpu.get_barrier_semaphore()
        for peer in (self.nx, self.ny, self.nc):
            pl.semaphore_signal(barrier, inc=1, device_id={"dp": peer}, device_id_type=MESH)
        if line:
            pl.semaphore_signal(barrier, inc=1, device_id={"mp": self.pair}, device_id_type=MESH)

            @pl.when(self.inner)
            def _():
                pl.semaphore_signal(barrier, inc=1, device_id={"mp": self.across}, device_id_type=MESH)

            @pl.when(self.inner)
            def _():
                pl.semaphore_wait(barrier, 5)

            @pl.when(self.outer)
            def _():
                pl.semaphore_wait(barrier, 4)
        else:
            pl.semaphore_wait(barrier, 3)


def send_to(axis, peer, src, dst, send, recv):
    return pltpu.make_async_remote_copy(src_ref=src, dst_ref=dst, send_sem=send, recv_sem=recv, device_id={axis: peer}, device_id_type=MESH)


class Gather:
    copies = 9

    def __init__(self, spot, items, send, recv, local):
        self.spot, self.items, self.send, self.recv, self.local = spot, items, send, recv, local
        self.sent = []
        self.own = []

    def go(self, k, n, peer, src, dst):
        send_to("dp", peer, src, dst, self.send.at[k, n], self.recv.at[k, n]).start()
        self.sent.append((k, n, peer, src, dst))

    def arrived(self, k, n, dst):
        send_to("dp", self.spot.nc, dst, dst, self.send.at[k, n], self.recv.at[k, n]).wait_recv()

    def first(self, k):
        s, (src, out) = self.spot, self.items[k]
        for n, peer in enumerate((s.nx, s.ny, s.nc)):
            self.go(k, n, peer, src, out.at[s.me])
        pltpu.make_async_copy(src, out.at[s.me], self.local.at[k]).start()
        self.own.append(k)

    def halves(self, k):
        h = self.items[k][1].shape[1] // 2
        return pl.ds(0, h), pl.ds(h, h)

    def second(self, k):
        s, (_, out) = self.spot, self.items[k]
        low, high = self.halves(k)
        self.arrived(k, 0, out.at[s.nx])
        self.go(k, 3, s.ny, out.at[s.nx, high], out.at[s.nx, high])
        self.go(k, 4, s.nc, out.at[s.nx], out.at[s.nx])
        self.arrived(k, 1, out.at[s.ny])
        self.go(k, 5, s.nx, out.at[s.ny, low], out.at[s.ny, low])
        self.go(k, 6, s.nc, out.at[s.ny], out.at[s.ny])

    def third(self, k):
        s, (_, out) = self.spot, self.items[k]
        low, high = self.halves(k)
        self.arrived(k, 3, out.at[s.diag, high])
        self.go(k, 7, s.nc, out.at[s.diag, high], out.at[s.diag, high])
        self.arrived(k, 5, out.at[s.diag, low])
        self.go(k, 8, s.nc, out.at[s.diag, low], out.at[s.diag, low])

    def last(self, k):
        s, (_, out) = self.spot, self.items[k]
        low, high = self.halves(k)
        self.arrived(k, 2, out.at[s.nc])
        self.arrived(k, 4, out.at[s.nx + s.dc])
        self.arrived(k, 6, out.at[s.ny + s.dc])
        self.arrived(k, 7, out.at[s.diag + s.dc, high])
        self.arrived(k, 8, out.at[s.diag + s.dc, low])

    def close(self):
        for k in self.own:
            src, out = self.items[k]
            pltpu.make_async_copy(src, out.at[self.spot.me], self.local.at[k]).wait()
        for k, n, peer, src, dst in self.sent:
            send_to("dp", peer, src, dst, self.send.at[k, n], self.recv.at[k, n]).wait_send()


AHEAD, LAG, BACK = 3, 1, 5


class LineSum:
    copies = 3

    def __init__(self, spot, pairs, stage, land, swap, send, recv, local):
        self.spot, self.stage, self.land, self.swap = spot, stage, land, swap
        self.send, self.recv, self.local = send, recv, local
        self.rows = stage.shape[1]
        self.parts, self.outs = [], []
        for part, start, out, rows in pairs:
            for at in range(0, rows, self.rows):
                self.parts.append(part.at[pl.ds(start + at, self.rows)])
                self.outs.append(out.at[pl.ds(at, self.rows)])
        self.chunks = len(self.parts)

    def cut(self, k):
        return pl.ds(k * self.rows, self.rows)

    def copy(self, k, n):
        s, rows = self.spot, self.cut(k)
        if n == 0:
            peer, src, dst = s.pair, self.parts[k], self.land
        elif n == 1:
            peer, src, dst = s.across, self.land.at[rows], self.swap
        else:
            peer, src, dst = s.pair, self.swap.at[rows], self.swap
        return send_to("mp", peer, src, dst.at[rows], self.send.at[k, n], self.recv.at[k, n])

    def keep(self, k):
        rows = self.cut(k)
        return pltpu.make_async_copy(self.swap.at[rows], self.outs[k], self.local.at[k])

    def load(self, k):
        return pltpu.make_async_copy(self.parts[k], self.stage.at[k % 2], self.local.at[self.chunks + k % 2])

    def add(self, k, dst, one, two, base):
        step = 32

        @pl.loop(0, self.rows // step)
        def _(i):
            rows = pl.ds(pl.multiple_of(k * self.rows + i * step, step), step)
            there = pl.ds(pl.multiple_of(base + i * step, step), step)
            dst[rows, :] = (one[there, :].astype(F32) + two[rows, :].astype(F32)).astype(BF)

    def send_step(self, t):
        n = self.chunks

        @pl.when(self.spot.outer)
        def _():
            if 0 <= t - AHEAD < n:
                self.copy(t - AHEAD, 0).wait_send()
            if t < n:
                self.copy(t, 0).start()
            if 0 <= t - BACK < n:
                self.copy(t - BACK, 2).wait_recv()
                self.keep(t - BACK).start()

    def add_step(self, t):
        n = self.chunks

        @pl.when(self.spot.inner)
        def _():
            if t < n:
                if t == 0:
                    self.load(0).start()
                if t + 1 < n:
                    self.load(t + 1).start()
                self.load(t).wait()
                self.copy(t, 0).wait_recv()
                self.add(t, self.land, self.stage.at[t % 2], self.land, 0)
                self.copy(t, 1).start()
            if 0 <= t - LAG < n:
                self.copy(t - LAG, 1).wait_recv()
                self.copy(t - LAG, 1).wait_send()
                self.add(t - LAG, self.swap, self.land, self.swap, (t - LAG) * self.rows)
                self.copy(t - LAG, 2).start()
                self.keep(t - LAG).start()

    def begin(self):
        self.sent_to, self.added_to = 0, 0
        for _ in range(AHEAD):
            self.send_step(self.sent_to)
            self.sent_to += 1

    def slot(self):
        if self.added_to < self.chunks + LAG:
            self.add_step(self.added_to)
            self.added_to += 1
        if self.sent_to < self.chunks + BACK:
            self.send_step(self.sent_to)
            self.sent_to += 1

    def finish(self):
        while self.added_to < self.chunks + LAG or self.sent_to < self.chunks + BACK:
            self.slot()

    def close(self):
        for k in range(self.chunks):
            self.keep(k).wait()

        @pl.when(self.spot.inner)
        def _():
            for k in range(self.chunks):
                self.copy(k, 2).wait_send()


class Scatter:
    copies = 10

    def __init__(self, spot, items, own, sib, fx, fy, gx, gy, send, recv, local):
        self.spot, self.items = spot, items
        self.own, self.sib, self.fx, self.fy, self.gx, self.gy = own, sib, fx, fy, gx, gy
        self.send, self.recv, self.local = send, recv, local
        self.sent = []

    def go(self, k, n, peer, src, dst):
        send_to("dp", peer(), src(), dst(), self.send.at[k, n], self.recv.at[k, n]).start()
        self.sent.append((k, n, src))

    def arrived(self, k, n, dst):
        send_to("dp", self.spot.nc, dst, dst, self.send.at[k, n], self.recv.at[k, n]).wait_recv()

    def hand(self, k):
        s, grad = self.spot, self.items[k][0]
        for m, slot in enumerate((s.me, s.nx, s.ny, s.diag)):
            self.go(k, m, lambda: s.nc, lambda slot=slot: grad.at[slot + s.dc], lambda m=m: self.sib[k].at[m])

    def hold(self, k):
        for m in range(4):
            self.load(k, m).start()

    def first(self, k):
        self.hand(k)
        self.hold(k)

    def load(self, k, m):
        s = self.spot
        slot = (s.me, s.nx, s.ny, s.diag)[m]
        return pltpu.make_async_copy(self.items[k][0].at[slot], self.own[k].at[m], self.local.at[k, m])

    def over(self, r, c, body, start=0):
        step = 16
        while step * 2 * c <= 32768 and r % (step * 2) == 0:
            step *= 2

        @pl.loop(0, r // step)
        def _(i):
            body(pl.ds(pl.multiple_of(i * step, step), step), pl.ds(pl.multiple_of(start + i * step, step), step))

    def second(self, k):
        s = self.spot
        own, sib = self.own[k], self.sib[k]
        _, r, c = own.shape
        h = r // 2
        low, high = pl.ds(0, h), pl.ds(h, h)
        for m in (3, 1, 2, 0):
            self.load(k, m).wait()
            self.arrived(k, m, sib.at[m])

            def add(rows, _, m=m):
                own[m, rows, :] = (own[m, rows, :].astype(F32) + sib[m, rows, :].astype(F32)).astype(BF)

            self.over(r, c, add)
            if m == 3:
                self.go(k, 5, lambda: s.nx, lambda: own.at[3, low], lambda: self.fx[k].at[1])
                self.go(k, 7, lambda: s.ny, lambda: own.at[3, high], lambda: self.fy[k].at[1])
            if m == 1:
                self.go(k, 4, lambda: s.nx, lambda: own.at[1, low], lambda: self.fx[k].at[0])
            if m == 2:
                self.go(k, 6, lambda: s.ny, lambda: own.at[2, high], lambda: self.fy[k].at[0])

    def third(self, k):
        s = self.spot
        own, fx, fy = self.own[k], self.fx[k], self.fy[k]
        _, r, c = own.shape
        h = r // 2
        self.arrived(k, 5, fx.at[1])

        def add_low(rows, _):
            fx[1, rows, :] = (own[2, rows, :].astype(F32) + fx[1, rows, :].astype(F32)).astype(BF)

        self.over(h, c, add_low)
        self.go(k, 8, lambda: s.ny, lambda: fx.at[1], lambda: self.gy[k])
        self.arrived(k, 7, fy.at[1])

        def add_high(rows, there):
            fy[1, rows, :] = (own[1, there, :].astype(F32) + fy[1, rows, :].astype(F32)).astype(BF)

        self.over(h, c, add_high, h)
        self.go(k, 9, lambda: s.nx, lambda: fy.at[1], lambda: self.gx[k])

    def last(self, k):
        own, out = self.own[k], self.items[k][1]
        fx, fy, gx, gy = self.fx[k], self.fy[k], self.gx[k], self.gy[k]
        _, r, c = own.shape
        h = r // 2
        self.arrived(k, 4, fx.at[0])
        self.arrived(k, 8, gy)

        def low(rows, _):
            out[rows, :] = own[0, rows, :].astype(F32) + fx[0, rows, :].astype(F32) + gy[rows, :].astype(F32)

        self.over(h, c, low)
        self.arrived(k, 6, fy.at[0])
        self.arrived(k, 9, gx)

        def high(rows, there):
            out[there, :] = own[0, there, :].astype(F32) + fy[0, rows, :].astype(F32) + gx[rows, :].astype(F32)

        self.over(h, c, high, h)

    def close(self):
        for k, n, src in self.sent:
            send_to("dp", self.spot.nc, src(), src(), self.send.at[k, n], self.recv.at[k, n]).wait_send()


def link_kernel(name, ident, shards, layers, part=None, chunks=16):
    ng = len(shards)
    HBM = pl.BlockSpec(memory_space=pl.ANY)
    DMA = pltpu.SemaphoreType.DMA
    parts = [] if part is None else [part]
    shapes = [jax.ShapeDtypeStruct((8,) + (v.shape if l is None else v.shape[1:]), v.dtype) for v, l in zip(shards, layers)]
    shapes += [jax.ShapeDtypeStruct(v.shape, BF) for v in parts]
    scratch = [DMA((ng, 9)), DMA((ng, 9)), DMA((ng,))]
    for v in parts:
        scratch += [pltpu.VMEM((2, v.shape[0] // chunks, v.shape[1]), BF), pltpu.VMEM(v.shape, BF), pltpu.VMEM(v.shape, BF), DMA((chunks, 3)), DMA((chunks, 3)), DMA((chunks + 2,))]

    def kernel(*refs):
        refs = list(refs)
        take = lambda n: [refs.pop(0) for _ in range(n)]
        src, ins, full, totals = take(ng), take(len(parts)), take(ng), take(len(parts))
        spot = Spot()
        spot.meet(bool(parts))
        G = Gather(spot, [(a if l is None else a.at[l], b) for a, l, b in zip(src, layers, full)], *take(3))
        if parts:
            stage, land, swap, send, recv, local = take(6)
            line = LineSum(spot, [(ins[0], 0, totals[0], ins[0].shape[0])], stage, land, swap, send, recv, local)
            plan_sum_gather(G, line)
            line.close()
        else:
            plan_gather(G)
        G.close()

    nbytes = sum(v.size * 2 for v in parts) + sum(8 * v.size for v in shards)
    return pl.pallas_call(
        kernel, in_specs=[HBM] * (ng + len(parts)), out_specs=[HBM] * (ng + len(parts)), out_shape=shapes, scratch_shapes=scratch,
        compiler_params=pltpu.CompilerParams(vmem_limit_bytes=VM, collective_id=ident, has_side_effects=True),
        cost_estimate=pl.CostEstimate(flops=0, bytes_accessed=nbytes, transcendentals=0), name=name)(*shards, *parts)


def plan_gather(G):
    n = len(G.items)
    for stage in (G.first, G.second, G.third, G.last):
        for k in range(n):
            stage(k)


class Products:
    def __init__(self, core, lefts, rights, grads, rhs, lbuf, obuf, rsem, lsem, osem):
        self.core = core
        self.lefts, self.rights, self.grads = lefts, rights, grads
        self.rhs, self.lbuf, self.obuf, self.rsem, self.lsem, self.osem = rhs, lbuf, obuf, rsem, lsem, osem

    def right(self, i, slot):
        return pltpu.make_async_copy(self.rights[i], self.rhs[slot], self.rsem.at[i])

    def split(self, k):
        slots, r, _ = self.grads[k].shape
        return r == 256 and self.lefts[k].shape[1] == slots * r

    def block(self, k, m):
        if self.split(k):
            late = m // 4 if isinstance(m, int) else lax.div(m, 4)
            return 2 * (m - 4 * late) + 1 - self.core - late + 2 * late * self.core
        return m

    def columns(self, block):
        return pl.ds(block * 256 if isinstance(block, int) else pl.multiple_of(block * 256, 256), 256)

    def left(self, k, m):
        odd = m % 2 if isinstance(m, int) else lax.rem(m, 2)
        return pltpu.make_async_copy(self.lefts[k].at[:, self.columns(self.block(k, m))], self.lbuf.at[odd], self.lsem.at[odd])

    def stores(self, k, m):
        odd = m % 2 if isinstance(m, int) else lax.rem(m, 2)
        grad, o, sem = self.grads[k], self.obuf.at[odd], self.osem.at[odd]
        slots, _, c = grad.shape
        block = self.block(k, m)
        if self.split(k):
            return [pltpu.make_async_copy(o.at[:, pl.ds(0, c)], grad.at[block], sem.at[0])]
        return [pltpu.make_async_copy(o.at[:, pl.ds(s * c, c)], grad.at[s, self.columns(block)], sem.at[s]) for s in range(slots)]

    def run(self, k, slot, start, stop, hooks):
        right = self.rhs[slot]
        width = right.shape[1]
        self.left(k, start).start()

        @pl.loop(start, stop)
        def _(m):
            self.left(k, m).wait()

            @pl.when(m + 1 < stop)
            def _():
                self.left(k, m + 1).start()

            @pl.when(m >= start + 2)
            def _():
                for copy in self.stores(k, m - 2):
                    copy.wait()

            g = lax.dot_general(self.lbuf[lax.rem(m, 2)], right[...], (((0,), (0,)), ((), ())), preferred_element_type=F32)
            self.obuf[lax.rem(m, 2), :, :width] = g.astype(BF)
            for copy in self.stores(k, m):
                copy.start()
            for at in sorted(hooks):
                pl.when(m == at)(hooks[at])

        for m in (stop - 2, stop - 1):
            for copy in self.stores(k, m):
                copy.wait()

    def sums(self, slot, out):
        right = self.rhs[slot]
        out[...] = jnp.zeros_like(out)

        @pl.loop(0, right.shape[0] // 64)
        def _(i):
            out[...] += jnp.sum(right[pl.ds(pl.multiple_of(i * 64, 64), 64), :].astype(F32), axis=0, keepdims=True)


def plan_sum_gather(G, line):
    for k in range(4):
        G.first(k)
    stages = {5: [("second", 0), ("second", 1)], 9: [("second", 2)], 12: [("second", 3)], 14: [("third", 0), ("third", 1)], 15: [("third", 2)],
              17: [("third", 3)]}
    line.begin()
    for at in range(18):
        line.slot()
        for name, k in stages.get(at, ()):
            getattr(G, name)(k)
    line.finish()
    for k in range(4):
        G.last(k)


def sum_scatter(ident, e, more, lefts, rights, step=64):
    n, D = e.shape
    HBM = pl.BlockSpec(memory_space=pl.ANY)
    VM_ = pl.BlockSpec(memory_space=pltpu.VMEM)
    C, U = rights[1].shape[1], rights[2].shape[1]
    w = D // 8
    dims = [(lefts[0].shape[1], w), (lefts[1].shape[1], w), (w, C), (w, U)]
    DMA = pltpu.SemaphoreType.DMA
    more_rows = more.shape[0]
    chunks = (n + more_rows) // step
    outs = [HBM] * 2 + [HBM] * 4 + [VM_] * 4 + [VM_] * 3
    shapes = [jax.ShapeDtypeStruct(e.shape, BF), jax.ShapeDtypeStruct((more_rows, D), BF)] + [jax.ShapeDtypeStruct((8,) + d, BF) for d in dims] + [jax.ShapeDtypeStruct(d, F32) for d in dims]
    shapes += [jax.ShapeDtypeStruct((1, C), F32), jax.ShapeDtypeStruct((1, U), F32), jax.ShapeDtypeStruct((1, D), F32)]
    scratch = [pltpu.VMEM((2, step, D), BF)] + [pltpu.VMEM((n + more_rows, D), BF)] * 2 + [DMA((chunks, 3)), DMA((chunks, 3)), DMA((chunks + 2,))]
    cut = [dims[0], (dims[1][0] // 2, w), (dims[1][0] // 2, w), dims[2], dims[3]]
    scratch += [DMA((5, 10)), DMA((5, 10)), DMA((5, 4))]
    for r, c in cut:
        scratch += [pltpu.VMEM((4, r, c), BF), pltpu.VMEM((4, r, c), BF), pltpu.VMEM((2, r // 2, c), BF), pltpu.VMEM((2, r // 2, c), BF),
                    pltpu.VMEM((r // 2, c), BF), pltpu.VMEM((r // 2, c), BF)]
    wide = max(D, U)
    scratch += [pltpu.VMEM((n, wide), BF), pltpu.VMEM((n, C), BF), pltpu.VMEM((2, n, 256), BF), pltpu.VMEM((2, 256, wide), BF), DMA((3,)), DMA((2,)), DMA((2, 8))]
    assert D == U

    def kernel(*refs):
        refs = list(refs)
        take = lambda k: [refs.pop(0) for _ in range(k)]
        (e_r, more_r), left_rs, right_rs = take(2), take(4), take(3)
        (total, more_total), grads, owned, sum_rs = take(2), take(4), take(4), take(3)
        stage, land, swap, send, recv, local = take(6)
        spot = Spot()
        spot.meet(True)
        line = LineSum(spot, [(e_r, 0, total, n), (more_r, 0, more_total, more_rows)], stage, land, swap, send, recv, local)
        send, recv, local = take(3)
        bufs = [take(6) for _ in range(5)]
        half = cut[1][0]
        low, high = pl.ds(0, half), pl.ds(half, half)
        items = [(grads[0], owned[0]), (grads[1].at[:, low], owned[1].at[low]), (grads[1].at[:, high], owned[1].at[high])]
        items += [(grads[2], owned[2]), (grads[3], owned[3])]
        S = Scatter(spot, items, *[[b[i] for b in bufs] for i in range(6)], send, recv, local)
        wide_r, narrow_r, lbuf, obuf, rsem, lsem, osem = take(7)
        W = Products(spot.core, left_rs, right_rs, grads, (wide_r, narrow_r), lbuf, obuf, rsem, lsem, osem)
        W.right(0, 0).start()
        W.right(1, 1).start()
        def steps(*what):
            def go():
                for step, *args in what:
                    step(*args)

            return go

        slot = (line.slot,)
        line.begin()
        W.right(0, 0).wait()
        W.run(1, 0, 0, 4, {1: steps(slot)})
        S.first(1)
        line.slot()
        W.run(0, 0, 0, left_rs[0].shape[1] // 256, {})
        S.first(0)
        S.second(1)
        line.slot()
        W.run(1, 0, 4, 8, {5: steps(slot)})
        S.first(2)
        W.sums(0, sum_rs[2])
        W.right(2, 0).start()
        S.second(0)
        line.slot()
        W.right(1, 1).wait()
        W.run(2, 1, 0, 8, {0: steps((S.second, 2), (S.third, 1)), 2: steps(slot), 5: steps((S.hand, 3), slot)})
        S.hold(3)
        line.slot()
        S.third(0)
        S.second(3)
        W.right(2, 0).wait()
        W.run(3, 0, 0, 8, {1: steps(slot), 3: steps((S.third, 2)), 4: steps(slot), 5: steps((S.hand, 4)), 6: steps(slot)})
        S.hold(4)
        line.slot()
        S.second(4)
        W.sums(1, sum_rs[0])
        line.slot()
        S.third(3)
        line.slot()
        W.sums(0, sum_rs[1])
        line.slot()
        S.last(0)
        S.last(1)
        line.slot()
        S.last(2)
        line.slot()
        line.slot()
        S.third(4)
        line.slot()
        S.last(3)
        line.finish()
        S.last(4)
        line.close()
        S.close()

    flops = 2 * n * D * (lefts[0].shape[1] + lefts[1].shape[1] + C + U)
    got = pl.pallas_call(
        kernel, in_specs=[HBM] * 9, out_specs=outs, out_shape=shapes, scratch_shapes=scratch,
        compiler_params=pltpu.CompilerParams(vmem_limit_bytes=VM2, collective_id=ident, has_side_effects=True),
        cost_estimate=pl.CostEstimate(flops=flops, bytes_accessed=2 * n * D * 12, transcendentals=0), name="sum_scatter")(e, more, *lefts, *rights)
    gd, gn, gq, gu = got[6:10]
    return got[0], got[1], (gq, gd, gu, gn), got[10], got[11], got[12]


def small_sum(pieces, shared):
    ndp, r, _ = pieces.shape
    nmp = lax.axis_size("mp")

    def kernel(x_r, o_r, land, line, send, recv, send2, recv2):
        i, z = lax.axis_index("dp"), lax.axis_index("mp")
        barrier = pltpu.get_barrier_semaphore()
        for s in range(1, ndp):
            pl.semaphore_signal(barrier, inc=1, device_id={"dp": lax.rem(i + s, ndp)}, device_id_type=MESH)
        for s in range(1, nmp):
            pl.semaphore_signal(barrier, inc=1, device_id={"mp": lax.rem(z + s, nmp)}, device_id_type=MESH)
        pl.semaphore_wait(barrier, ndp + nmp - 2)
        first = [send_to("dp", lax.rem(i + s, ndp), x_r.at[lax.rem(i + s, ndp)], land.at[i], send.at[s], recv.at[s]) for s in range(1, ndp)]
        for copy in first:
            copy.start()
        land[pl.ds(i, 1)] = x_r[pl.ds(i, 1)]
        for s in range(1, ndp):
            there = land.at[lax.rem(i - s + ndp, ndp)]
            send_to("dp", i, there, there, send.at[s], recv.at[s]).wait_recv()
        acc = land[0]
        for j in range(1, ndp):
            acc = acc + land[j]
        o_r[...] = acc
        line[pl.ds(z, 1)] = acc[None, :shared]
        second = [send_to("mp", lax.rem(z + s, nmp), line.at[z], line.at[z], send2.at[s], recv2.at[s]) for s in range(1, nmp)]
        for copy in second:
            copy.start()
        for s in range(1, nmp):
            there = line.at[lax.rem(z - s + nmp, nmp)]
            send_to("mp", z, there, there, send2.at[s], recv2.at[s]).wait_recv()
        acc = line[0]
        for j in range(1, nmp):
            acc = acc + line[j]
        o_r[:shared] = acc
        for copy in first + second:
            copy.wait_send()

    VM_ = pl.BlockSpec(memory_space=pltpu.VMEM)
    DMA = pltpu.SemaphoreType.DMA
    return pl.pallas_call(
        kernel, in_specs=[VM_], out_specs=VM_, out_shape=jax.ShapeDtypeStruct((r, 128), F32),
        scratch_shapes=[pltpu.VMEM(pieces.shape, F32), pltpu.VMEM((nmp, shared, 128), F32), DMA((ndp,)), DMA((ndp,)), DMA((nmp,)), DMA((nmp,))],
        compiler_params=pltpu.CompilerParams(vmem_limit_bytes=VM // 4, collective_id=6, has_side_effects=True), name="small_sum")(pieces)


def adam_update(weight, grad, first, second):
    first_new = beta_one * first + (1.0 - beta_one) * grad
    second_new = beta_two * second + (1.0 - beta_two) * grad * grad
    mean_hat = first_new / (1.0 - beta_one**ADAM_STEP)
    square_hat = second_new / (1.0 - beta_two**ADAM_STEP)
    new_weight = weight - rate * (mean_hat / (jnp.sqrt(square_hat) + adam_eps) + decay * weight)
    return grad, first_new, second_new, new_weight - weight


def adam_layer(layer, weights, grads, firsts, seconds, before):
    steps = 4
    blocks = [(w.shape[1] // steps, w.shape[2]) for w in weights]

    def kernel(*refs):
        ins, outs = refs[:16], refs[-16:]
        for i in range(4):
            g = ins[4 + i][...].astype(F32)
            made = adam_update(ins[i][...].astype(F32), g, ins[8 + i][...], ins[12 + i][...])
            for k in range(4):
                outs[4 * i + k][...] = made[k]

    at = lambda b: spec((None,) + b, lambda j: (layer, j, 0))
    ins = [at(b) for b in blocks] + [spec(b, lambda j: (j, 0)) for b in blocks] + [at(b) for b in blocks] * 2
    args = [*weights, *grads, *firsts, *seconds]
    alias = {}
    if before is not None:
        ins += [pl.BlockSpec(memory_space=pl.ANY)] * 16
        args += list(before)
        alias = {16 + i: i for i in range(16)}
    shapes = [jax.ShapeDtypeStruct(w.shape, F32) for w in weights for _ in range(4)]
    count = sum(w.shape[1] * w.shape[2] for w in weights)
    return pl.pallas_call(
        kernel, grid=(steps,), in_specs=ins, out_specs=[at(b) for b in blocks for _ in range(4)], out_shape=shapes,
        input_output_aliases=alias, compiler_params=pltpu.CompilerParams(vmem_limit_bytes=VM),
        cost_estimate=pl.CostEstimate(flops=20 * count, bytes_accessed=30 * count, transcendentals=0), name="adam")(*args)


def layout(lengths_row, rows):
    slots = lengths_row.shape[0]
    number = jnp.arange(slots, dtype=jnp.int32)
    ends = jnp.sum(jnp.where(number[None, :] <= number[:, None], lengths_row[None, :], 0), axis=1)
    starts = ends - lengths_row
    index = jnp.arange(rows, dtype=jnp.int32)
    inside = (index[:, None] >= starts[None, :]) & (index[:, None] < ends[None, :])
    valid = jnp.any(inside, axis=1)
    slot = jnp.sum(jnp.where(inside, number[None, :], 0), axis=1)
    first = jnp.sum(jnp.where(inside, starts[None, :], 0), axis=1)
    segment = jnp.where(valid, slot, slots + index)
    return segment, index - first, valid


class PlainLinks:
    def weights(self, shards, layer):
        wq, wd, wu, wn = [w[layer] for w in shards]
        rows = lambda v: lax.all_gather(v, "dp", axis=0, tiled=True)
        stack = lambda v: lax.all_gather(v, "dp", axis=0, tiled=False)
        return rows(wq), stack(wd), rows(wu), stack(wn)

    def share(self, v):
        return lax.psum(v, "mp")

    def owned(self, grads):
        cut = lambda g: lax.psum_scatter(g, "dp", scatter_dimension=0, tiled=True)
        gq, gd, gu, gn = grads
        return cut(gq), cut(gd)[0], cut(gu), cut(gn)[0]

    def small(self, pieces, shared):
        total = lax.psum(pieces, "dp")[lax.axis_index("dp")]
        return jnp.concatenate([lax.psum(total[:shared], "mp"), total[shared:]])

    def begin(self, shards, flat):
        return self.weights(shards, 0), lax.all_gather(flat, "dp", axis=0, tiled=False), None

    def middle(self, branch, shards):
        return self.share(branch), self.weights(shards, 1)

    def turn(self, e, more, lefts, rights, ident):
        ctx, act, h1, h2 = lefts
        gr, dmix, df = rights
        w = gr.shape[1] // lax.axis_size("dp")
        gd, low_sums = weight_grad(ctx, gr, w=w)
        gn, _ = weight_grad(act, gr, w=w)
        gq, qsum = weight_grad(h1, dmix)
        gu, usum = weight_grad(h2, df)
        return self.share(e), self.share(more), self.owned((gq, gd, gu, gn)), qsum, usum, low_sums


class ChipLinks:
    def full(self, got):
        wq, wd, wu, wn = got
        return wq.reshape(-1, wq.shape[2]), wd, wu.reshape(-1, wu.shape[2]), wn

    def begin(self, shards, flat):
        wq, wd, wu, wn = shards
        flat, wq, wu, wd = link_kernel("gather", 1, [flat, wq, wu, wd], [None, 0, 0, 0])
        return (wq.reshape(-1, wq.shape[2]), wd, wu.reshape(-1, wu.shape[2]), None), flat, (wn,)

    def middle(self, branch, shards):
        got = link_kernel("sum_gather", 2, shards, [1] * 4, branch)
        return got[4], self.full(got[:4])

    def turn(self, e, more, lefts, rights, ident):
        return sum_scatter(ident, e, more, lefts, rights)

    def small(self, pieces, shared):
        return small_sum(pieces, shared)


def flatten_small(parts):
    flat = jnp.concatenate([p.reshape(-1) for p in parts])
    return jnp.pad(flat, (0, -flat.size % 4096)).reshape(-1, 128)


def unpack_small(got, parts):
    got = got.reshape(got.shape[0], -1)
    out, at = [], 0
    for p in parts:
        piece = got[:, at:at + p.size].reshape((-1,) + p.shape)
        out.append(jnp.moveaxis(piece, 0, 2).reshape(p.shape[0], p.shape[1], -1))
        at += p.size
    return out


def body(links, tokens_in, cotangent, seq_lengths, *params):
    weights, small = params[:4], params[4:7]
    firsts, small_firsts = params[7:11], params[11:14]
    seconds, small_seconds = params[14:18], params[18:21]
    rows, D = tokens_in.shape
    segment, position, valid = layout(seq_lengths[0], rows)
    cos, sin = rope_tables(position)
    seg_col, seg_row = segment[:, None], segment[None, :]
    live = valid[:, None]
    first_full, got, later = links.begin(weights, flatten_small(small))
    qb, ub, vecs = unpack_small(got, small)
    qb = qb.reshape(LAYERS, 1, -1).astype(F32)
    ub = ub.reshape(LAYERS, 1, -1).astype(F32)
    vecs = vecs.astype(F32)

    held = [jnp.concatenate([vecs[layer, :4], vecs[layer - 1, 4:]]) for layer in range(LAYERS)]

    full, kept, extra = [first_full], [], None
    for layer in range(LAYERS):
        wq, wd, wu, wn = full[layer]
        h1, h2, mixed, act, gp, stats, *more = project(tokens_in, extra, held[layer], wq, qb[layer], cos, sin, wu, ub[layer], later if layer == 0 else None)
        if more:
            wn = more[0]
            full[0] = wq, wd, wu, wn
        ctx = attend_forward(mixed, seg_col, seg_row)
        branch = branch_out(ctx, act, wd, wn, [0, rows // 4, rows * 3 // 8, rows * 3 // 4, rows] if layer else None)
        kept.append((h1, h2, mixed, act, gp, stats, ctx, extra))
        if layer == 0:
            extra, made = links.middle(branch[0], weights)
            full.append(made)
        else:
            gout = gr = jnp.where(live, cotangent, 0).astype(BF)
            sums = None
            branch, gr = lax.optimization_barrier((branch, gr))
            branch_sum = [lax.psum(branch[0], "mp"), None, None, None]
    big, little = [None] * LAYERS, [None] * LAYERS
    for layer in reversed(range(LAYERS)):
        wq, wd, wu, wn = full[layer]
        h1, h2, mixed, act, gp, stats, ctx, extra = kept[layer]
        dctx, df = back_in(gr, gp, wd, wn)
        dmix = attend_backward(mixed, dctx, seg_col, seg_row, cos, sin)
        e, norm_sums = back_out(dmix, df, wq, wu, tokens_in, extra, held[layer], stats)
        before = 0 if layer else 2
        branch_sum[before], e = lax.optimization_barrier((branch_sum[before], e))
        at = 1 if layer else 3
        e, branch_sum[at], big[layer], qsum, usum, low_sums = links.turn(e, branch[at], (ctx, act, h1, h2), (gr, dmix, df), 3 + layer)
        little[layer] = (qsum, usum, norm_sums, low_sums if sums is None else sums)
        if layer:
            e, third = lax.optimization_barrier((e, branch[2]))
            branch_sum[2] = lax.psum(third, "mp")
        if layer:
            gout, gr, sums = norm_back(gout, e, tokens_in, extra, held[layer], stats)
    every = (vecs[0, 4:5] + vecs[0, 5:6]) + (vecs[1, 4:5] + vecs[1, 5:6])
    input_grad, output = finish(gout, e, tokens_in, kept[1][-1], branch_sum, every, live.astype(F32), stats)

    done = None
    for layer in reversed(range(LAYERS)):
        done = adam_layer(layer, weights, big[layer], firsts, seconds, done)

    ndp = lax.axis_size("dp")

    def pieces(v, width):
        v = v.reshape(-1, ndp, width // ndp)
        return jnp.moveaxis(v, 1, 0).reshape(ndp, -1)

    norms = jnp.concatenate([pieces(t[2], D) for t in little], axis=1)
    rest = [pieces(t[i], BROW) for i in (0, 1) for t in little] + [pieces(t[3], D) for t in little]
    rest = jnp.concatenate(rest, axis=1)
    shared, count = norms.shape[1] // 128, rest.shape[1]
    rest = jnp.pad(rest, ((0, 0), (0, -count % 1024)))
    total = links.small(jnp.concatenate([norms, rest], axis=1).reshape(ndp, -1, 128), shared)
    norms, rest = total[:shared].reshape(LAYERS, 4, -1), total[shared:].reshape(-1)
    small_grads, at = [], 0
    for p in small[:2]:
        small_grads.append(rest[at:at + p.size].reshape(p.shape))
        at += p.size
    tops_sum = rest[at:count].reshape(LAYERS, 1, -1)
    small_grads.append(jnp.concatenate([norms, tops_sum, tops_sum], axis=1))
    small_out = []
    for p, g, first, second in zip(small, small_grads, small_firsts, small_seconds):
        small_out += adam_update(p.astype(F32), g, first, second)
    return (output, input_grad, *done, *small_out)


def solution(mesh):
    rows_dp = P("dp", None)
    wide, tall, vec = P(None, "dp", "mp"), P(None, "mp", "dp"), P(None, None, "dp")
    group = (wide, tall, wide, tall, tall, tall, vec)
    return jax.shard_map(
        functools.partial(body, ChipLinks() if dict(mesh.shape) == {"dp": 8, "mp": 4} else PlainLinks()),
        mesh=mesh,
        in_specs=(rows_dp,) * 3 + group * 3,
        out_specs=(rows_dp,) * 2 + tuple(s for s in group for _ in range(4)),
        check_vma=False,
    )
```
